32 devices in a mesh: dp: 8 (over z, x), tensor: 4 (over y, core).
Axes of the slice: x: 2, y: 2, z: 4, core: 2. Of those that a mesh axis runs over, the one named last changes fastest.
Arguments:
- inputs: bfloat16 [8192, 2048], P('dp'), may hold values from -8 to 8
- gain_attn: float32 [2048], replicated, may hold values from 0.5 to 1.5
- w_query: bfloat16 [2048, 2048], P(None, 'tensor'), may hold values from -0.125 to 0.125
- w_key: bfloat16 [2048, 2048], P(None, 'tensor'), may hold values from -0.125 to 0.125
- w_value: bfloat16 [2048, 2048], P(None, 'tensor'), may hold values from -0.125 to 0.125
- gate_logit: float32 [16], P('tensor'), may hold values from -1.5 to 1.5
- w_out: bfloat16 [2048, 2048], P('tensor'), may hold values from -0.25 to 0.25
- gain_mlp: float32 [2048], replicated, may hold values from 0.5 to 1.5
- w_up: bfloat16 [2048, 8192], P(None, 'tensor'), may hold values from -0.125 to 0.125
- w_down: bfloat16 [8192, 2048], P('tensor'), may hold values from -0.0625 to 0.0625
- seg_parent: int32 [16], replicated, may hold values from -1 to 15, as said below
- out_grad: bfloat16 [8192, 2048], P('dp'), may hold values from -6 to 6
Outputs:
- outputs: bfloat16 [8192, 2048], P('dp')
- input_grad: bfloat16 [8192, 2048], P('dp')
- gain_attn_grad: float32 [2048], P('dp')
- w_query_grad: float32 [2048, 2048], P('dp', 'tensor')
- w_key_grad: float32 [2048, 2048], P('dp', 'tensor')
- w_value_grad: float32 [2048, 2048], P('dp', 'tensor')
- gate_grad: float32 [16], P('tensor')
- w_out_grad: float32 [2048, 2048], P('tensor', 'dp')
- gain_mlp_grad: float32 [2048], P('dp')
- w_up_grad: float32 [2048, 8192], P('dp', 'tensor')
- w_down_grad: float32 [8192, 2048], P('tensor', 'dp')
The draws below stay inside these ranges and needn't reach their ends.
Inputs may be any that keep to these rules, and one draw needn't show every extreme that they name: `seg_parent`: segments form trees of 16 segments: a chain of 4 trunk segments whose first has parent -1, 4 branch segments whose parent is the trunk's last, and 2 leaves whose parent is one branch, for each branch. Segments of a tree lie on any devices; segment 16 - 1 is the last trunk segment of some tree.
All inputs are finite; a program needn't handle non-finite values.
Results may differ from the reference program's by a relative error of at most 0.015.
Values sent between devices are 32-bit elements; how exact they have to be, the bound alone decides.
A program may use at most 256 MiB of HBM per device.

```python
from functools import partial
import jax
import jax.numpy as jnp
from jax import lax

D = 2048
H = 16
DH = 128
FF = 8192
SEG = 512
TRUNK = 4
BRANCHES = 4
LEAVES = 2
DEPTH = 5
NSEG = 16
TOKENS = 8192


def draw_inputs(key, part):
    noise_key, common_key = jax.random.split(key)
    noise = jax.random.normal(noise_key, (NSEG, SEG, D), jnp.float32)
    common = 0.8 * jax.random.normal(common_key, (NSEG, 1, D), jnp.float32)
    return jnp.clip(noise + common, -8.0, 8.0).reshape(TOKENS, D).astype(jnp.bfloat16)


def draw_seg_parent(key, part):
    tree_size = TRUNK + BRANCHES + BRANCHES * LEAVES
    slot_ids = jnp.arange(NSEG, dtype=jnp.int32)
    within = slot_ids % tree_size
    anchor = slot_ids - within
    branch_index = (within - TRUNK - BRANCHES) // LEAVES
    parent_role = jnp.where(within < TRUNK, within - 1, jnp.where(within < TRUNK + BRANCHES, TRUNK - 1, TRUNK + branch_index))
    parent_index = jnp.where(parent_role < 0, -1, anchor + parent_role).astype(jnp.int32)
    shuffled = jax.random.permutation(key, NSEG).astype(jnp.int32)
    displaced = shuffled[TRUNK - 1]
    placed = jnp.where(shuffled == NSEG - 1, displaced, shuffled).astype(jnp.int32)
    placed = placed.at[TRUNK - 1].set(NSEG - 1)
    parent_slot = jnp.where(parent_index < 0, -1, placed[jnp.maximum(parent_index, 0)]).astype(jnp.int32)
    return jnp.zeros((NSEG,), jnp.int32).at[placed].set(parent_slot)


def with_spikes(array, own_key, source, target, blocks, factor):
    owner, partner = [(jnp.arange(array.shape[axis_at]) // (array.shape[axis_at] // blocks)).reshape([-1 if axis == axis_at else 1 for axis in range(array.ndim)]) for axis_at in (source, target)]
    chosen = jax.random.permutation(own_key, blocks)[partner]
    strong = (owner == chosen) | (owner == (partner + blocks // 2) % blocks)
    return jnp.where(strong, factor * array, array)


def levels(rng, shape, shards, least, largest):
    gain, own = 1.0, jax.random.fold_in(rng, 6)
    for dim, shards_of in shards:
        steps = jnp.exp(jax.random.uniform(jax.random.fold_in(own, dim), (shards_of,), jnp.float32, least / len(shards), largest / len(shards)))
        gain = gain * jnp.repeat(steps, shape[dim] // shards_of).reshape([-1 if axis == dim else 1 for axis in range(len(shape))])
    return gain


def normal_values(stream_key, shape, width, reach, cuts=(), held_as=jnp.bfloat16):
    array = jax.random.normal(stream_key, shape, jnp.float32) * width
    if len(cuts) > 0:
        array = levels(stream_key, shape, cuts, -0.22, 0.18) * array
    return jnp.clip(array, min=-reach, max=reach).astype(held_as)


def gaussian_with(own_key, dims, deviation, bound, pieces, heavy, kind=jnp.bfloat16):
    array = deviation * jax.random.normal(own_key, dims, jnp.float32)
    if pieces:
        array = array * levels(own_key, dims, pieces, -0.22, 0.18)
    return jnp.clip(with_spikes(array, jax.random.fold_in(own_key, 3), *heavy), -bound, bound).astype(kind)


def setup_inputs(seed: int = 0) -> dict:
    key_of = jax.random.split(jax.random.key(seed), 13)
    return {
        "inputs": draw_inputs(jax.random.fold_in(key_of[12], 71), 0),
        "gain_attn": jnp.clip(1.0 + 0.1 * jax.random.normal(key_of[1], (D,), jnp.float32), 0.5, 1.5),
        "w_query": normal_values(key_of[2], (D, H * DH), D ** -0.5, 0.125, ((1, 4),)),
        "w_key": normal_values(key_of[3], (D, H * DH), D ** -0.5, 0.125, ((1, 4),)),
        "w_value": normal_values(key_of[4], (D, H * DH), D ** -0.5, 0.125, ((1, 4),)),
        "gate_logit": jnp.clip(jax.random.uniform(key_of[5], (H,), jnp.float32, -1.5, 1.5) * levels(key_of[5], (H,), ((0, 4),), -0.4, 0.0), -1.5, 1.5),
        "w_out": normal_values(key_of[6], (H * DH, D), (H * DH // 4) ** -0.5, 0.25, ((0, 4),)),
        "gain_mlp": jnp.clip(1.0 + 0.1 * jax.random.normal(key_of[7], (D,), jnp.float32), 0.5, 1.5),
        "w_up": normal_values(key_of[8], (D, FF), D ** -0.5, 0.125, ((1, 4),)),
        "w_down": normal_values(key_of[9], (FF, D), FF ** -0.5, 0.0625, ((0, 4),)),
        "seg_parent": draw_seg_parent(jax.random.fold_in(key_of[12], 71), 0),
        "out_grad": gaussian_with(key_of[11], (TOKENS, D), 1.0, 6.0, ((0, 8),), (0, 1, 8, 2.0)),
    }


@jax.custom_vjp
def low(v):
    return lax.optimization_barrier(v.astype(jnp.bfloat16)).astype(jnp.float32)

@jax.custom_vjp
def low_back(v):
    return v

def low_keep(v):
    return (low(v), None)

def low_pass(kept, grad):
    return (grad,)

def back_keep(v):
    return (v, None)

def back_low(kept, grad):
    return (low(grad),)
low.defvjp(low_keep, low_pass)
low_back.defvjp(back_keep, back_low)
topmost_level = lax.Precision.HIGHEST
norm_eps = 1e-06

def feature_map(values):
    return jnp.where(values > 0, values + 1.0, jnp.exp(jnp.minimum(values, 0.0)))

def ancestor_table(seg_parent):
    seg_total = seg_parent.shape[0]
    columns = jnp.arange(seg_total, dtype=jnp.int32)
    current = seg_parent.astype(jnp.int32)
    lineage_table = jnp.zeros((seg_total, seg_total), jnp.float32)
    for depth_level in range(DEPTH):
        onehot = current[:, None] == columns[None, :]
        lineage_table = lineage_table + onehot.astype(jnp.float32)
        lifted = lax.optimization_barrier(jnp.sum(jnp.where(onehot, seg_parent[None, :].astype(jnp.int32), 0), axis=1)).astype(jnp.int32)
        current = jnp.where(current >= 0, lifted, -1).astype(jnp.int32)
    return lineage_table

def matmul(left_side, right_side):
    return jnp.dot(left_side, right_side, precision=topmost_level, preferred_element_type=jnp.float32)

def rms_scale(values, gain_vec):
    return values * lax.rsqrt(lax.optimization_barrier(jnp.mean(values * values, axis=-1, keepdims=True)) + norm_eps) * gain_vec

def forward(lineage_table, input_float, gain_attn, w_query, w_key, w_value, gate_logit, w_out, gain_mlp, w_up, w_down):
    hidden_attn = low(rms_scale(input_float, gain_attn))

    def project(weight):
        return low_back(low(matmul(hidden_attn, weight))).reshape(NSEG, SEG, H, DH)
    query_heads = project(w_query)
    key_heads = project(w_key)
    value_heads = project(w_value)
    key_feat = feature_map(key_heads)
    mem_delta = jnp.einsum('nshd,nshe->nhde', key_feat, value_heads, precision=topmost_level)
    key_feature_sum = lax.optimization_barrier(jnp.sum(key_feat, axis=1))
    memory = jnp.einsum('mn,nhde->mhde', lineage_table, mem_delta, precision=topmost_level)
    memory_norm_term = jnp.einsum('zr,rqp->zqp', lineage_table, key_feature_sum, precision=topmost_level)
    gate_open = jax.nn.sigmoid(gate_logit)[None, :, None]
    causal = jnp.arange(SEG)[:, None] >= jnp.arange(SEG)[None, :]

    def segment(operands):
        queries, key_rows, value_rows, mem_state, norm_state = operands
        scores = low_back(jnp.einsum('shd,thd->hst', queries, key_rows, precision=topmost_level) * DH ** (-0.5))
        probs = low(jax.nn.softmax(jnp.where(causal[None], scores, -1e+30), axis=-1))
        local = jnp.einsum('hst,thd->shd', probs, value_rows, precision=topmost_level)
        query_feat = feature_map(queries)
        numerator = jnp.einsum('shd,hde->she', query_feat, mem_state, precision=topmost_level)
        denominator = jnp.einsum('shd,hd->sh', query_feat, norm_state, precision=topmost_level)[..., None] + 1.0
        return gate_open * (numerator / denominator) + (1.0 - gate_open) * local
    mixed = lax.map(jax.checkpoint(segment), (query_heads, key_heads, value_heads, memory, memory_norm_term))
    mixed_low = low_back(low(mixed.reshape(NSEG * SEG, H * DH)))
    residual = input_float + low_back(matmul(mixed_low, w_out))
    hidden_mlp = low(rms_scale(residual, gain_mlp))
    preact = low_back(matmul(hidden_mlp, w_up))
    activated = low(jax.nn.gelu(preact, approximate=True))
    return residual + matmul(activated, w_down)

def reference(inputs, gain_attn, w_query, w_key, w_value, gate_logit, w_out, gain_mlp, w_up, w_down, seg_parent, out_grad):
    lineage_table = ancestor_table(seg_parent)
    primals = (inputs.astype(jnp.float32), gain_attn.astype(jnp.float32), w_query.astype(jnp.float32), w_key.astype(jnp.float32), w_value.astype(jnp.float32), gate_logit.astype(jnp.float32), w_out.astype(jnp.float32), gain_mlp.astype(jnp.float32), w_up.astype(jnp.float32), w_down.astype(jnp.float32))
    result, pullback = jax.vjp(partial(forward, lineage_table), *primals)
    grads = pullback(out_grad.astype(jnp.float32))
    return (result.astype(jnp.bfloat16), grads[0].astype(jnp.bfloat16), grads[1], grads[2], grads[3], grads[4], grads[5], grads[6], grads[7], grads[8], grads[9])
```

```python
import jax
import jax.numpy as jnp
from jax import lax
from jax.sharding import PartitionSpec as P

DH = 128
SEG = 512
DEPTH = 5
EPS = 1e-06

F32 = jnp.float32
BF16 = jnp.bfloat16


def feature_map(values):
    return jnp.where(values > 0, values + 1.0, jnp.exp(jnp.minimum(values, 0.0)))


def feature_slope(values):
    return jnp.where(values > 0, 1.0, jnp.exp(jnp.minimum(values, 0.0)))


def gelu_tanh(values):
    return jax.nn.gelu(values, approximate=True)


def ancestor_table(seg_parent):
    seg_total = seg_parent.shape[0]
    columns = jnp.arange(seg_total, dtype=jnp.int32)
    current = seg_parent
    lineage_table = jnp.zeros((seg_total, seg_total), F32)
    for _ in range(DEPTH):
        onehot = current[:, None] == columns[None, :]
        lineage_table = lineage_table + onehot.astype(F32)
        lifted = jnp.sum(jnp.where(onehot, seg_parent[None, :], 0), axis=1)
        current = jnp.where(current >= 0, lifted, -1)
    return lineage_table


def dot(a, b):
    return jnp.dot(a, b, preferred_element_type=F32)


def dot_t(a, b):
    return lax.dot_general(a, b, (((0,), (0,)), ((), ())), preferred_element_type=F32)


def dot_nt(a, b):
    return lax.dot_general(a, b, (((1,), (1,)), ((), ())), preferred_element_type=F32)


def body(
    inputs,
    gain_attn,
    w_query,
    w_key,
    w_value,
    gate_logit,
    w_out,
    gain_mlp,
    w_up,
    w_down,
    seg_parent,
    out_grad,
):
    tokens, width = inputs.shape
    half = tokens // 2
    segs = tokens // SEG
    heads = w_query.shape[1] // DH
    units = w_up.shape[1]
    scale = DH ** (-0.5)
    dp = lax.axis_size("dp")
    tn = lax.axis_size("tensor")
    depth = dp // 2
    rows = width // dp
    di = lax.axis_index("dp")
    ti = lax.axis_index("tensor")
    core = ti % 2
    xi = di % 2
    zi = di // 2

    one = jnp.where(seg_parent[0] < tokens * dp, 1.0, 2.0)

    def low_after_wire(v):
        return (v * one).astype(BF16)

    def swap_core(v):
        return lax.ppermute(v, "tensor", [(i, i ^ 1) for i in range(tn)])

    def swap_y(v):
        return lax.ppermute(v, "tensor", [(i, i ^ 2) for i in range(tn)])

    def swap_x(v):
        return lax.ppermute(v, "dp", [(i, i ^ 1) for i in range(dp)])

    z_groups = [[z * 2 + x for z in range(depth)] for x in range(2)]

    def scatter_z(v):
        return lax.psum_scatter(v, "dp", scatter_dimension=0, axis_index_groups=z_groups, tiled=True)

    def pick(v, index, axis):
        size = v.shape[axis] // 2
        return lax.dynamic_slice_in_dim(v, index * size, size, axis)

    def place(own, other, index, axis):
        return jnp.where(
            index == 0,
            jnp.concatenate([own, other], axis),
            jnp.concatenate([other, own], axis),
        )

    def tensor_sum(lhs, weight_dot, chunks=1):
        out = []
        step = half // chunks
        for c in range(chunks):
            lo = c * step
            send = swap_core(weight_dot(lhs[half + lo : half + lo + step]))
            part = weight_dot(lhs[lo : lo + step]) + send
            out.append(part + swap_y(part))
        return out

    x_own = pick(inputs, core, 0).astype(F32)
    x_oth = pick(inputs, 1 - core, 0).astype(F32)
    og_own = pick(out_grad, core, 0)
    og_oth = pick(out_grad, 1 - core, 0)
    og = jnp.concatenate([og_own, og_oth], 0)

    def inv_rms(v):
        return lax.rsqrt(jnp.mean(v * v, axis=-1, keepdims=True) + EPS)

    inv_own = inv_rms(x_own)
    inv_oth = inv_rms(x_oth)
    h1 = jnp.concatenate(
        [
            (x_own * inv_own * gain_attn).astype(BF16),
            (x_oth * inv_oth * gain_attn).astype(BF16),
        ],
        0,
    )

    def heads_of(matrix):
        return dot(h1, matrix).astype(BF16).reshape(segs, SEG, heads, DH)

    kh = heads_of(w_key)
    vh = heads_of(w_value)
    kf = kh.astype(F32)
    sk = feature_map(kf)
    sk16 = sk.astype(BF16)
    delta = jnp.einsum("nshd,nshe->nhde", sk16, vh, preferred_element_type=F32)
    zsum = jnp.sum(sk, axis=1)

    lineage = ancestor_table(seg_parent)
    sub = segs // 2

    def seg_ids(z, x, c):
        base = (z * 2 + x) * segs
        ids = jnp.arange(sub, dtype=jnp.int32)
        return jnp.concatenate([base + c * sub + ids, base + (1 - c) * sub + ids])

    mine = seg_ids(zi, xi, core)

    def pack(big, small):
        return jnp.concatenate([big.reshape(-1, DH), small.reshape(-1, DH)], 0)

    def unpack(v):
        n = segs * heads
        return v[: n * DH].reshape(segs, heads, DH, DH), v[n * DH :].reshape(segs, heads, DH)

    def zup(v):
        return lax.ppermute(v, "dp", [(i, i + 2) for i in range(dp - 2)])

    def zdn(v):
        return lax.ppermute(v, "dp", [(i + 2, i) for i in range(dp - 2)])

    def exchange(block, table):
        if depth == 4:
            xs = [swap_x(block)]
            r1 = zup(block)
            d1 = zdn(block)
            r2 = zup(r1)
            d2 = zdn(d1)
            r3 = zup(r2)
            d3 = zdn(d2)
            s1 = jnp.where(zi <= 1, d1, r1)
            s2 = jnp.where(zi == 0, d2, jnp.where(zi == 1, r1, jnp.where(zi == 2, d1, r2)))
            s3 = jnp.where(zi == 0, d3, jnp.where(zi == 1, d2, jnp.where(zi == 2, r2, r3)))
            xs = xs + [swap_x(s) for s in (s1, s2, s3)]
            q1 = jnp.where(zi <= 1, zi + 1, zi - 1)
            q2 = jnp.where(zi == 0, 2, jnp.where(zi == 1, 0, jnp.where(zi == 2, 3, 1)))
            q3 = jnp.where(zi == 0, 3, jnp.where(zi == 1, 3, 0))
            zs = [zi, q1, q2, q3]
            blocks = [block, s1, s2, s3]
            pairs = [(b, seg_ids(q, xi, core)) for b, q in zip(blocks, zs)]
            pairs += [(b, seg_ids(q, 1 - xi, core)) for b, q in zip(xs, zs)]
        else:
            every = lax.all_gather(block, "dp", axis=0, tiled=False)
            pairs = [(every[d], seg_ids(d // 2, d % 2, core)) for d in range(dp)]
        big = 0.0
        small = 0.0
        mine_rows = jnp.take(table, mine, axis=0)
        for b, ids in pairs:
            weight = jnp.take(mine_rows, ids, axis=1)
            bb, bs = unpack(b)
            for n in range(segs):
                big = big + weight[:, n][:, None, None, None] * bb[n][None]
                small = small + weight[:, n][:, None, None] * bs[n][None]
        return big, small

    memory, zin = exchange(pack(delta, zsum), lineage)

    og_b_own = swap_x(og_own.astype(F32))
    x_b_own = swap_x(x_own)

    qh = heads_of(w_query)
    qf = qh.astype(F32)
    causal = jnp.arange(SEG)[:, None] >= jnp.arange(SEG)[None, :]
    scores = jnp.einsum("nshd,nthd->nhst", qh, kh, preferred_element_type=F32) * scale
    masked = jnp.where(causal, scores, -1e30)
    row_top = jnp.max(masked, axis=-1, keepdims=True)
    lse = row_top + jnp.log(jnp.sum(jnp.exp(masked - row_top), axis=-1, keepdims=True))
    prob_low = jnp.exp(masked - lse).astype(BF16)
    local = jnp.einsum("nhst,nthd->nshd", prob_low, vh, preferred_element_type=F32)
    sq = feature_map(qf)
    sq16 = sq.astype(BF16)

    wu_keep = pick(w_up, xi, 1)
    wu_send = pick(w_up, 1 - xi, 1)
    wd_keep = pick(w_down, xi, 0)
    wd_send = pick(w_down, 1 - xi, 0)
    ug_keep = dot_nt(og, wd_keep)
    ug_send = dot_nt(og, wd_send)

    mem16 = memory.astype(BF16)
    den = jnp.einsum("nshd,nhd->nsh", sq, zin)[..., None] + 1.0
    retrieved = jnp.einsum("nshd,nhde->nshe", sq16, mem16, preferred_element_type=F32) / den
    gate = jax.nn.sigmoid(gate_logit)
    g4 = gate[None, None, :, None]
    a16 = (g4 * retrieved + (1.0 - g4) * local).reshape(tokens, heads * DH).astype(BF16)

    resid = x_own + jnp.concatenate(tensor_sum(a16, lambda l: dot(l, w_out), 2), 0)
    inv_mlp = inv_rms(resid)
    normed = resid * inv_mlp
    h2 = jnp.concatenate(
        [(normed * gain_mlp).astype(BF16), (swap_core(normed) * gain_mlp).astype(BF16)], 0
    )

    pre_send = dot(h2, wu_send)
    act_send = gelu_tanh(pre_send).astype(BF16)
    act_b = [swap_x(p.astype(F32)) for p in jnp.split(act_send, 2, axis=1)]
    pre_keep = dot(h2, wu_keep)
    act_keep = gelu_tanh(pre_keep).astype(BF16)
    dp_send = jax.vjp(gelu_tanh, pre_send)[1](ug_send)[0].astype(BF16)
    dp_keep = jax.vjp(gelu_tanh, pre_keep)[1](ug_keep)[0].astype(BF16)

    dh2 = jnp.concatenate(
        tensor_sum(
            jnp.concatenate([dp_keep, dp_send], 1),
            lambda l: dot_nt(l[:, : units // 2], wu_keep) + dot_nt(l[:, units // 2 :], wu_send),
            2,
        ),
        0,
    )

    og_b = jnp.concatenate(
        [low_after_wire(og_b_own), low_after_wire(swap_core(og_b_own))], 0
    )
    down = []
    for k, p in zip(jnp.split(act_keep, 2, axis=1), act_b):
        down.append(scatter_z(dot_t(og, k) + dot_t(og_b, low_after_wire(p))))
    down = jnp.concatenate(down, 1)
    down_mine = pick(down, xi, 0)
    down_theirs = swap_x(pick(down, 1 - xi, 0))
    w_down_grad = place(down_mine, down_theirs, xi, 1).T

    def columns_of(v, x):
        return lax.dynamic_index_in_dim(
            v.reshape(tokens, depth, 2, rows), x, 2, keepdims=False
        ).reshape(tokens, depth * rows)

    h2_keep = columns_of(h2, xi)
    h2_send = columns_of(h2, 1 - xi)
    to_send = swap_x(dot_t(h2_send, dp_keep))
    to_keep = swap_x(dot_t(h2_send, dp_send))
    up_send = scatter_z(dot_t(h2_keep, dp_send) + to_send)
    up_keep = scatter_z(dot_t(h2_keep, dp_keep) + to_keep)
    w_up_grad = place(up_keep, up_send, xi, 1)

    mlp_out = jnp.concatenate(
        tensor_sum(
            jnp.concatenate([act_keep, act_send], 1),
            lambda l: dot(l[:, : units // 2], wd_keep) + dot(l[:, units // 2 :], wd_send),
            2,
        ),
        0,
    )
    out_own = (resid + mlp_out).astype(BF16)
    outputs = place(out_own, low_after_wire(swap_core(out_own.astype(F32))), core, 0)

    gs = dh2 * gain_mlp
    dresid = (
        og_own.astype(F32)
        + inv_mlp * gs
        - resid * inv_mlp * inv_mlp * inv_mlp * jnp.mean(gs * resid, axis=-1, keepdims=True)
    )
    gain_mlp_part = jnp.sum(dh2 * resid * inv_mlp, axis=0)
    dr_own = dresid.astype(BF16)
    dr = jnp.concatenate([dr_own, low_after_wire(swap_core(dr_own.astype(F32)))], 0)

    da = dot_nt(dr, w_out).astype(BF16).reshape(segs, SEG, heads, DH)
    daf = da.astype(F32)
    gate_part = jnp.sum(daf * (retrieved - local), axis=(0, 1, 3)) * gate * (1.0 - gate)

    dnum = g4 * daf / den
    dden = -jnp.sum(dnum * retrieved, axis=-1)
    dnum16 = dnum.astype(BF16)
    dmem = jnp.einsum("nshd,nshe->nhde", sq16, dnum16, preferred_element_type=F32)
    dzin = jnp.einsum("nshd,nsh->nhd", sq, dden)
    ddelta, dzsum = exchange(pack(dmem, dzin), lineage.T)

    keep_s = (1.0 - gate)[None, :, None, None]
    dprobs = keep_s * jnp.einsum("nshd,nthd->nhst", da, vh, preferred_element_type=F32)
    scores2 = jnp.einsum("nshd,nthd->nhst", qh, kh, preferred_element_type=F32) * scale
    probs = jnp.exp(jnp.where(causal, scores2, -1e30) - lse)
    p16 = probs.astype(BF16)
    ds16 = (probs * (dprobs - jnp.sum(dprobs * probs, axis=-1, keepdims=True))).astype(BF16)
    dv = (1.0 - g4) * jnp.einsum("nhst,nshd->nthd", p16, da, preferred_element_type=F32)
    dq = jnp.einsum("nhst,nthd->nshd", ds16, kh, preferred_element_type=F32) * scale
    dk = jnp.einsum("nhst,nshd->nthd", ds16, qh, preferred_element_type=F32) * scale
    dsq = (
        jnp.einsum("nshe,nhde->nshd", dnum16, mem16, preferred_element_type=F32)
        + dden[..., None] * zin[:, None]
    )
    dq = dq + dsq * feature_slope(qf)

    g_out_send = swap_x(dot_t(columns_of(dr, 1 - xi), a16))
    w_out_rows = scatter_z(dot_t(columns_of(dr, xi), a16) + g_out_send)
    w_out_grad = w_out_rows.T

    dd16 = ddelta.astype(BF16)
    dsk = (
        jnp.einsum("nshe,nhde->nshd", vh, dd16, preferred_element_type=F32) + dzsum[:, None]
    )
    dk = dk + dsk * feature_slope(kf)
    dv = dv + jnp.einsum("nshd,nhde->nshe", sk16, dd16, preferred_element_type=F32)

    flat = (tokens, heads * DH)
    dq16 = dq.reshape(flat).astype(BF16)
    dk16 = dk.reshape(flat).astype(BF16)
    dv16 = dv.reshape(flat).astype(BF16)

    d_keep = jnp.concatenate([pick(v, xi, 1) for v in (dq16, dk16, dv16)], 1)
    d_send = jnp.concatenate([pick(v, 1 - xi, 1) for v in (dq16, dk16, dv16)], 1)
    d_b = low_after_wire(swap_x(d_send.astype(F32)))
    x_b_oth = swap_core(x_b_own)
    h1_b = jnp.concatenate(
        [(v * inv_rms(v) * gain_attn).astype(BF16) for v in (x_b_own, x_b_oth)], 0
    )
    qkv = scatter_z(dot_t(h1, d_keep) + dot_t(h1_b, d_b))
    qkv_mine = pick(qkv, xi, 0)
    qkv_theirs = swap_x(pick(qkv, 1 - xi, 0))
    n3 = qkv.shape[1] // 3
    w_query_grad, w_key_grad, w_value_grad = (
        place(qkv_mine[:, i * n3 : (i + 1) * n3], qkv_theirs[:, i * n3 : (i + 1) * n3], xi, 1)
        for i in range(3)
    )

    n1 = heads * DH
    dh1 = jnp.concatenate(
        tensor_sum(
            jnp.concatenate([dq16, dk16, dv16], 1),
            lambda l: dot_nt(l[:, :n1], w_query)
            + dot_nt(l[:, n1 : 2 * n1], w_key)
            + dot_nt(l[:, 2 * n1 :], w_value),
            2,
        ),
        0,
    )
    gs1 = dh1 * gain_attn
    dx = (
        dresid
        + inv_own * gs1
        - x_own * inv_own * inv_own * inv_own * jnp.mean(gs1 * x_own, axis=-1, keepdims=True)
    )
    gain_attn_part = jnp.sum(dh1 * x_own * inv_own, axis=0)
    dx_own = dx.astype(BF16)
    input_grad = place(dx_own, low_after_wire(swap_core(dx_own.astype(F32))), core, 0)

    gains = jnp.concatenate([gain_attn_part, gain_mlp_part])
    small = jnp.concatenate([gains + swap_core(gains), jnp.pad(gate_part, (0, DH - heads))])
    bit = 1
    while bit < dp:
        small = small + lax.ppermute(small, "dp", [(i, i ^ bit) for i in range(dp)])
        bit *= 2
    gain_attn_grad = lax.dynamic_slice_in_dim(small, di * rows, rows, 0)
    gain_mlp_grad = lax.dynamic_slice_in_dim(small, width + di * rows, rows, 0)
    gate_grad = small[2 * width : 2 * width + heads]

    return (
        outputs,
        input_grad,
        gain_attn_grad,
        w_query_grad,
        w_key_grad,
        w_value_grad,
        gate_grad,
        w_out_grad,
        gain_mlp_grad,
        w_up_grad,
        w_down_grad,
    )


def solution(mesh):
    placed = (
        P("dp", None),
        P(),
        P(None, "tensor"),
        P(None, "tensor"),
        P(None, "tensor"),
        P("tensor"),
        P("tensor", None),
        P(),
        P(None, "tensor"),
        P("tensor", None),
        P(),
        P("dp", None),
    )
    return jax.shard_map(
        body,
        mesh=mesh,
        in_specs=placed,
        out_specs=(
            P("dp", None),
            P("dp", None),
            P("dp"),
            P("dp", "tensor"),
            P("dp", "tensor"),
            P("dp", "tensor"),
            P("tensor"),
            P("tensor", "dp"),
            P("dp"),
            P("dp", "tensor"),
            P("tensor", "dp"),
        ),
        check_vma=False,
    )
```

```python
import functools

import jax
import jax.numpy as jnp
from jax import lax
from jax.experimental import pallas as pl
from jax.experimental.pallas import tpu as pltpu
from jax.sharding import PartitionSpec as P

DH = 128
SEG = 512
DEPTH = 5
EPS = 1e-06

F32 = jnp.float32
BF16 = jnp.bfloat16

AG_CHUNKS = 2
SUM_CHUNKS = 2
ACT_PIECES = (256, 256, 512)
UP_PIECES = (512, 512, 512, 512)


def feature_map(values):
    return jnp.where(values > 0, values + 1.0, jnp.exp(jnp.minimum(values, 0.0)))


def feature_slope(values):
    return jnp.where(values > 0, 1.0, jnp.exp(jnp.minimum(values, 0.0)))


def ancestor_table(seg_parent):
    seg_total = seg_parent.shape[0]
    columns = jnp.arange(seg_total, dtype=jnp.int32)
    current = seg_parent
    lineage_table = jnp.zeros((seg_total, seg_total), F32)
    for _ in range(DEPTH):
        onehot = current[:, None] == columns[None, :]
        lineage_table = lineage_table + onehot.astype(F32)
        lifted = jnp.sum(jnp.where(onehot, seg_parent[None, :], 0), axis=1)
        current = jnp.where(current >= 0, lifted, -1)
    return lineage_table


def dot(a, b):
    return jnp.dot(a, b, preferred_element_type=F32)


def dot_t(a, b):
    return lax.dot_general(a, b, (((0,), (0,)), ((), ())), preferred_element_type=F32)


def dot_nt(a, b):
    return lax.dot_general(a, b, (((1,), (1,)), ((), ())), preferred_element_type=F32)


def after(value, *earlier):
    return lax.optimization_barrier((value, earlier))[0]


def nbytes(*arrays):
    return sum(a.size * a.dtype.itemsize for a in arrays)


def copy_kernel(ids_ref, in_ref, out_ref):
    out_ref[...] = in_ref[...]


def block_columns(v, ids, size):
    if size % 128:
        return jnp.concatenate([lax.dynamic_slice_in_dim(v, i * size, size, 1) for i in ids], 1)
    height, width = v.shape
    return pl.pallas_call(
        copy_kernel,
        out_shape=jax.ShapeDtypeStruct(v.shape, v.dtype),
        grid_spec=pltpu.PrefetchScalarGridSpec(
            num_scalar_prefetch=1,
            grid=(width // size,),
            in_specs=[pl.BlockSpec((height, size), lambda k, ids: (0, ids[k]))],
            out_specs=pl.BlockSpec((height, size), lambda k, ids: (0, k)),
        ),
        cost_estimate=pl.CostEstimate(flops=0, transcendentals=0, bytes_accessed=2 * nbytes(v)),
    )(jnp.stack(ids), v)


SMEM = pl.BlockSpec(memory_space=pltpu.SMEM)


def causal_mask():
    row = lax.broadcasted_iota(jnp.int32, (SEG, SEG), 0)
    col = lax.broadcasted_iota(jnp.int32, (SEG, SEG), 1)
    return row >= col


def softmax_rows(q, k, scale):
    scores = dot_nt(q, k) * scale
    scores = jnp.where(causal_mask(), scores, -1e30)
    top = jnp.max(scores, axis=-1, keepdims=True)
    e = jnp.exp(scores - top)
    return e * (1.0 / jnp.sum(e, axis=-1, keepdims=True))


def head_part(heads, p):
    s, h = p // heads, p % heads
    return pl.ds(pl.multiple_of(s * SEG, SEG), SEG), pl.ds(pl.multiple_of(h * DH, DH), DH)


def matrix_part(p):
    return pl.ds(pl.multiple_of(p * DH, DH), DH)


def weighted(w_ref, p, heads, segs, blocks_ref):
    s, h = p // heads, p % heads
    pairs = segs * heads
    big = jnp.zeros((DH, DH), F32)
    small = jnp.zeros((1, DH), F32)
    for d in range(blocks_ref.shape[0]):
        for n in range(segs):
            w = w_ref[s, d * segs + n]
            o = n * heads + h
            big = big + w * blocks_ref[d, matrix_part(o), :]
            small = small + w * blocks_ref[d, pl.ds(pairs * DH + o, 1), :]
    return big, small


def spread_order(dp):
    low = [0]
    for b in reversed(range(1, dp.bit_length() - 1)):
        low = low + [v ^ (1 << b) for v in low]
    return low + [v ^ 1 for v in low]


def greet(dp):
    me = lax.axis_index("dp")
    barrier = pltpu.get_barrier_semaphore()
    bits = dp.bit_length() - 1
    for b in range(bits):
        pl.semaphore_signal(
            barrier,
            inc=1,
            device_id={"dp": me ^ (1 << b)},
            device_id_type=pl.DeviceIdType.MESH,
        )
    pl.semaphore_wait(barrier, bits)


def spread(dp, blocks_ref, send_sem, recv_sem, compute):
    me = lax.axis_index("dp")
    slot = {j: k for k, j in enumerate(spread_order(dp))}
    copies = {}

    def send(j, mask):
        to = j ^ mask
        k = slot[to]
        copies[to] = pltpu.make_async_remote_copy(
            src_ref=blocks_ref.at[slot[j]],
            dst_ref=blocks_ref.at[k],
            send_sem=send_sem.at[k],
            recv_sem=recv_sem.at[k],
            device_id={"dp": me ^ mask},
            device_id_type=pl.DeviceIdType.MESH,
        )
        copies[to].start()

    bits = [1 << b for b in range(1, dp.bit_length() - 1)]
    for m in bits:
        send(0, m)
    send(0, 1)
    compute()
    for m in bits:
        copies[m].wait_recv()
        if m == bits[-1]:
            near = [0, m]
            for n in reversed(bits[:-1]):
                for j in near[1:]:
                    send(j, n)
                near = near + [n] + [j ^ n for j in near[1:]]
                if n != bits[0]:
                    for j in near:
                        if j & n and j != n:
                            copies[j].wait_recv()
        send(m, 1)
    last = [j for j in near if j and j not in bits]
    for j in last:
        if j & bits[0] or len(bits) == 1:
            copies[j].wait_recv()
        send(j, 1)
    for j in near:
        copies[j ^ 1].wait_recv()
    for c in copies.values():
        c.wait_send()


def attention_kernel(
    dp, heads, segs, scale, w_ref, g_ref, q_ref, k_ref, v_ref,
    a16_ref, a32_ref, local_ref, mem_ref, zin_ref, blocks_ref, send_sem, recv_sem,
):
    pairs = segs * heads
    greet(dp)

    @pl.loop(0, pairs)
    def _(p):
        at = head_part(heads, p)
        sk = feature_map(k_ref[at].astype(F32))
        blocks_ref[0, matrix_part(p), :] = dot_t(sk.astype(BF16), v_ref[at])
        blocks_ref[0, pl.ds(pairs * DH + p, 1), :] = jnp.sum(sk, axis=0, keepdims=True)

    def compute():
        @pl.loop(0, pairs)
        def _(p):
            at = head_part(heads, p)
            probs = softmax_rows(q_ref[at], k_ref[at], scale)
            local_ref[at] = dot(probs.astype(BF16), v_ref[at])

    spread(dp, blocks_ref, send_sem, recv_sem, compute)

    @pl.loop(0, pairs)
    def _(p):
        at = head_part(heads, p)
        mem, zin = weighted(w_ref, p, heads, segs, blocks_ref)
        mem_ref[matrix_part(p), :] = mem
        zin_ref[pl.ds(p, 1), :] = zin
        g = g_ref[0, p % heads]
        sq = feature_map(q_ref[at].astype(F32))
        den = jnp.sum(sq * zin, axis=-1, keepdims=True) + 1.0
        retrieved = dot(sq.astype(BF16), mem.astype(BF16)) / den
        mixed = (g * retrieved + (1.0 - g) * local_ref[at]).astype(BF16)
        a16_ref[at] = mixed
        a32_ref[at] = mixed.astype(F32)


def attention_back_kernel(
    dp, heads, segs, scale, w_ref, g_ref, q_ref, k_ref, v_ref, da_ref, local_ref, mem_ref, zin_ref,
    dq_ref, dk_ref, dv_ref, gate_ref, dqm_ref, dkl_ref, dvl_ref, blocks_ref, send_sem, recv_sem,
):
    pairs = segs * heads
    greet(dp)

    @pl.loop(0, pairs)
    def _(p):
        at = head_part(heads, p)
        g = g_ref[0, p % heads]
        qf = q_ref[at].astype(F32)
        sq = feature_map(qf)
        sq16 = sq.astype(BF16)
        mem16 = mem_ref[matrix_part(p), :].astype(BF16)
        zin = zin_ref[pl.ds(p, 1), :]
        inv_den = 1.0 / (jnp.sum(sq * zin, axis=-1, keepdims=True) + 1.0)
        retrieved = dot(sq16, mem16) * inv_den
        da = da_ref[at].astype(F32)
        gate_ref[pl.ds(p, 1), :] = jnp.sum(da * (retrieved - local_ref[at]), axis=0, keepdims=True)
        dnum = g * da * inv_den
        dden = -jnp.sum(dnum * retrieved, axis=-1, keepdims=True)
        dnum16 = dnum.astype(BF16)
        blocks_ref[0, matrix_part(p), :] = dot_t(sq16, dnum16)
        blocks_ref[0, pl.ds(pairs * DH + p, 1), :] = jnp.sum(sq * dden, axis=0, keepdims=True)
        dsq = dot_nt(dnum16, mem16) + dden * zin
        dqm_ref[at] = dsq * feature_slope(qf)

    def compute():
        @pl.loop(0, pairs)
        def _(p):
            at = head_part(heads, p)
            g = g_ref[0, p % heads]
            q, k, v, da = q_ref[at], k_ref[at], v_ref[at], da_ref[at]
            probs = softmax_rows(q, k, scale)
            dprobs = (1.0 - g) * dot_nt(da, v)
            inner = jnp.sum(dprobs * probs, axis=-1, keepdims=True)
            ds16 = (probs * (dprobs - inner)).astype(BF16)
            dq_ref[at] = (dot(ds16, k) * scale + dqm_ref[at]).astype(BF16)
            dkl_ref[at] = dot_t(ds16, q) * scale
            dvl_ref[at] = (1.0 - g) * dot_t(probs.astype(BF16), da)

    spread(dp, blocks_ref, send_sem, recv_sem, compute)

    @pl.loop(0, pairs)
    def _(p):
        at = head_part(heads, p)
        dd, dz = weighted(w_ref, p, heads, segs, blocks_ref)
        dd16 = dd.astype(BF16)
        kf = k_ref[at].astype(F32)
        dsk = dot_nt(v_ref[at], dd16) + dz
        dk_ref[at] = (dkl_ref[at] + dsk * feature_slope(kf)).astype(BF16)
        dv_ref[at] = (dvl_ref[at] + dot(feature_map(kf).astype(BF16), dd16)).astype(BF16)


def greet_core():
    me = lax.axis_index("tensor")
    barrier = pltpu.get_barrier_semaphore()
    pl.semaphore_signal(
        barrier, inc=1, device_id={"tensor": me ^ 1}, device_id_type=pl.DeviceIdType.MESH
    )
    pl.semaphore_wait(barrier, 1)
    return me ^ 1


def core_copy(peer, src, dst, send_sem, recv_sem):
    return pltpu.make_async_remote_copy(
        src_ref=src,
        dst_ref=dst,
        send_sem=send_sem,
        recv_sem=recv_sem,
        device_id={"tensor": peer},
        device_id_type=pl.DeviceIdType.MESH,
    )


def core_sum_kernel(transposed, tiles, l_ref, w_ref, out_ref, send_ref, recv_ref, send_sem, recv_sem):
    peer = greet_core()
    half = out_ref.shape[0]
    size = out_ref.shape[1] // tiles
    copies = []

    def term(rows, c):
        cols = slice(c * size, (c + 1) * size)
        if transposed:
            return dot_nt(l_ref[rows, :], w_ref[cols, :])
        return dot(l_ref[rows, :], w_ref[:, cols])

    for c in range(tiles):
        send_ref[c] = term(slice(half, 2 * half), c)
        copies.append(
            core_copy(peer, send_ref.at[c], recv_ref.at[c], send_sem.at[c], recv_sem.at[c])
        )
        copies[-1].start()
    for c in range(tiles):
        part = term(slice(0, half), c)
        copies[c].wait_recv()
        out_ref[:, c * size : (c + 1) * size] = part + recv_ref[c]
    for c in copies:
        c.wait_send()


def core_sum(ident, lhs, w, transposed):
    tokens = lhs.shape[0]
    half = tokens // 2
    n = w.shape[0] if transposed else w.shape[1]
    tiles = 4
    out = jax.ShapeDtypeStruct((half, n), F32)
    full = pl.BlockSpec(memory_space=pltpu.VMEM)
    return pl.pallas_call(
        functools.partial(core_sum_kernel, transposed, tiles),
        out_shape=out,
        in_specs=[full, full],
        out_specs=full,
        scratch_shapes=[
            pltpu.VMEM((tiles, half, n // tiles), F32),
            pltpu.VMEM((tiles, half, n // tiles), F32),
            pltpu.SemaphoreType.DMA((tiles,)),
            pltpu.SemaphoreType.DMA((tiles,)),
        ],
        compiler_params=pltpu.CompilerParams(
            collective_id=ident, has_side_effects=True, vmem_limit_bytes=52 << 20
        ),
        cost_estimate=pl.CostEstimate(
            flops=2 * tokens * w.size, transcendentals=0, bytes_accessed=nbytes(lhs, w, out)
        ),
    )(lhs, w)


def core_gather_kernel(norm, tiles, v_ref, gain_ref, out_ref, send_ref, recv_ref, send_sem, recv_sem):
    peer = greet_core()
    half = v_ref.shape[0]
    size = half // tiles
    copies = []
    for c in range(tiles):
        rows = slice(c * size, (c + 1) * size)
        v = v_ref[rows, :]
        if norm:
            inv = lax.rsqrt(jnp.mean(v * v, axis=-1, keepdims=True) + EPS)
            v = v * inv * gain_ref[...]
            send_ref[rows, :] = v
        out_ref[rows, :] = v.astype(BF16)
        src = send_ref if norm else v_ref
        copies.append(
            core_copy(
                peer, src.at[rows, :], recv_ref.at[rows, :], send_sem.at[c], recv_sem.at[c]
            )
        )
        copies[-1].start()
    for c in range(tiles):
        rows = slice(c * size, (c + 1) * size)
        copies[c].wait_recv()
        out_ref[half + c * size : half + (c + 1) * size, :] = recv_ref[rows, :].astype(BF16)
    for c in copies:
        c.wait_send()


def core_gather(ident, v, gain=None):
    half, n = v.shape
    tiles = 4
    out = jax.ShapeDtypeStruct((2 * half, n), BF16)
    full = pl.BlockSpec(memory_space=pltpu.VMEM)
    norm = gain is not None
    return pl.pallas_call(
        functools.partial(core_gather_kernel, norm, tiles),
        out_shape=out,
        in_specs=[full, full],
        out_specs=full,
        scratch_shapes=[
            pltpu.VMEM((half, n) if norm else (8, DH), F32),
            pltpu.VMEM((half, n), F32),
            pltpu.SemaphoreType.DMA((tiles,)),
            pltpu.SemaphoreType.DMA((tiles,)),
        ],
        compiler_params=pltpu.CompilerParams(
            collective_id=ident, has_side_effects=True, vmem_limit_bytes=48 << 20
        ),
        cost_estimate=pl.CostEstimate(
            flops=0, transcendentals=0, bytes_accessed=nbytes(v, v, v, out)
        ),
    )(v, gain[None, :] if norm else jnp.zeros((8, DH), F32))


def feed_kernel(wire, off_ref, h_ref, w_ref, u_ref, *refs):
    act_ref, dpre_ref, extra_ref = refs[-3:]
    pre = dot(h_ref[...], w_ref[...])
    c = 0.7978845608028654
    sq = pre * pre
    th = jnp.tanh(c * pre * (1.0 + 0.044715 * sq))
    half = 0.5 * (1.0 + th)
    act = (pre * half).astype(BF16)
    act_ref[...] = act
    extra_ref[...] = act.astype(F32) if wire else act
    slope = half + 0.5 * pre * (1.0 - th * th) * (c * (1.0 + 0.134145 * sq))
    dpre_ref[...] = (u_ref[...] * slope).astype(BF16)


def feed(h2, w_up, up_grad, offset, count, tile, wire, held):
    tokens, width = h2.shape
    units = w_up.shape[1]
    full = jax.ShapeDtypeStruct((tokens, units), BF16)
    extra = jax.ShapeDtypeStruct((tokens, count), F32 if wire else BF16)
    at = lambda j, off: (0, off[0] + j)
    held = list(held)
    return pl.pallas_call(
        functools.partial(feed_kernel, wire),
        out_shape=[full, full, extra],
        grid_spec=pltpu.PrefetchScalarGridSpec(
            num_scalar_prefetch=1,
            grid=(count // tile,),
            in_specs=[
                pl.BlockSpec((tokens, width), lambda j, off: (0, 0)),
                pl.BlockSpec((width, tile), at),
                pl.BlockSpec((tokens, tile), at),
            ]
            + [pl.BlockSpec(memory_space=pl.ANY)] * len(held),
            out_specs=[
                pl.BlockSpec((tokens, tile), at),
                pl.BlockSpec((tokens, tile), at),
                pl.BlockSpec((tokens, tile), lambda j, off: (0, j)),
            ],
        ),
        input_output_aliases={4: 0, 5: 1} if held else {},
        compiler_params=pltpu.CompilerParams(vmem_limit_bytes=48 << 20),
        cost_estimate=pl.CostEstimate(
            flops=2 * tokens * width * count,
            transcendentals=tokens * count,
            bytes_accessed=2 * width * (tokens + count) + 12 * tokens * count,
        ),
    )((offset // tile)[None], h2, w_up, up_grad, *held)


def body(
    inputs,
    gain_attn,
    w_query,
    w_key,
    w_value,
    gate_logit,
    w_out,
    gain_mlp,
    w_up,
    w_down,
    seg_parent,
    out_grad,
):
    tokens, width = inputs.shape
    half = tokens // 2
    segs = tokens // SEG
    heads = w_query.shape[1] // DH
    pairs = segs * heads
    units = w_up.shape[1]
    flat = heads * DH
    scale = DH ** (-0.5)
    dp = lax.axis_size("dp")
    tn = lax.axis_size("tensor")
    rows = width // dp
    di = lax.axis_index("dp")
    core = lax.axis_index("tensor") % 2

    one = jnp.where(seg_parent[0] < tokens * dp, 1.0, 2.0)

    def low_after_wire(v):
        return (v * one).astype(BF16)

    def swap_core(v):
        return lax.ppermute(v, "tensor", [(i, i ^ 1) for i in range(tn)])

    def swap_y(v):
        return lax.ppermute(v, "tensor", [(i, i ^ 2) for i in range(tn)])

    def swap_dp(v, mask):
        return lax.ppermute(v, "dp", [(i, i ^ mask) for i in range(dp)])

    z_groups = [[z * 2 + x for z in range(dp // 2)] for x in range(2)]

    def scatter_z(v):
        return lax.psum_scatter(v, "dp", scatter_dimension=0, axis_index_groups=z_groups, tiled=True)

    xi = di % 2

    def columns(v):
        ids = [2 * z + 1 - xi for z in range(dp // 2)] + [2 * z + xi for z in range(dp // 2)]
        return block_columns(v, ids, rows)

    cut = width // 2

    class Reduce:
        def __init__(self, lhs, rhs):
            self.lhs, self.rhs = lhs, rhs
            self.term = dot_t(lhs[:, :cut], rhs)
            self.got = swap_dp(self.term, 1)

        def scatter(self, *earlier):
            got = after(self.got, *earlier)
            self.part = dot_t(self.lhs[:, cut:], self.rhs) + got
            self.out = scatter_z(self.part)
            return self.part

    def pick(v, index, axis):
        size = v.shape[axis] // 2
        return lax.dynamic_slice_in_dim(v, index * size, size, axis)

    def place(own, other, index, axis):
        return jnp.where(
            index == 0,
            jnp.concatenate([own, other], axis),
            jnp.concatenate([other, own], axis),
        )

    def inv_rms(v):
        return lax.rsqrt(jnp.mean(v * v, axis=-1, keepdims=True) + EPS)

    w_out_all = lax.all_gather(w_out.astype(F32), "tensor", axis=0, tiled=True)

    x_own = pick(inputs, core, 0).astype(F32)
    x_oth = pick(inputs, 1 - core, 0).astype(F32)
    inv_own = inv_rms(x_own)
    inv_oth = inv_rms(x_oth)
    h1 = jnp.concatenate(
        [
            (x_own * inv_own * gain_attn).astype(BF16),
            (x_oth * inv_oth * gain_attn).astype(BF16),
        ],
        0,
    )

    def project(matrix):
        return dot(h1, matrix).astype(BF16)

    qh = project(w_query)
    kh = project(w_key)
    vh = project(w_value)

    sub = segs // 2
    every = jnp.arange(seg_parent.shape[0], dtype=jnp.int32)
    sub_ids = jnp.arange(sub, dtype=jnp.int32)
    seg_local = jnp.concatenate([core * sub + sub_ids, (1 - core) * sub + sub_ids])
    order = spread_order(dp)
    ids = jnp.concatenate([(di ^ j) * segs + seg_local for j in order])
    mine_hot = (ids[:segs, None] == every[None, :]).astype(F32)
    ids_hot = (ids[:, None] == every[None, :]).astype(F32)
    lineage = ancestor_table(seg_parent)

    def weights_of(table):
        mine_rows = jnp.sum(mine_hot[:, :, None] * table[None], axis=1)
        return jnp.sum(mine_rows[:, None, :] * ids_hot[None], axis=-1)

    up_weight = weights_of(lineage)
    down_weight = weights_of(lineage.T)

    gate = jax.nn.sigmoid(gate_logit)
    gate_row = gate[None, :]

    og_own = pick(out_grad, core, 0)
    og = jnp.concatenate([og_own, pick(out_grad, 1 - core, 0)], 0)
    block_rows = pairs * DH + pairs
    act_f32 = jax.ShapeDtypeStruct((tokens, flat), F32)
    act_b16 = jax.ShapeDtypeStruct((tokens, flat), BF16)
    mem_shape = jax.ShapeDtypeStruct((pairs * DH, DH), F32)
    zin_shape = jax.ShapeDtypeStruct((pairs, DH), F32)
    full = pl.BlockSpec(memory_space=pltpu.VMEM)

    def attention_call(kernel, ident, outs, scratch, args, n_smem, flops):
        return pl.pallas_call(
            functools.partial(kernel, dp, heads, segs, scale),
            out_shape=outs,
            in_specs=[SMEM] * n_smem + [full] * (len(args) - n_smem),
            out_specs=[full] * len(outs),
            scratch_shapes=scratch
            + [
                pltpu.VMEM((dp, block_rows, DH), F32),
                pltpu.SemaphoreType.DMA((dp,)),
                pltpu.SemaphoreType.DMA((dp,)),
            ],
            compiler_params=pltpu.CompilerParams(
                collective_id=ident, has_side_effects=True, vmem_limit_bytes=56 << 20
            ),
            cost_estimate=pl.CostEstimate(
                flops=flops, transcendentals=0, bytes_accessed=64 << 20
            ),
        )(*args)

    head_flops = 2 * segs * heads * SEG * SEG * DH
    a16, a32, local, memory, zin = attention_call(
        attention_kernel,
        0,
        [act_b16, act_f32, act_f32, mem_shape, zin_shape],
        [],
        (up_weight, gate_row, qh, kh, vh),
        2,
        3 * head_flops,
    )
    og_pair = lax.all_gather(
        after(og_own, a32).astype(F32), "dp", axis=0, tiled=True,
        axis_index_groups=[[2 * i, 2 * i + 1] for i in range(dp // 2)],
    )

    up_grad = dot_nt(og, after(w_down, a32))

    step = half // AG_CHUNKS
    a_core = [
        swap_core(a32[half + c * step : half + (c + 1) * step]) for c in range(AG_CHUNKS)
    ]
    a_pair = [
        jnp.concatenate([a32[c * step : (c + 1) * step], a_core[c]], 1) for c in range(AG_CHUNKS)
    ]
    a_far = [swap_y(v) for v in a_pair]
    ti = lax.axis_index("tensor")

    def w_rows(j):
        return low_after_wire(lax.dynamic_slice_in_dim(w_out_all, (ti ^ j) * flat, flat, 0))

    w_out_core = w_rows(1)
    w_out_far = jnp.concatenate([w_rows(2), w_rows(3)], 0)
    near = [
        x_own[c * step : (c + 1) * step]
        + dot(a16[c * step : (c + 1) * step], w_out)
        + dot(low_after_wire(a_core[c]), w_out_core)
        for c in range(AG_CHUNKS)
    ]
    h1_a = columns(after(h1, up_grad))
    resids = [
        n + dot(low_after_wire(after(f, w_out_far, h1_a)), w_out_far)
        for n, f in zip(near, a_far)
    ]
    resid = jnp.concatenate(resids, 0)
    inv_mlp = inv_rms(resid)
    h2 = core_gather(1, resid, gain_mlp)

    part = units // 2
    held = ()
    act_b = []
    at = (1 - xi) * part
    for n in ACT_PIECES:
        act, dpre, wire = feed(h2, w_up, up_grad, at, n, 256, True, held)
        held = (act, dpre)
        act_b.append(swap_dp(wire, 1))
        at = at + n
    act, dpre, act_keep = feed(h2, w_up, up_grad, xi * part, part, 256, False, held)

    def tensor_sum_start(ident, lhs, w, transposed):
        total = core_sum(ident, lhs, w, transposed)
        size = half // SUM_CHUNKS
        parts = [total[c * size : (c + 1) * size] for c in range(SUM_CHUNKS)]
        return [(p, swap_y(p)) for p in parts]

    def tensor_sum_end(parts, *earlier):
        return jnp.concatenate([p + after(r, *earlier) for p, r in parts], 0)

    dh2_parts = tensor_sum_start(2, dpre, w_up, True)
    sent = [p for p, _ in dh2_parts]

    h2_a = columns(after(h2, *sent))
    up = []
    starts = [0]
    for n in UP_PIECES:
        starts.append(starts[-1] + n)

    def up_piece(p, *earlier):
        up.append(Reduce(h2_a, after(dpre, *earlier)[:, starts[p] : starts[p + 1]]))
        return up[-1].term

    og_b_own = lax.dynamic_slice_in_dim(og_pair, (1 - xi) * half, half, 0)
    og_b = core_gather(3, after(og_b_own, h2_a))
    down = []

    def down_piece(p, *earlier):
        lo = sum(ACT_PIECES[:p])
        piece = act_keep[:, lo : lo + ACT_PIECES[p]]
        got = low_after_wire(after(act_b[p], *earlier))
        total = dot_t(og, piece) + dot_t(og_b, got)
        down.append(scatter_z(total))
        return total

    e = up_piece(0, *sent)
    e = down_piece(0, e)
    e = up_piece(1, e)
    e = down_piece(1, e)

    dh2 = tensor_sum_end(dh2_parts, e)
    gs = dh2 * gain_mlp
    dresid = (
        og_own.astype(F32)
        + inv_mlp * gs
        - resid * inv_mlp * inv_mlp * inv_mlp * jnp.mean(gs * resid, axis=-1, keepdims=True)
    )
    gain_mlp_part = jnp.sum(dh2 * resid * inv_mlp, axis=0)
    dr = core_gather(4, dresid)

    e = down_piece(2, dr)
    da = dot_nt(after(dr, e), w_out).astype(BF16)
    e = up[0].scatter(da)
    e = up_piece(2, e)
    dq16, dk16, dv16, gate_rows = attention_call(
        attention_back_kernel,
        5,
        [act_b16, act_b16, act_b16, zin_shape],
        [pltpu.VMEM((tokens, flat), F32)] * 3,
        (down_weight, gate_row, qh, kh, vh, after(da, e), local, memory, zin),
        2,
        9 * head_flops,
    )
    gate_part = jnp.sum(gate_rows.reshape(segs, heads, DH), axis=(0, 2)) * gate * (1.0 - gate)

    e = up[1].scatter(dq16)
    e = up_piece(3, e)
    out_w = Reduce(columns(after(dr, e)), a16)

    out_parts = tensor_sum_start(6, after(act, out_w.term), w_down, False)
    query = Reduce(h1_a, after(dq16, *[p for p, _ in out_parts]))

    w_qkv = jnp.concatenate([after(w, up_grad) for w in (w_query, w_key, w_value)], 1)
    d_qkv = jnp.concatenate([dq16, dk16, dv16], 1)
    dh1_parts = tensor_sum_start(7, after(d_qkv, query.term), w_qkv, True)
    sent = [p for p, _ in dh1_parts]
    e = up[2].scatter(*sent)
    key = Reduce(h1_a, after(dk16, e))
    e = up[3].scatter(key.term)
    value = Reduce(h1_a, after(dv16, e))
    e = out_w.scatter(value.term)

    out_own = (resid + tensor_sum_end(out_parts, e)).astype(BF16)
    outputs = place(out_own, low_after_wire(swap_core(out_own.astype(F32))), core, 0)

    e = query.scatter(out_own)
    e = key.scatter(e)

    dh1 = tensor_sum_end(dh1_parts, e)
    gs1 = dh1 * gain_attn
    dx = (
        dresid
        + inv_own * gs1
        - x_own * inv_own * inv_own * inv_own * jnp.mean(gs1 * x_own, axis=-1, keepdims=True)
    )
    gain_attn_part = jnp.sum(dh1 * x_own * inv_own, axis=0)
    dx_own = dx.astype(BF16)
    input_grad = place(dx_own, low_after_wire(swap_core(dx_own.astype(F32))), core, 0)

    e = value.scatter(dx_own)

    down = jnp.concatenate(down, 1)
    down_theirs = swap_dp(pick(down, 1 - xi, 0), 1)
    w_down_grad = place(pick(down, xi, 0), down_theirs, xi, 1).T
    w_up_grad = jnp.concatenate([v.out for v in up], 1)
    w_out_grad = out_w.out.T
    w_query_grad, w_key_grad, w_value_grad = query.out, key.out, value.out

    gains = jnp.concatenate([gain_attn_part, gain_mlp_part])
    small = jnp.concatenate([gains + swap_core(gains), jnp.pad(gate_part, (0, DH - heads))])
    bit = 1
    while bit < dp:
        small = small + swap_dp(small, bit)
        bit *= 2
    gain_attn_grad = lax.dynamic_slice_in_dim(small, di * rows, rows, 0)
    gain_mlp_grad = lax.dynamic_slice_in_dim(small, width + di * rows, rows, 0)
    gate_grad = small[2 * width : 2 * width + heads]

    return (
        outputs,
        input_grad,
        gain_attn_grad,
        w_query_grad,
        w_key_grad,
        w_value_grad,
        gate_grad,
        w_out_grad,
        gain_mlp_grad,
        w_up_grad,
        w_down_grad,
    )


def solution(mesh):
    placed = (
        P("dp", None),
        P(),
        P(None, "tensor"),
        P(None, "tensor"),
        P(None, "tensor"),
        P("tensor"),
        P("tensor", None),
        P(),
        P(None, "tensor"),
        P("tensor", None),
        P(),
        P("dp", None),
    )
    return jax.shard_map(
        body,
        mesh=mesh,
        in_specs=placed,
        out_specs=(
            P("dp", None),
            P("dp", None),
            P("dp"),
            P("dp", "tensor"),
            P("dp", "tensor"),
            P("dp", "tensor"),
            P("tensor"),
            P("tensor", "dp"),
            P("dp"),
            P("dp", "tensor"),
            P("tensor", "dp"),
        ),
        check_vma=False,
    )
```

```python
import functools

import jax
import jax.numpy as jnp
from jax import lax
from jax.experimental import pallas as pl
from jax.experimental.pallas import tpu as pltpu
from jax.sharding import PartitionSpec as P

DH = 128
SEG = 512
DEPTH = 5
EPS = 1e-06

F32 = jnp.float32
BF16 = jnp.bfloat16

AG_CHUNKS = 2
Z_FIRST = (1, 0)
X_FIRST = (0, 1)


def feature_map(values):
    return jnp.where(values > 0, values + 1.0, jnp.exp(jnp.minimum(values, 0.0)))


def feature_slope(values):
    return jnp.where(values > 0, 1.0, jnp.exp(jnp.minimum(values, 0.0)))


def ancestor_table(seg_parent):
    seg_total = seg_parent.shape[0]
    columns = jnp.arange(seg_total, dtype=jnp.int32)
    current = seg_parent
    lineage_table = jnp.zeros((seg_total, seg_total), F32)
    for _ in range(DEPTH):
        onehot = current[:, None] == columns[None, :]
        lineage_table = lineage_table + onehot.astype(F32)
        lifted = jnp.sum(jnp.where(onehot, seg_parent[None, :], 0), axis=1)
        current = jnp.where(current >= 0, lifted, -1)
    return lineage_table


def dot(a, b):
    return jnp.dot(a, b, preferred_element_type=F32)


def dot_t(a, b):
    return lax.dot_general(a, b, (((0,), (0,)), ((), ())), preferred_element_type=F32)


def dot_nt(a, b):
    return lax.dot_general(a, b, (((1,), (1,)), ((), ())), preferred_element_type=F32)


def after(value, *earlier):
    return lax.optimization_barrier((value, earlier))[0]


def nbytes(*arrays):
    return sum(a.size * a.dtype.itemsize for a in arrays)


def copy_kernel(ids_ref, in_ref, out_ref):
    out_ref[...] = in_ref[...]


def block_columns(v, ids, size):
    if size % 128:
        return jnp.concatenate([lax.dynamic_slice_in_dim(v, i * size, size, 1) for i in ids], 1)
    height, width = v.shape
    return pl.pallas_call(
        copy_kernel,
        out_shape=jax.ShapeDtypeStruct(v.shape, v.dtype),
        grid_spec=pltpu.PrefetchScalarGridSpec(
            num_scalar_prefetch=1,
            grid=(width // size,),
            in_specs=[pl.BlockSpec((height, size), lambda k, ids: (0, ids[k]))],
            out_specs=pl.BlockSpec((height, size), lambda k, ids: (0, k)),
        ),
        cost_estimate=pl.CostEstimate(flops=0, transcendentals=0, bytes_accessed=2 * nbytes(v)),
    )(jnp.stack(ids), v)


SMEM = pl.BlockSpec(memory_space=pltpu.SMEM)


def causal_mask():
    row = lax.broadcasted_iota(jnp.int32, (SEG, SEG), 0)
    col = lax.broadcasted_iota(jnp.int32, (SEG, SEG), 1)
    return row >= col


def softmax_rows(q, k, scale):
    scores = dot_nt(q, k) * scale
    scores = jnp.where(causal_mask(), scores, -1e30)
    top = jnp.max(scores, axis=-1, keepdims=True)
    e = jnp.exp(scores - top)
    return e * (1.0 / jnp.sum(e, axis=-1, keepdims=True))


def head_part(heads, p):
    s, h = p // heads, p % heads
    return pl.ds(pl.multiple_of(s * SEG, SEG), SEG), pl.ds(pl.multiple_of(h * DH, DH), DH)


def matrix_part(p):
    return pl.ds(pl.multiple_of(p * DH, DH), DH)


def weighted(w_ref, p, heads, segs, blocks_ref):
    s, h = p // heads, p % heads
    pairs = segs * heads
    big = jnp.zeros((DH, DH), F32)
    small = jnp.zeros((1, DH), F32)
    for d in range(blocks_ref.shape[0]):
        for n in range(segs):
            w = w_ref[s, d * segs + n]
            o = n * heads + h
            big = big + w * blocks_ref[d, matrix_part(o), :]
            small = small + w * blocks_ref[d, pl.ds(pairs * DH + o, 1), :]
    return big, small


def spread_order(dp):
    low = [0]
    for b in reversed(range(1, dp.bit_length() - 1)):
        low = low + [v ^ (1 << b) for v in low]
    return low + [v ^ 1 for v in low]


def greet(*peers):
    barrier = pltpu.get_barrier_semaphore()
    for peer in peers:
        pl.semaphore_signal(barrier, inc=1, device_id=peer, device_id_type=pl.DeviceIdType.MESH)
    pl.semaphore_wait(barrier, len(peers))


def dp_peers(dp):
    me = lax.axis_index("dp")
    return [{"dp": me ^ (1 << b)} for b in range(dp.bit_length() - 1)]


def tensor_peer(mask):
    return {"tensor": lax.axis_index("tensor") ^ mask}


def halving(dp, order):
    masks = [1 << b for b in order]
    masks += [1 << b for b in range(len(order), dp.bit_length() - 1)]
    seq = [0]
    for m in reversed(masks):
        seq = [m ^ v for v in seq] + seq
    return masks, seq


def block_of(ref, dp, order, k):
    rows = ref.shape[1] // dp
    if rows % DH:
        return ref[:, k * rows : (k + 1) * rows]
    at = (lax.axis_index("dp") ^ halving(dp, order)[1][k]) * rows
    return ref[:, pl.ds(pl.multiple_of(at, rows), rows)]


def remote(src, dst, send_sem, recv_sem, peer):
    return pltpu.make_async_remote_copy(
        src_ref=src,
        dst_ref=dst,
        send_sem=send_sem,
        recv_sem=recv_sem,
        device_id=peer,
        device_id_type=pl.DeviceIdType.MESH,
    )


def spread(dp, blocks_ref, send_sem, recv_sem, compute):
    me = lax.axis_index("dp")
    slot = {j: k for k, j in enumerate(spread_order(dp))}
    copies = {}

    def send(j, mask):
        to = j ^ mask
        k = slot[to]
        copies[to] = pltpu.make_async_remote_copy(
            src_ref=blocks_ref.at[slot[j]],
            dst_ref=blocks_ref.at[k],
            send_sem=send_sem.at[k],
            recv_sem=recv_sem.at[k],
            device_id={"dp": me ^ mask},
            device_id_type=pl.DeviceIdType.MESH,
        )
        copies[to].start()

    bits = [1 << b for b in range(1, dp.bit_length() - 1)]
    for m in bits:
        send(0, m)
    send(0, 1)
    compute()
    for m in bits:
        copies[m].wait_recv()
        if m == bits[-1]:
            near = [0, m]
            for n in reversed(bits[:-1]):
                for j in near[1:]:
                    send(j, n)
                near = near + [n] + [j ^ n for j in near[1:]]
                if n != bits[0]:
                    for j in near:
                        if j & n and j != n:
                            copies[j].wait_recv()
        send(m, 1)
    last = [j for j in near if j and j not in bits]
    for j in last:
        if j & bits[0] or len(bits) == 1:
            copies[j].wait_recv()
        send(j, 1)
    for j in near:
        copies[j ^ 1].wait_recv()
    for c in copies.values():
        c.wait_send()


W_CHUNKS = 4


def attention_kernel(
    dp, heads, segs, scale, w_ref, g_ref, h_ref, wq_ref, wk_ref, wv_ref, wo_ref,
    q_ref, k_ref, v_ref, a16_ref, pair_ref, local_ref, mem_ref, zin_ref, all_ref,
    wf_ref, asend_ref, w_send, w_recv, a_send, a_recv, blocks_ref, send_sem, recv_sem,
):
    pairs = segs * heads
    flat = heads * DH
    half = segs * SEG // 2
    core, far = tensor_peer(1), tensor_peer(2)
    greet(*dp_peers(dp), core, far)

    size = flat // W_CHUNKS
    w_copies = {}

    def w_send_chunk(j, c, to, peer):
        rows = pl.ds(c * size, size)
        k = (to - 1) * W_CHUNKS + c
        w_copies[to, c] = remote(
            wf_ref.at[j, rows, :], wf_ref.at[to, rows, :], w_send.at[k], w_recv.at[k], peer
        )
        w_copies[to, c].start()

    def w_done(to, c):
        rows = slice(c * size, (c + 1) * size)
        w_copies[to, c].wait_recv()
        all_ref[to * flat + c * size : to * flat + (c + 1) * size, :] = wf_ref[to, rows, :].astype(
            BF16
        )

    for c in range(W_CHUNKS):
        rows = slice(c * size, (c + 1) * size)
        wf_ref[0, rows, :] = wo_ref[rows, :].astype(F32)
        w_send_chunk(0, c, 2, far)
        w_send_chunk(0, c, 1, core)
    all_ref[:flat, :] = wo_ref[...]

    def project(matrix_ref, out_ref):
        @pl.loop(0, segs * SEG // 256)
        def _(i):
            rows = pl.ds(pl.multiple_of(i * 256, 256), 256)
            out_ref[rows, :] = dot(h_ref[rows, :], matrix_ref[...]).astype(BF16)

    project(wk_ref, k_ref)
    project(wv_ref, v_ref)

    @pl.loop(0, pairs)
    def _(p):
        at = head_part(heads, p)
        sk = feature_map(k_ref[at].astype(F32))
        blocks_ref[0, matrix_part(p), :] = dot_t(sk.astype(BF16), v_ref[at])
        blocks_ref[0, pl.ds(pairs * DH + p, 1), :] = jnp.sum(sk, axis=0, keepdims=True)

    def compute():
        project(wq_ref, q_ref)

        @pl.loop(0, pairs)
        def _(p):
            at = head_part(heads, p)
            probs = softmax_rows(q_ref[at], k_ref[at], scale)
            local_ref[at] = dot(probs.astype(BF16), v_ref[at])

    spread(dp, blocks_ref, send_sem, recv_sem, compute)

    @pl.loop(0, pairs)
    def _(p):
        at = head_part(heads, p)
        mem, zin = weighted(w_ref, p, heads, segs, blocks_ref)
        mem_ref[matrix_part(p), :] = mem
        zin_ref[pl.ds(p, 1), :] = zin
        g = g_ref[0, p % heads]
        sq = feature_map(q_ref[at].astype(F32))
        den = jnp.sum(sq * zin, axis=-1, keepdims=True) + 1.0
        retrieved = dot(sq.astype(BF16), mem.astype(BF16)) / den
        a16_ref[at] = (g * retrieved + (1.0 - g) * local_ref[at]).astype(BF16)

    asend_ref[...] = a16_ref[half:, :].astype(F32)
    a_copy = remote(asend_ref, pair_ref.at[:, pl.ds(flat, flat)], a_send, a_recv, core)
    a_copy.start()
    pair_ref[:, :flat] = a16_ref[:half, :].astype(F32)
    for c in range(W_CHUNKS):
        w_done(1, c)
    a_copy.wait_recv()
    for c in range(W_CHUNKS):
        w_copies[2, c].wait_recv()
        w_send_chunk(2, c, 3, core)
        rows = slice(c * size, (c + 1) * size)
        all_ref[2 * flat + c * size : 2 * flat + (c + 1) * size, :] = wf_ref[2, rows, :].astype(BF16)
    for c in range(W_CHUNKS):
        w_done(3, c)
    for copy in w_copies.values():
        copy.wait_send()
    a_copy.wait_send()


def attention_back_kernel(
    dp, heads, segs, scale, w_ref, g_ref, q_ref, k_ref, v_ref, da_ref, local_ref, mem_ref, zin_ref,
    dr_ref, a16_ref, d_pre_ref, u_pre_ref, out_part_ref,
    dq_ref, dk_ref, dv_ref, gate_ref, o_pre_ref, d_rode_ref, u_rode_ref, out_far_ref,
    dqm_ref, dkl_ref, dvl_ref, os_ref, ride_send, ride_recv, blocks_ref, send_sem, recv_sem,
):
    pairs = segs * heads
    me = lax.axis_index("dp")
    far = tensor_peer(2)
    greet(*dp_peers(dp), far)
    quarter = d_rode_ref.shape[0]
    first = pl.ds(0, quarter)
    riders = [
        remote(src, dst, ride_send.at[i], ride_recv.at[i], peer)
        for i, (src, dst, peer) in enumerate(
            (
                (d_pre_ref.at[first, :], d_rode_ref, {"dp": me ^ 1}),
                (u_pre_ref.at[first, :], u_rode_ref, {"dp": me ^ 2}),
                (out_part_ref, out_far_ref, far),
                (os_ref, o_pre_ref, {"dp": me ^ 2}),
            )
        )
    ]

    @pl.loop(0, pairs)
    def _(p):
        at = head_part(heads, p)
        g = g_ref[0, p % heads]
        qf = q_ref[at].astype(F32)
        sq = feature_map(qf)
        sq16 = sq.astype(BF16)
        mem16 = mem_ref[matrix_part(p), :].astype(BF16)
        zin = zin_ref[pl.ds(p, 1), :]
        inv_den = 1.0 / (jnp.sum(sq * zin, axis=-1, keepdims=True) + 1.0)
        retrieved = dot(sq16, mem16) * inv_den
        da = da_ref[at].astype(F32)
        gate_ref[pl.ds(p, 1), :] = jnp.sum(da * (retrieved - local_ref[at]), axis=0, keepdims=True)
        dnum = g * da * inv_den
        dden = -jnp.sum(dnum * retrieved, axis=-1, keepdims=True)
        dnum16 = dnum.astype(BF16)
        blocks_ref[0, matrix_part(p), :] = dot_t(sq16, dnum16)
        blocks_ref[0, pl.ds(pairs * DH + p, 1), :] = jnp.sum(sq * dden, axis=0, keepdims=True)
        dsq = dot_nt(dnum16, mem16) + dden * zin
        dqm_ref[at] = dsq * feature_slope(qf)

    rows = dr_ref.shape[1] // dp
    half_blocks = dp // 2

    def compute():
        for r in riders[:3]:
            r.start()
        for j in range(half_blocks):
            os_ref[j * rows : (j + 1) * rows, :] = dot_t(
                block_of(dr_ref, dp, Z_FIRST, j), a16_ref[...]
            )
        riders[3].start()

        @pl.loop(0, pairs)
        def _(p):
            at = head_part(heads, p)
            g = g_ref[0, p % heads]
            q, k, v, da = q_ref[at], k_ref[at], v_ref[at], da_ref[at]
            probs = softmax_rows(q, k, scale)
            dprobs = (1.0 - g) * dot_nt(da, v)
            inner = jnp.sum(dprobs * probs, axis=-1, keepdims=True)
            ds16 = (probs * (dprobs - inner)).astype(BF16)
            dq_ref[at] = (dot(ds16, k) * scale + dqm_ref[at]).astype(BF16)
            dkl_ref[at] = dot_t(ds16, q) * scale
            dvl_ref[at] = (1.0 - g) * dot_t(probs.astype(BF16), da)

    spread(dp, blocks_ref, send_sem, recv_sem, compute)

    @pl.loop(0, pairs)
    def _(p):
        at = head_part(heads, p)
        dd, dz = weighted(w_ref, p, heads, segs, blocks_ref)
        dd16 = dd.astype(BF16)
        kf = k_ref[at].astype(F32)
        dsk = dot_nt(v_ref[at], dd16) + dz
        dk_ref[at] = (dkl_ref[at] + dsk * feature_slope(kf)).astype(BF16)
        dv_ref[at] = (dvl_ref[at] + dot(feature_map(kf).astype(BF16), dd16)).astype(BF16)

    riders[3].wait()
    for j in range(half_blocks):
        o_pre_ref[j * rows : (j + 1) * rows, :] += dot_t(
            block_of(dr_ref, dp, Z_FIRST, half_blocks + j), a16_ref[...]
        )
    for r in riders[:3]:
        r.wait()


def tail_kernel(
    dp, order, o_order, ht_ref, dq_ref, dk_ref, dv_ref, wq_ref, wk_ref, wv_ref, o_pre_ref, d3_ref, u3_ref,
    gq_ref, gk_ref, gv_ref, go_ref, part_ref, far_ref, d3_got_ref, u3_got_ref,
    cs_ref, cr_ref, c_send, c_recv, y_send, y_recv, ride_send, ride_recv, e_send, e_recv, *bufs,
):
    me = lax.axis_index("dp")
    core, far = tensor_peer(1), tensor_peer(2)
    greet(*dp_peers(dp), core, far)
    masks, _ = halving(dp, order)
    o_masks, _ = halving(dp, o_order)
    steps = len(masks)
    rows = ht_ref.shape[0] // dp
    half, width = part_ref.shape
    lhs = (dq_ref, dk_ref, dv_ref, None)
    outs = (gq_ref, gk_ref, gv_ref, go_ref)
    copies = {}

    def buffers(i, step):
        k = 2 * (i * steps + step)
        return bufs[k], bufs[k + 1]

    def term(i, step):
        lo = rows * sum(dp >> (n + 1) for n in range(step))
        count = rows * (dp >> (step + 1)) if step < steps else rows
        start = 0
        if i < 3:
            value = dot(ht_ref[lo : lo + count, :], lhs[i][...])
        else:
            base = rows * (dp // 2)
            value = o_pre_ref[lo - base : lo - base + count, :]
            start = 1
        for n in range(start, step):
            at = lo - rows * sum(dp >> (m + 1) for m in range(n + 1))
            value = value + buffers(i, n)[1][at : at + count, :]
        return value

    def advance(i, step):
        if step > (1 if i == 3 else 0):
            copies[i, step - 1].wait_recv()
        if step == steps:
            outs[i][...] = term(i, step)
            return
        send, recv = buffers(i, step)
        send[...] = term(i, step)
        mask = (o_masks if i == 3 else masks)[step]
        k = i * steps + step
        copies[i, step] = remote(send, recv, e_send.at[k], e_recv.at[k], {"dp": me ^ mask})
        copies[i, step].start()

    third = masks[2] if steps > 2 else masks[-1]
    riders = [
        remote(src, dst, ride_send.at[i], ride_recv.at[i], {"dp": me ^ third})
        for i, (src, dst) in enumerate(((d3_ref, d3_got_ref), (u3_ref, u3_got_ref)))
    ]
    advance(0, 0)
    for r in riders:
        r.start()
    advance(3, 1)
    advance(1, 0)
    advance(2, 0)

    part_cols = width // 4
    weights = (wq_ref, wk_ref, wv_ref)

    def back(row, c):
        cols = slice(c * part_cols, (c + 1) * part_cols)
        return sum(
            dot_nt(v[row * half : (row + 1) * half, :], w[cols, :])
            for v, w in zip(lhs[:3], weights)
        )

    core_copies, far_copies = [], []
    for c in range(4):
        cs_ref[c] = back(1, c)
        core_copies.append(remote(cs_ref.at[c], cr_ref.at[c], c_send.at[c], c_recv.at[c], core))
        core_copies[-1].start()
    for c in range(4):
        cols = pl.ds(c * part_cols, part_cols)
        value = back(0, c)
        core_copies[c].wait_recv()
        part_ref[:, c * part_cols : (c + 1) * part_cols] = value + cr_ref[c]
        far_copies.append(
            remote(part_ref.at[:, cols], far_ref.at[:, cols], y_send.at[c], y_recv.at[c], far)
        )
        far_copies[-1].start()

    for step in range(1, steps + 1):
        if step > 1:
            advance(3, step)
        for i in range(3):
            advance(i, step)
    for c in core_copies:
        c.wait_send()
    for c in copies.values():
        c.wait_send()
    for c in far_copies + riders:
        c.wait()


def tail(ident, dp, ht, grads, weights, o_pre, d3, u3):
    width, tokens = ht.shape
    flat = grads[0].shape[1]
    half = tokens // 2
    rows = width // dp
    steps = dp.bit_length() - 1
    full = pl.BlockSpec(memory_space=pltpu.VMEM)
    anywhere = pl.BlockSpec(memory_space=pl.ANY)
    f32 = lambda *shape: jax.ShapeDtypeStruct(shape, F32)
    dma = pltpu.SemaphoreType.DMA
    bufs = []
    for i in range(4):
        for step in range(steps):
            count = rows * (dp >> (step + 1)) if i < 3 or step else 8
            bufs += [pltpu.VMEM((count, flat), F32)] * 2
    return pl.pallas_call(
        functools.partial(tail_kernel, dp, X_FIRST, Z_FIRST),
        out_shape=[f32(rows, flat)] * 4
        + [f32(half, width), f32(half, width), f32(*d3.shape), f32(*u3.shape)],
        in_specs=[full] * 8 + [anywhere] * 2,
        out_specs=[full] * 5 + [anywhere] * 3,
        scratch_shapes=[
            pltpu.VMEM((4, half, width // 4), F32),
            pltpu.VMEM((4, half, width // 4), F32),
            dma((4,)), dma((4,)), dma((4,)), dma((4,)), dma((2,)), dma((2,)),
            dma((4 * steps,)), dma((4 * steps,)),
        ]
        + bufs,
        compiler_params=pltpu.CompilerParams(
            collective_id=ident, has_side_effects=True, vmem_limit_bytes=63 << 20
        ),
        cost_estimate=pl.CostEstimate(
            flops=12 * tokens * width * flat, transcendentals=0, bytes_accessed=64 << 20
        ),
    )(ht, *grads, *weights, o_pre, d3, u3)


def core_gather_kernel(norm, tiles, v_ref, gain_ref, out_ref, send_ref, recv_ref, send_sem, recv_sem):
    peer = tensor_peer(1)
    greet(peer)
    half = v_ref.shape[0]
    size = half // tiles
    copies = []
    for c in range(tiles):
        rows = slice(c * size, (c + 1) * size)
        v = v_ref[rows, :]
        if norm:
            inv = lax.rsqrt(jnp.mean(v * v, axis=-1, keepdims=True) + EPS)
            v = v * inv * gain_ref[...]
            send_ref[rows, :] = v
        out_ref[rows, :] = v.astype(BF16)
        src = send_ref if norm else v_ref
        copies.append(
            remote(
                src.at[rows, :], recv_ref.at[rows, :], send_sem.at[c], recv_sem.at[c], peer
            )
        )
        copies[-1].start()
    for c in range(tiles):
        rows = slice(c * size, (c + 1) * size)
        copies[c].wait_recv()
        out_ref[half + c * size : half + (c + 1) * size, :] = recv_ref[rows, :].astype(BF16)
    for c in copies:
        c.wait_send()


def core_gather(ident, v, gain=None):
    half, n = v.shape
    tiles = 4
    out = jax.ShapeDtypeStruct((2 * half, n), BF16)
    full = pl.BlockSpec(memory_space=pltpu.VMEM)
    norm = gain is not None
    return pl.pallas_call(
        functools.partial(core_gather_kernel, norm, tiles),
        out_shape=out,
        in_specs=[full, full],
        out_specs=full,
        scratch_shapes=[
            pltpu.VMEM((half, n) if norm else (8, DH), F32),
            pltpu.VMEM((half, n), F32),
            pltpu.SemaphoreType.DMA((tiles,)),
            pltpu.SemaphoreType.DMA((tiles,)),
        ],
        compiler_params=pltpu.CompilerParams(
            collective_id=ident, has_side_effects=True, vmem_limit_bytes=48 << 20
        ),
        cost_estimate=pl.CostEstimate(
            flops=0, transcendentals=0, bytes_accessed=nbytes(v, v, v, out)
        ),
    )(v, gain[None, :] if norm else jnp.zeros((8, DH), F32))


TILE = 256
SLOTS = 4


def feed_kernel(
    dp, turn, h_ref, ogt_ref, ht_ref, wup_hbm, wdn_hbm, ug_hbm,
    act_ref, dpre_ref, part_ref, part2_ref, far_ref, d_ref, u_ref, d_pre_ref, u_pre_ref,
    w_ref, ug_ref, ds_ref, us_ref, cs_ref, cr_ref,
    w_sem, ug_sem, d_send, d_recv, u_send, u_recv, c_send, c_recv, y_send, y_recv, free_sem,
):
    tokens, units = act_ref.shape
    half = tokens // 2
    width = h_ref.shape[1]
    cut = width // 2
    rows = width // dp
    me = lax.axis_index("dp")
    core, far = tensor_peer(1), tensor_peer(2)
    x_peer, z_peer = {"dp": me ^ 1}, {"dp": me ^ 2}
    greet(core, far, x_peer, z_peer)
    count = units // TILE

    load_w = pltpu.make_async_copy(wup_hbm, w_ref, w_sem)
    load_w.start()

    def tile_cols(t):
        return pl.ds(pl.multiple_of(t * TILE, TILE), TILE)

    def load_ug(t, k):
        return pltpu.make_async_copy(ug_hbm.at[:, tile_cols(t)], ug_ref.at[k], ug_sem.at[k])

    load_ug(0, 0).start()
    load_ug(1, 1).start()
    for j in range(dp // 2 if turn else 0):
        ht_ref[j * rows : (j + 1) * rows, :] = block_of(h_ref, dp, X_FIRST, j).T
    load_w.wait()

    def wire(t, k):
        cols = tile_cols(t)
        d = remote(ds_ref.at[k], d_ref.at[:, cols], d_send.at[t], d_recv.at[t], z_peer)
        u = remote(us_ref.at[k], u_ref.at[:, cols], u_send.at[t], u_recv.at[t], x_peer)
        return d, u

    def terms(t, k):
        cols = tile_cols(t)
        d, u = wire(t, k)
        ds_ref[k] = dot(ogt_ref[:cut, :], act_ref[:, cols])
        d.start()
        us_ref[k] = dot(ht_ref[:cut, :], dpre_ref[:, cols])
        u.start()

    @pl.loop(0, count)
    def _(t):
        k = t % 2
        cols = tile_cols(t)
        load_ug(t, k).wait()
        pre = dot(h_ref[...], w_ref[:, cols])
        c = 0.7978845608028654
        sq = pre * pre
        th = jnp.tanh(c * pre * (1.0 + 0.044715 * sq))
        mid = 0.5 * (1.0 + th)
        act_ref[:, cols] = (pre * mid).astype(BF16)
        slope = mid + 0.5 * pre * (1.0 - th * th) * (c * (1.0 + 0.134145 * sq))
        dpre_ref[:, cols] = (ug_ref[k] * slope).astype(BF16)

        @pl.when(t + 2 < count)
        def _():
            load_ug(t + 2, k).start()

        @pl.when(t < SLOTS)
        def _():
            terms(t, t)

    part_cols = width // 4

    def core_wire(c):
        return remote(cs_ref.at[c], cr_ref.at[c], c_send.at[c], c_recv.at[c], core)

    def far_wire(c):
        cols = pl.ds(c * part_cols, part_cols)
        return remote(part_ref.at[:, cols], far_ref.at[:, cols], y_send.at[c], y_recv.at[c], far)

    def summed(lhs_ref, transposed, out_ref, travels):
        def term(row, c):
            cols = slice(c * part_cols, (c + 1) * part_cols)
            lhs = lhs_ref[row * half : (row + 1) * half, :]
            if transposed:
                return dot_nt(lhs, w_ref[cols, :])
            return dot(lhs, w_ref[:, cols])

        for c in range(4):
            cs_ref[c] = term(1, c)
            core_wire(c).start()
        for c in range(4):
            part = term(0, c)
            core_wire(c).wait()
            out_ref[:, c * part_cols : (c + 1) * part_cols] = part + cr_ref[c]
            if travels:
                far_wire(c).start()

    summed(dpre_ref, True, part_ref, True)
    load_down = pltpu.make_async_copy(wdn_hbm, w_ref, w_sem)
    load_down.start()
    pl.semaphore_signal(free_sem, inc=1, device_id=core, device_id_type=pl.DeviceIdType.MESH)
    for j in range(dp // 2, dp if turn else 0):
        ht_ref[j * rows : (j + 1) * rows, :] = block_of(h_ref, dp, X_FIRST, j).T

    @pl.loop(SLOTS, count)
    def _(t):
        d, u = wire(t - SLOTS, t - SLOTS)
        d.wait_send()
        u.wait_send()
        terms(t, t - SLOTS)

    load_down.wait()
    pl.semaphore_wait(free_sem, 1)
    summed(act_ref, False, part2_ref, False)

    def load_got(src_ref, t, k):
        return pltpu.make_async_copy(src_ref.at[:, tile_cols(t)], ug_ref.at[k], ug_sem.at[k])

    def store_pre(dst_ref, t, k):
        return pltpu.make_async_copy(ug_ref.at[k], dst_ref.at[:, tile_cols(t)], ug_sem.at[k])

    @pl.loop(0, count)
    def _(t):
        d, u = wire(t, 0)

        @pl.when(t > 0)
        def _():
            store_pre(d_pre_ref, t - 1, 0).wait()
            store_pre(u_pre_ref, t - 1, 1).wait()

        d.wait_recv()
        load_got(d_ref, t, 0).start()
        u.wait_recv()
        load_got(u_ref, t, 1).start()
        load_got(d_ref, t, 0).wait()
        ug_ref[0] += dot(ogt_ref[cut:, :], act_ref[:, tile_cols(t)])
        store_pre(d_pre_ref, t, 0).start()
        load_got(u_ref, t, 1).wait()
        ug_ref[1] += dot(ht_ref[cut:, :], dpre_ref[:, tile_cols(t)])
        store_pre(u_pre_ref, t, 1).start()

    store_pre(d_pre_ref, count - 1, 0).wait()
    store_pre(u_pre_ref, count - 1, 1).wait()

    @pl.loop(count - SLOTS, count)
    def _(t):
        d, u = wire(t, t - (count - SLOTS))
        d.wait_send()
        u.wait_send()

    for c in range(4):
        far_wire(c).wait()


def feed(ident, dp, h2, og_t, h_t, w_up, w_down, up_grad):
    tokens, width = h2.shape
    units = w_up.shape[1]
    half = tokens // 2
    cut = width // 2
    count = units // TILE
    full = pl.BlockSpec(memory_space=pltpu.VMEM)
    anywhere = pl.BlockSpec(memory_space=pl.ANY)
    f32 = lambda *shape: jax.ShapeDtypeStruct(shape, F32)
    b16 = jax.ShapeDtypeStruct((tokens, units), BF16)
    dma = pltpu.SemaphoreType.DMA
    turn = h_t is None
    kernel = functools.partial(feed_kernel, dp, turn)
    if turn:

        def kernel(h_ref, ogt_ref, *refs):
            feed_kernel(dp, turn, h_ref, ogt_ref, refs[-1], *refs[:-1])

    return pl.pallas_call(
        kernel,
        out_shape=[b16, b16, f32(half, width), f32(half, width), f32(half, width)]
        + [f32(cut, units)] * 4,
        in_specs=[full] * (2 if turn else 3) + [anywhere] * 3,
        out_specs=[full] * 4 + [anywhere] * 5,
        scratch_shapes=[
            pltpu.VMEM((width, units), BF16),
            pltpu.VMEM((2, tokens, TILE), F32),
            pltpu.VMEM((SLOTS, cut, TILE), F32),
            pltpu.VMEM((SLOTS, cut, TILE), F32),
            pltpu.VMEM((4, half, width // 4), F32),
            pltpu.VMEM((4, half, width // 4), F32),
            dma, dma((2,)), dma((count,)), dma((count,)), dma((count,)), dma((count,)),
            dma((4,)), dma((4,)), dma((4,)), dma((4,)), pltpu.SemaphoreType.REGULAR,
        ]
        + ([pltpu.VMEM((width, tokens), BF16)] if turn else []),
        compiler_params=pltpu.CompilerParams(
            collective_id=ident, has_side_effects=True, vmem_limit_bytes=62 << 20
        ),
        cost_estimate=pl.CostEstimate(
            flops=10 * tokens * width * units, transcendentals=tokens * units,
            bytes_accessed=64 << 20,
        ),
    )(h2, og_t, *([] if turn else [h_t]), w_up, w_down, up_grad)


def body(
    inputs,
    gain_attn,
    w_query,
    w_key,
    w_value,
    gate_logit,
    w_out,
    gain_mlp,
    w_up,
    w_down,
    seg_parent,
    out_grad,
):
    tokens, width = inputs.shape
    half = tokens // 2
    segs = tokens // SEG
    heads = w_query.shape[1] // DH
    pairs = segs * heads
    units = w_up.shape[1]
    flat = heads * DH
    scale = DH ** (-0.5)
    dp = lax.axis_size("dp")
    tn = lax.axis_size("tensor")
    rows = width // dp
    di = lax.axis_index("dp")
    core = lax.axis_index("tensor") % 2

    one = jnp.where(seg_parent[0] < tokens * dp, 1.0, 2.0)

    def low_after_wire(v):
        return (v * one).astype(BF16)

    def swap_core(v):
        return lax.ppermute(v, "tensor", [(i, i ^ 1) for i in range(tn)])

    def swap_y(v):
        return lax.ppermute(v, "tensor", [(i, i ^ 2) for i in range(tn)])

    def swap_dp(v, mask):
        return lax.ppermute(v, "dp", [(i, i ^ mask) for i in range(dp)])

    def columns(v, order):
        _, seq = halving(dp, order)
        return block_columns(v, [di ^ k for k in seq], rows)

    def blocks_for(v, order):
        return columns(v, order) if rows % DH else v

    cut = width // 2
    quarter = cut // 2

    def pick(v, index, axis):
        size = v.shape[axis] // 2
        return lax.dynamic_slice_in_dim(v, index * size, size, axis)

    def place(own, other, index, axis):
        return jnp.where(
            index == 0,
            jnp.concatenate([own, other], axis),
            jnp.concatenate([other, own], axis),
        )

    def inv_rms(v):
        return lax.rsqrt(jnp.mean(v * v, axis=-1, keepdims=True) + EPS)

    x_own = pick(inputs, core, 0).astype(F32)
    x_oth = pick(inputs, 1 - core, 0).astype(F32)
    inv_own = inv_rms(x_own)
    inv_oth = inv_rms(x_oth)
    h1 = jnp.concatenate(
        [
            (x_own * inv_own * gain_attn).astype(BF16),
            (x_oth * inv_oth * gain_attn).astype(BF16),
        ],
        0,
    )

    sub = segs // 2
    every = jnp.arange(seg_parent.shape[0], dtype=jnp.int32)
    sub_ids = jnp.arange(sub, dtype=jnp.int32)
    seg_local = jnp.concatenate([core * sub + sub_ids, (1 - core) * sub + sub_ids])
    order = spread_order(dp)
    ids = jnp.concatenate([(di ^ j) * segs + seg_local for j in order])
    mine_hot = (ids[:segs, None] == every[None, :]).astype(F32)
    ids_hot = (ids[:, None] == every[None, :]).astype(F32)
    lineage = ancestor_table(seg_parent)

    def weights_of(table):
        mine_rows = jnp.sum(mine_hot[:, :, None] * table[None], axis=1)
        return jnp.sum(mine_rows[:, None, :] * ids_hot[None], axis=-1)

    up_weight = weights_of(lineage)
    down_weight = weights_of(lineage.T)

    gate = jax.nn.sigmoid(gate_logit)
    gate_row = gate[None, :]

    og_own = pick(out_grad, core, 0)
    og = jnp.concatenate([og_own, pick(out_grad, 1 - core, 0)], 0)
    block_rows = pairs * DH + pairs
    act_f32 = jax.ShapeDtypeStruct((tokens, flat), F32)
    act_b16 = jax.ShapeDtypeStruct((tokens, flat), BF16)
    mem_shape = jax.ShapeDtypeStruct((pairs * DH, DH), F32)
    zin_shape = jax.ShapeDtypeStruct((pairs, DH), F32)
    full = pl.BlockSpec(memory_space=pltpu.VMEM)

    def attention_call(kernel, ident, outs, out_specs, scratch, args, in_specs, flops):
        return pl.pallas_call(
            functools.partial(kernel, dp, heads, segs, scale),
            out_shape=outs,
            in_specs=in_specs,
            out_specs=out_specs,
            scratch_shapes=scratch
            + [
                pltpu.VMEM((dp, block_rows, DH), F32),
                pltpu.SemaphoreType.DMA((dp,)),
                pltpu.SemaphoreType.DMA((dp,)),
            ],
            compiler_params=pltpu.CompilerParams(
                collective_id=ident, has_side_effects=True, vmem_limit_bytes=63 << 20
            ),
            cost_estimate=pl.CostEstimate(
                flops=flops, transcendentals=0, bytes_accessed=64 << 20
            ),
        )(*args)

    head_flops = 2 * segs * heads * SEG * SEG * DH
    dma = pltpu.SemaphoreType.DMA
    qh, kh, vh, a16, a_pair, local, memory, zin, w_out_all = attention_call(
        attention_kernel,
        0,
        [
            act_b16, act_b16, act_b16, act_b16,
            jax.ShapeDtypeStruct((half, 2 * flat), F32),
            act_f32, mem_shape, zin_shape,
            jax.ShapeDtypeStruct((4 * flat, width), BF16),
        ],
        [full] * 9,
        [
            pltpu.VMEM((4, flat, width), F32),
            pltpu.VMEM((half, flat), F32),
            dma((3 * W_CHUNKS,)), dma((3 * W_CHUNKS,)), dma, dma,
        ],
        (up_weight, gate_row, h1, w_query, w_key, w_value, w_out),
        [SMEM, SMEM] + [full] * 5,
        3 * head_flops + 6 * tokens * width * flat,
    )
    up_grad = dot_nt(og, after(w_down, a_pair))

    step = half // AG_CHUNKS
    a_near = [a_pair[c * step : (c + 1) * step] for c in range(AG_CHUNKS)]
    a_far = [swap_y(v) for v in a_near]
    near = [
        x_own[c * step : (c + 1) * step] + dot(v.astype(BF16), w_out_all[: 2 * flat])
        for c, v in enumerate(a_near)
    ]
    og_t = columns(after(og, up_grad), Z_FIRST).T
    h1_a = columns(after(h1, og_t), X_FIRST).T
    resids = [
        n + dot(low_after_wire(after(f, og_t, h1_a)), w_out_all[2 * flat :])
        for n, f in zip(near, a_far)
    ]
    resid = jnp.concatenate(resids, 0)
    inv_mlp = inv_rms(resid)
    h2 = core_gather(1, resid, gain_mlp)

    h_t = columns(h2, X_FIRST).T if rows % DH else None
    act, dpre, dh2_part, out_part, dh2_far, _, _, d_pre, u_pre = feed(
        2, dp, h2, og_t, h_t, w_up, w_down, up_grad
    )

    dh2 = dh2_part + dh2_far
    gs = dh2 * gain_mlp
    dresid = (
        og_own.astype(F32)
        + inv_mlp * gs
        - resid * inv_mlp * inv_mlp * inv_mlp * jnp.mean(gs * resid, axis=-1, keepdims=True)
    )
    gain_mlp_part = jnp.sum(dh2 * resid * inv_mlp, axis=0)
    dr = core_gather(4, dresid)

    da = dot_nt(dr, w_out).astype(BF16)
    anywhere = pl.BlockSpec(memory_space=pl.ANY)
    ride = jax.ShapeDtypeStruct((quarter, units), F32)
    o_shape = jax.ShapeDtypeStruct((cut, flat), F32)
    dq16, dk16, dv16, gate_rows, o_pre, d_rode, u_rode, out_far = attention_call(
        attention_back_kernel,
        5,
        [
            act_b16, act_b16, act_b16, zin_shape, o_shape, ride, ride,
            jax.ShapeDtypeStruct((half, width), F32),
        ],
        [full] * 5 + [anywhere] * 3,
        [pltpu.VMEM((tokens, flat), F32)] * 3
        + [pltpu.VMEM((cut, flat), F32)]
        + [dma((4,)), dma((4,))],
        (
            down_weight, gate_row, qh, kh, vh, da, local, memory, zin,
            blocks_for(dr, Z_FIRST), a16, d_pre, u_pre, out_part,
        ),
        [SMEM, SMEM] + [full] * 9 + [anywhere] * 3,
        9 * head_flops,
    )
    gate_part = jnp.sum(gate_rows.reshape(segs, heads, DH), axis=(0, 2)) * gate * (1.0 - gate)

    eighth = quarter // 2
    third = [p[quarter : quarter + eighth] + r[:eighth] for p, r in ((d_pre, d_rode), (u_pre, u_rode))]
    w_query_grad, w_key_grad, w_value_grad, w_out_rows, dh1_part, dh1_far, d3, u3 = tail(
        7, dp, h1_a, (dq16, dk16, dv16), (w_query, w_key, w_value), o_pre, *third
    )
    w_out_grad = w_out_rows.T

    def finish(pre, rode, got, order):
        masks, _ = halving(dp, order)
        value = pre[quarter + eighth :] + rode[eighth:] + got
        for m in masks[3:]:
            n = value.shape[0] // 2
            value = value[n:] + swap_dp(value[:n], m)
        return value

    w_down_grad = finish(d_pre, d_rode, d3, Z_FIRST).T
    w_up_grad = finish(u_pre, u_rode, u3, X_FIRST)

    out_own = (resid + out_part + out_far).astype(BF16)
    outputs = place(out_own, low_after_wire(swap_core(out_own.astype(F32))), core, 0)

    dh1 = dh1_part + dh1_far
    gs1 = dh1 * gain_attn
    dx = (
        dresid
        + inv_own * gs1
        - x_own * inv_own * inv_own * inv_own * jnp.mean(gs1 * x_own, axis=-1, keepdims=True)
    )
    gain_attn_part = jnp.sum(dh1 * x_own * inv_own, axis=0)
    dx_own = dx.astype(BF16)
    input_grad = place(dx_own, low_after_wire(swap_core(dx_own.astype(F32))), core, 0)

    gains = jnp.concatenate([gain_attn_part, gain_mlp_part])
    small = jnp.concatenate([gains + swap_core(gains), jnp.pad(gate_part, (0, DH - heads))])
    bit = 1
    while bit < dp:
        small = small + swap_dp(small, bit)
        bit *= 2
    gain_attn_grad = lax.dynamic_slice_in_dim(small, di * rows, rows, 0)
    gain_mlp_grad = lax.dynamic_slice_in_dim(small, width + di * rows, rows, 0)
    gate_grad = small[2 * width : 2 * width + heads]

    return (
        outputs,
        input_grad,
        gain_attn_grad,
        w_query_grad,
        w_key_grad,
        w_value_grad,
        gate_grad,
        w_out_grad,
        gain_mlp_grad,
        w_up_grad,
        w_down_grad,
    )


def solution(mesh):
    placed = (
        P("dp", None),
        P(),
        P(None, "tensor"),
        P(None, "tensor"),
        P(None, "tensor"),
        P("tensor"),
        P("tensor", None),
        P(),
        P(None, "tensor"),
        P("tensor", None),
        P(),
        P("dp", None),
    )
    return jax.shard_map(
        body,
        mesh=mesh,
        in_specs=placed,
        out_specs=(
            P("dp", None),
            P("dp", None),
            P("dp"),
            P("dp", "tensor"),
            P("dp", "tensor"),
            P("dp", "tensor"),
            P("tensor"),
            P("tensor", "dp"),
            P("dp"),
            P("dp", "tensor"),
            P("tensor", "dp"),
        ),
        check_vma=False,
    )
```

```python
import functools

import jax
import jax.numpy as jnp
from jax import lax
from jax.experimental import pallas as pl
from jax.experimental.pallas import tpu as pltpu
from jax.sharding import PartitionSpec as P

DH = 128
SEG = 512
DEPTH = 5
EPS = 1e-06

F32 = jnp.float32
BF16 = jnp.bfloat16

AG_CHUNKS = 2
Z_FIRST = (1, 0)
X_FIRST = (0, 1)


def feature_map(values):
    return jnp.where(values > 0, values + 1.0, jnp.exp(jnp.minimum(values, 0.0)))


def feature_slope(values):
    return jnp.where(values > 0, 1.0, jnp.exp(jnp.minimum(values, 0.0)))


def ancestor_table(seg_parent):
    seg_total = seg_parent.shape[0]
    columns = jnp.arange(seg_total, dtype=jnp.int32)
    current = seg_parent
    lineage_table = jnp.zeros((seg_total, seg_total), F32)
    for _ in range(DEPTH):
        onehot = current[:, None] == columns[None, :]
        lineage_table = lineage_table + onehot.astype(F32)
        lifted = jnp.sum(jnp.where(onehot, seg_parent[None, :], 0), axis=1)
        current = jnp.where(current >= 0, lifted, -1)
    return lineage_table


def dot(a, b):
    return jnp.dot(a, b, preferred_element_type=F32)


def dot_t(a, b):
    return lax.dot_general(a, b, (((0,), (0,)), ((), ())), preferred_element_type=F32)


def dot_nt(a, b):
    return lax.dot_general(a, b, (((1,), (1,)), ((), ())), preferred_element_type=F32)


def after(value, *earlier):
    return lax.optimization_barrier((value, earlier))[0]


def nbytes(*arrays):
    return sum(a.size * a.dtype.itemsize for a in arrays)


def copy_kernel(ids_ref, in_ref, out_ref):
    out_ref[...] = in_ref[...]


def block_columns(v, ids, size):
    if size % 128:
        return jnp.concatenate([lax.dynamic_slice_in_dim(v, i * size, size, 1) for i in ids], 1)
    height, width = v.shape
    return pl.pallas_call(
        copy_kernel,
        out_shape=jax.ShapeDtypeStruct(v.shape, v.dtype),
        grid_spec=pltpu.PrefetchScalarGridSpec(
            num_scalar_prefetch=1,
            grid=(width // size,),
            in_specs=[pl.BlockSpec((height, size), lambda k, ids: (0, ids[k]))],
            out_specs=pl.BlockSpec((height, size), lambda k, ids: (0, k)),
        ),
        cost_estimate=pl.CostEstimate(flops=0, transcendentals=0, bytes_accessed=2 * nbytes(v)),
    )(jnp.stack(ids), v)


SMEM = pl.BlockSpec(memory_space=pltpu.SMEM)


def causal_mask():
    row = lax.broadcasted_iota(jnp.int32, (SEG, SEG), 0)
    col = lax.broadcasted_iota(jnp.int32, (SEG, SEG), 1)
    return row >= col


def softmax_rows(q, k, scale):
    scores = dot_nt(q, k) * scale
    scores = jnp.where(causal_mask(), scores, -1e30)
    top = jnp.max(scores, axis=-1, keepdims=True)
    e = jnp.exp(scores - top)
    return e * (1.0 / jnp.sum(e, axis=-1, keepdims=True))


def head_part(heads, p):
    s, h = p // heads, p % heads
    return pl.ds(pl.multiple_of(s * SEG, SEG), SEG), pl.ds(pl.multiple_of(h * DH, DH), DH)


def matrix_part(p):
    return pl.ds(pl.multiple_of(p * DH, DH), DH)


def weighted(w_ref, p, heads, segs, blocks_ref):
    s, h = p // heads, p % heads
    pairs = segs * heads
    big = jnp.zeros((DH, DH), F32)
    small = jnp.zeros((1, DH), F32)
    for d in range(blocks_ref.shape[0]):
        for n in range(segs):
            w = w_ref[s, d * segs + n]
            o = n * heads + h
            big = big + w * blocks_ref[d, matrix_part(o), :]
            small = small + w * blocks_ref[d, pl.ds(pairs * DH + o, 1), :]
    return big, small


def spread_order(dp):
    low = [0]
    for b in reversed(range(1, dp.bit_length() - 1)):
        low = low + [v ^ (1 << b) for v in low]
    return low + [v ^ 1 for v in low]


def greet(*peers):
    barrier = pltpu.get_barrier_semaphore()
    for peer in peers:
        pl.semaphore_signal(barrier, inc=1, device_id=peer, device_id_type=pl.DeviceIdType.MESH)
    pl.semaphore_wait(barrier, len(peers))


def dp_peers(dp):
    me = lax.axis_index("dp")
    return [{"dp": me ^ (1 << b)} for b in range(dp.bit_length() - 1)]


def tensor_peer(mask):
    return {"tensor": lax.axis_index("tensor") ^ mask}


def halving(dp, order):
    masks = [1 << b for b in order]
    masks += [1 << b for b in range(len(order), dp.bit_length() - 1)]
    seq = [0]
    for m in reversed(masks):
        seq = [m ^ v for v in seq] + seq
    return masks, seq


def near_units(dp, units):
    return units // 4 if dp == 8 else units


def block_of(ref, dp, order, k):
    rows = ref.shape[1] // dp
    if rows % DH:
        return ref[:, k * rows : (k + 1) * rows]
    at = (lax.axis_index("dp") ^ halving(dp, order)[1][k]) * rows
    return ref[:, pl.ds(pl.multiple_of(at, rows), rows)]


def remote(src, dst, send_sem, recv_sem, peer):
    return pltpu.make_async_remote_copy(
        src_ref=src,
        dst_ref=dst,
        send_sem=send_sem,
        recv_sem=recv_sem,
        device_id=peer,
        device_id_type=pl.DeviceIdType.MESH,
    )


def spread(dp, blocks_ref, send_sem, recv_sem, compute):
    me = lax.axis_index("dp")
    slot = {j: k for k, j in enumerate(spread_order(dp))}
    copies = {}

    def send(j, mask):
        to = j ^ mask
        k = slot[to]
        copies[to] = pltpu.make_async_remote_copy(
            src_ref=blocks_ref.at[slot[j]],
            dst_ref=blocks_ref.at[k],
            send_sem=send_sem.at[k],
            recv_sem=recv_sem.at[k],
            device_id={"dp": me ^ mask},
            device_id_type=pl.DeviceIdType.MESH,
        )
        copies[to].start()

    bits = [1 << b for b in range(1, dp.bit_length() - 1)]
    for m in bits:
        send(0, m)
    send(0, 1)
    compute()
    for m in bits:
        copies[m].wait_recv()
        if m == bits[-1]:
            near = [0, m]
            for n in reversed(bits[:-1]):
                for j in near[1:]:
                    send(j, n)
                near = near + [n] + [j ^ n for j in near[1:]]
                if n != bits[0]:
                    for j in near:
                        if j & n and j != n:
                            copies[j].wait_recv()
        send(m, 1)
    last = [j for j in near if j and j not in bits]
    for j in last:
        if j & bits[0] or len(bits) == 1:
            copies[j].wait_recv()
        send(j, 1)
    for j in near:
        copies[j ^ 1].wait_recv()
    for c in copies.values():
        c.wait_send()


W_CHUNKS = 4


def attention_kernel(
    dp, heads, segs, scale, w_ref, g_ref, h_ref, wq_ref, wk_ref, wv_ref, wo_ref,
    q_ref, k_ref, v_ref, a16_ref, pair_ref, local_ref, mem_ref, zin_ref, all_ref,
    wf_ref, asend_ref, w_send, w_recv, a_send, a_recv, blocks_ref, send_sem, recv_sem,
):
    pairs = segs * heads
    flat = heads * DH
    half = segs * SEG // 2
    core, far = tensor_peer(1), tensor_peer(2)
    greet(*dp_peers(dp), core, far)

    size = flat // W_CHUNKS
    w_copies = {}

    def w_send_chunk(j, c, to, peer):
        rows = pl.ds(c * size, size)
        k = (to - 1) * W_CHUNKS + c
        w_copies[to, c] = remote(
            wf_ref.at[j, rows, :], wf_ref.at[to, rows, :], w_send.at[k], w_recv.at[k], peer
        )
        w_copies[to, c].start()

    def w_done(to, c):
        rows = slice(c * size, (c + 1) * size)
        w_copies[to, c].wait_recv()
        all_ref[to * flat + c * size : to * flat + (c + 1) * size, :] = wf_ref[to, rows, :].astype(
            BF16
        )

    for c in range(W_CHUNKS):
        rows = slice(c * size, (c + 1) * size)
        wf_ref[0, rows, :] = wo_ref[rows, :].astype(F32)
        w_send_chunk(0, c, 2, far)
        w_send_chunk(0, c, 1, core)
    all_ref[:flat, :] = wo_ref[...]

    def project(matrix_ref, out_ref):
        @pl.loop(0, segs * SEG // 256)
        def _(i):
            rows = pl.ds(pl.multiple_of(i * 256, 256), 256)
            out_ref[rows, :] = dot(h_ref[rows, :], matrix_ref[...]).astype(BF16)

    project(wk_ref, k_ref)
    project(wv_ref, v_ref)

    @pl.loop(0, pairs)
    def _(p):
        at = head_part(heads, p)
        sk = feature_map(k_ref[at].astype(F32))
        blocks_ref[0, matrix_part(p), :] = dot_t(sk.astype(BF16), v_ref[at])
        blocks_ref[0, pl.ds(pairs * DH + p, 1), :] = jnp.sum(sk, axis=0, keepdims=True)

    def compute():
        project(wq_ref, q_ref)

        @pl.loop(0, pairs)
        def _(p):
            at = head_part(heads, p)
            probs = softmax_rows(q_ref[at], k_ref[at], scale)
            local_ref[at] = dot(probs.astype(BF16), v_ref[at])

    spread(dp, blocks_ref, send_sem, recv_sem, compute)

    @pl.loop(0, pairs)
    def _(p):
        at = head_part(heads, p)
        mem, zin = weighted(w_ref, p, heads, segs, blocks_ref)
        mem_ref[matrix_part(p), :] = mem
        zin_ref[pl.ds(p, 1), :] = zin
        g = g_ref[0, p % heads]
        sq = feature_map(q_ref[at].astype(F32))
        den = jnp.sum(sq * zin, axis=-1, keepdims=True) + 1.0
        retrieved = dot(sq.astype(BF16), mem.astype(BF16)) / den
        a16_ref[at] = (g * retrieved + (1.0 - g) * local_ref[at]).astype(BF16)

    asend_ref[...] = a16_ref[half:, :].astype(F32)
    a_copy = remote(asend_ref, pair_ref.at[:, pl.ds(flat, flat)], a_send, a_recv, core)
    a_copy.start()
    pair_ref[:, :flat] = a16_ref[:half, :].astype(F32)
    for c in range(W_CHUNKS):
        w_done(1, c)
    a_copy.wait_recv()
    for c in range(W_CHUNKS):
        w_copies[2, c].wait_recv()
        w_send_chunk(2, c, 3, core)
        rows = slice(c * size, (c + 1) * size)
        all_ref[2 * flat + c * size : 2 * flat + (c + 1) * size, :] = wf_ref[2, rows, :].astype(BF16)
    for c in range(W_CHUNKS):
        w_done(3, c)
    for copy in w_copies.values():
        copy.wait_send()
    a_copy.wait_send()


def attention_back_kernel(
    dp, heads, segs, scale, w_ref, g_ref, q_ref, k_ref, v_ref, da_ref, local_ref, mem_ref, zin_ref,
    dr_ref, a16_ref, d_pre_ref, u_pre_ref, out_part_ref,
    dq_ref, dk_ref, dv_ref, gate_ref, o_pre_ref, d_rode_ref, u_rode_ref, out_far_ref,
    dqm_ref, dkl_ref, dvl_ref, os_ref, ride_send, ride_recv, blocks_ref, send_sem, recv_sem,
):
    pairs = segs * heads
    me = lax.axis_index("dp")
    far = tensor_peer(2)
    greet(*dp_peers(dp), far)
    legs = [
        (d_pre_ref, d_rode_ref, {"dp": me ^ 1}),
        (out_part_ref, out_far_ref, far),
        (os_ref, o_pre_ref, {"dp": me ^ 2}),
    ]
    quarter, units = d_rode_ref.shape
    eighth = quarter // 2
    legs[0] = (d_pre_ref.at[pl.ds(0, quarter), :], d_rode_ref, {"dp": me ^ 1})
    near = near_units(dp, units)
    cols = pl.ds(0, near)
    legs.append((u_pre_ref.at[pl.ds(0, quarter), cols], u_rode_ref.at[:, cols], {"dp": me ^ 2}))
    if near < units:
        cols = pl.ds(near, units - near)
        for k in range(2):
            legs.append(
                (
                    u_pre_ref.at[pl.ds(2 * k * eighth, eighth), cols],
                    u_rode_ref.at[pl.ds(k * eighth, eighth), cols],
                    {"dp": me ^ 4},
                )
            )
    riders = [
        remote(src, dst, ride_send.at[i], ride_recv.at[i], peer)
        for i, (src, dst, peer) in enumerate(legs)
    ]
    o_rider = riders[2]
    plain = riders[:2] + riders[3:]

    @pl.loop(0, pairs)
    def _(p):
        at = head_part(heads, p)
        g = g_ref[0, p % heads]
        qf = q_ref[at].astype(F32)
        sq = feature_map(qf)
        sq16 = sq.astype(BF16)
        mem16 = mem_ref[matrix_part(p), :].astype(BF16)
        zin = zin_ref[pl.ds(p, 1), :]
        inv_den = 1.0 / (jnp.sum(sq * zin, axis=-1, keepdims=True) + 1.0)
        retrieved = dot(sq16, mem16) * inv_den
        da = da_ref[at].astype(F32)
        gate_ref[pl.ds(p, 1), :] = jnp.sum(da * (retrieved - local_ref[at]), axis=0, keepdims=True)
        dnum = g * da * inv_den
        dden = -jnp.sum(dnum * retrieved, axis=-1, keepdims=True)
        dnum16 = dnum.astype(BF16)
        blocks_ref[0, matrix_part(p), :] = dot_t(sq16, dnum16)
        blocks_ref[0, pl.ds(pairs * DH + p, 1), :] = jnp.sum(sq * dden, axis=0, keepdims=True)
        dsq = dot_nt(dnum16, mem16) + dden * zin
        dqm_ref[at] = dsq * feature_slope(qf)

    rows = dr_ref.shape[1] // dp
    half_blocks = dp // 2

    def compute():
        for r in plain:
            r.start()
        for j in range(half_blocks):
            os_ref[j * rows : (j + 1) * rows, :] = dot_t(
                block_of(dr_ref, dp, Z_FIRST, j), a16_ref[...]
            )
        o_rider.start()

        @pl.loop(0, pairs)
        def _(p):
            at = head_part(heads, p)
            g = g_ref[0, p % heads]
            q, k, v, da = q_ref[at], k_ref[at], v_ref[at], da_ref[at]
            probs = softmax_rows(q, k, scale)
            dprobs = (1.0 - g) * dot_nt(da, v)
            inner = jnp.sum(dprobs * probs, axis=-1, keepdims=True)
            ds16 = (probs * (dprobs - inner)).astype(BF16)
            dq_ref[at] = (dot(ds16, k) * scale + dqm_ref[at]).astype(BF16)
            dkl_ref[at] = dot_t(ds16, q) * scale
            dvl_ref[at] = (1.0 - g) * dot_t(probs.astype(BF16), da)

    spread(dp, blocks_ref, send_sem, recv_sem, compute)

    @pl.loop(0, pairs)
    def _(p):
        at = head_part(heads, p)
        dd, dz = weighted(w_ref, p, heads, segs, blocks_ref)
        dd16 = dd.astype(BF16)
        kf = k_ref[at].astype(F32)
        dsk = dot_nt(v_ref[at], dd16) + dz
        dk_ref[at] = (dkl_ref[at] + dsk * feature_slope(kf)).astype(BF16)
        dv_ref[at] = (dvl_ref[at] + dot(feature_map(kf).astype(BF16), dd16)).astype(BF16)

    o_rider.wait()
    for j in range(half_blocks):
        o_pre_ref[j * rows : (j + 1) * rows, :] += dot_t(
            block_of(dr_ref, dp, Z_FIRST, half_blocks + j), a16_ref[...]
        )
    for r in plain:
        r.wait()


ROWS = 128


def tail_kernel(
    dp, turn, order, o_order,
    h_ref, dq_ref, dk_ref, dv_ref, wq_ref, wk_ref, wv_ref, o_pre_ref, gain_ref, vec_ref,
    d3_ref, u3_ref, resid_hbm, out_part_hbm, out_far_hbm, dresid_hbm, x_hbm,
    gq_ref, gk_ref, gv_ref, go_ref, vec_out_ref, far_ref, d3_got_ref, u3_got_ref, out_hbm, dx_hbm,
    part_ref, cs_ref, cr_ref, in_ref, own_ref, other_ref, vec_got_ref,
    c_send, c_recv, y_send, y_recv, ride_send, ride_recv, e_send, e_recv, v_send, v_recv,
    in_sem, st_sem, free_sem, *bufs,
):
    me = lax.axis_index("dp")
    side = lax.axis_index("tensor") % 2
    core, far = tensor_peer(1), tensor_peer(2)
    greet(*dp_peers(dp), core, far)
    masks, _ = halving(dp, order)
    o_masks, _ = halving(dp, o_order)
    steps = len(masks)
    half, width = far_ref.shape
    rows = width // dp
    chunks = half // ROWS
    ht_ref = bufs[-1] if turn else h_ref
    lhs = (dq_ref, dk_ref, dv_ref, None)
    outs = (gq_ref, gk_ref, gv_ref, go_ref)
    copies = {}

    def buffers(i, step):
        k = 2 * (i * steps + step)
        return bufs[k], bufs[k + 1]

    def term(i, step):
        lo = rows * sum(dp >> (n + 1) for n in range(step))
        count = rows * (dp >> (step + 1)) if step < steps else rows
        start = 0
        if i < 3:
            value = dot(ht_ref[lo : lo + count, :], lhs[i][...])
        else:
            base = rows * (dp // 2)
            value = o_pre_ref[lo - base : lo - base + count, :]
            start = 1
        for n in range(start, step):
            at = lo - rows * sum(dp >> (m + 1) for m in range(n + 1))
            value = value + buffers(i, n)[1][at : at + count, :]
        return value

    def advance(i, step):
        if step > (1 if i == 3 else 0):
            copies[i, step - 1].wait_recv()
        if step == steps:
            outs[i][...] = term(i, step)
            return
        send, recv = buffers(i, step)
        send[...] = term(i, step)
        mask = (o_masks if i == 3 else masks)[step]
        k = i * steps + step
        copies[i, step] = remote(send, recv, e_send.at[k], e_recv.at[k], {"dp": me ^ mask})
        copies[i, step].start()

    third = {"dp": me ^ masks[2]}
    units = u3_ref.shape[1]
    near = near_units(dp, units)
    cols = pl.ds(0, near)
    legs = [(d3_ref, d3_got_ref, third), (u3_ref.at[:, cols], u3_got_ref.at[:, cols], third)]
    if near < units:
        cols = pl.ds(near, units - near)
        legs.append((u3_ref.at[:, cols], u3_got_ref.at[:, cols], {"dp": me ^ 2}))
    riders = [
        remote(src, dst, ride_send.at[i], ride_recv.at[i], peer)
        for i, (src, dst, peer) in enumerate(legs)
    ]
    for r in riders:
        r.start()
    advance(3, 1)
    for j in range(dp // 2 if turn else 0):
        ht_ref[j * rows : (j + 1) * rows, :] = block_of(h_ref, dp, order, j).T
    for i in range(3):
        advance(i, 0)

    def part_rows(c):
        return pl.ds(c * ROWS, ROWS)

    def core_wire(c):
        return remote(cs_ref.at[c], cr_ref.at[c], c_send.at[c], c_recv.at[c], core)

    def core_free():
        pl.semaphore_signal(free_sem, inc=1, device_id=core, device_id_type=pl.DeviceIdType.MESH)

    def far_wire(c):
        return remote(part_ref.at[c], far_ref.at[part_rows(c), :], y_send.at[c], y_recv.at[c], far)

    def back(lo):
        return sum(
            dot_nt(v[lo : lo + ROWS, :], w[...])
            for v, w in zip(lhs[:3], (wq_ref, wk_ref, wv_ref))
        )

    for c in range(chunks):
        cs_ref[c] = back(half + c * ROWS)
        core_wire(c).start()
    for c in range(chunks):
        value = back(c * ROWS)
        core_wire(c).wait()
        part_ref[c] = value + cr_ref[c]
        far_wire(c).start()
    core_free()

    def both_cores(sources, compute, dst_hbm):
        pl.semaphore_wait(free_sem, 1)
        for c in range(chunks):
            loads = [
                pltpu.make_async_copy(src.at[part_rows(c), :], in_ref.at[k], in_sem.at[k])
                for k, src in enumerate(sources)
            ]
            for load in loads:
                load.start()
            for load in loads:
                load.wait()
            value = compute(c).astype(BF16)
            own_ref[...] = value
            cs_ref[c] = value.astype(F32)
            core_wire(c).start()
            at = pl.ds(pl.multiple_of(side * half + c * ROWS, ROWS), ROWS)
            store = pltpu.make_async_copy(own_ref, dst_hbm.at[at, :], st_sem.at[0])
            store.start()
            store.wait()
        for c in range(chunks):
            core_wire(c).wait()
            other_ref[...] = cr_ref[c].astype(BF16)
            at = pl.ds(pl.multiple_of((1 - side) * half + c * ROWS, ROWS), ROWS)
            store = pltpu.make_async_copy(other_ref, dst_hbm.at[at, :], st_sem.at[1])
            store.start()
            store.wait()

    def output_rows(c):
        return in_ref[0] + in_ref[1] + in_ref[2]

    def input_rows(c):
        x, grad = in_ref[2], part_ref[c] + in_ref[0]
        inv = lax.rsqrt(jnp.mean(x * x, axis=-1, keepdims=True) + EPS)
        gs = grad * gain_ref[...]
        inner = jnp.mean(gs * x, axis=-1, keepdims=True)
        vec_out_ref[0:1, :] += jnp.sum(grad * x * inv, axis=0, keepdims=True)
        return in_ref[1] + inv * gs - x * inv * inv * inv * inner

    for j in range(dp // 2, dp if turn else 0):
        ht_ref[j * rows : (j + 1) * rows, :] = block_of(h_ref, dp, order, j).T
    if steps == 3:
        advance(3, 2)
    both_cores((resid_hbm, out_part_hbm, out_far_hbm), output_rows, out_hbm)
    core_free()
    if steps == 3:
        for i, step in ((0, 1), (1, 1), (0, 2), (1, 2), (2, 1), (3, 3)):
            advance(i, step)
        rest = ((0, 3), (2, 2), (1, 3), (2, 3))
    else:
        for step in range(1, steps):
            for i in (3, 0, 1, 2) if step > 1 else (0, 1, 2):
                advance(i, step)
        rest = [(i, steps) for i in (3, 0, 1, 2)]

    for c in range(chunks):
        far_wire(c).wait()
    vec_out_ref[...] = vec_ref[...]
    both_cores((far_ref, dresid_hbm, x_hbm), input_rows, dx_hbm)
    for i, step in rest:
        advance(i, step)

    for k, peer in enumerate([core] + dp_peers(dp)):
        hop = remote(vec_out_ref, vec_got_ref.at[k], v_send.at[k], v_recv.at[k], peer)
        hop.start()
        hop.wait()
        got = vec_got_ref[k]
        if k == 0:
            got = jnp.where(lax.broadcasted_iota(jnp.int32, got.shape, 0) < 2, got, 0.0)
        vec_out_ref[...] += got
    for c in copies.values():
        c.wait_send()
    for r in riders:
        r.wait()


def tail(ident, dp, h1, h1_t, grads, weights, o_pre, gain, vec, d3, u3, streams):
    tokens, width = h1.shape
    turn = h1_t is None
    flat = grads[0].shape[1]
    half = tokens // 2
    rows = width // dp
    steps = dp.bit_length() - 1
    full = pl.BlockSpec(memory_space=pltpu.VMEM)
    anywhere = pl.BlockSpec(memory_space=pl.ANY)
    f32 = lambda *shape: jax.ShapeDtypeStruct(shape, F32)
    dma = pltpu.SemaphoreType.DMA
    bufs = []
    for i in range(4):
        for step in range(steps):
            count = rows * (dp >> (step + 1)) if i < 3 or step else 8
            bufs += [pltpu.VMEM((count, flat), F32)] * 2
    chunks = half // ROWS
    b16 = jax.ShapeDtypeStruct((tokens, width), BF16)
    return pl.pallas_call(
        functools.partial(tail_kernel, dp, turn, X_FIRST, Z_FIRST),
        out_shape=[f32(rows, flat)] * 4
        + [f32(*vec.shape), f32(half, width), f32(*d3.shape), f32(*u3.shape), b16, b16],
        in_specs=[full] * 10 + [anywhere] * 7,
        out_specs=[full] * 5 + [anywhere] * 5,
        scratch_shapes=[
            pltpu.VMEM((chunks, ROWS, width), F32),
            pltpu.VMEM((chunks, ROWS, width), F32),
            pltpu.VMEM((chunks, ROWS, width), F32),
            pltpu.VMEM((3, ROWS, width), F32),
            pltpu.VMEM((ROWS, width), BF16),
            pltpu.VMEM((ROWS, width), BF16),
            pltpu.VMEM((steps + 1,) + vec.shape, F32),
            dma((chunks,)), dma((chunks,)), dma((chunks,)), dma((chunks,)),
            dma((3,)), dma((3,)), dma((4 * steps,)), dma((4 * steps,)),
            dma((steps + 1,)), dma((steps + 1,)), dma((3,)), dma((2,)),
            pltpu.SemaphoreType.REGULAR,
        ]
        + bufs
        + ([pltpu.VMEM((width, tokens), BF16)] if turn else []),
        compiler_params=pltpu.CompilerParams(
            collective_id=ident, has_side_effects=True, vmem_limit_bytes=63 << 20
        ),
        cost_estimate=pl.CostEstimate(
            flops=12 * tokens * width * flat, transcendentals=0, bytes_accessed=96 << 20
        ),
    )(
        h1 if turn else h1_t, *grads, *weights, o_pre, gain[None, :], vec, d3, u3, *streams
    )


def core_gather_kernel(norm, tiles, v_ref, gain_ref, out_ref, send_ref, recv_ref, send_sem, recv_sem):
    peer = tensor_peer(1)
    greet(peer)
    half = v_ref.shape[0]
    size = half // tiles
    copies = []
    for c in range(tiles):
        rows = slice(c * size, (c + 1) * size)
        v = v_ref[rows, :]
        if norm:
            inv = lax.rsqrt(jnp.mean(v * v, axis=-1, keepdims=True) + EPS)
            v = v * inv * gain_ref[...]
            send_ref[rows, :] = v
        out_ref[rows, :] = v.astype(BF16)
        src = send_ref if norm else v_ref
        copies.append(
            remote(
                src.at[rows, :], recv_ref.at[rows, :], send_sem.at[c], recv_sem.at[c], peer
            )
        )
        copies[-1].start()
    for c in range(tiles):
        rows = slice(c * size, (c + 1) * size)
        copies[c].wait_recv()
        out_ref[half + c * size : half + (c + 1) * size, :] = recv_ref[rows, :].astype(BF16)
    for c in copies:
        c.wait_send()


def core_gather(ident, v, gain=None):
    half, n = v.shape
    tiles = 4
    out = jax.ShapeDtypeStruct((2 * half, n), BF16)
    full = pl.BlockSpec(memory_space=pltpu.VMEM)
    norm = gain is not None
    return pl.pallas_call(
        functools.partial(core_gather_kernel, norm, tiles),
        out_shape=out,
        in_specs=[full, full],
        out_specs=full,
        scratch_shapes=[
            pltpu.VMEM((half, n) if norm else (8, DH), F32),
            pltpu.VMEM((half, n), F32),
            pltpu.SemaphoreType.DMA((tiles,)),
            pltpu.SemaphoreType.DMA((tiles,)),
        ],
        compiler_params=pltpu.CompilerParams(
            collective_id=ident, has_side_effects=True, vmem_limit_bytes=48 << 20
        ),
        cost_estimate=pl.CostEstimate(
            flops=0, transcendentals=0, bytes_accessed=nbytes(v, v, v, out)
        ),
    )(v, gain[None, :] if norm else jnp.zeros((8, DH), F32))


TILE = 256
SLOTS = 4


def feed_kernel(
    dp, turn, h_ref, ogt_ref, ht_ref, wup_hbm, wdn_hbm, ug_hbm,
    act_ref, dpre_ref, part_ref, part2_ref, far_ref, d_ref, u_ref, d_pre_ref, u_pre_ref,
    w_ref, ug_ref, ds_ref, us_ref, cs_ref, cr_ref,
    w_sem, ug_sem, d_send, d_recv, u_send, u_recv, c_send, c_recv, y_send, y_recv, free_sem,
):
    tokens, units = act_ref.shape
    half = tokens // 2
    width = h_ref.shape[1]
    cut = width // 2
    rows = width // dp
    me = lax.axis_index("dp")
    core, far = tensor_peer(1), tensor_peer(2)
    x_peer, z_peer = {"dp": me ^ 1}, {"dp": me ^ 2}
    greet(core, far, x_peer, z_peer)
    count = units // TILE

    load_w = pltpu.make_async_copy(wup_hbm, w_ref, w_sem)
    load_w.start()

    def tile_cols(t):
        return pl.ds(pl.multiple_of(t * TILE, TILE), TILE)

    def load_ug(t, k):
        return pltpu.make_async_copy(ug_hbm.at[:, tile_cols(t)], ug_ref.at[k], ug_sem.at[k])

    load_ug(0, 0).start()
    load_ug(1, 1).start()
    for j in range(dp // 2 if turn else 0):
        ht_ref[j * rows : (j + 1) * rows, :] = block_of(h_ref, dp, X_FIRST, j).T
    load_w.wait()

    def wire(t, k):
        cols = tile_cols(t)
        d = remote(ds_ref.at[k], d_ref.at[:, cols], d_send.at[t], d_recv.at[t], z_peer)
        u = remote(us_ref.at[k], u_ref.at[:, cols], u_send.at[t], u_recv.at[t], x_peer)
        return d, u

    def terms(t, k):
        cols = tile_cols(t)
        d, u = wire(t, k)
        ds_ref[k] = dot(ogt_ref[:cut, :], act_ref[:, cols])
        d.start()
        us_ref[k] = dot(ht_ref[:cut, :], dpre_ref[:, cols])
        u.start()

    @pl.loop(0, count)
    def _(t):
        k = t % 2
        cols = tile_cols(t)
        load_ug(t, k).wait()
        pre = dot(h_ref[...], w_ref[:, cols])
        c = 0.7978845608028654
        sq = pre * pre
        th = jnp.tanh(c * pre * (1.0 + 0.044715 * sq))
        mid = 0.5 * (1.0 + th)
        act_ref[:, cols] = (pre * mid).astype(BF16)
        slope = mid + 0.5 * pre * (1.0 - th * th) * (c * (1.0 + 0.134145 * sq))
        dpre_ref[:, cols] = (ug_ref[k] * slope).astype(BF16)

        @pl.when(t + 2 < count)
        def _():
            load_ug(t + 2, k).start()

        @pl.when(t < SLOTS)
        def _():
            terms(t, t)

    part_cols = width // 4

    def core_wire(c):
        return remote(cs_ref.at[c], cr_ref.at[c], c_send.at[c], c_recv.at[c], core)

    def far_wire(c):
        cols = pl.ds(c * part_cols, part_cols)
        return remote(part_ref.at[:, cols], far_ref.at[:, cols], y_send.at[c], y_recv.at[c], far)

    def summed(lhs_ref, transposed, out_ref, travels):
        def term(row, c):
            cols = slice(c * part_cols, (c + 1) * part_cols)
            lhs = lhs_ref[row * half : (row + 1) * half, :]
            if transposed:
                return dot_nt(lhs, w_ref[cols, :])
            return dot(lhs, w_ref[:, cols])

        for c in range(4):
            cs_ref[c] = term(1, c)
            core_wire(c).start()
        for c in range(4):
            part = term(0, c)
            core_wire(c).wait()
            out_ref[:, c * part_cols : (c + 1) * part_cols] = part + cr_ref[c]
            if travels:
                far_wire(c).start()

    summed(dpre_ref, True, part_ref, True)
    load_down = pltpu.make_async_copy(wdn_hbm, w_ref, w_sem)
    load_down.start()
    pl.semaphore_signal(free_sem, inc=1, device_id=core, device_id_type=pl.DeviceIdType.MESH)
    for j in range(dp // 2, dp if turn else 0):
        ht_ref[j * rows : (j + 1) * rows, :] = block_of(h_ref, dp, X_FIRST, j).T

    @pl.loop(SLOTS, count)
    def _(t):
        d, u = wire(t - SLOTS, t - SLOTS)
        d.wait_send()
        u.wait_send()
        terms(t, t - SLOTS)

    load_down.wait()
    pl.semaphore_wait(free_sem, 1)
    summed(act_ref, False, part2_ref, False)

    def load_got(src_ref, t, k):
        return pltpu.make_async_copy(src_ref.at[:, tile_cols(t)], ug_ref.at[k], ug_sem.at[k])

    def store_pre(dst_ref, t, k):
        return pltpu.make_async_copy(ug_ref.at[k], dst_ref.at[:, tile_cols(t)], ug_sem.at[k])

    @pl.loop(0, count)
    def _(t):
        d, u = wire(t, 0)

        @pl.when(t > 0)
        def _():
            store_pre(d_pre_ref, t - 1, 0).wait()
            store_pre(u_pre_ref, t - 1, 1).wait()

        d.wait_recv()
        load_got(d_ref, t, 0).start()
        u.wait_recv()
        load_got(u_ref, t, 1).start()
        load_got(d_ref, t, 0).wait()
        ug_ref[0] += dot(ogt_ref[cut:, :], act_ref[:, tile_cols(t)])
        store_pre(d_pre_ref, t, 0).start()
        load_got(u_ref, t, 1).wait()
        ug_ref[1] += dot(ht_ref[cut:, :], dpre_ref[:, tile_cols(t)])
        store_pre(u_pre_ref, t, 1).start()

    store_pre(d_pre_ref, count - 1, 0).wait()
    store_pre(u_pre_ref, count - 1, 1).wait()

    @pl.loop(count - SLOTS, count)
    def _(t):
        d, u = wire(t, t - (count - SLOTS))
        d.wait_send()
        u.wait_send()

    for c in range(4):
        far_wire(c).wait()


def feed(ident, dp, h2, og_t, h_t, w_up, w_down, up_grad):
    tokens, width = h2.shape
    units = w_up.shape[1]
    half = tokens // 2
    cut = width // 2
    count = units // TILE
    full = pl.BlockSpec(memory_space=pltpu.VMEM)
    anywhere = pl.BlockSpec(memory_space=pl.ANY)
    f32 = lambda *shape: jax.ShapeDtypeStruct(shape, F32)
    b16 = jax.ShapeDtypeStruct((tokens, units), BF16)
    dma = pltpu.SemaphoreType.DMA
    turn = h_t is None
    kernel = functools.partial(feed_kernel, dp, turn)
    if turn:

        def kernel(h_ref, ogt_ref, *refs):
            feed_kernel(dp, turn, h_ref, ogt_ref, refs[-1], *refs[:-1])

    return pl.pallas_call(
        kernel,
        out_shape=[b16, b16, f32(half, width), f32(half, width), f32(half, width)]
        + [f32(cut, units)] * 4,
        in_specs=[full] * (2 if turn else 3) + [anywhere] * 3,
        out_specs=[full] * 4 + [anywhere] * 5,
        scratch_shapes=[
            pltpu.VMEM((width, units), BF16),
            pltpu.VMEM((2, tokens, TILE), F32),
            pltpu.VMEM((SLOTS, cut, TILE), F32),
            pltpu.VMEM((SLOTS, cut, TILE), F32),
            pltpu.VMEM((4, half, width // 4), F32),
            pltpu.VMEM((4, half, width // 4), F32),
            dma, dma((2,)), dma((count,)), dma((count,)), dma((count,)), dma((count,)),
            dma((4,)), dma((4,)), dma((4,)), dma((4,)), pltpu.SemaphoreType.REGULAR,
        ]
        + ([pltpu.VMEM((width, tokens), BF16)] if turn else []),
        compiler_params=pltpu.CompilerParams(
            collective_id=ident, has_side_effects=True, vmem_limit_bytes=62 << 20
        ),
        cost_estimate=pl.CostEstimate(
            flops=10 * tokens * width * units, transcendentals=tokens * units,
            bytes_accessed=64 << 20,
        ),
    )(h2, og_t, *([] if turn else [h_t]), w_up, w_down, up_grad)


def body(
    inputs,
    gain_attn,
    w_query,
    w_key,
    w_value,
    gate_logit,
    w_out,
    gain_mlp,
    w_up,
    w_down,
    seg_parent,
    out_grad,
):
    tokens, width = inputs.shape
    half = tokens // 2
    segs = tokens // SEG
    heads = w_query.shape[1] // DH
    pairs = segs * heads
    units = w_up.shape[1]
    flat = heads * DH
    scale = DH ** (-0.5)
    dp = lax.axis_size("dp")
    tn = lax.axis_size("tensor")
    rows = width // dp
    di = lax.axis_index("dp")
    core = lax.axis_index("tensor") % 2

    one = jnp.where(seg_parent[0] < tokens * dp, 1.0, 2.0)

    def low_after_wire(v):
        return (v * one).astype(BF16)

    def swap_core(v):
        return lax.ppermute(v, "tensor", [(i, i ^ 1) for i in range(tn)])

    def swap_y(v):
        return lax.ppermute(v, "tensor", [(i, i ^ 2) for i in range(tn)])

    def swap_dp(v, mask):
        return lax.ppermute(v, "dp", [(i, i ^ mask) for i in range(dp)])

    def columns(v, order):
        _, seq = halving(dp, order)
        return block_columns(v, [di ^ k for k in seq], rows)

    def blocks_for(v, order):
        return columns(v, order) if rows % DH else v

    cut = width // 2
    quarter = cut // 2

    def pick(v, index, axis):
        size = v.shape[axis] // 2
        return lax.dynamic_slice_in_dim(v, index * size, size, axis)

    def place(own, other, index, axis):
        return jnp.where(
            index == 0,
            jnp.concatenate([own, other], axis),
            jnp.concatenate([other, own], axis),
        )

    def inv_rms(v):
        return lax.rsqrt(jnp.mean(v * v, axis=-1, keepdims=True) + EPS)

    x_own = pick(inputs, core, 0).astype(F32)
    x_oth = pick(inputs, 1 - core, 0).astype(F32)
    inv_own = inv_rms(x_own)
    inv_oth = inv_rms(x_oth)
    h1 = jnp.concatenate(
        [
            (x_own * inv_own * gain_attn).astype(BF16),
            (x_oth * inv_oth * gain_attn).astype(BF16),
        ],
        0,
    )

    sub = segs // 2
    every = jnp.arange(seg_parent.shape[0], dtype=jnp.int32)
    sub_ids = jnp.arange(sub, dtype=jnp.int32)
    seg_local = jnp.concatenate([core * sub + sub_ids, (1 - core) * sub + sub_ids])
    order = spread_order(dp)
    ids = jnp.concatenate([(di ^ j) * segs + seg_local for j in order])
    mine_hot = (ids[:segs, None] == every[None, :]).astype(F32)
    ids_hot = (ids[:, None] == every[None, :]).astype(F32)
    lineage = ancestor_table(seg_parent)

    def weights_of(table):
        mine_rows = jnp.sum(mine_hot[:, :, None] * table[None], axis=1)
        return jnp.sum(mine_rows[:, None, :] * ids_hot[None], axis=-1)

    up_weight = weights_of(lineage)
    down_weight = weights_of(lineage.T)

    gate = jax.nn.sigmoid(gate_logit)
    gate_row = gate[None, :]

    og_own = pick(out_grad, core, 0)
    og = jnp.concatenate([og_own, pick(out_grad, 1 - core, 0)], 0)
    block_rows = pairs * DH + pairs
    act_f32 = jax.ShapeDtypeStruct((tokens, flat), F32)
    act_b16 = jax.ShapeDtypeStruct((tokens, flat), BF16)
    mem_shape = jax.ShapeDtypeStruct((pairs * DH, DH), F32)
    zin_shape = jax.ShapeDtypeStruct((pairs, DH), F32)
    full = pl.BlockSpec(memory_space=pltpu.VMEM)

    def attention_call(kernel, ident, outs, out_specs, scratch, args, in_specs, flops):
        return pl.pallas_call(
            functools.partial(kernel, dp, heads, segs, scale),
            out_shape=outs,
            in_specs=in_specs,
            out_specs=out_specs,
            scratch_shapes=scratch
            + [
                pltpu.VMEM((dp, block_rows, DH), F32),
                pltpu.SemaphoreType.DMA((dp,)),
                pltpu.SemaphoreType.DMA((dp,)),
            ],
            compiler_params=pltpu.CompilerParams(
                collective_id=ident, has_side_effects=True, vmem_limit_bytes=63 << 20
            ),
            cost_estimate=pl.CostEstimate(
                flops=flops, transcendentals=0, bytes_accessed=64 << 20
            ),
        )(*args)

    head_flops = 2 * segs * heads * SEG * SEG * DH
    dma = pltpu.SemaphoreType.DMA
    qh, kh, vh, a16, a_pair, local, memory, zin, w_out_all = attention_call(
        attention_kernel,
        0,
        [
            act_b16, act_b16, act_b16, act_b16,
            jax.ShapeDtypeStruct((half, 2 * flat), F32),
            act_f32, mem_shape, zin_shape,
            jax.ShapeDtypeStruct((4 * flat, width), BF16),
        ],
        [full] * 9,
        [
            pltpu.VMEM((4, flat, width), F32),
            pltpu.VMEM((half, flat), F32),
            dma((3 * W_CHUNKS,)), dma((3 * W_CHUNKS,)), dma, dma,
        ],
        (up_weight, gate_row, h1, w_query, w_key, w_value, w_out),
        [SMEM, SMEM] + [full] * 5,
        3 * head_flops + 6 * tokens * width * flat,
    )
    up_grad = dot_nt(og, after(w_down, a_pair))

    step = half // AG_CHUNKS
    a_near = [a_pair[c * step : (c + 1) * step] for c in range(AG_CHUNKS)]
    a_far = [swap_y(v) for v in a_near]
    near = [
        x_own[c * step : (c + 1) * step] + dot(v.astype(BF16), w_out_all[: 2 * flat])
        for c, v in enumerate(a_near)
    ]
    og_t = columns(after(og, up_grad), Z_FIRST).T
    resids = [
        n + dot(low_after_wire(after(f, og_t, *near)), w_out_all[2 * flat :])
        for n, f in zip(near, a_far)
    ]
    resid = jnp.concatenate(resids, 0)
    inv_mlp = inv_rms(resid)
    h2 = core_gather(1, resid, gain_mlp)

    h_t = columns(h2, X_FIRST).T if rows % DH else None
    act, dpre, dh2_part, out_part, dh2_far, _, _, d_pre, u_pre = feed(
        2, dp, h2, og_t, h_t, w_up, w_down, up_grad
    )

    dh2 = dh2_part + dh2_far
    gs = dh2 * gain_mlp
    dresid = (
        og_own.astype(F32)
        + inv_mlp * gs
        - resid * inv_mlp * inv_mlp * inv_mlp * jnp.mean(gs * resid, axis=-1, keepdims=True)
    )
    gain_mlp_part = jnp.sum(dh2 * resid * inv_mlp, axis=0)
    dr = core_gather(4, dresid)

    da = dot_nt(dr, w_out).astype(BF16)
    anywhere = pl.BlockSpec(memory_space=pl.ANY)
    ride = jax.ShapeDtypeStruct((quarter, units), F32)
    o_shape = jax.ShapeDtypeStruct((cut, flat), F32)
    dq16, dk16, dv16, gate_rows, o_pre, d_rode, u_rode, out_far = attention_call(
        attention_back_kernel,
        5,
        [
            act_b16, act_b16, act_b16, zin_shape, o_shape, ride, ride,
            jax.ShapeDtypeStruct((half, width), F32),
        ],
        [full] * 5 + [anywhere] * 3,
        [pltpu.VMEM((tokens, flat), F32)] * 3
        + [pltpu.VMEM((cut, flat), F32)]
        + [dma((6,)), dma((6,))],
        (
            down_weight, gate_row, qh, kh, vh, da, local, memory, zin,
            blocks_for(dr, Z_FIRST), a16, d_pre, u_pre, out_part,
        ),
        [SMEM, SMEM] + [full] * 9 + [anywhere] * 3,
        9 * head_flops,
    )
    gate_part = jnp.sum(gate_rows.reshape(segs, heads, DH), axis=(0, 2)) * gate * (1.0 - gate)

    eighth = quarter // 2
    d3 = d_pre[quarter : quarter + eighth] + d_rode[:eighth]
    close = near_units(dp, units)
    u3 = u_rode[:eighth] + jnp.where(
        jnp.arange(units)[None, :] < close, u_pre[quarter : quarter + eighth], u_pre[eighth:quarter]
    )
    h1_t = columns(h1, X_FIRST).T if rows % DH else None
    lane = jnp.pad(gate_part, (0, width - heads))
    vec = jnp.zeros((8, width), F32).at[1].set(gain_mlp_part).at[2].set(lane)
    (
        w_query_grad, w_key_grad, w_value_grad, w_out_rows, vec, _, d3, u3, outputs, input_grad
    ) = tail(
        7, dp, h1, h1_t, (dq16, dk16, dv16), (w_query, w_key, w_value), o_pre, gain_attn, vec,
        d3, u3, (resid, out_part, out_far, dresid, x_own),
    )
    w_out_grad = w_out_rows.T

    def finish(pre, rode, got, order):
        masks, _ = halving(dp, order)
        value = pre[quarter + eighth :] + rode[eighth:] + got
        for m in masks[3:]:
            n = value.shape[0] // 2
            value = value[n:] + swap_dp(value[:n], m)
        return value

    w_down_grad = finish(d_pre, d_rode, d3, Z_FIRST).T
    w_up_grad = finish(u_pre, u_rode, u3, X_FIRST)

    gain_attn_grad = lax.dynamic_slice_in_dim(vec[0], di * rows, rows, 0)
    gain_mlp_grad = lax.dynamic_slice_in_dim(vec[1], di * rows, rows, 0)
    gate_grad = vec[2, :heads]

    return (
        outputs,
        input_grad,
        gain_attn_grad,
        w_query_grad,
        w_key_grad,
        w_value_grad,
        gate_grad,
        w_out_grad,
        gain_mlp_grad,
        w_up_grad,
        w_down_grad,
    )


def solution(mesh):
    placed = (
        P("dp", None),
        P(),
        P(None, "tensor"),
        P(None, "tensor"),
        P(None, "tensor"),
        P("tensor"),
        P("tensor", None),
        P(),
        P(None, "tensor"),
        P("tensor", None),
        P(),
        P("dp", None),
    )
    return jax.shard_map(
        body,
        mesh=mesh,
        in_specs=placed,
        out_specs=(
            P("dp", None),
            P("dp", None),
            P("dp"),
            P("dp", "tensor"),
            P("dp", "tensor"),
            P("dp", "tensor"),
            P("tensor"),
            P("tensor", "dp"),
            P("dp"),
            P("dp", "tensor"),
            P("tensor", "dp"),
        ),
        check_vma=False,
    )
```

```python
import functools

import jax
import jax.numpy as jnp
from jax import lax
from jax.experimental import pallas as pl
from jax.experimental.pallas import tpu as pltpu
from jax.sharding import PartitionSpec as P

DH = 128
SEG = 512
DEPTH = 5
EPS = 1e-06

F32 = jnp.float32
BF16 = jnp.bfloat16

AG_CHUNKS = 2
Z_FIRST = (1, 0)
X_FIRST = (0, 1)


def feature_map(values):
    return jnp.where(values > 0, values + 1.0, jnp.exp(jnp.minimum(values, 0.0)))


def feature_slope(values):
    return jnp.where(values > 0, 1.0, jnp.exp(jnp.minimum(values, 0.0)))


def ancestor_table(seg_parent):
    seg_total = seg_parent.shape[0]
    columns = jnp.arange(seg_total, dtype=jnp.int32)
    current = seg_parent
    lineage_table = jnp.zeros((seg_total, seg_total), F32)
    for _ in range(DEPTH):
        onehot = current[:, None] == columns[None, :]
        lineage_table = lineage_table + onehot.astype(F32)
        lifted = jnp.sum(jnp.where(onehot, seg_parent[None, :], 0), axis=1)
        current = jnp.where(current >= 0, lifted, -1)
    return lineage_table


def dot(a, b):
    return jnp.dot(a, b, preferred_element_type=F32)


def dot_t(a, b):
    return lax.dot_general(a, b, (((0,), (0,)), ((), ())), preferred_element_type=F32)


def dot_nt(a, b):
    return lax.dot_general(a, b, (((1,), (1,)), ((), ())), preferred_element_type=F32)


def after(value, *earlier):
    return lax.optimization_barrier((value, earlier))[0]


def nbytes(*arrays):
    return sum(a.size * a.dtype.itemsize for a in arrays)


def copy_kernel(ids_ref, in_ref, out_ref):
    out_ref[...] = in_ref[...]


def block_columns(v, ids, size):
    if size % 128:
        return jnp.concatenate([lax.dynamic_slice_in_dim(v, i * size, size, 1) for i in ids], 1)
    height, width = v.shape
    return pl.pallas_call(
        copy_kernel,
        out_shape=jax.ShapeDtypeStruct(v.shape, v.dtype),
        grid_spec=pltpu.PrefetchScalarGridSpec(
            num_scalar_prefetch=1,
            grid=(width // size,),
            in_specs=[pl.BlockSpec((height, size), lambda k, ids: (0, ids[k]))],
            out_specs=pl.BlockSpec((height, size), lambda k, ids: (0, k)),
        ),
        cost_estimate=pl.CostEstimate(flops=0, transcendentals=0, bytes_accessed=2 * nbytes(v)),
    )(jnp.stack(ids), v)


SMEM = pl.BlockSpec(memory_space=pltpu.SMEM)


def causal_mask():
    row = lax.broadcasted_iota(jnp.int32, (SEG, SEG), 0)
    col = lax.broadcasted_iota(jnp.int32, (SEG, SEG), 1)
    return row >= col


def softmax_rows(q, k, scale):
    scores = dot_nt(q, k) * scale
    scores = jnp.where(causal_mask(), scores, -1e30)
    top = jnp.max(scores, axis=-1, keepdims=True)
    e = jnp.exp(scores - top)
    return e * (1.0 / jnp.sum(e, axis=-1, keepdims=True))


def head_part(heads, p):
    s, h = p // heads, p % heads
    return pl.ds(pl.multiple_of(s * SEG, SEG), SEG), pl.ds(pl.multiple_of(h * DH, DH), DH)


def matrix_part(p):
    return pl.ds(pl.multiple_of(p * DH, DH), DH)


def weighted(w_ref, p, heads, segs, blocks_ref):
    s, h = p // heads, p % heads
    pairs = segs * heads
    big = jnp.zeros((DH, DH), F32)
    small = jnp.zeros((1, DH), F32)
    for d in range(blocks_ref.shape[0]):
        for n in range(segs):
            w = w_ref[s, d * segs + n]
            o = n * heads + h
            big = big + w * blocks_ref[d, matrix_part(o), :]
            small = small + w * blocks_ref[d, pl.ds(pairs * DH + o, 1), :]
    return big, small


def spread_order(dp):
    low = [0]
    for b in reversed(range(1, dp.bit_length() - 1)):
        low = low + [v ^ (1 << b) for v in low]
    return low + [v ^ 1 for v in low]


def greet(*peers):
    barrier = pltpu.get_barrier_semaphore()
    for peer in peers:
        pl.semaphore_signal(barrier, inc=1, device_id=peer, device_id_type=pl.DeviceIdType.MESH)
    pl.semaphore_wait(barrier, len(peers))


def dp_peers(dp):
    me = lax.axis_index("dp")
    return [{"dp": me ^ (1 << b)} for b in range(dp.bit_length() - 1)]


def tensor_peer(mask):
    return {"tensor": lax.axis_index("tensor") ^ mask}


def halving(dp, order):
    masks = [1 << b for b in order]
    masks += [1 << b for b in range(len(order), dp.bit_length() - 1)]
    seq = [0]
    for m in reversed(masks):
        seq = [m ^ v for v in seq] + seq
    return masks, seq


def near_units(dp, units):
    return units // 4 if dp == 8 else units


def block_of(ref, dp, order, k):
    rows = ref.shape[1] // dp
    if rows % DH:
        return ref[:, k * rows : (k + 1) * rows]
    at = (lax.axis_index("dp") ^ halving(dp, order)[1][k]) * rows
    return ref[:, pl.ds(pl.multiple_of(at, rows), rows)]


def remote(src, dst, send_sem, recv_sem, peer):
    return pltpu.make_async_remote_copy(
        src_ref=src,
        dst_ref=dst,
        send_sem=send_sem,
        recv_sem=recv_sem,
        device_id=peer,
        device_id_type=pl.DeviceIdType.MESH,
    )


def spread(dp, blocks_ref, send_sem, recv_sem, compute, then=None):
    me = lax.axis_index("dp")
    slot = {j: k for k, j in enumerate(spread_order(dp))}
    copies = {}

    def send(j, mask):
        to = j ^ mask
        k = slot[to]
        copies[to] = pltpu.make_async_remote_copy(
            src_ref=blocks_ref.at[slot[j]],
            dst_ref=blocks_ref.at[k],
            send_sem=send_sem.at[k],
            recv_sem=recv_sem.at[k],
            device_id={"dp": me ^ mask},
            device_id_type=pl.DeviceIdType.MESH,
        )
        copies[to].start()

    bits = [1 << b for b in range(1, dp.bit_length() - 1)]
    for m in bits:
        send(0, m)
    send(0, 1)
    compute()
    for m in bits:
        copies[m].wait_recv()
        if m == bits[-1]:
            near = [0, m]
            for n in reversed(bits[:-1]):
                for j in near[1:]:
                    send(j, n)
                near = near + [n] + [j ^ n for j in near[1:]]
                if n != bits[0]:
                    for j in near:
                        if j & n and j != n:
                            copies[j].wait_recv()
        send(m, 1)
    if then is not None:
        then()
    last = [j for j in near if j and j not in bits]
    for j in last:
        if j & bits[0] or len(bits) == 1:
            copies[j].wait_recv()
        send(j, 1)
    for j in near:
        copies[j ^ 1].wait_recv()
    for c in copies.values():
        c.wait_send()


W_CHUNKS = 4


def attention_kernel(
    dp, heads, segs, scale, w_ref, g_ref, h_ref, wq_ref, wk_ref, wv_ref, wo_ref,
    q_ref, k_ref, v_ref, a16_ref, pair_ref, local_ref, mem_ref, zin_ref, all_ref,
    wf_ref, asend_ref, w_send, w_recv, a_send, a_recv, blocks_ref, send_sem, recv_sem,
):
    pairs = segs * heads
    flat = heads * DH
    half = segs * SEG // 2
    core, far = tensor_peer(1), tensor_peer(2)
    greet(*dp_peers(dp), core, far)

    size = flat // W_CHUNKS
    w_copies = {}

    def w_send_chunk(j, c, to, peer):
        rows = pl.ds(c * size, size)
        k = (to - 1) * W_CHUNKS + c
        w_copies[to, c] = remote(
            wf_ref.at[j, rows, :], wf_ref.at[to, rows, :], w_send.at[k], w_recv.at[k], peer
        )
        w_copies[to, c].start()

    def w_done(to, c):
        rows = slice(c * size, (c + 1) * size)
        w_copies[to, c].wait_recv()
        all_ref[to * flat + c * size : to * flat + (c + 1) * size, :] = wf_ref[to, rows, :].astype(
            BF16
        )

    for c in range(W_CHUNKS):
        rows = slice(c * size, (c + 1) * size)
        wf_ref[0, rows, :] = wo_ref[rows, :].astype(F32)
        w_send_chunk(0, c, 2, far)
        w_send_chunk(0, c, 1, core)
    all_ref[:flat, :] = wo_ref[...]

    def project(matrix_ref, out_ref):
        @pl.loop(0, segs * SEG // 256)
        def _(i):
            rows = pl.ds(pl.multiple_of(i * 256, 256), 256)
            out_ref[rows, :] = dot(h_ref[rows, :], matrix_ref[...]).astype(BF16)

    project(wk_ref, k_ref)
    project(wv_ref, v_ref)

    @pl.loop(0, pairs)
    def _(p):
        at = head_part(heads, p)
        sk = feature_map(k_ref[at].astype(F32))
        blocks_ref[0, matrix_part(p), :] = dot_t(sk.astype(BF16), v_ref[at])
        blocks_ref[0, pl.ds(pairs * DH + p, 1), :] = jnp.sum(sk, axis=0, keepdims=True)

    def compute():
        project(wq_ref, q_ref)

        @pl.loop(0, pairs)
        def _(p):
            at = head_part(heads, p)
            probs = softmax_rows(q_ref[at], k_ref[at], scale)
            local_ref[at] = dot(probs.astype(BF16), v_ref[at])

    spread(dp, blocks_ref, send_sem, recv_sem, compute)

    @pl.loop(0, pairs)
    def _(p):
        at = head_part(heads, p)
        mem, zin = weighted(w_ref, p, heads, segs, blocks_ref)
        mem_ref[matrix_part(p), :] = mem
        zin_ref[pl.ds(p, 1), :] = zin
        g = g_ref[0, p % heads]
        sq = feature_map(q_ref[at].astype(F32))
        den = jnp.sum(sq * zin, axis=-1, keepdims=True) + 1.0
        retrieved = dot(sq.astype(BF16), mem.astype(BF16)) / den
        a16_ref[at] = (g * retrieved + (1.0 - g) * local_ref[at]).astype(BF16)

    asend_ref[...] = a16_ref[half:, :].astype(F32)
    a_copy = remote(asend_ref, pair_ref.at[:, pl.ds(flat, flat)], a_send, a_recv, core)
    a_copy.start()
    pair_ref[:, :flat] = a16_ref[:half, :].astype(F32)
    for c in range(W_CHUNKS):
        w_done(1, c)
    a_copy.wait_recv()
    for c in range(W_CHUNKS):
        w_copies[2, c].wait_recv()
        w_send_chunk(2, c, 3, core)
        rows = slice(c * size, (c + 1) * size)
        all_ref[2 * flat + c * size : 2 * flat + (c + 1) * size, :] = wf_ref[2, rows, :].astype(BF16)
    for c in range(W_CHUNKS):
        w_done(3, c)
    for copy in w_copies.values():
        copy.wait_send()
    a_copy.wait_send()


def attention_back_kernel(
    dp, heads, segs, scale, w_ref, g_ref, q_ref, k_ref, v_ref, da_ref, local_ref, mem_ref, zin_ref,
    dr_ref, a16_ref, d_pre_ref, u_pre_ref, out_part_ref,
    dq_ref, dk_ref, dv_ref, gate_ref, o_pre_ref, d_rode_ref, u_rode_ref, out_far_ref,
    dqm_ref, dkl_ref, dvl_ref, os_ref, ride_send, ride_recv, blocks_ref, send_sem, recv_sem,
):
    pairs = segs * heads
    me = lax.axis_index("dp")
    far = tensor_peer(2)
    greet(*dp_peers(dp), far)
    legs = [
        (d_pre_ref, d_rode_ref, {"dp": me ^ 1}),
        (out_part_ref, out_far_ref, far),
        (os_ref, o_pre_ref, {"dp": me ^ 2}),
    ]
    quarter, units = d_rode_ref.shape
    eighth = quarter // 2
    legs[0] = (d_pre_ref.at[pl.ds(0, quarter), :], d_rode_ref, {"dp": me ^ 1})
    near = near_units(dp, units)
    cols = pl.ds(0, near)
    legs.append((u_pre_ref.at[pl.ds(0, quarter), cols], u_rode_ref.at[:, cols], {"dp": me ^ 2}))
    if near < units:
        cols = pl.ds(near, units - near)
        for k in range(2):
            legs.append(
                (
                    u_pre_ref.at[pl.ds(2 * k * eighth, eighth), cols],
                    u_rode_ref.at[pl.ds(k * eighth, eighth), cols],
                    {"dp": me ^ 4},
                )
            )
    riders = [
        remote(src, dst, ride_send.at[i], ride_recv.at[i], peer)
        for i, (src, dst, peer) in enumerate(legs)
    ]
    o_rider = riders[2]
    plain = riders[:2] + riders[3:]
    for r in riders[:2] + riders[3:4]:
        r.start()

    @pl.loop(0, pairs)
    def _(p):
        at = head_part(heads, p)
        g = g_ref[0, p % heads]
        qf = q_ref[at].astype(F32)
        sq = feature_map(qf)
        sq16 = sq.astype(BF16)
        mem16 = mem_ref[matrix_part(p), :].astype(BF16)
        zin = zin_ref[pl.ds(p, 1), :]
        inv_den = 1.0 / (jnp.sum(sq * zin, axis=-1, keepdims=True) + 1.0)
        retrieved = dot(sq16, mem16) * inv_den
        da = da_ref[at].astype(F32)
        gate_ref[pl.ds(p, 1), :] = jnp.sum(da * (retrieved - local_ref[at]), axis=0, keepdims=True)
        dnum = g * da * inv_den
        dden = -jnp.sum(dnum * retrieved, axis=-1, keepdims=True)
        dnum16 = dnum.astype(BF16)
        blocks_ref[0, matrix_part(p), :] = dot_t(sq16, dnum16)
        blocks_ref[0, pl.ds(pairs * DH + p, 1), :] = jnp.sum(sq * dden, axis=0, keepdims=True)
        dsq = dot_nt(dnum16, mem16) + dden * zin
        dqm_ref[at] = dsq * feature_slope(qf)

    rows = dr_ref.shape[1] // dp
    half_blocks = dp // 2

    def compute():
        for j in range(half_blocks):
            os_ref[j * rows : (j + 1) * rows, :] = dot_t(
                block_of(dr_ref, dp, Z_FIRST, j), a16_ref[...]
            )

        @pl.loop(0, pairs)
        def _(p):
            at = head_part(heads, p)
            g = g_ref[0, p % heads]
            q, k, v, da = q_ref[at], k_ref[at], v_ref[at], da_ref[at]
            probs = softmax_rows(q, k, scale)
            dprobs = (1.0 - g) * dot_nt(da, v)
            inner = jnp.sum(dprobs * probs, axis=-1, keepdims=True)
            ds16 = (probs * (dprobs - inner)).astype(BF16)
            dq_ref[at] = (dot(ds16, k) * scale + dqm_ref[at]).astype(BF16)
            dkl_ref[at] = dot_t(ds16, q) * scale
            dvl_ref[at] = (1.0 - g) * dot_t(probs.astype(BF16), da)

    def then():
        o_rider.start()
        for r in riders[4:]:
            r.start()

    spread(dp, blocks_ref, send_sem, recv_sem, compute, then)

    @pl.loop(0, pairs)
    def _(p):
        at = head_part(heads, p)
        dd, dz = weighted(w_ref, p, heads, segs, blocks_ref)
        dd16 = dd.astype(BF16)
        kf = k_ref[at].astype(F32)
        dsk = dot_nt(v_ref[at], dd16) + dz
        dk_ref[at] = (dkl_ref[at] + dsk * feature_slope(kf)).astype(BF16)
        dv_ref[at] = (dvl_ref[at] + dot(feature_map(kf).astype(BF16), dd16)).astype(BF16)

    o_rider.wait()
    for j in range(half_blocks):
        o_pre_ref[j * rows : (j + 1) * rows, :] += dot_t(
            block_of(dr_ref, dp, Z_FIRST, half_blocks + j), a16_ref[...]
        )
    for r in plain:
        r.wait()


ROWS = 128


def tail_items(flat):
    full = slice(0, flat)
    return [
        (0, full), (1, full), (2, slice(0, flat // 2)), (2, slice(flat // 2, flat)), (3, full)
    ]


def tail_kernel(
    dp, turn, order, o_order,
    h_ref, dq_ref, dk_ref, dv_ref, wq_ref, wk_ref, wv_ref, o_pre_ref, gain_ref, vec_ref,
    d3_ref, u3_ref, resid_hbm, out_part_hbm, out_far_hbm, dresid_hbm, x_hbm,
    gq_ref, gk_ref, gv_ref, go_ref, vec_out_ref, far_ref, d3_got_ref, u3_got_ref, out_hbm, dx_hbm,
    part_ref, cs_ref, cr_ref, in_ref, own_ref, other_ref, turn_ref, vec_got_ref,
    c_send, c_recv, y_send, y_recv, ride_send, ride_recv, e_send, e_recv, v_send, v_recv,
    in_sem, st_sem, turn_sem, free_sem, *bufs,
):
    me = lax.axis_index("dp")
    side = lax.axis_index("tensor") % 2
    core, far = tensor_peer(1), tensor_peer(2)
    greet(*dp_peers(dp), core, far)
    masks, _ = halving(dp, order)
    o_masks, _ = halving(dp, o_order)
    steps = len(masks)
    half, width = far_ref.shape
    rows = width // dp
    chunks = half // ROWS
    ht_ref = bufs[-1] if turn else h_ref
    depth = in_ref.shape[0]
    flat = dq_ref.shape[1]
    lhs = (dq_ref, dk_ref, dv_ref)
    outs = (gq_ref, gk_ref, gv_ref, go_ref)
    items = tail_items(flat)
    copies = {}

    def buffers(i, step):
        k = 2 * (i * steps + step)
        return bufs[k], bufs[k + 1]

    def term(i, step):
        lo = rows * sum(dp >> (n + 1) for n in range(step))
        count = rows * (dp >> (step + 1)) if step < steps else rows
        start = 0
        which, cols = items[i]
        if which < 3:
            value = dot(ht_ref[lo : lo + count, :], lhs[which][:, cols])
        else:
            base = rows * (dp // 2)
            value = o_pre_ref[lo - base : lo - base + count, :]
            start = 1
        for n in range(start, step):
            at = lo - rows * sum(dp >> (m + 1) for m in range(n + 1))
            value = value + buffers(i, n)[1][at : at + count, :]
        return value

    def advance(i, step):
        which, cols = items[i]
        if step > (1 if which == 3 else 0):
            copies[i, step - 1].wait_recv()
        if step == steps:
            outs[which][:, cols] = term(i, step)
            return
        send, recv = buffers(i, step)
        send[...] = term(i, step)
        mask = (o_masks if which == 3 else masks)[step]
        k = i * steps + step
        copies[i, step] = remote(send, recv, e_send.at[k], e_recv.at[k], {"dp": me ^ mask})
        copies[i, step].start()

    third = {"dp": me ^ masks[2]}
    units = u3_ref.shape[1]
    near = near_units(dp, units)
    cols = pl.ds(0, near)
    legs = [(d3_ref, d3_got_ref, third), (u3_ref.at[:, cols], u3_got_ref.at[:, cols], third)]
    if near < units:
        cols = pl.ds(near, units - near)
        legs.append((u3_ref.at[:, cols], u3_got_ref.at[:, cols], {"dp": me ^ 2}))
    riders = [
        remote(src, dst, ride_send.at[i], ride_recv.at[i], peer)
        for i, (src, dst, peer) in enumerate(legs)
    ]
    out_item = len(items) - 1
    advance(out_item, 1)
    for r in riders:
        r.start()

    def block_load(j):
        at = (me ^ halving(dp, order)[1][j]) * rows
        return pltpu.make_async_copy(
            h_ref.at[:, pl.ds(pl.multiple_of(at, rows), rows)],
            turn_ref.at[j % 2],
            turn_sem.at[j % 2],
        )

    def turn_blocks(lo, hi):
        for j in range(lo, hi if turn else lo):
            block_load(j).wait()
            ht_ref[j * rows : (j + 1) * rows, :] = turn_ref[j % 2].T
            if j + 2 < dp:
                block_load(j + 2).start()

    for j in range(2 if turn else 0):
        block_load(j).start()
    turn_blocks(0, dp // 2)
    for i in range(out_item):
        advance(i, 0)

    def part_rows(c):
        return pl.ds(c * ROWS, ROWS)

    def core_wire(c):
        return remote(cs_ref.at[c], cr_ref.at[c], c_send.at[c], c_recv.at[c], core)

    def core_free():
        pl.semaphore_signal(free_sem, inc=1, device_id=core, device_id_type=pl.DeviceIdType.MESH)

    def far_wire(c):
        return remote(part_ref.at[c], far_ref.at[part_rows(c), :], y_send.at[c], y_recv.at[c], far)

    def back(lo):
        return sum(
            dot_nt(v[lo : lo + 2 * ROWS, :], w[...])
            for v, w in zip(lhs, (wq_ref, wk_ref, wv_ref))
        )

    for c in range(0, chunks, 2):
        value = back(half + c * ROWS)
        for k in range(2):
            cs_ref[c + k] = value[k * ROWS : (k + 1) * ROWS, :]
            core_wire(c + k).start()
    for c in range(0, chunks, 2):
        value = back(c * ROWS)
        for k in range(2):
            core_wire(c + k).wait()
            part_ref[c + k] = value[k * ROWS : (k + 1) * ROWS, :] + cr_ref[c + k]
            far_wire(c + k).start()
    core_free()

    def both_cores(sources, compute, dst_hbm):
        def loads(c):
            k = c % depth
            return [
                pltpu.make_async_copy(src.at[part_rows(c), :], in_ref.at[k, i], in_sem.at[k, i])
                for i, src in enumerate(sources)
            ]

        def begin(c):
            if c < chunks:
                for load in loads(c):
                    load.start()

        def store(src_ref, which, c, k):
            at = pl.ds(pl.multiple_of(which * half + c * ROWS, ROWS), ROWS)
            return pltpu.make_async_copy(src_ref, dst_hbm.at[at, :], st_sem.at[k])

        pl.semaphore_wait(free_sem, 1)
        for c in range(depth):
            begin(c)
        for c in range(chunks):
            for load in loads(c):
                load.wait()
            value = compute(c, *(in_ref[c % depth, i] for i in range(3))).astype(BF16)
            if c:
                store(own_ref, side, c - 1, 0).wait()
            own_ref[...] = value
            store(own_ref, side, c, 0).start()
            cs_ref[c] = value.astype(F32)
            core_wire(c).start()
            begin(c + depth)
        for c in range(chunks):
            core_wire(c).wait()
            if c:
                store(other_ref, 1 - side, c - 1, 1).wait()
            other_ref[...] = cr_ref[c].astype(BF16)
            store(other_ref, 1 - side, c, 1).start()
        store(own_ref, side, chunks - 1, 0).wait()
        store(other_ref, 1 - side, chunks - 1, 1).wait()

    def output_rows(c, a, b, d):
        return a + b + d

    def input_rows(c, there, dresid, x):
        grad = part_ref[c] + there
        inv = lax.rsqrt(jnp.mean(x * x, axis=-1, keepdims=True) + EPS)
        gs = grad * gain_ref[...]
        inner = jnp.mean(gs * x, axis=-1, keepdims=True)
        vec_out_ref[0:1, :] += jnp.sum(grad * x * inv, axis=0, keepdims=True)
        return dresid + inv * gs - x * inv * inv * inv * inner

    turn_blocks(dp // 2, dp)
    if steps == 3:
        advance(out_item, 2)
    both_cores((resid_hbm, out_part_hbm, out_far_hbm), output_rows, out_hbm)
    core_free()
    if steps == 3:
        for i, step in ((0, 1), (1, 1), (0, 2), (2, 1), (1, 2)):
            advance(i, step)
        rest = ((3, 1), (2, 2), (3, 2))
    else:
        for step in range(1, steps):
            for i in range(len(items)):
                if step > 1 or i < out_item:
                    advance(i, step)
        rest = ()
    last = [(i, steps) for i in (out_item,) + tuple(range(out_item))]

    for c in range(chunks):
        far_wire(c).wait()
    vec_out_ref[...] = vec_ref[...]
    both_cores((far_ref, dresid_hbm, x_hbm), input_rows, dx_hbm)
    for i, step in rest:
        advance(i, step)

    for k, peer in enumerate([core] + dp_peers(dp)):
        hop = remote(vec_out_ref, vec_got_ref.at[k], v_send.at[k], v_recv.at[k], peer)
        hop.start()
        hop.wait()
        got = vec_got_ref[k]
        if k == 0:
            got = jnp.where(lax.broadcasted_iota(jnp.int32, got.shape, 0) < 2, got, 0.0)
        vec_out_ref[...] += got
    for i, step in last:
        advance(i, step)
    for c in copies.values():
        c.wait_send()
    for r in riders:
        r.wait()


def tail(ident, dp, h1, h1_t, grads, weights, o_pre, gain, vec, d3, u3, streams):
    tokens, width = h1.shape
    turn = h1_t is None
    flat = grads[0].shape[1]
    half = tokens // 2
    rows = width // dp
    steps = dp.bit_length() - 1
    full = pl.BlockSpec(memory_space=pltpu.VMEM)
    anywhere = pl.BlockSpec(memory_space=pl.ANY)
    f32 = lambda *shape: jax.ShapeDtypeStruct(shape, F32)
    dma = pltpu.SemaphoreType.DMA
    bufs = []
    items = tail_items(flat)
    for which, cols in items:
        for step in range(steps):
            count = rows * (dp >> (step + 1)) if which < 3 or step else 8
            bufs += [pltpu.VMEM((count, cols.stop - cols.start), F32)] * 2
    chunks = half // ROWS
    b16 = jax.ShapeDtypeStruct((tokens, width), BF16)
    return pl.pallas_call(
        functools.partial(tail_kernel, dp, turn, X_FIRST, Z_FIRST),
        out_shape=[f32(rows, flat)] * 4
        + [f32(*vec.shape), f32(half, width), f32(*d3.shape), f32(*u3.shape), b16, b16],
        in_specs=[anywhere if turn else full] + [full] * 9 + [anywhere] * 7,
        out_specs=[full] * 5 + [anywhere] * 5,
        scratch_shapes=[
            pltpu.VMEM((chunks, ROWS, width), F32),
            pltpu.VMEM((chunks, ROWS, width), F32),
            pltpu.VMEM((chunks, ROWS, width), F32),
            pltpu.VMEM((2 if turn else 1, 3, ROWS, width), F32),
            pltpu.VMEM((ROWS, width), BF16),
            pltpu.VMEM((ROWS, width), BF16),
            pltpu.VMEM((2, tokens, rows) if turn else (8, DH), BF16),
            pltpu.VMEM((steps + 1,) + vec.shape, F32),
            dma((chunks,)), dma((chunks,)), dma((chunks,)), dma((chunks,)),
            dma((3,)), dma((3,)), dma((len(items) * steps,)), dma((len(items) * steps,)),
            dma((steps + 1,)), dma((steps + 1,)), dma((2, 3)), dma((2,)), dma((2,)),
            pltpu.SemaphoreType.REGULAR,
        ]
        + bufs
        + ([pltpu.VMEM((width, tokens), BF16)] if turn else []),
        compiler_params=pltpu.CompilerParams(
            collective_id=ident, has_side_effects=True, vmem_limit_bytes=63 << 20
        ),
        cost_estimate=pl.CostEstimate(
            flops=12 * tokens * width * flat, transcendentals=0, bytes_accessed=96 << 20
        ),
    )(
        h1 if turn else h1_t, *grads, *weights, o_pre, gain[None, :], vec, d3, u3, *streams
    )


def core_gather_kernel(norm, tiles, v_ref, gain_ref, out_ref, send_ref, recv_ref, send_sem, recv_sem):
    peer = tensor_peer(1)
    greet(peer)
    half = v_ref.shape[0]
    size = half // tiles
    copies = []
    for c in range(tiles):
        rows = slice(c * size, (c + 1) * size)
        v = v_ref[rows, :]
        if norm:
            inv = lax.rsqrt(jnp.mean(v * v, axis=-1, keepdims=True) + EPS)
            v = v * inv * gain_ref[...]
            send_ref[rows, :] = v
        out_ref[rows, :] = v.astype(BF16)
        src = send_ref if norm else v_ref
        copies.append(
            remote(
                src.at[rows, :], recv_ref.at[rows, :], send_sem.at[c], recv_sem.at[c], peer
            )
        )
        copies[-1].start()
    for c in range(tiles):
        rows = slice(c * size, (c + 1) * size)
        copies[c].wait_recv()
        out_ref[half + c * size : half + (c + 1) * size, :] = recv_ref[rows, :].astype(BF16)
    for c in copies:
        c.wait_send()


def core_gather(ident, v, gain=None):
    half, n = v.shape
    tiles = 4
    out = jax.ShapeDtypeStruct((2 * half, n), BF16)
    full = pl.BlockSpec(memory_space=pltpu.VMEM)
    norm = gain is not None
    return pl.pallas_call(
        functools.partial(core_gather_kernel, norm, tiles),
        out_shape=out,
        in_specs=[full, full],
        out_specs=full,
        scratch_shapes=[
            pltpu.VMEM((half, n) if norm else (8, DH), F32),
            pltpu.VMEM((half, n), F32),
            pltpu.SemaphoreType.DMA((tiles,)),
            pltpu.SemaphoreType.DMA((tiles,)),
        ],
        compiler_params=pltpu.CompilerParams(
            collective_id=ident, has_side_effects=True, vmem_limit_bytes=48 << 20
        ),
        cost_estimate=pl.CostEstimate(
            flops=0, transcendentals=0, bytes_accessed=nbytes(v, v, v, out)
        ),
    )(v, gain[None, :] if norm else jnp.zeros((8, DH), F32))


TILE = 256
SLOTS = 4


def feed_kernel(
    dp, turn, h_ref, ogt_ref, ht_ref, wup_hbm, wdn_hbm, ug_hbm,
    act_ref, dpre_ref, part_ref, part2_ref, far_ref, d_ref, u_ref, d_pre_ref, u_pre_ref,
    w_ref, ug_ref, ds_ref, us_ref, cs_ref, cr_ref,
    w_sem, ug_sem, d_send, d_recv, u_send, u_recv, c_send, c_recv, y_send, y_recv, free_sem,
):
    tokens, units = act_ref.shape
    half = tokens // 2
    width = h_ref.shape[1]
    cut = width // 2
    rows = width // dp
    me = lax.axis_index("dp")
    core, far = tensor_peer(1), tensor_peer(2)
    x_peer, z_peer = {"dp": me ^ 1}, {"dp": me ^ 2}
    greet(core, far, x_peer, z_peer)
    count = units // TILE

    load_w = pltpu.make_async_copy(wup_hbm, w_ref, w_sem)
    load_w.start()

    def tile_cols(t):
        return pl.ds(pl.multiple_of(t * TILE, TILE), TILE)

    def load_ug(t, k):
        return pltpu.make_async_copy(ug_hbm.at[:, tile_cols(t)], ug_ref.at[k], ug_sem.at[k])

    load_ug(0, 0).start()
    load_ug(1, 1).start()
    for j in range(dp // 2 if turn else 0):
        ht_ref[j * rows : (j + 1) * rows, :] = block_of(h_ref, dp, X_FIRST, j).T
    load_w.wait()

    def wire(t, k):
        cols = tile_cols(t)
        d = remote(ds_ref.at[k], d_ref.at[:, cols], d_send.at[t], d_recv.at[t], z_peer)
        u = remote(us_ref.at[k], u_ref.at[:, cols], u_send.at[t], u_recv.at[t], x_peer)
        return d, u

    def terms(t, k):
        cols = tile_cols(t)
        d, u = wire(t, k)
        ds_ref[k] = dot(ogt_ref[:cut, :], act_ref[:, cols])
        d.start()
        us_ref[k] = dot(ht_ref[:cut, :], dpre_ref[:, cols])
        u.start()

    @pl.loop(0, count)
    def _(t):
        k = t % 2
        cols = tile_cols(t)
        load_ug(t, k).wait()
        pre = dot(h_ref[...], w_ref[:, cols])
        c = 0.7978845608028654
        sq = pre * pre
        th = jnp.tanh(c * pre * (1.0 + 0.044715 * sq))
        mid = 0.5 * (1.0 + th)
        act_ref[:, cols] = (pre * mid).astype(BF16)
        slope = mid + 0.5 * pre * (1.0 - th * th) * (c * (1.0 + 0.134145 * sq))
        dpre_ref[:, cols] = (ug_ref[k] * slope).astype(BF16)

        @pl.when(t + 2 < count)
        def _():
            load_ug(t + 2, k).start()

        @pl.when(t < SLOTS)
        def _():
            terms(t, t)

    part_cols = width // 4

    def core_wire(c):
        return remote(cs_ref.at[c], cr_ref.at[c], c_send.at[c], c_recv.at[c], core)

    def far_wire(c):
        cols = pl.ds(c * part_cols, part_cols)
        return remote(part_ref.at[:, cols], far_ref.at[:, cols], y_send.at[c], y_recv.at[c], far)

    def summed(lhs_ref, transposed, out_ref, travels):
        def term(row, c):
            cols = slice(c * part_cols, (c + 1) * part_cols)
            lhs = lhs_ref[row * half : (row + 1) * half, :]
            if transposed:
                return dot_nt(lhs, w_ref[cols, :])
            return dot(lhs, w_ref[:, cols])

        for c in range(4):
            cs_ref[c] = term(1, c)
            core_wire(c).start()
        for c in range(4):
            part = term(0, c)
            core_wire(c).wait()
            out_ref[:, c * part_cols : (c + 1) * part_cols] = part + cr_ref[c]
            if travels:
                far_wire(c).start()

    summed(dpre_ref, True, part_ref, True)
    load_down = pltpu.make_async_copy(wdn_hbm, w_ref, w_sem)
    load_down.start()
    pl.semaphore_signal(free_sem, inc=1, device_id=core, device_id_type=pl.DeviceIdType.MESH)
    for j in range(dp // 2, dp if turn else 0):
        ht_ref[j * rows : (j + 1) * rows, :] = block_of(h_ref, dp, X_FIRST, j).T

    @pl.loop(SLOTS, count)
    def _(t):
        d, u = wire(t - SLOTS, t - SLOTS)
        d.wait_send()
        u.wait_send()
        terms(t, t - SLOTS)

    load_down.wait()
    pl.semaphore_wait(free_sem, 1)
    summed(act_ref, False, part2_ref, False)

    def load_got(src_ref, t, k):
        return pltpu.make_async_copy(src_ref.at[:, tile_cols(t)], ug_ref.at[k], ug_sem.at[k])

    def store_pre(dst_ref, t, k):
        return pltpu.make_async_copy(ug_ref.at[k], dst_ref.at[:, tile_cols(t)], ug_sem.at[k])

    @pl.loop(0, count)
    def _(t):
        d, u = wire(t, 0)

        @pl.when(t > 0)
        def _():
            store_pre(d_pre_ref, t - 1, 0).wait()
            store_pre(u_pre_ref, t - 1, 1).wait()

        d.wait_recv()
        load_got(d_ref, t, 0).start()
        u.wait_recv()
        load_got(u_ref, t, 1).start()
        load_got(d_ref, t, 0).wait()
        ug_ref[0] += dot(ogt_ref[cut:, :], act_ref[:, tile_cols(t)])
        store_pre(d_pre_ref, t, 0).start()
        load_got(u_ref, t, 1).wait()
        ug_ref[1] += dot(ht_ref[cut:, :], dpre_ref[:, tile_cols(t)])
        store_pre(u_pre_ref, t, 1).start()

    store_pre(d_pre_ref, count - 1, 0).wait()
    store_pre(u_pre_ref, count - 1, 1).wait()

    @pl.loop(count - SLOTS, count)
    def _(t):
        d, u = wire(t, t - (count - SLOTS))
        d.wait_send()
        u.wait_send()

    for c in range(4):
        far_wire(c).wait()


def feed(ident, dp, h2, og_t, h_t, w_up, w_down, up_grad):
    tokens, width = h2.shape
    units = w_up.shape[1]
    half = tokens // 2
    cut = width // 2
    count = units // TILE
    full = pl.BlockSpec(memory_space=pltpu.VMEM)
    anywhere = pl.BlockSpec(memory_space=pl.ANY)
    f32 = lambda *shape: jax.ShapeDtypeStruct(shape, F32)
    b16 = jax.ShapeDtypeStruct((tokens, units), BF16)
    dma = pltpu.SemaphoreType.DMA
    turn = h_t is None
    kernel = functools.partial(feed_kernel, dp, turn)
    if turn:

        def kernel(h_ref, ogt_ref, *refs):
            feed_kernel(dp, turn, h_ref, ogt_ref, refs[-1], *refs[:-1])

    return pl.pallas_call(
        kernel,
        out_shape=[b16, b16, f32(half, width), f32(half, width), f32(half, width)]
        + [f32(cut, units)] * 4,
        in_specs=[full] * (2 if turn else 3) + [anywhere] * 3,
        out_specs=[full] * 4 + [anywhere] * 5,
        scratch_shapes=[
            pltpu.VMEM((width, units), BF16),
            pltpu.VMEM((2, tokens, TILE), F32),
            pltpu.VMEM((SLOTS, cut, TILE), F32),
            pltpu.VMEM((SLOTS, cut, TILE), F32),
            pltpu.VMEM((4, half, width // 4), F32),
            pltpu.VMEM((4, half, width // 4), F32),
            dma, dma((2,)), dma((count,)), dma((count,)), dma((count,)), dma((count,)),
            dma((4,)), dma((4,)), dma((4,)), dma((4,)), pltpu.SemaphoreType.REGULAR,
        ]
        + ([pltpu.VMEM((width, tokens), BF16)] if turn else []),
        compiler_params=pltpu.CompilerParams(
            collective_id=ident, has_side_effects=True, vmem_limit_bytes=62 << 20
        ),
        cost_estimate=pl.CostEstimate(
            flops=10 * tokens * width * units, transcendentals=tokens * units,
            bytes_accessed=64 << 20,
        ),
    )(h2, og_t, *([] if turn else [h_t]), w_up, w_down, up_grad)


def body(
    inputs,
    gain_attn,
    w_query,
    w_key,
    w_value,
    gate_logit,
    w_out,
    gain_mlp,
    w_up,
    w_down,
    seg_parent,
    out_grad,
):
    tokens, width = inputs.shape
    half = tokens // 2
    segs = tokens // SEG
    heads = w_query.shape[1] // DH
    pairs = segs * heads
    units = w_up.shape[1]
    flat = heads * DH
    scale = DH ** (-0.5)
    dp = lax.axis_size("dp")
    tn = lax.axis_size("tensor")
    rows = width // dp
    di = lax.axis_index("dp")
    core = lax.axis_index("tensor") % 2

    one = jnp.where(seg_parent[0] < tokens * dp, 1.0, 2.0)

    def low_after_wire(v):
        return (v * one).astype(BF16)

    def swap_core(v):
        return lax.ppermute(v, "tensor", [(i, i ^ 1) for i in range(tn)])

    def swap_y(v):
        return lax.ppermute(v, "tensor", [(i, i ^ 2) for i in range(tn)])

    def swap_dp(v, mask):
        return lax.ppermute(v, "dp", [(i, i ^ mask) for i in range(dp)])

    def columns(v, order):
        _, seq = halving(dp, order)
        return block_columns(v, [di ^ k for k in seq], rows)

    def blocks_for(v, order):
        return columns(v, order) if rows % DH else v

    cut = width // 2
    quarter = cut // 2

    def pick(v, index, axis):
        size = v.shape[axis] // 2
        return lax.dynamic_slice_in_dim(v, index * size, size, axis)

    def place(own, other, index, axis):
        return jnp.where(
            index == 0,
            jnp.concatenate([own, other], axis),
            jnp.concatenate([other, own], axis),
        )

    def inv_rms(v):
        return lax.rsqrt(jnp.mean(v * v, axis=-1, keepdims=True) + EPS)

    x_own = pick(inputs, core, 0).astype(F32)
    x_oth = pick(inputs, 1 - core, 0).astype(F32)
    inv_own = inv_rms(x_own)
    inv_oth = inv_rms(x_oth)
    h1 = jnp.concatenate(
        [
            (x_own * inv_own * gain_attn).astype(BF16),
            (x_oth * inv_oth * gain_attn).astype(BF16),
        ],
        0,
    )

    sub = segs // 2
    every = jnp.arange(seg_parent.shape[0], dtype=jnp.int32)
    sub_ids = jnp.arange(sub, dtype=jnp.int32)
    seg_local = jnp.concatenate([core * sub + sub_ids, (1 - core) * sub + sub_ids])
    order = spread_order(dp)
    ids = jnp.concatenate([(di ^ j) * segs + seg_local for j in order])
    mine_hot = (ids[:segs, None] == every[None, :]).astype(F32)
    ids_hot = (ids[:, None] == every[None, :]).astype(F32)
    lineage = ancestor_table(seg_parent)

    def weights_of(table):
        mine_rows = jnp.sum(mine_hot[:, :, None] * table[None], axis=1)
        return jnp.sum(mine_rows[:, None, :] * ids_hot[None], axis=-1)

    up_weight = weights_of(lineage)
    down_weight = weights_of(lineage.T)

    gate = jax.nn.sigmoid(gate_logit)
    gate_row = gate[None, :]

    og_own = pick(out_grad, core, 0)
    og = jnp.concatenate([og_own, pick(out_grad, 1 - core, 0)], 0)
    block_rows = pairs * DH + pairs
    act_f32 = jax.ShapeDtypeStruct((tokens, flat), F32)
    act_b16 = jax.ShapeDtypeStruct((tokens, flat), BF16)
    mem_shape = jax.ShapeDtypeStruct((pairs * DH, DH), F32)
    zin_shape = jax.ShapeDtypeStruct((pairs, DH), F32)
    full = pl.BlockSpec(memory_space=pltpu.VMEM)

    def attention_call(kernel, ident, outs, out_specs, scratch, args, in_specs, flops):
        return pl.pallas_call(
            functools.partial(kernel, dp, heads, segs, scale),
            out_shape=outs,
            in_specs=in_specs,
            out_specs=out_specs,
            scratch_shapes=scratch
            + [
                pltpu.VMEM((dp, block_rows, DH), F32),
                pltpu.SemaphoreType.DMA((dp,)),
                pltpu.SemaphoreType.DMA((dp,)),
            ],
            compiler_params=pltpu.CompilerParams(
                collective_id=ident, has_side_effects=True, vmem_limit_bytes=63 << 20
            ),
            cost_estimate=pl.CostEstimate(
                flops=flops, transcendentals=0, bytes_accessed=64 << 20
            ),
        )(*args)

    head_flops = 2 * segs * heads * SEG * SEG * DH
    dma = pltpu.SemaphoreType.DMA
    qh, kh, vh, a16, a_pair, local, memory, zin, w_out_all = attention_call(
        attention_kernel,
        0,
        [
            act_b16, act_b16, act_b16, act_b16,
            jax.ShapeDtypeStruct((half, 2 * flat), F32),
            act_f32, mem_shape, zin_shape,
            jax.ShapeDtypeStruct((4 * flat, width), BF16),
        ],
        [full] * 9,
        [
            pltpu.VMEM((4, flat, width), F32),
            pltpu.VMEM((half, flat), F32),
            dma((3 * W_CHUNKS,)), dma((3 * W_CHUNKS,)), dma, dma,
        ],
        (up_weight, gate_row, h1, w_query, w_key, w_value, w_out),
        [SMEM, SMEM] + [full] * 5,
        3 * head_flops + 6 * tokens * width * flat,
    )
    up_grad = dot_nt(og, after(w_down, a_pair))

    step = half // AG_CHUNKS
    a_near = [a_pair[c * step : (c + 1) * step] for c in range(AG_CHUNKS)]
    a_far = [swap_y(v) for v in a_near]
    near = [
        x_own[c * step : (c + 1) * step] + dot(v.astype(BF16), w_out_all[: 2 * flat])
        for c, v in enumerate(a_near)
    ]
    og_t = columns(after(og, up_grad), Z_FIRST).T
    resids = [
        n + dot(low_after_wire(after(f, og_t, *near)), w_out_all[2 * flat :])
        for n, f in zip(near, a_far)
    ]
    resid = jnp.concatenate(resids, 0)
    inv_mlp = inv_rms(resid)
    h2 = core_gather(1, resid, gain_mlp)

    h_t = columns(h2, X_FIRST).T if rows % DH else None
    act, dpre, dh2_part, out_part, dh2_far, _, _, d_pre, u_pre = feed(
        2, dp, h2, og_t, h_t, w_up, w_down, up_grad
    )

    dh2 = dh2_part + dh2_far
    gs = dh2 * gain_mlp
    dresid = (
        og_own.astype(F32)
        + inv_mlp * gs
        - resid * inv_mlp * inv_mlp * inv_mlp * jnp.mean(gs * resid, axis=-1, keepdims=True)
    )
    gain_mlp_part = jnp.sum(dh2 * resid * inv_mlp, axis=0)
    dr = core_gather(4, dresid)

    da = dot_nt(dr, w_out).astype(BF16)
    anywhere = pl.BlockSpec(memory_space=pl.ANY)
    ride = jax.ShapeDtypeStruct((quarter, units), F32)
    o_shape = jax.ShapeDtypeStruct((cut, flat), F32)
    dq16, dk16, dv16, gate_rows, o_pre, d_rode, u_rode, out_far = attention_call(
        attention_back_kernel,
        5,
        [
            act_b16, act_b16, act_b16, zin_shape, o_shape, ride, ride,
            jax.ShapeDtypeStruct((half, width), F32),
        ],
        [full] * 5 + [anywhere] * 3,
        [pltpu.VMEM((tokens, flat), F32)] * 3
        + [pltpu.VMEM((cut, flat), F32)]
        + [dma((6,)), dma((6,))],
        (
            down_weight, gate_row, qh, kh, vh, da, local, memory, zin,
            blocks_for(dr, Z_FIRST), a16, d_pre, u_pre, out_part,
        ),
        [SMEM, SMEM] + [full] * 9 + [anywhere] * 3,
        9 * head_flops,
    )
    gate_part = jnp.sum(gate_rows.reshape(segs, heads, DH), axis=(0, 2)) * gate * (1.0 - gate)

    eighth = quarter // 2
    d3 = d_pre[quarter : quarter + eighth] + d_rode[:eighth]
    close = near_units(dp, units)
    u3 = u_rode[:eighth] + jnp.where(
        jnp.arange(units)[None, :] < close, u_pre[quarter : quarter + eighth], u_pre[eighth:quarter]
    )
    h1_t = columns(h1, X_FIRST).T if rows % DH else None
    lane = jnp.pad(gate_part, (0, width - heads))
    vec = jnp.zeros((8, width), F32).at[1].set(gain_mlp_part).at[2].set(lane)
    (
        w_query_grad, w_key_grad, w_value_grad, w_out_rows, vec, _, d3, u3, outputs, input_grad
    ) = tail(
        7, dp, h1, h1_t, (dq16, dk16, dv16), (w_query, w_key, w_value), o_pre, gain_attn, vec,
        d3, u3, (resid, out_part, out_far, dresid, x_own),
    )
    w_out_grad = w_out_rows.T

    def finish(pre, rode, got, order):
        masks, _ = halving(dp, order)
        value = pre[quarter + eighth :] + rode[eighth:] + got
        for m in masks[3:]:
            n = value.shape[0] // 2
            value = value[n:] + swap_dp(value[:n], m)
        return value

    w_down_grad = finish(d_pre, d_rode, d3, Z_FIRST).T
    w_up_grad = finish(u_pre, u_rode, u3, X_FIRST)

    gain_attn_grad = lax.dynamic_slice_in_dim(vec[0], di * rows, rows, 0)
    gain_mlp_grad = lax.dynamic_slice_in_dim(vec[1], di * rows, rows, 0)
    gate_grad = vec[2, :heads]

    return (
        outputs,
        input_grad,
        gain_attn_grad,
        w_query_grad,
        w_key_grad,
        w_value_grad,
        gate_grad,
        w_out_grad,
        gain_mlp_grad,
        w_up_grad,
        w_down_grad,
    )


def solution(mesh):
    placed = (
        P("dp", None),
        P(),
        P(None, "tensor"),
        P(None, "tensor"),
        P(None, "tensor"),
        P("tensor"),
        P("tensor", None),
        P(),
        P(None, "tensor"),
        P("tensor", None),
        P(),
        P("dp", None),
    )
    return jax.shard_map(
        body,
        mesh=mesh,
        in_specs=placed,
        out_specs=(
            P("dp", None),
            P("dp", None),
            P("dp"),
            P("dp", "tensor"),
            P("dp", "tensor"),
            P("dp", "tensor"),
            P("tensor"),
            P("tensor", "dp"),
            P("dp"),
            P("dp", "tensor"),
            P("tensor", "dp"),
        ),
        check_vma=False,
    )
```

```python
import functools

import jax
import jax.numpy as jnp
from jax import lax
from jax.experimental import pallas as pl
from jax.experimental.pallas import tpu as pltpu
from jax.sharding import PartitionSpec as P

DH = 128
SEG = 512
DEPTH = 5
EPS = 1e-06

F32 = jnp.float32
BF16 = jnp.bfloat16

AG_CHUNKS = 1
Z_FIRST = (1, 0)
X_FIRST = (0, 1)


def feature_map(values):
    return jnp.where(values > 0, values + 1.0, jnp.exp(jnp.minimum(values, 0.0)))


def feature_slope(values):
    return jnp.where(values > 0, 1.0, jnp.exp(jnp.minimum(values, 0.0)))


def ancestor_table(seg_parent):
    seg_total = seg_parent.shape[0]
    columns = jnp.arange(seg_total, dtype=jnp.int32)
    current = seg_parent
    lineage_table = jnp.zeros((seg_total, seg_total), F32)
    for _ in range(DEPTH):
        onehot = current[:, None] == columns[None, :]
        lineage_table = lineage_table + onehot.astype(F32)
        lifted = jnp.sum(jnp.where(onehot, seg_parent[None, :], 0), axis=1)
        current = jnp.where(current >= 0, lifted, -1)
    return lineage_table


def dot(a, b):
    return jnp.dot(a, b, preferred_element_type=F32)


def dot_t(a, b):
    return lax.dot_general(a, b, (((0,), (0,)), ((), ())), preferred_element_type=F32)


def dot_nt(a, b):
    return lax.dot_general(a, b, (((1,), (1,)), ((), ())), preferred_element_type=F32)


def after(value, *earlier):
    return lax.optimization_barrier((value, earlier))[0]


def nbytes(*arrays):
    return sum(a.size * a.dtype.itemsize for a in arrays)


def copy_kernel(ids_ref, in_ref, out_ref):
    out_ref[...] = in_ref[...]


def block_columns(v, ids, size):
    if size % 128:
        return jnp.concatenate([lax.dynamic_slice_in_dim(v, i * size, size, 1) for i in ids], 1)
    height, width = v.shape
    return pl.pallas_call(
        copy_kernel,
        out_shape=jax.ShapeDtypeStruct(v.shape, v.dtype),
        grid_spec=pltpu.PrefetchScalarGridSpec(
            num_scalar_prefetch=1,
            grid=(width // size,),
            in_specs=[pl.BlockSpec((height, size), lambda k, ids: (0, ids[k]))],
            out_specs=pl.BlockSpec((height, size), lambda k, ids: (0, k)),
        ),
        cost_estimate=pl.CostEstimate(flops=0, transcendentals=0, bytes_accessed=2 * nbytes(v)),
    )(jnp.stack(ids), v)


SMEM = pl.BlockSpec(memory_space=pltpu.SMEM)


def causal_mask():
    row = lax.broadcasted_iota(jnp.int32, (SEG, SEG), 0)
    col = lax.broadcasted_iota(jnp.int32, (SEG, SEG), 1)
    return row >= col


def softmax_rows(q, k, scale):
    scores = dot_nt(q, k) * scale
    scores = jnp.where(causal_mask(), scores, -1e30)
    top = jnp.max(scores, axis=-1, keepdims=True)
    e = jnp.exp(scores - top)
    return e * (1.0 / jnp.sum(e, axis=-1, keepdims=True))


def head_part(heads, p):
    s, h = p // heads, p % heads
    return pl.ds(pl.multiple_of(s * SEG, SEG), SEG), pl.ds(pl.multiple_of(h * DH, DH), DH)


def matrix_part(p):
    return pl.ds(pl.multiple_of(p * DH, DH), DH)


def weighted(w_ref, p, heads, segs, blocks_ref):
    s, h = p // heads, p % heads
    pairs = segs * heads
    big = jnp.zeros((DH, DH), F32)
    small = jnp.zeros((1, DH), F32)
    for d in range(blocks_ref.shape[0]):
        for n in range(segs):
            w = w_ref[s, d * segs + n]
            o = n * heads + h
            big = big + w * blocks_ref[d, matrix_part(o), :]
            small = small + w * blocks_ref[d, pl.ds(pairs * DH + o, 1), :]
    return big, small


def spread_order(dp):
    low = [0]
    for b in reversed(range(1, dp.bit_length() - 1)):
        low = low + [v ^ (1 << b) for v in low]
    return low + [v ^ 1 for v in low]


def greet(*peers):
    barrier = pltpu.get_barrier_semaphore()
    for peer in peers:
        pl.semaphore_signal(barrier, inc=1, device_id=peer, device_id_type=pl.DeviceIdType.MESH)
    pl.semaphore_wait(barrier, len(peers))


def dp_peers(dp):
    me = lax.axis_index("dp")
    return [{"dp": me ^ (1 << b)} for b in range(dp.bit_length() - 1)]


def tensor_peer(mask):
    return {"tensor": lax.axis_index("tensor") ^ mask}


def halving(dp, order):
    masks = [1 << b for b in order]
    masks += [1 << b for b in range(len(order), dp.bit_length() - 1)]
    seq = [0]
    for m in reversed(masks):
        seq = [m ^ v for v in seq] + seq
    return masks, seq


def near_units(dp, units):
    return units // 4 if dp == 8 else units


def block_of(ref, dp, order, k):
    rows = ref.shape[1] // dp
    if rows % DH:
        return ref[:, k * rows : (k + 1) * rows]
    at = (lax.axis_index("dp") ^ halving(dp, order)[1][k]) * rows
    return ref[:, pl.ds(pl.multiple_of(at, rows), rows)]


def remote(src, dst, send_sem, recv_sem, peer):
    return pltpu.make_async_remote_copy(
        src_ref=src,
        dst_ref=dst,
        send_sem=send_sem,
        recv_sem=recv_sem,
        device_id=peer,
        device_id_type=pl.DeviceIdType.MESH,
    )


def spread(dp, blocks_ref, send_sem, recv_sem, compute, then=None):
    me = lax.axis_index("dp")
    slot = {j: k for k, j in enumerate(spread_order(dp))}
    copies = {}

    def send(j, mask):
        to = j ^ mask
        k = slot[to]
        copies[to] = pltpu.make_async_remote_copy(
            src_ref=blocks_ref.at[slot[j]],
            dst_ref=blocks_ref.at[k],
            send_sem=send_sem.at[k],
            recv_sem=recv_sem.at[k],
            device_id={"dp": me ^ mask},
            device_id_type=pl.DeviceIdType.MESH,
        )
        copies[to].start()

    bits = [1 << b for b in range(1, dp.bit_length() - 1)]
    for m in bits:
        send(0, m)
    send(0, 1)
    compute()
    for m in bits:
        copies[m].wait_recv()
        if m == bits[-1]:
            near = [0, m]
            for n in reversed(bits[:-1]):
                for j in near[1:]:
                    send(j, n)
                near = near + [n] + [j ^ n for j in near[1:]]
                if n != bits[0]:
                    for j in near:
                        if j & n and j != n:
                            copies[j].wait_recv()
        send(m, 1)
    if then is not None:
        then()
    last = [j for j in near if j and j not in bits]
    for j in last:
        if j & bits[0] or len(bits) == 1:
            copies[j].wait_recv()
        send(j, 1)
    for j in near:
        copies[j ^ 1].wait_recv()
    for c in copies.values():
        c.wait_send()


W_CHUNKS = 4


def attention_kernel(
    dp, heads, segs, scale, w_ref, g_ref, h_ref, wq_ref, wk_ref, wv_ref, wo_ref,
    q_ref, k_ref, v_ref, a16_ref, pair_ref, local_ref, mem_ref, zin_ref, all_ref,
    wf_ref, asend_ref, w_send, w_recv, a_send, a_recv, blocks_ref, send_sem, recv_sem,
):
    pairs = segs * heads
    flat = heads * DH
    half = segs * SEG // 2
    core, far = tensor_peer(1), tensor_peer(2)
    greet(*dp_peers(dp), core, far)

    size = flat // W_CHUNKS
    w_copies = {}

    def w_send_chunk(j, c, to, peer):
        rows = pl.ds(c * size, size)
        k = (to - 1) * W_CHUNKS + c
        w_copies[to, c] = remote(
            wf_ref.at[j, rows, :], wf_ref.at[to, rows, :], w_send.at[k], w_recv.at[k], peer
        )
        w_copies[to, c].start()

    def w_done(to, c):
        rows = slice(c * size, (c + 1) * size)
        w_copies[to, c].wait_recv()
        all_ref[to * flat + c * size : to * flat + (c + 1) * size, :] = wf_ref[to, rows, :].astype(
            BF16
        )

    for c in range(W_CHUNKS):
        rows = slice(c * size, (c + 1) * size)
        wf_ref[0, rows, :] = wo_ref[rows, :].astype(F32)
        w_send_chunk(0, c, 2, far)
        w_send_chunk(0, c, 1, core)
    all_ref[:flat, :] = wo_ref[...]

    def project(matrix_ref, out_ref):
        @pl.loop(0, segs * SEG // 256)
        def _(i):
            rows = pl.ds(pl.multiple_of(i * 256, 256), 256)
            out_ref[rows, :] = dot(h_ref[rows, :], matrix_ref[...]).astype(BF16)

    project(wk_ref, k_ref)
    project(wv_ref, v_ref)

    @pl.loop(0, pairs)
    def _(p):
        at = head_part(heads, p)
        sk = feature_map(k_ref[at].astype(F32))
        blocks_ref[0, matrix_part(p), :] = dot_t(sk.astype(BF16), v_ref[at])
        blocks_ref[0, pl.ds(pairs * DH + p, 1), :] = jnp.sum(sk, axis=0, keepdims=True)

    def compute():
        project(wq_ref, q_ref)

        @pl.loop(0, pairs)
        def _(p):
            at = head_part(heads, p)
            probs = softmax_rows(q_ref[at], k_ref[at], scale)
            local_ref[at] = dot(probs.astype(BF16), v_ref[at])

    spread(dp, blocks_ref, send_sem, recv_sem, compute)

    @pl.loop(0, pairs)
    def _(p):
        at = head_part(heads, p)
        mem, zin = weighted(w_ref, p, heads, segs, blocks_ref)
        mem_ref[matrix_part(p), :] = mem
        zin_ref[pl.ds(p, 1), :] = zin
        g = g_ref[0, p % heads]
        sq = feature_map(q_ref[at].astype(F32))
        den = jnp.sum(sq * zin, axis=-1, keepdims=True) + 1.0
        retrieved = dot(sq.astype(BF16), mem.astype(BF16)) / den
        a16_ref[at] = (g * retrieved + (1.0 - g) * local_ref[at]).astype(BF16)

    asend_ref[...] = a16_ref[half:, :].astype(F32)
    a_copy = remote(asend_ref, pair_ref.at[:, pl.ds(flat, flat)], a_send, a_recv, core)
    a_copy.start()
    pair_ref[:, :flat] = a16_ref[:half, :].astype(F32)
    for c in range(W_CHUNKS):
        w_done(1, c)
    a_copy.wait_recv()
    for c in range(W_CHUNKS):
        w_copies[2, c].wait_recv()
        w_send_chunk(2, c, 3, core)
        rows = slice(c * size, (c + 1) * size)
        all_ref[2 * flat + c * size : 2 * flat + (c + 1) * size, :] = wf_ref[2, rows, :].astype(BF16)
    for c in range(W_CHUNKS):
        w_done(3, c)
    for copy in w_copies.values():
        copy.wait_send()
    a_copy.wait_send()


def attention_back_kernel(
    dp, heads, segs, scale, w_ref, g_ref, q_ref, k_ref, v_ref, da_ref, local_ref, mem_ref, zin_ref,
    dr_ref, a16_ref, d_pre_ref, u_pre_ref, out_part_ref,
    dq_ref, dk_ref, dv_ref, gate_ref, o_pre_ref, d_rode_ref, u_rode_ref, out_far_ref,
    dqm_ref, dkl_ref, dvl_ref, os_ref, ride_send, ride_recv, blocks_ref, send_sem, recv_sem,
):
    pairs = segs * heads
    me = lax.axis_index("dp")
    far = tensor_peer(2)
    greet(*dp_peers(dp), far)
    legs = [
        (d_pre_ref, d_rode_ref, {"dp": me ^ 1}),
        (out_part_ref, out_far_ref, far),
        (os_ref, o_pre_ref, {"dp": me ^ 2}),
    ]
    quarter, units = d_rode_ref.shape
    eighth = quarter // 2
    legs[0] = (d_pre_ref.at[pl.ds(0, quarter), :], d_rode_ref, {"dp": me ^ 1})
    near = near_units(dp, units)
    cols = pl.ds(0, near)
    legs.append((u_pre_ref.at[pl.ds(0, quarter), cols], u_rode_ref.at[:, cols], {"dp": me ^ 2}))
    if near < units:
        cols = pl.ds(near, units - near)
        for k in range(2):
            legs.append(
                (
                    u_pre_ref.at[pl.ds(2 * k * eighth, eighth), cols],
                    u_rode_ref.at[pl.ds(k * eighth, eighth), cols],
                    {"dp": me ^ 4},
                )
            )
    riders = [
        remote(src, dst, ride_send.at[i], ride_recv.at[i], peer)
        for i, (src, dst, peer) in enumerate(legs)
    ]
    o_rider = riders[2]
    plain = riders[:2] + riders[3:]
    for r in riders[:2] + riders[3:4]:
        r.start()

    @pl.loop(0, pairs)
    def _(p):
        at = head_part(heads, p)
        g = g_ref[0, p % heads]
        qf = q_ref[at].astype(F32)
        sq = feature_map(qf)
        sq16 = sq.astype(BF16)
        mem16 = mem_ref[matrix_part(p), :].astype(BF16)
        zin = zin_ref[pl.ds(p, 1), :]
        inv_den = 1.0 / (jnp.sum(sq * zin, axis=-1, keepdims=True) + 1.0)
        retrieved = dot(sq16, mem16) * inv_den
        da = da_ref[at].astype(F32)
        gate_ref[pl.ds(p, 1), :] = jnp.sum(da * (retrieved - local_ref[at]), axis=0, keepdims=True)
        dnum = g * da * inv_den
        dden = -jnp.sum(dnum * retrieved, axis=-1, keepdims=True)
        dnum16 = dnum.astype(BF16)
        blocks_ref[0, matrix_part(p), :] = dot_t(sq16, dnum16)
        blocks_ref[0, pl.ds(pairs * DH + p, 1), :] = jnp.sum(sq * dden, axis=0, keepdims=True)
        dsq = dot_nt(dnum16, mem16) + dden * zin
        dqm_ref[at] = dsq * feature_slope(qf)

    rows = dr_ref.shape[1] // dp
    half_blocks = dp // 2

    def compute():
        for j in range(half_blocks):
            os_ref[j * rows : (j + 1) * rows, :] = dot_t(
                block_of(dr_ref, dp, Z_FIRST, j), a16_ref[...]
            )

        @pl.loop(0, pairs)
        def _(p):
            at = head_part(heads, p)
            g = g_ref[0, p % heads]
            q, k, v, da = q_ref[at], k_ref[at], v_ref[at], da_ref[at]
            probs = softmax_rows(q, k, scale)
            dprobs = (1.0 - g) * dot_nt(da, v)
            inner = jnp.sum(dprobs * probs, axis=-1, keepdims=True)
            ds16 = (probs * (dprobs - inner)).astype(BF16)
            dq_ref[at] = (dot(ds16, k) * scale + dqm_ref[at]).astype(BF16)
            dkl_ref[at] = dot_t(ds16, q) * scale
            dvl_ref[at] = (1.0 - g) * dot_t(probs.astype(BF16), da)

    def then():
        o_rider.start()
        for r in riders[4:]:
            r.start()

    spread(dp, blocks_ref, send_sem, recv_sem, compute, then)

    @pl.loop(0, pairs)
    def _(p):
        at = head_part(heads, p)
        dd, dz = weighted(w_ref, p, heads, segs, blocks_ref)
        dd16 = dd.astype(BF16)
        kf = k_ref[at].astype(F32)
        dsk = dot_nt(v_ref[at], dd16) + dz
        dk_ref[at] = (dkl_ref[at] + dsk * feature_slope(kf)).astype(BF16)
        dv_ref[at] = (dvl_ref[at] + dot(feature_map(kf).astype(BF16), dd16)).astype(BF16)

    o_rider.wait()
    for j in range(half_blocks):
        o_pre_ref[j * rows : (j + 1) * rows, :] += dot_t(
            block_of(dr_ref, dp, Z_FIRST, half_blocks + j), a16_ref[...]
        )
    for r in plain:
        r.wait()


ROWS = 128


def tail_items(flat):
    full = slice(0, flat)
    return [
        (0, full), (1, full), (2, slice(0, flat // 2)), (2, slice(flat // 2, flat)), (3, full)
    ]


def tail_kernel(
    dp, turn, order, o_order,
    h_ref, dq_ref, dk_ref, dv_ref, wq_ref, wk_ref, wv_ref, o_pre_ref, gain_ref, vec_ref,
    d3_ref, u3_ref, resid_hbm, out_part_hbm, out_far_hbm, dresid_hbm, x_hbm,
    gq_ref, gk_ref, gv_ref, go_ref, vec_out_ref, far_ref, d3_got_ref, u3_got_ref, out_hbm, dx_hbm,
    part_ref, cs_ref, cr_ref, in_ref, own_ref, other_ref, turn_ref, vec_got_ref,
    c_send, c_recv, y_send, y_recv, ride_send, ride_recv, e_send, e_recv, v_send, v_recv,
    in_sem, st_sem, turn_sem, free_sem, *bufs,
):
    me = lax.axis_index("dp")
    side = lax.axis_index("tensor") % 2
    core, far = tensor_peer(1), tensor_peer(2)
    greet(*dp_peers(dp), core, far)
    masks, _ = halving(dp, order)
    o_masks, _ = halving(dp, o_order)
    steps = len(masks)
    half, width = far_ref.shape
    rows = width // dp
    chunks = half // ROWS
    ht_ref = bufs[-1] if turn else h_ref
    depth = in_ref.shape[0]
    flat = dq_ref.shape[1]
    lhs = (dq_ref, dk_ref, dv_ref)
    outs = (gq_ref, gk_ref, gv_ref, go_ref)
    items = tail_items(flat)
    copies = {}

    def buffers(i, step):
        k = 2 * (i * steps + step)
        return bufs[k], bufs[k + 1]

    def term(i, step):
        lo = rows * sum(dp >> (n + 1) for n in range(step))
        count = rows * (dp >> (step + 1)) if step < steps else rows
        start = 0
        which, cols = items[i]
        if which < 3:
            value = dot(ht_ref[lo : lo + count, :], lhs[which][:, cols])
        else:
            base = rows * (dp // 2)
            value = o_pre_ref[lo - base : lo - base + count, :]
            start = 1
        for n in range(start, step):
            at = lo - rows * sum(dp >> (m + 1) for m in range(n + 1))
            value = value + buffers(i, n)[1][at : at + count, :]
        return value

    def advance(i, step):
        which, cols = items[i]
        if step > (1 if which == 3 else 0):
            copies[i, step - 1].wait_recv()
        if step == steps:
            outs[which][:, cols] = term(i, step)
            return
        send, recv = buffers(i, step)
        send[...] = term(i, step)
        mask = (o_masks if which == 3 else masks)[step]
        k = i * steps + step
        copies[i, step] = remote(send, recv, e_send.at[k], e_recv.at[k], {"dp": me ^ mask})
        copies[i, step].start()

    third = {"dp": me ^ masks[2]}
    units = u3_ref.shape[1]
    near = near_units(dp, units)
    cols = pl.ds(0, near)
    legs = [(d3_ref, d3_got_ref, third), (u3_ref.at[:, cols], u3_got_ref.at[:, cols], third)]
    if near < units:
        cols = pl.ds(near, units - near)
        legs.append((u3_ref.at[:, cols], u3_got_ref.at[:, cols], {"dp": me ^ 2}))
    riders = [
        remote(src, dst, ride_send.at[i], ride_recv.at[i], peer)
        for i, (src, dst, peer) in enumerate(legs)
    ]
    out_item = len(items) - 1
    advance(out_item, 1)
    for r in riders:
        r.start()

    def block_load(j):
        at = (me ^ halving(dp, order)[1][j]) * rows
        return pltpu.make_async_copy(
            h_ref.at[:, pl.ds(pl.multiple_of(at, rows), rows)],
            turn_ref.at[j % 2],
            turn_sem.at[j % 2],
        )

    def turn_blocks(lo, hi):
        for j in range(lo, hi if turn else lo):
            block_load(j).wait()
            ht_ref[j * rows : (j + 1) * rows, :] = turn_ref[j % 2].T
            if j + 2 < dp:
                block_load(j + 2).start()

    for j in range(2 if turn else 0):
        block_load(j).start()
    turn_blocks(0, dp // 2)
    for i in range(out_item):
        advance(i, 0)

    def part_rows(c):
        return pl.ds(c * ROWS, ROWS)

    def core_wire(c):
        return remote(cs_ref.at[c], cr_ref.at[c], c_send.at[c], c_recv.at[c], core)

    def core_free():
        pl.semaphore_signal(free_sem, inc=1, device_id=core, device_id_type=pl.DeviceIdType.MESH)

    def far_wire(c):
        return remote(part_ref.at[c], far_ref.at[part_rows(c), :], y_send.at[c], y_recv.at[c], far)

    def back(lo):
        return sum(
            dot_nt(v[lo : lo + 2 * ROWS, :], w[...])
            for v, w in zip(lhs, (wq_ref, wk_ref, wv_ref))
        )

    for c in range(0, chunks, 2):
        value = back(half + c * ROWS)
        for k in range(2):
            cs_ref[c + k] = value[k * ROWS : (k + 1) * ROWS, :]
            core_wire(c + k).start()
    for c in range(0, chunks, 2):
        value = back(c * ROWS)
        for k in range(2):
            core_wire(c + k).wait()
            part_ref[c + k] = value[k * ROWS : (k + 1) * ROWS, :] + cr_ref[c + k]
            far_wire(c + k).start()
    core_free()

    def both_cores(sources, compute, dst_hbm):
        def loads(c):
            k = c % depth
            return [
                pltpu.make_async_copy(src.at[part_rows(c), :], in_ref.at[k, i], in_sem.at[k, i])
                for i, src in enumerate(sources)
            ]

        def begin(c):
            if c < chunks:
                for load in loads(c):
                    load.start()

        def store(src_ref, which, c, k):
            at = pl.ds(pl.multiple_of(which * half + c * ROWS, ROWS), ROWS)
            return pltpu.make_async_copy(src_ref, dst_hbm.at[at, :], st_sem.at[k])

        pl.semaphore_wait(free_sem, 1)
        for c in range(depth):
            begin(c)
        for c in range(chunks):
            for load in loads(c):
                load.wait()
            value = compute(c, *(in_ref[c % depth, i] for i in range(3))).astype(BF16)
            if c:
                store(own_ref, side, c - 1, 0).wait()
            own_ref[...] = value
            store(own_ref, side, c, 0).start()
            cs_ref[c] = value.astype(F32)
            core_wire(c).start()
            begin(c + depth)
        for c in range(chunks):
            core_wire(c).wait()
            if c:
                store(other_ref, 1 - side, c - 1, 1).wait()
            other_ref[...] = cr_ref[c].astype(BF16)
            store(other_ref, 1 - side, c, 1).start()
        store(own_ref, side, chunks - 1, 0).wait()
        store(other_ref, 1 - side, chunks - 1, 1).wait()

    def output_rows(c, a, b, d):
        return a + b + d

    def input_rows(c, there, dresid, x):
        grad = part_ref[c] + there
        inv = lax.rsqrt(jnp.mean(x * x, axis=-1, keepdims=True) + EPS)
        gs = grad * gain_ref[...]
        inner = jnp.mean(gs * x, axis=-1, keepdims=True)
        vec_out_ref[0:1, :] += jnp.sum(grad * x * inv, axis=0, keepdims=True)
        return dresid + inv * gs - x * inv * inv * inv * inner

    turn_blocks(dp // 2, dp)
    if steps == 3:
        advance(out_item, 2)
    both_cores((resid_hbm, out_part_hbm, out_far_hbm), output_rows, out_hbm)
    core_free()
    if steps == 3:
        for i, step in ((0, 1), (1, 1), (0, 2), (2, 1), (1, 2)):
            advance(i, step)
        rest = ((3, 1), (2, 2), (3, 2))
    else:
        for step in range(1, steps):
            for i in range(len(items)):
                if step > 1 or i < out_item:
                    advance(i, step)
        rest = ()
    last = [(i, steps) for i in (out_item,) + tuple(range(out_item))]

    for c in range(chunks):
        far_wire(c).wait()
    vec_out_ref[...] = vec_ref[...]
    both_cores((far_ref, dresid_hbm, x_hbm), input_rows, dx_hbm)
    for i, step in rest:
        advance(i, step)

    for k, peer in enumerate([core] + dp_peers(dp)):
        hop = remote(vec_out_ref, vec_got_ref.at[k], v_send.at[k], v_recv.at[k], peer)
        hop.start()
        hop.wait()
        got = vec_got_ref[k]
        if k == 0:
            got = jnp.where(lax.broadcasted_iota(jnp.int32, got.shape, 0) < 2, got, 0.0)
        vec_out_ref[...] += got
    for i, step in last:
        advance(i, step)
    for c in copies.values():
        c.wait_send()
    for r in riders:
        r.wait()


def tail(ident, dp, h1, h1_t, grads, weights, o_pre, gain, vec, d3, u3, streams):
    tokens, width = h1.shape
    turn = h1_t is None
    flat = grads[0].shape[1]
    half = tokens // 2
    rows = width // dp
    steps = dp.bit_length() - 1
    full = pl.BlockSpec(memory_space=pltpu.VMEM)
    anywhere = pl.BlockSpec(memory_space=pl.ANY)
    f32 = lambda *shape: jax.ShapeDtypeStruct(shape, F32)
    dma = pltpu.SemaphoreType.DMA
    bufs = []
    items = tail_items(flat)
    for which, cols in items:
        for step in range(steps):
            count = rows * (dp >> (step + 1)) if which < 3 or step else 8
            bufs += [pltpu.VMEM((count, cols.stop - cols.start), F32)] * 2
    chunks = half // ROWS
    b16 = jax.ShapeDtypeStruct((tokens, width), BF16)
    return pl.pallas_call(
        functools.partial(tail_kernel, dp, turn, X_FIRST, Z_FIRST),
        out_shape=[f32(rows, flat)] * 4
        + [f32(*vec.shape), f32(half, width), f32(*d3.shape), f32(*u3.shape), b16, b16],
        in_specs=[anywhere if turn else full] + [full] * 9 + [anywhere] * 7,
        out_specs=[full] * 5 + [anywhere] * 5,
        scratch_shapes=[
            pltpu.VMEM((chunks, ROWS, width), F32),
            pltpu.VMEM((chunks, ROWS, width), F32),
            pltpu.VMEM((chunks, ROWS, width), F32),
            pltpu.VMEM((2 if turn else 1, 3, ROWS, width), F32),
            pltpu.VMEM((ROWS, width), BF16),
            pltpu.VMEM((ROWS, width), BF16),
            pltpu.VMEM((2, tokens, rows) if turn else (8, DH), BF16),
            pltpu.VMEM((steps + 1,) + vec.shape, F32),
            dma((chunks,)), dma((chunks,)), dma((chunks,)), dma((chunks,)),
            dma((3,)), dma((3,)), dma((len(items) * steps,)), dma((len(items) * steps,)),
            dma((steps + 1,)), dma((steps + 1,)), dma((2, 3)), dma((2,)), dma((2,)),
            pltpu.SemaphoreType.REGULAR,
        ]
        + bufs
        + ([pltpu.VMEM((width, tokens), BF16)] if turn else []),
        compiler_params=pltpu.CompilerParams(
            collective_id=ident, has_side_effects=True, vmem_limit_bytes=63 << 20
        ),
        cost_estimate=pl.CostEstimate(
            flops=12 * tokens * width * flat, transcendentals=0, bytes_accessed=96 << 20
        ),
    )(
        h1 if turn else h1_t, *grads, *weights, o_pre, gain[None, :], vec, d3, u3, *streams
    )


def core_gather_kernel(norm, tiles, v_ref, gain_ref, out_ref, send_ref, recv_ref, send_sem, recv_sem):
    peer = tensor_peer(1)
    greet(peer)
    half = v_ref.shape[0]
    size = half // tiles
    copies = []
    for c in range(tiles):
        rows = slice(c * size, (c + 1) * size)
        v = v_ref[rows, :]
        if norm:
            inv = lax.rsqrt(jnp.mean(v * v, axis=-1, keepdims=True) + EPS)
            v = v * inv * gain_ref[...]
            send_ref[rows, :] = v
        out_ref[rows, :] = v.astype(BF16)
        src = send_ref if norm else v_ref
        copies.append(
            remote(
                src.at[rows, :], recv_ref.at[rows, :], send_sem.at[c], recv_sem.at[c], peer
            )
        )
        copies[-1].start()
    for c in range(tiles):
        rows = slice(c * size, (c + 1) * size)
        copies[c].wait_recv()
        out_ref[half + c * size : half + (c + 1) * size, :] = recv_ref[rows, :].astype(BF16)
    for c in copies:
        c.wait_send()


def core_gather(ident, v, gain=None):
    half, n = v.shape
    tiles = 4
    out = jax.ShapeDtypeStruct((2 * half, n), BF16)
    full = pl.BlockSpec(memory_space=pltpu.VMEM)
    norm = gain is not None
    return pl.pallas_call(
        functools.partial(core_gather_kernel, norm, tiles),
        out_shape=out,
        in_specs=[full, full],
        out_specs=full,
        scratch_shapes=[
            pltpu.VMEM((half, n) if norm else (8, DH), F32),
            pltpu.VMEM((half, n), F32),
            pltpu.SemaphoreType.DMA((tiles,)),
            pltpu.SemaphoreType.DMA((tiles,)),
        ],
        compiler_params=pltpu.CompilerParams(
            collective_id=ident, has_side_effects=True, vmem_limit_bytes=48 << 20
        ),
        cost_estimate=pl.CostEstimate(
            flops=0, transcendentals=0, bytes_accessed=nbytes(v, v, v, out)
        ),
    )(v, gain[None, :] if norm else jnp.zeros((8, DH), F32))


def norm_back_kernel(
    part_hbm, far_hbm, resid_hbm, grad_hbm, gain_ref, dresid_hbm, dr_ref, sum_ref,
    in_ref, og_ref, send_ref, recv_ref, c_send, c_recv, in_sem, og_sem, out_sem,
):
    peer = tensor_peer(1)
    greet(peer)
    half, width = dresid_hbm.shape
    chunks = half // ROWS
    sources = (part_hbm, far_hbm, resid_hbm)

    def rows(c):
        return pl.ds(c * ROWS, ROWS)

    def loads(c):
        k = c % 2
        wide = [
            pltpu.make_async_copy(src.at[rows(c), :], in_ref.at[k, i], in_sem.at[k, i])
            for i, src in enumerate(sources)
        ]
        return wide + [
            pltpu.make_async_copy(grad_hbm.at[rows(c), :], og_ref.at[k], og_sem.at[k])
        ]

    def wire(c):
        return remote(send_ref.at[c], recv_ref.at[c], c_send.at[c], c_recv.at[c], peer)

    def store(c):
        return pltpu.make_async_copy(send_ref.at[c], dresid_hbm.at[rows(c), :], out_sem.at[c])

    for c in range(2):
        for load in loads(c):
            load.start()
    sum_ref[...] = jnp.zeros_like(sum_ref)
    for c in range(chunks):
        k = c % 2
        for load in loads(c):
            load.wait()
        grad = in_ref[k, 0] + in_ref[k, 1]
        x = in_ref[k, 2]
        inv = lax.rsqrt(jnp.mean(x * x, axis=-1, keepdims=True) + EPS)
        gs = grad * gain_ref[...]
        inner = jnp.mean(gs * x, axis=-1, keepdims=True)
        sum_ref[0:1, :] += jnp.sum(grad * x * inv, axis=0, keepdims=True)
        value = og_ref[k].astype(F32) + inv * gs - x * inv * inv * inv * inner
        send_ref[c] = value
        wire(c).start()
        store(c).start()
        dr_ref[c * ROWS : (c + 1) * ROWS, :] = value.astype(BF16)
        if c + 2 < chunks:
            for load in loads(c + 2):
                load.start()
    for c in range(chunks):
        wire(c).wait()
        dr_ref[half + c * ROWS : half + (c + 1) * ROWS, :] = recv_ref[c].astype(BF16)
    for c in range(chunks):
        store(c).wait()


def norm_back(ident, part, far, resid, out_grad, gain):
    half, width = resid.shape
    chunks = half // ROWS
    outs = [
        jax.ShapeDtypeStruct((half, width), F32),
        jax.ShapeDtypeStruct((2 * half, width), BF16),
        jax.ShapeDtypeStruct((8, width), F32),
    ]
    full = pl.BlockSpec(memory_space=pltpu.VMEM)
    anywhere = pl.BlockSpec(memory_space=pl.ANY)
    dma = pltpu.SemaphoreType.DMA
    return pl.pallas_call(
        norm_back_kernel,
        out_shape=outs,
        in_specs=[anywhere] * 4 + [full],
        out_specs=[anywhere, full, full],
        scratch_shapes=[
            pltpu.VMEM((2, 3, ROWS, width), F32),
            pltpu.VMEM((2, ROWS, width), BF16),
            pltpu.VMEM((chunks, ROWS, width), F32),
            pltpu.VMEM((chunks, ROWS, width), F32),
            dma((chunks,)), dma((chunks,)), dma((2, 3)), dma((2,)), dma((chunks,)),
        ],
        compiler_params=pltpu.CompilerParams(
            collective_id=ident, has_side_effects=True, vmem_limit_bytes=48 << 20
        ),
        cost_estimate=pl.CostEstimate(
            flops=0, transcendentals=0, bytes_accessed=nbytes(part, far, resid, out_grad, *outs)
        ),
    )(part, far, resid, out_grad, gain[None, :])


TILE = 256
SLOTS = 4


def feed_kernel(
    dp, turn, h_ref, ogt_ref, ht_ref, wup_hbm, wdn_hbm, ug_hbm,
    act_ref, dpre_ref, part_ref, part2_ref, far_ref, d_ref, u_ref, d_pre_ref, u_pre_ref,
    w_ref, ug_ref, ds_ref, us_ref, cs_ref, cr_ref,
    w_sem, ug_sem, d_send, d_recv, u_send, u_recv, c_send, c_recv, y_send, y_recv, free_sem,
):
    tokens, units = act_ref.shape
    half = tokens // 2
    width = h_ref.shape[1]
    cut = width // 2
    rows = width // dp
    me = lax.axis_index("dp")
    core, far = tensor_peer(1), tensor_peer(2)
    x_peer, z_peer = {"dp": me ^ 1}, {"dp": me ^ 2}
    greet(core, far, x_peer, z_peer)
    count = units // TILE

    load_w = pltpu.make_async_copy(wup_hbm, w_ref, w_sem)
    load_w.start()

    def tile_cols(t):
        return pl.ds(pl.multiple_of(t * TILE, TILE), TILE)

    def load_ug(t, k):
        return pltpu.make_async_copy(ug_hbm.at[:, tile_cols(t)], ug_ref.at[k], ug_sem.at[k])

    load_ug(0, 0).start()
    load_ug(1, 1).start()
    for j in range(dp // 2 if turn else 0):
        ht_ref[j * rows : (j + 1) * rows, :] = block_of(h_ref, dp, X_FIRST, j).T
    load_w.wait()

    def wire(t, k):
        cols = tile_cols(t)
        d = remote(ds_ref.at[k], d_ref.at[:, cols], d_send.at[t], d_recv.at[t], z_peer)
        u = remote(us_ref.at[k], u_ref.at[:, cols], u_send.at[t], u_recv.at[t], x_peer)
        return d, u

    def terms(t, k):
        cols = tile_cols(t)
        d, u = wire(t, k)
        ds_ref[k] = dot(ogt_ref[:cut, :], act_ref[:, cols])
        d.start()
        us_ref[k] = dot(ht_ref[:cut, :], dpre_ref[:, cols])
        u.start()

    @pl.loop(0, count)
    def _(t):
        k = t % 2
        cols = tile_cols(t)
        load_ug(t, k).wait()
        pre = dot(h_ref[...], w_ref[:, cols])
        c = 0.7978845608028654
        sq = pre * pre
        th = jnp.tanh(c * pre * (1.0 + 0.044715 * sq))
        mid = 0.5 * (1.0 + th)
        act_ref[:, cols] = (pre * mid).astype(BF16)
        slope = mid + 0.5 * pre * (1.0 - th * th) * (c * (1.0 + 0.134145 * sq))
        dpre_ref[:, cols] = (ug_ref[k] * slope).astype(BF16)

        @pl.when(t + 2 < count)
        def _():
            load_ug(t + 2, k).start()

        @pl.when(t < SLOTS)
        def _():
            terms(t, t)

    part_cols = width // 4

    def core_wire(c):
        return remote(cs_ref.at[c], cr_ref.at[c], c_send.at[c], c_recv.at[c], core)

    def far_wire(c):
        cols = pl.ds(c * part_cols, part_cols)
        return remote(part_ref.at[:, cols], far_ref.at[:, cols], y_send.at[c], y_recv.at[c], far)

    def summed(lhs_ref, transposed, out_ref, travels):
        def term(row, c):
            cols = slice(c * part_cols, (c + 1) * part_cols)
            lhs = lhs_ref[row * half : (row + 1) * half, :]
            if transposed:
                return dot_nt(lhs, w_ref[cols, :])
            return dot(lhs, w_ref[:, cols])

        for c in range(4):
            cs_ref[c] = term(1, c)
            core_wire(c).start()
        for c in range(4):
            part = term(0, c)
            core_wire(c).wait()
            out_ref[:, c * part_cols : (c + 1) * part_cols] = part + cr_ref[c]
            if travels:
                far_wire(c).start()

    summed(dpre_ref, True, part_ref, True)
    load_down = pltpu.make_async_copy(wdn_hbm, w_ref, w_sem)
    load_down.start()
    pl.semaphore_signal(free_sem, inc=1, device_id=core, device_id_type=pl.DeviceIdType.MESH)
    for j in range(dp // 2, dp if turn else 0):
        ht_ref[j * rows : (j + 1) * rows, :] = block_of(h_ref, dp, X_FIRST, j).T

    @pl.loop(SLOTS, count)
    def _(t):
        d, u = wire(t - SLOTS, t - SLOTS)
        d.wait_send()
        u.wait_send()
        terms(t, t - SLOTS)

    load_down.wait()
    pl.semaphore_wait(free_sem, 1)
    summed(act_ref, False, part2_ref, False)

    def load_got(src_ref, t, k):
        return pltpu.make_async_copy(src_ref.at[:, tile_cols(t)], ug_ref.at[k], ug_sem.at[k])

    def store_pre(dst_ref, t, k):
        return pltpu.make_async_copy(ug_ref.at[k], dst_ref.at[:, tile_cols(t)], ug_sem.at[k])

    @pl.loop(0, count)
    def _(t):
        d, u = wire(t, 0)

        @pl.when(t > 0)
        def _():
            store_pre(d_pre_ref, t - 1, 0).wait()
            store_pre(u_pre_ref, t - 1, 1).wait()

        d.wait_recv()
        load_got(d_ref, t, 0).start()
        u.wait_recv()
        load_got(u_ref, t, 1).start()
        load_got(d_ref, t, 0).wait()
        ug_ref[0] += dot(ogt_ref[cut:, :], act_ref[:, tile_cols(t)])
        store_pre(d_pre_ref, t, 0).start()
        load_got(u_ref, t, 1).wait()
        ug_ref[1] += dot(ht_ref[cut:, :], dpre_ref[:, tile_cols(t)])
        store_pre(u_pre_ref, t, 1).start()

    store_pre(d_pre_ref, count - 1, 0).wait()
    store_pre(u_pre_ref, count - 1, 1).wait()

    @pl.loop(count - SLOTS, count)
    def _(t):
        d, u = wire(t, t - (count - SLOTS))
        d.wait_send()
        u.wait_send()

    for c in range(4):
        far_wire(c).wait()


def feed(ident, dp, h2, og_t, h_t, w_up, w_down, up_grad):
    tokens, width = h2.shape
    units = w_up.shape[1]
    half = tokens // 2
    cut = width // 2
    count = units // TILE
    full = pl.BlockSpec(memory_space=pltpu.VMEM)
    anywhere = pl.BlockSpec(memory_space=pl.ANY)
    f32 = lambda *shape: jax.ShapeDtypeStruct(shape, F32)
    b16 = jax.ShapeDtypeStruct((tokens, units), BF16)
    dma = pltpu.SemaphoreType.DMA
    turn = h_t is None
    kernel = functools.partial(feed_kernel, dp, turn)
    if turn:

        def kernel(h_ref, ogt_ref, *refs):
            feed_kernel(dp, turn, h_ref, ogt_ref, refs[-1], *refs[:-1])

    return pl.pallas_call(
        kernel,
        out_shape=[b16, b16, f32(half, width), f32(half, width), f32(half, width)]
        + [f32(cut, units)] * 4,
        in_specs=[full] * (2 if turn else 3) + [anywhere] * 3,
        out_specs=[full] * 4 + [anywhere] * 5,
        scratch_shapes=[
            pltpu.VMEM((width, units), BF16),
            pltpu.VMEM((2, tokens, TILE), F32),
            pltpu.VMEM((SLOTS, cut, TILE), F32),
            pltpu.VMEM((SLOTS, cut, TILE), F32),
            pltpu.VMEM((4, half, width // 4), F32),
            pltpu.VMEM((4, half, width // 4), F32),
            dma, dma((2,)), dma((count,)), dma((count,)), dma((count,)), dma((count,)),
            dma((4,)), dma((4,)), dma((4,)), dma((4,)), pltpu.SemaphoreType.REGULAR,
        ]
        + ([pltpu.VMEM((width, tokens), BF16)] if turn else []),
        compiler_params=pltpu.CompilerParams(
            collective_id=ident, has_side_effects=True, vmem_limit_bytes=62 << 20
        ),
        cost_estimate=pl.CostEstimate(
            flops=10 * tokens * width * units, transcendentals=tokens * units,
            bytes_accessed=64 << 20,
        ),
    )(h2, og_t, *([] if turn else [h_t]), w_up, w_down, up_grad)


def body(
    inputs,
    gain_attn,
    w_query,
    w_key,
    w_value,
    gate_logit,
    w_out,
    gain_mlp,
    w_up,
    w_down,
    seg_parent,
    out_grad,
):
    tokens, width = inputs.shape
    half = tokens // 2
    segs = tokens // SEG
    heads = w_query.shape[1] // DH
    pairs = segs * heads
    units = w_up.shape[1]
    flat = heads * DH
    scale = DH ** (-0.5)
    dp = lax.axis_size("dp")
    tn = lax.axis_size("tensor")
    rows = width // dp
    di = lax.axis_index("dp")
    core = lax.axis_index("tensor") % 2

    one = jnp.where(seg_parent[0] < tokens * dp, 1.0, 2.0)

    def low_after_wire(v):
        return (v * one).astype(BF16)

    def swap_core(v):
        return lax.ppermute(v, "tensor", [(i, i ^ 1) for i in range(tn)])

    def swap_y(v):
        return lax.ppermute(v, "tensor", [(i, i ^ 2) for i in range(tn)])

    def swap_dp(v, mask):
        return lax.ppermute(v, "dp", [(i, i ^ mask) for i in range(dp)])

    def columns(v, order):
        _, seq = halving(dp, order)
        return block_columns(v, [di ^ k for k in seq], rows)

    def blocks_for(v, order):
        return columns(v, order) if rows % DH else v

    cut = width // 2
    quarter = cut // 2

    def pick(v, index, axis):
        size = v.shape[axis] // 2
        return lax.dynamic_slice_in_dim(v, index * size, size, axis)

    def place(own, other, index, axis):
        return jnp.where(
            index == 0,
            jnp.concatenate([own, other], axis),
            jnp.concatenate([other, own], axis),
        )

    def inv_rms(v):
        return lax.rsqrt(jnp.mean(v * v, axis=-1, keepdims=True) + EPS)

    x_own = pick(inputs, core, 0).astype(F32)
    x_oth = pick(inputs, 1 - core, 0).astype(F32)
    inv_own = inv_rms(x_own)
    inv_oth = inv_rms(x_oth)
    h1 = jnp.concatenate(
        [
            (x_own * inv_own * gain_attn).astype(BF16),
            (x_oth * inv_oth * gain_attn).astype(BF16),
        ],
        0,
    )

    sub = segs // 2
    every = jnp.arange(seg_parent.shape[0], dtype=jnp.int32)
    sub_ids = jnp.arange(sub, dtype=jnp.int32)
    seg_local = jnp.concatenate([core * sub + sub_ids, (1 - core) * sub + sub_ids])
    order = spread_order(dp)
    ids = jnp.concatenate([(di ^ j) * segs + seg_local for j in order])
    mine_hot = (ids[:segs, None] == every[None, :]).astype(F32)
    ids_hot = (ids[:, None] == every[None, :]).astype(F32)
    lineage = ancestor_table(seg_parent)

    def weights_of(table):
        mine_rows = jnp.sum(mine_hot[:, :, None] * table[None], axis=1)
        return jnp.sum(mine_rows[:, None, :] * ids_hot[None], axis=-1)

    up_weight = weights_of(lineage)
    down_weight = weights_of(lineage.T)

    gate = jax.nn.sigmoid(gate_logit)
    gate_row = gate[None, :]

    og_own = pick(out_grad, core, 0)
    og = jnp.concatenate([og_own, pick(out_grad, 1 - core, 0)], 0)
    block_rows = pairs * DH + pairs
    act_f32 = jax.ShapeDtypeStruct((tokens, flat), F32)
    act_b16 = jax.ShapeDtypeStruct((tokens, flat), BF16)
    mem_shape = jax.ShapeDtypeStruct((pairs * DH, DH), F32)
    zin_shape = jax.ShapeDtypeStruct((pairs, DH), F32)
    full = pl.BlockSpec(memory_space=pltpu.VMEM)

    def attention_call(kernel, ident, outs, out_specs, scratch, args, in_specs, flops):
        return pl.pallas_call(
            functools.partial(kernel, dp, heads, segs, scale),
            out_shape=outs,
            in_specs=in_specs,
            out_specs=out_specs,
            scratch_shapes=scratch
            + [
                pltpu.VMEM((dp, block_rows, DH), F32),
                pltpu.SemaphoreType.DMA((dp,)),
                pltpu.SemaphoreType.DMA((dp,)),
            ],
            compiler_params=pltpu.CompilerParams(
                collective_id=ident, has_side_effects=True, vmem_limit_bytes=63 << 20
            ),
            cost_estimate=pl.CostEstimate(
                flops=flops, transcendentals=0, bytes_accessed=64 << 20
            ),
        )(*args)

    head_flops = 2 * segs * heads * SEG * SEG * DH
    dma = pltpu.SemaphoreType.DMA
    qh, kh, vh, a16, a_pair, local, memory, zin, w_out_all = attention_call(
        attention_kernel,
        0,
        [
            act_b16, act_b16, act_b16, act_b16,
            jax.ShapeDtypeStruct((half, 2 * flat), F32),
            act_f32, mem_shape, zin_shape,
            jax.ShapeDtypeStruct((4 * flat, width), BF16),
        ],
        [full] * 9,
        [
            pltpu.VMEM((4, flat, width), F32),
            pltpu.VMEM((half, flat), F32),
            dma((3 * W_CHUNKS,)), dma((3 * W_CHUNKS,)), dma, dma,
        ],
        (up_weight, gate_row, h1, w_query, w_key, w_value, w_out),
        [SMEM, SMEM] + [full] * 5,
        3 * head_flops + 6 * tokens * width * flat,
    )
    up_grad = dot_nt(og, after(w_down, a_pair))

    step = half // AG_CHUNKS
    a_near = [a_pair[c * step : (c + 1) * step] for c in range(AG_CHUNKS)]
    a_far = [swap_y(v) for v in a_near]
    near = [
        x_own[c * step : (c + 1) * step] + dot(v.astype(BF16), w_out_all[: 2 * flat])
        for c, v in enumerate(a_near)
    ]
    og_t = columns(after(og, up_grad), Z_FIRST).T
    resids = [
        n + dot(low_after_wire(after(f, og_t, *near)), w_out_all[2 * flat :])
        for n, f in zip(near, a_far)
    ]
    resid = jnp.concatenate(resids, 0)
    h2 = core_gather(1, resid, gain_mlp)

    h_t = columns(h2, X_FIRST).T if rows % DH else None
    act, dpre, dh2_part, out_part, dh2_far, _, _, d_pre, u_pre = feed(
        2, dp, h2, og_t, h_t, w_up, w_down, up_grad
    )

    dresid, dr, gain_mlp_sum = norm_back(4, dh2_part, dh2_far, resid, og_own, gain_mlp)
    gain_mlp_part = gain_mlp_sum[0]

    da = dot_nt(dr, w_out).astype(BF16)
    anywhere = pl.BlockSpec(memory_space=pl.ANY)
    ride = jax.ShapeDtypeStruct((quarter, units), F32)
    o_shape = jax.ShapeDtypeStruct((cut, flat), F32)
    dq16, dk16, dv16, gate_rows, o_pre, d_rode, u_rode, out_far = attention_call(
        attention_back_kernel,
        5,
        [
            act_b16, act_b16, act_b16, zin_shape, o_shape, ride, ride,
            jax.ShapeDtypeStruct((half, width), F32),
        ],
        [full] * 5 + [anywhere] * 3,
        [pltpu.VMEM((tokens, flat), F32)] * 3
        + [pltpu.VMEM((cut, flat), F32)]
        + [dma((6,)), dma((6,))],
        (
            down_weight, gate_row, qh, kh, vh, da, local, memory, zin,
            blocks_for(dr, Z_FIRST), a16, d_pre, u_pre, out_part,
        ),
        [SMEM, SMEM] + [full] * 9 + [anywhere] * 3,
        9 * head_flops,
    )
    gate_part = jnp.sum(gate_rows.reshape(segs, heads, DH), axis=(0, 2)) * gate * (1.0 - gate)

    eighth = quarter // 2
    d3 = d_pre[quarter : quarter + eighth] + d_rode[:eighth]
    close = near_units(dp, units)
    u3 = u_rode[:eighth] + jnp.where(
        jnp.arange(units)[None, :] < close, u_pre[quarter : quarter + eighth], u_pre[eighth:quarter]
    )
    h1_t = columns(h1, X_FIRST).T if rows % DH else None
    lane = jnp.pad(gate_part, (0, width - heads))
    vec = jnp.zeros((8, width), F32).at[1].set(gain_mlp_part).at[2].set(lane)
    (
        w_query_grad, w_key_grad, w_value_grad, w_out_rows, vec, _, d3, u3, outputs, input_grad
    ) = tail(
        7, dp, h1, h1_t, (dq16, dk16, dv16), (w_query, w_key, w_value), o_pre, gain_attn, vec,
        d3, u3, (resid, out_part, out_far, dresid, x_own),
    )
    w_out_grad = w_out_rows.T

    def finish(pre, rode, got, order):
        masks, _ = halving(dp, order)
        value = pre[quarter + eighth :] + rode[eighth:] + got
        for m in masks[3:]:
            n = value.shape[0] // 2
            value = value[n:] + swap_dp(value[:n], m)
        return value

    w_down_grad = finish(d_pre, d_rode, d3, Z_FIRST).T
    w_up_grad = finish(u_pre, u_rode, u3, X_FIRST)

    gain_attn_grad = lax.dynamic_slice_in_dim(vec[0], di * rows, rows, 0)
    gain_mlp_grad = lax.dynamic_slice_in_dim(vec[1], di * rows, rows, 0)
    gate_grad = vec[2, :heads]

    return (
        outputs,
        input_grad,
        gain_attn_grad,
        w_query_grad,
        w_key_grad,
        w_value_grad,
        gate_grad,
        w_out_grad,
        gain_mlp_grad,
        w_up_grad,
        w_down_grad,
    )


def solution(mesh):
    placed = (
        P("dp", None),
        P(),
        P(None, "tensor"),
        P(None, "tensor"),
        P(None, "tensor"),
        P("tensor"),
        P("tensor", None),
        P(),
        P(None, "tensor"),
        P("tensor", None),
        P(),
        P("dp", None),
    )
    return jax.shard_map(
        body,
        mesh=mesh,
        in_specs=placed,
        out_specs=(
            P("dp", None),
            P("dp", None),
            P("dp"),
            P("dp", "tensor"),
            P("dp", "tensor"),
            P("dp", "tensor"),
            P("tensor"),
            P("tensor", "dp"),
            P("dp"),
            P("dp", "tensor"),
            P("tensor", "dp"),
        ),
        check_vma=False,
    )
```

```python
import functools

import jax
import jax.numpy as jnp
from jax import lax
from jax.experimental import pallas as pl
from jax.experimental.pallas import tpu as pltpu
from jax.sharding import PartitionSpec as P

DH = 128
SEG = 512
DEPTH = 5
EPS = 1e-06

F32 = jnp.float32
BF16 = jnp.bfloat16

AG_CHUNKS = 1
Z_FIRST = (1, 0)
X_FIRST = (0, 1)


def feature_map(values):
    return jnp.where(values > 0, values + 1.0, jnp.exp(jnp.minimum(values, 0.0)))


def feature_slope(values):
    return jnp.where(values > 0, 1.0, jnp.exp(jnp.minimum(values, 0.0)))


def ancestor_table(seg_parent):
    seg_total = seg_parent.shape[0]
    columns = jnp.arange(seg_total, dtype=jnp.int32)
    current = seg_parent
    lineage_table = jnp.zeros((seg_total, seg_total), F32)
    for _ in range(DEPTH):
        onehot = current[:, None] == columns[None, :]
        lineage_table = lineage_table + onehot.astype(F32)
        lifted = jnp.sum(jnp.where(onehot, seg_parent[None, :], 0), axis=1)
        current = jnp.where(current >= 0, lifted, -1)
    return lineage_table


def dot(a, b):
    return jnp.dot(a, b, preferred_element_type=F32)


def dot_t(a, b):
    return lax.dot_general(a, b, (((0,), (0,)), ((), ())), preferred_element_type=F32)


def dot_nt(a, b):
    return lax.dot_general(a, b, (((1,), (1,)), ((), ())), preferred_element_type=F32)


def after(value, *earlier):
    return lax.optimization_barrier((value, earlier))[0]


def nbytes(*arrays):
    return sum(a.size * a.dtype.itemsize for a in arrays)


def copy_kernel(ids_ref, in_ref, out_ref):
    out_ref[...] = in_ref[...]


def block_columns(v, ids, size):
    if size % 128:
        return jnp.concatenate([lax.dynamic_slice_in_dim(v, i * size, size, 1) for i in ids], 1)
    height, width = v.shape
    return pl.pallas_call(
        copy_kernel,
        out_shape=jax.ShapeDtypeStruct(v.shape, v.dtype),
        grid_spec=pltpu.PrefetchScalarGridSpec(
            num_scalar_prefetch=1,
            grid=(width // size,),
            in_specs=[pl.BlockSpec((height, size), lambda k, ids: (0, ids[k]))],
            out_specs=pl.BlockSpec((height, size), lambda k, ids: (0, k)),
        ),
        cost_estimate=pl.CostEstimate(flops=0, transcendentals=0, bytes_accessed=2 * nbytes(v)),
    )(jnp.stack(ids), v)


SMEM = pl.BlockSpec(memory_space=pltpu.SMEM)


def causal_mask():
    row = lax.broadcasted_iota(jnp.int32, (SEG, SEG), 0)
    col = lax.broadcasted_iota(jnp.int32, (SEG, SEG), 1)
    return row >= col


def softmax_rows(q, k, scale):
    scores = dot_nt(q, k) * scale
    scores = jnp.where(causal_mask(), scores, -1e30)
    top = jnp.max(scores, axis=-1, keepdims=True)
    e = jnp.exp(scores - top)
    return e * (1.0 / jnp.sum(e, axis=-1, keepdims=True))


def head_part(heads, p):
    s, h = p // heads, p % heads
    return pl.ds(pl.multiple_of(s * SEG, SEG), SEG), pl.ds(pl.multiple_of(h * DH, DH), DH)


def matrix_part(p):
    return pl.ds(pl.multiple_of(p * DH, DH), DH)


def weighted(w_ref, p, heads, segs, blocks_ref):
    s, h = p // heads, p % heads
    pairs = segs * heads
    big = jnp.zeros((DH, DH), F32)
    small = jnp.zeros((1, DH), F32)
    for d in range(blocks_ref.shape[0]):
        for n in range(segs):
            w = w_ref[s, d * segs + n]
            o = n * heads + h
            big = big + w * blocks_ref[d, matrix_part(o), :]
            small = small + w * blocks_ref[d, pl.ds(pairs * DH + o, 1), :]
    return big, small


def spread_order(dp):
    low = [0]
    for b in reversed(range(1, dp.bit_length() - 1)):
        low = low + [v ^ (1 << b) for v in low]
    return low + [v ^ 1 for v in low]


def greet(*peers):
    barrier = pltpu.get_barrier_semaphore()
    for peer in peers:
        pl.semaphore_signal(barrier, inc=1, device_id=peer, device_id_type=pl.DeviceIdType.MESH)
    pl.semaphore_wait(barrier, len(peers))


def dp_peers(dp):
    me = lax.axis_index("dp")
    return [{"dp": me ^ (1 << b)} for b in range(dp.bit_length() - 1)]


def tensor_peer(mask):
    return {"tensor": lax.axis_index("tensor") ^ mask}


def preload(kernel, ins, which):
    def wrapped(*refs):
        extra = refs[len(refs) - len(which) - 1 :]
        refs = list(refs[: len(refs) - len(which) - 1])
        loads = {}
        for k, i in enumerate(which):
            loads[i] = pltpu.make_async_copy(refs[i], extra[k], extra[-1].at[k])
            loads[i].start()
            refs[i] = extra[k]

        def ready(*places):
            for i in places or tuple(loads):
                loads.pop(i).wait()

        kernel(ready, *refs)

    scratch = [pltpu.VMEM(ins[i].shape, ins[i].dtype) for i in which]
    return wrapped, scratch + [pltpu.SemaphoreType.DMA((len(which),))]


def halving(dp, order):
    masks = [1 << b for b in order]
    masks += [1 << b for b in range(len(order), dp.bit_length() - 1)]
    seq = [0]
    for m in reversed(masks):
        seq = [m ^ v for v in seq] + seq
    return masks, seq


def near_units(dp, units):
    return units // 4 if dp == 8 else units


def block_of(ref, dp, order, k):
    rows = ref.shape[1] // dp
    if rows % DH:
        return ref[:, k * rows : (k + 1) * rows]
    at = (lax.axis_index("dp") ^ halving(dp, order)[1][k]) * rows
    return ref[:, pl.ds(pl.multiple_of(at, rows), rows)]


def remote(src, dst, send_sem, recv_sem, peer):
    return pltpu.make_async_remote_copy(
        src_ref=src,
        dst_ref=dst,
        send_sem=send_sem,
        recv_sem=recv_sem,
        device_id=peer,
        device_id_type=pl.DeviceIdType.MESH,
    )


def spread(dp, blocks_ref, send_sem, recv_sem, compute, then=None):
    me = lax.axis_index("dp")
    slot = {j: k for k, j in enumerate(spread_order(dp))}
    copies = {}

    def send(j, mask):
        to = j ^ mask
        k = slot[to]
        copies[to] = pltpu.make_async_remote_copy(
            src_ref=blocks_ref.at[slot[j]],
            dst_ref=blocks_ref.at[k],
            send_sem=send_sem.at[k],
            recv_sem=recv_sem.at[k],
            device_id={"dp": me ^ mask},
            device_id_type=pl.DeviceIdType.MESH,
        )
        copies[to].start()

    bits = [1 << b for b in range(1, dp.bit_length() - 1)]
    for m in bits:
        send(0, m)
    send(0, 1)
    compute()
    for m in bits:
        copies[m].wait_recv()
        if m == bits[-1]:
            near = [0, m]
            for n in reversed(bits[:-1]):
                for j in near[1:]:
                    send(j, n)
                near = near + [n] + [j ^ n for j in near[1:]]
                if n != bits[0]:
                    for j in near:
                        if j & n and j != n:
                            copies[j].wait_recv()
        send(m, 1)
    if then is not None:
        then()
    last = [j for j in near if j and j not in bits]
    for j in last:
        if j & bits[0] or len(bits) == 1:
            copies[j].wait_recv()
        send(j, 1)
    for j in near:
        copies[j ^ 1].wait_recv()
    for c in copies.values():
        c.wait_send()


W_CHUNKS = 4


def attention_kernel(
    dp, heads, segs, scale, ready, w_ref, g_ref, h_ref, wq_ref, wk_ref, wv_ref, wo_ref,
    q_ref, k_ref, v_ref, a16_ref, pair_ref, local_ref, mem_ref, zin_ref, all_ref,
    wf_ref, asend_ref, w_send, w_recv, a_send, a_recv, blocks_ref, send_sem, recv_sem,
):
    pairs = segs * heads
    flat = heads * DH
    half = segs * SEG // 2
    core, far = tensor_peer(1), tensor_peer(2)
    greet(*dp_peers(dp), core, far)

    size = flat // W_CHUNKS
    w_copies = {}

    def w_send_chunk(j, c, to, peer):
        rows = pl.ds(c * size, size)
        k = (to - 1) * W_CHUNKS + c
        w_copies[to, c] = remote(
            wf_ref.at[j, rows, :], wf_ref.at[to, rows, :], w_send.at[k], w_recv.at[k], peer
        )
        w_copies[to, c].start()

    def w_done(to, c):
        rows = slice(c * size, (c + 1) * size)
        w_copies[to, c].wait_recv()
        all_ref[to * flat + c * size : to * flat + (c + 1) * size, :] = wf_ref[to, rows, :].astype(
            BF16
        )

    ready(6)
    for c in range(W_CHUNKS):
        rows = slice(c * size, (c + 1) * size)
        wf_ref[0, rows, :] = wo_ref[rows, :].astype(F32)
        w_send_chunk(0, c, 2, far)
        w_send_chunk(0, c, 1, core)
    all_ref[:flat, :] = wo_ref[...]

    def project(matrix_ref, out_ref):
        @pl.loop(0, segs * SEG // 256)
        def _(i):
            rows = pl.ds(pl.multiple_of(i * 256, 256), 256)
            out_ref[rows, :] = dot(h_ref[rows, :], matrix_ref[...]).astype(BF16)

    ready()
    project(wk_ref, k_ref)
    project(wv_ref, v_ref)

    @pl.loop(0, pairs)
    def _(p):
        at = head_part(heads, p)
        sk = feature_map(k_ref[at].astype(F32))
        blocks_ref[0, matrix_part(p), :] = dot_t(sk.astype(BF16), v_ref[at])
        blocks_ref[0, pl.ds(pairs * DH + p, 1), :] = jnp.sum(sk, axis=0, keepdims=True)

    def compute():
        project(wq_ref, q_ref)

        @pl.loop(0, pairs)
        def _(p):
            at = head_part(heads, p)
            probs = softmax_rows(q_ref[at], k_ref[at], scale)
            local_ref[at] = dot(probs.astype(BF16), v_ref[at])

    spread(dp, blocks_ref, send_sem, recv_sem, compute)

    @pl.loop(0, pairs)
    def _(p):
        at = head_part(heads, p)
        mem, zin = weighted(w_ref, p, heads, segs, blocks_ref)
        mem_ref[matrix_part(p), :] = mem
        zin_ref[pl.ds(p, 1), :] = zin
        g = g_ref[0, p % heads]
        sq = feature_map(q_ref[at].astype(F32))
        den = jnp.sum(sq * zin, axis=-1, keepdims=True) + 1.0
        retrieved = dot(sq.astype(BF16), mem.astype(BF16)) / den
        a16_ref[at] = (g * retrieved + (1.0 - g) * local_ref[at]).astype(BF16)

    asend_ref[...] = a16_ref[half:, :].astype(F32)
    a_copy = remote(asend_ref, pair_ref.at[:, pl.ds(flat, flat)], a_send, a_recv, core)
    a_copy.start()
    pair_ref[:, :flat] = a16_ref[:half, :].astype(F32)
    for c in range(W_CHUNKS):
        w_done(1, c)
    a_copy.wait_recv()
    for c in range(W_CHUNKS):
        w_copies[2, c].wait_recv()
        w_send_chunk(2, c, 3, core)
        rows = slice(c * size, (c + 1) * size)
        all_ref[2 * flat + c * size : 2 * flat + (c + 1) * size, :] = wf_ref[2, rows, :].astype(BF16)
    for c in range(W_CHUNKS):
        w_done(3, c)
    for copy in w_copies.values():
        copy.wait_send()
    a_copy.wait_send()


def attention_back_kernel(
    dp, heads, segs, scale, ready, w_ref, g_ref, q_ref, k_ref, v_ref, da_ref, local_ref, mem_ref,
    zin_ref, dr_ref, a16_ref, d_pre_ref, u_pre_ref, out_part_ref,
    dq_ref, dk_ref, dv_ref, gate_ref, o_pre_ref, d_rode_ref, u_rode_ref, out_far_ref,
    dqm_ref, dkl_ref, dvl_ref, os_ref, ride_send, ride_recv, blocks_ref, send_sem, recv_sem,
):
    pairs = segs * heads
    me = lax.axis_index("dp")
    far = tensor_peer(2)
    greet(*dp_peers(dp), far)
    legs = [
        (d_pre_ref, d_rode_ref, {"dp": me ^ 1}),
        (out_part_ref, out_far_ref, far),
        (os_ref, o_pre_ref, {"dp": me ^ 2}),
    ]
    quarter, units = d_rode_ref.shape
    eighth = quarter // 2
    legs[0] = (d_pre_ref.at[pl.ds(0, quarter), :], d_rode_ref, {"dp": me ^ 1})
    near = near_units(dp, units)
    cols = pl.ds(0, near)
    legs.append((u_pre_ref.at[pl.ds(0, quarter), cols], u_rode_ref.at[:, cols], {"dp": me ^ 2}))
    if near < units:
        cols = pl.ds(near, units - near)
        for k in range(2):
            legs.append(
                (
                    u_pre_ref.at[pl.ds(2 * k * eighth, eighth), cols],
                    u_rode_ref.at[pl.ds(k * eighth, eighth), cols],
                    {"dp": me ^ 4},
                )
            )
    riders = [
        remote(src, dst, ride_send.at[i], ride_recv.at[i], peer)
        for i, (src, dst, peer) in enumerate(legs)
    ]
    o_rider = riders[2]
    plain = riders[:2] + riders[3:]
    for r in riders[:2] + riders[3:4]:
        r.start()
    ready()

    @pl.loop(0, pairs)
    def _(p):
        at = head_part(heads, p)
        g = g_ref[0, p % heads]
        qf = q_ref[at].astype(F32)
        sq = feature_map(qf)
        sq16 = sq.astype(BF16)
        mem16 = mem_ref[matrix_part(p), :].astype(BF16)
        zin = zin_ref[pl.ds(p, 1), :]
        inv_den = 1.0 / (jnp.sum(sq * zin, axis=-1, keepdims=True) + 1.0)
        retrieved = dot(sq16, mem16) * inv_den
        da = da_ref[at].astype(F32)
        gate_ref[pl.ds(p, 1), :] = jnp.sum(da * (retrieved - local_ref[at]), axis=0, keepdims=True)
        dnum = g * da * inv_den
        dden = -jnp.sum(dnum * retrieved, axis=-1, keepdims=True)
        dnum16 = dnum.astype(BF16)
        blocks_ref[0, matrix_part(p), :] = dot_t(sq16, dnum16)
        blocks_ref[0, pl.ds(pairs * DH + p, 1), :] = jnp.sum(sq * dden, axis=0, keepdims=True)
        dsq = dot_nt(dnum16, mem16) + dden * zin
        dqm_ref[at] = dsq * feature_slope(qf)

    rows = dr_ref.shape[1] // dp
    half_blocks = dp // 2

    def compute():
        for j in range(half_blocks):
            os_ref[j * rows : (j + 1) * rows, :] = dot_t(
                block_of(dr_ref, dp, Z_FIRST, j), a16_ref[...]
            )

        @pl.loop(0, pairs)
        def _(p):
            at = head_part(heads, p)
            g = g_ref[0, p % heads]
            q, k, v, da = q_ref[at], k_ref[at], v_ref[at], da_ref[at]
            probs = softmax_rows(q, k, scale)
            dprobs = (1.0 - g) * dot_nt(da, v)
            inner = jnp.sum(dprobs * probs, axis=-1, keepdims=True)
            ds16 = (probs * (dprobs - inner)).astype(BF16)
            dq_ref[at] = (dot(ds16, k) * scale + dqm_ref[at]).astype(BF16)
            dkl_ref[at] = dot_t(ds16, q) * scale
            dvl_ref[at] = (1.0 - g) * dot_t(probs.astype(BF16), da)

    def then():
        o_rider.start()
        for r in riders[4:]:
            r.start()

    spread(dp, blocks_ref, send_sem, recv_sem, compute, then)

    @pl.loop(0, pairs)
    def _(p):
        at = head_part(heads, p)
        dd, dz = weighted(w_ref, p, heads, segs, blocks_ref)
        dd16 = dd.astype(BF16)
        kf = k_ref[at].astype(F32)
        dsk = dot_nt(v_ref[at], dd16) + dz
        dk_ref[at] = (dkl_ref[at] + dsk * feature_slope(kf)).astype(BF16)
        dv_ref[at] = (dvl_ref[at] + dot(feature_map(kf).astype(BF16), dd16)).astype(BF16)

    o_rider.wait()
    for j in range(half_blocks):
        o_pre_ref[j * rows : (j + 1) * rows, :] += dot_t(
            block_of(dr_ref, dp, Z_FIRST, half_blocks + j), a16_ref[...]
        )
    for r in plain:
        r.wait()


ROWS = 128


def tail_items(flat):
    full = slice(0, flat)
    return [
        (0, full), (1, full), (2, slice(0, flat // 2)), (2, slice(flat // 2, flat)), (3, full)
    ]


def tail_kernel(
    dp, turn, order, o_order, ready,
    h_ref, dq_ref, dk_ref, dv_ref, wq_ref, wk_ref, wv_ref, o_pre_ref, gain_ref, vec_ref,
    d3_ref, u3_ref, resid_hbm, out_part_hbm, out_far_hbm, dresid_hbm, x_hbm,
    gq_ref, gk_ref, gv_ref, go_ref, vec_out_ref, far_ref, d3_got_ref, u3_got_ref, out_hbm, dx_hbm,
    part_ref, cs_ref, cr_ref, in_ref, own_ref, other_ref, turn_ref, vec_got_ref,
    c_send, c_recv, y_send, y_recv, ride_send, ride_recv, e_send, e_recv, v_send, v_recv,
    in_sem, st_sem, turn_sem, free_sem, *bufs,
):
    me = lax.axis_index("dp")
    side = lax.axis_index("tensor") % 2
    core, far = tensor_peer(1), tensor_peer(2)
    greet(*dp_peers(dp), core, far)
    masks, _ = halving(dp, order)
    o_masks, _ = halving(dp, o_order)
    steps = len(masks)
    half, width = far_ref.shape
    rows = width // dp
    chunks = half // ROWS
    ht_ref = bufs[-1] if turn else h_ref
    depth = in_ref.shape[0]
    flat = dq_ref.shape[1]
    lhs = (dq_ref, dk_ref, dv_ref)
    outs = (gq_ref, gk_ref, gv_ref, go_ref)
    items = tail_items(flat)
    copies = {}

    def buffers(i, step):
        k = 2 * (i * steps + step)
        return bufs[k], bufs[k + 1]

    def term(i, step):
        lo = rows * sum(dp >> (n + 1) for n in range(step))
        count = rows * (dp >> (step + 1)) if step < steps else rows
        start = 0
        which, cols = items[i]
        if which < 3:
            value = dot(ht_ref[lo : lo + count, :], lhs[which][:, cols])
        else:
            base = rows * (dp // 2)
            value = o_pre_ref[lo - base : lo - base + count, :]
            start = 1
        for n in range(start, step):
            at = lo - rows * sum(dp >> (m + 1) for m in range(n + 1))
            value = value + buffers(i, n)[1][at : at + count, :]
        return value

    def advance(i, step):
        which, cols = items[i]
        if step > (1 if which == 3 else 0):
            copies[i, step - 1].wait_recv()
        if step == steps:
            outs[which][:, cols] = term(i, step)
            return
        send, recv = buffers(i, step)
        send[...] = term(i, step)
        mask = (o_masks if which == 3 else masks)[step]
        k = i * steps + step
        copies[i, step] = remote(send, recv, e_send.at[k], e_recv.at[k], {"dp": me ^ mask})
        copies[i, step].start()

    third = {"dp": me ^ masks[2]}
    units = u3_ref.shape[1]
    near = near_units(dp, units)
    cols = pl.ds(0, near)
    legs = [(d3_ref, d3_got_ref, third), (u3_ref.at[:, cols], u3_got_ref.at[:, cols], third)]
    if near < units:
        cols = pl.ds(near, units - near)
        legs.append((u3_ref.at[:, cols], u3_got_ref.at[:, cols], {"dp": me ^ 2}))
    riders = [
        remote(src, dst, ride_send.at[i], ride_recv.at[i], peer)
        for i, (src, dst, peer) in enumerate(legs)
    ]
    out_item = len(items) - 1
    ready(7)
    advance(out_item, 1)
    for r in riders:
        r.start()

    def block_load(j):
        at = (me ^ halving(dp, order)[1][j]) * rows
        return pltpu.make_async_copy(
            h_ref.at[:, pl.ds(pl.multiple_of(at, rows), rows)],
            turn_ref.at[j % 2],
            turn_sem.at[j % 2],
        )

    def turn_blocks(lo, hi):
        for j in range(lo, hi if turn else lo):
            block_load(j).wait()
            ht_ref[j * rows : (j + 1) * rows, :] = turn_ref[j % 2].T
            if j + 2 < dp:
                block_load(j + 2).start()

    for j in range(2 if turn else 0):
        block_load(j).start()
    ready()
    turn_blocks(0, dp // 2)
    for i in range(out_item):
        advance(i, 0)

    def part_rows(c):
        return pl.ds(c * ROWS, ROWS)

    def core_wire(c):
        return remote(cs_ref.at[c], cr_ref.at[c], c_send.at[c], c_recv.at[c], core)

    def core_free():
        pl.semaphore_signal(free_sem, inc=1, device_id=core, device_id_type=pl.DeviceIdType.MESH)

    def far_wire(c):
        return remote(part_ref.at[c], far_ref.at[part_rows(c), :], y_send.at[c], y_recv.at[c], far)

    def back(lo):
        return sum(
            dot_nt(v[lo : lo + 2 * ROWS, :], w[...])
            for v, w in zip(lhs, (wq_ref, wk_ref, wv_ref))
        )

    for c in range(0, chunks, 2):
        value = back(half + c * ROWS)
        for k in range(2):
            cs_ref[c + k] = value[k * ROWS : (k + 1) * ROWS, :]
            core_wire(c + k).start()
    for c in range(0, chunks, 2):
        value = back(c * ROWS)
        for k in range(2):
            core_wire(c + k).wait()
            part_ref[c + k] = value[k * ROWS : (k + 1) * ROWS, :] + cr_ref[c + k]
            far_wire(c + k).start()
    core_free()

    def both_cores(sources, compute, dst_hbm):
        def loads(c):
            k = c % depth
            return [
                pltpu.make_async_copy(src.at[part_rows(c), :], in_ref.at[k, i], in_sem.at[k, i])
                for i, src in enumerate(sources)
            ]

        def begin(c):
            if c < chunks:
                for load in loads(c):
                    load.start()

        def store(src_ref, which, c, k):
            at = pl.ds(pl.multiple_of(which * half + c * ROWS, ROWS), ROWS)
            return pltpu.make_async_copy(src_ref, dst_hbm.at[at, :], st_sem.at[k])

        pl.semaphore_wait(free_sem, 1)
        for c in range(depth):
            begin(c)
        for c in range(chunks):
            for load in loads(c):
                load.wait()
            value = compute(c, *(in_ref[c % depth, i] for i in range(3))).astype(BF16)
            if c:
                store(own_ref, side, c - 1, 0).wait()
            own_ref[...] = value
            store(own_ref, side, c, 0).start()
            cs_ref[c] = value.astype(F32)
            core_wire(c).start()
            begin(c + depth)
        for c in range(chunks):
            core_wire(c).wait()
            if c:
                store(other_ref, 1 - side, c - 1, 1).wait()
            other_ref[...] = cr_ref[c].astype(BF16)
            store(other_ref, 1 - side, c, 1).start()
        store(own_ref, side, chunks - 1, 0).wait()
        store(other_ref, 1 - side, chunks - 1, 1).wait()

    def output_rows(c, a, b, d):
        return a + b + d

    def input_rows(c, there, dresid, x):
        grad = part_ref[c] + there
        inv = lax.rsqrt(jnp.mean(x * x, axis=-1, keepdims=True) + EPS)
        gs = grad * gain_ref[...]
        inner = jnp.mean(gs * x, axis=-1, keepdims=True)
        vec_out_ref[0:1, :] += jnp.sum(grad * x * inv, axis=0, keepdims=True)
        return dresid + inv * gs - x * inv * inv * inv * inner

    turn_blocks(dp // 2, dp)
    if steps == 3:
        advance(out_item, 2)
    both_cores((resid_hbm, out_part_hbm, out_far_hbm), output_rows, out_hbm)
    core_free()
    if steps == 3:
        for i, step in ((0, 1), (1, 1), (0, 2), (2, 1), (1, 2)):
            advance(i, step)
        rest = ((3, 1), (2, 2), (3, 2))
    else:
        for step in range(1, steps):
            for i in range(len(items)):
                if step > 1 or i < out_item:
                    advance(i, step)
        rest = ()
    last = [(i, steps) for i in (out_item,) + tuple(range(out_item))]

    for c in range(chunks):
        far_wire(c).wait()
    vec_out_ref[...] = vec_ref[...]
    both_cores((far_ref, dresid_hbm, x_hbm), input_rows, dx_hbm)
    for i, step in rest:
        advance(i, step)

    for k, peer in enumerate([core] + dp_peers(dp)):
        hop = remote(vec_out_ref, vec_got_ref.at[k], v_send.at[k], v_recv.at[k], peer)
        hop.start()
        hop.wait()
        got = vec_got_ref[k]
        if k == 0:
            got = jnp.where(lax.broadcasted_iota(jnp.int32, got.shape, 0) < 2, got, 0.0)
        vec_out_ref[...] += got
    for i, step in last:
        advance(i, step)
    for c in copies.values():
        c.wait_send()
    for r in riders:
        r.wait()


def tail(ident, dp, h1, h1_t, grads, weights, o_pre, gain, vec, d3, u3, streams):
    tokens, width = h1.shape
    turn = h1_t is None
    flat = grads[0].shape[1]
    half = tokens // 2
    rows = width // dp
    steps = dp.bit_length() - 1
    full = pl.BlockSpec(memory_space=pltpu.VMEM)
    anywhere = pl.BlockSpec(memory_space=pl.ANY)
    f32 = lambda *shape: jax.ShapeDtypeStruct(shape, F32)
    dma = pltpu.SemaphoreType.DMA
    bufs = []
    items = tail_items(flat)
    for which, cols in items:
        for step in range(steps):
            count = rows * (dp >> (step + 1)) if which < 3 or step else 8
            bufs += [pltpu.VMEM((count, cols.stop - cols.start), F32)] * 2
    chunks = half // ROWS
    b16 = jax.ShapeDtypeStruct((tokens, width), BF16)
    operands = (
        h1 if turn else h1_t, *grads, *weights, o_pre, gain[None, :], vec, d3, u3, *streams
    )
    kernel, held = preload(
        functools.partial(tail_kernel, dp, turn, X_FIRST, Z_FIRST),
        operands,
        range(1 if turn else 0, 10),
    )
    return pl.pallas_call(
        kernel,
        out_shape=[f32(rows, flat)] * 4
        + [f32(*vec.shape), f32(half, width), f32(*d3.shape), f32(*u3.shape), b16, b16],
        in_specs=[anywhere] * len(operands),
        out_specs=[full] * 5 + [anywhere] * 5,
        scratch_shapes=[
            pltpu.VMEM((chunks, ROWS, width), F32),
            pltpu.VMEM((chunks, ROWS, width), F32),
            pltpu.VMEM((chunks, ROWS, width), F32),
            pltpu.VMEM((2 if turn else 1, 3, ROWS, width), F32),
            pltpu.VMEM((ROWS, width), BF16),
            pltpu.VMEM((ROWS, width), BF16),
            pltpu.VMEM((2, tokens, rows) if turn else (8, DH), BF16),
            pltpu.VMEM((steps + 1,) + vec.shape, F32),
            dma((chunks,)), dma((chunks,)), dma((chunks,)), dma((chunks,)),
            dma((3,)), dma((3,)), dma((len(items) * steps,)), dma((len(items) * steps,)),
            dma((steps + 1,)), dma((steps + 1,)), dma((2, 3)), dma((2,)), dma((2,)),
            pltpu.SemaphoreType.REGULAR,
        ]
        + bufs
        + ([pltpu.VMEM((width, tokens), BF16)] if turn else [])
        + held,
        compiler_params=pltpu.CompilerParams(
            collective_id=ident, has_side_effects=True, vmem_limit_bytes=63 << 20
        ),
        cost_estimate=pl.CostEstimate(
            flops=12 * tokens * width * flat, transcendentals=0, bytes_accessed=96 << 20
        ),
    )(*operands)


def core_gather_kernel(norm, tiles, v_ref, gain_ref, out_ref, send_ref, recv_ref, send_sem, recv_sem):
    peer = tensor_peer(1)
    greet(peer)
    half = v_ref.shape[0]
    size = half // tiles
    copies = []
    for c in range(tiles):
        rows = slice(c * size, (c + 1) * size)
        v = v_ref[rows, :]
        if norm:
            inv = lax.rsqrt(jnp.mean(v * v, axis=-1, keepdims=True) + EPS)
            v = v * inv * gain_ref[...]
            send_ref[rows, :] = v
        out_ref[rows, :] = v.astype(BF16)
        src = send_ref if norm else v_ref
        copies.append(
            remote(
                src.at[rows, :], recv_ref.at[rows, :], send_sem.at[c], recv_sem.at[c], peer
            )
        )
        copies[-1].start()
    for c in range(tiles):
        rows = slice(c * size, (c + 1) * size)
        copies[c].wait_recv()
        out_ref[half + c * size : half + (c + 1) * size, :] = recv_ref[rows, :].astype(BF16)
    for c in copies:
        c.wait_send()


def core_gather(ident, v, gain=None):
    half, n = v.shape
    tiles = 4
    out = jax.ShapeDtypeStruct((2 * half, n), BF16)
    full = pl.BlockSpec(memory_space=pltpu.VMEM)
    norm = gain is not None
    return pl.pallas_call(
        functools.partial(core_gather_kernel, norm, tiles),
        out_shape=out,
        in_specs=[full, full],
        out_specs=full,
        scratch_shapes=[
            pltpu.VMEM((half, n) if norm else (8, DH), F32),
            pltpu.VMEM((half, n), F32),
            pltpu.SemaphoreType.DMA((tiles,)),
            pltpu.SemaphoreType.DMA((tiles,)),
        ],
        compiler_params=pltpu.CompilerParams(
            collective_id=ident, has_side_effects=True, vmem_limit_bytes=48 << 20
        ),
        cost_estimate=pl.CostEstimate(
            flops=0, transcendentals=0, bytes_accessed=nbytes(v, v, v, out)
        ),
    )(v, gain[None, :] if norm else jnp.zeros((8, DH), F32))


def norm_back_kernel(
    part_hbm, far_hbm, resid_hbm, grad_hbm, gain_ref, dresid_hbm, dr_ref, sum_ref,
    in_ref, og_ref, send_ref, recv_ref, c_send, c_recv, in_sem, og_sem, out_sem,
):
    peer = tensor_peer(1)
    greet(peer)
    half, width = dresid_hbm.shape
    chunks = half // ROWS
    sources = (part_hbm, far_hbm, resid_hbm)

    def rows(c):
        return pl.ds(c * ROWS, ROWS)

    def loads(c):
        k = c % 2
        wide = [
            pltpu.make_async_copy(src.at[rows(c), :], in_ref.at[k, i], in_sem.at[k, i])
            for i, src in enumerate(sources)
        ]
        return wide + [
            pltpu.make_async_copy(grad_hbm.at[rows(c), :], og_ref.at[k], og_sem.at[k])
        ]

    def wire(c):
        return remote(send_ref.at[c], recv_ref.at[c], c_send.at[c], c_recv.at[c], peer)

    def store(c):
        return pltpu.make_async_copy(send_ref.at[c], dresid_hbm.at[rows(c), :], out_sem.at[c])

    for c in range(2):
        for load in loads(c):
            load.start()
    sum_ref[...] = jnp.zeros_like(sum_ref)
    for c in range(chunks):
        k = c % 2
        for load in loads(c):
            load.wait()
        grad = in_ref[k, 0] + in_ref[k, 1]
        x = in_ref[k, 2]
        inv = lax.rsqrt(jnp.mean(x * x, axis=-1, keepdims=True) + EPS)
        gs = grad * gain_ref[...]
        inner = jnp.mean(gs * x, axis=-1, keepdims=True)
        sum_ref[0:1, :] += jnp.sum(grad * x * inv, axis=0, keepdims=True)
        value = og_ref[k].astype(F32) + inv * gs - x * inv * inv * inv * inner
        send_ref[c] = value
        wire(c).start()
        store(c).start()
        dr_ref[c * ROWS : (c + 1) * ROWS, :] = value.astype(BF16)
        if c + 2 < chunks:
            for load in loads(c + 2):
                load.start()
    for c in range(chunks):
        wire(c).wait()
        dr_ref[half + c * ROWS : half + (c + 1) * ROWS, :] = recv_ref[c].astype(BF16)
    for c in range(chunks):
        store(c).wait()


def norm_back(ident, part, far, resid, out_grad, gain):
    half, width = resid.shape
    chunks = half // ROWS
    outs = [
        jax.ShapeDtypeStruct((half, width), F32),
        jax.ShapeDtypeStruct((2 * half, width), BF16),
        jax.ShapeDtypeStruct((8, width), F32),
    ]
    full = pl.BlockSpec(memory_space=pltpu.VMEM)
    anywhere = pl.BlockSpec(memory_space=pl.ANY)
    dma = pltpu.SemaphoreType.DMA
    return pl.pallas_call(
        norm_back_kernel,
        out_shape=outs,
        in_specs=[anywhere] * 4 + [full],
        out_specs=[anywhere, full, full],
        scratch_shapes=[
            pltpu.VMEM((2, 3, ROWS, width), F32),
            pltpu.VMEM((2, ROWS, width), BF16),
            pltpu.VMEM((chunks, ROWS, width), F32),
            pltpu.VMEM((chunks, ROWS, width), F32),
            dma((chunks,)), dma((chunks,)), dma((2, 3)), dma((2,)), dma((chunks,)),
        ],
        compiler_params=pltpu.CompilerParams(
            collective_id=ident, has_side_effects=True, vmem_limit_bytes=48 << 20
        ),
        cost_estimate=pl.CostEstimate(
            flops=0, transcendentals=0, bytes_accessed=nbytes(part, far, resid, out_grad, *outs)
        ),
    )(part, far, resid, out_grad, gain[None, :])


TILE = 256
SLOTS = 4


def feed_kernel(
    dp, turn, ready, h_ref, ogt_ref, ht_ref, wup_hbm, wdn_hbm, ug_hbm,
    act_ref, dpre_ref, part_ref, part2_ref, far_ref, d_ref, u_ref, d_pre_ref, u_pre_ref,
    w_ref, ug_ref, ds_ref, us_ref, cs_ref, cr_ref,
    w_sem, ug_sem, d_send, d_recv, u_send, u_recv, c_send, c_recv, y_send, y_recv, free_sem,
):
    tokens, units = act_ref.shape
    half = tokens // 2
    width = h_ref.shape[1]
    cut = width // 2
    rows = width // dp
    me = lax.axis_index("dp")
    core, far = tensor_peer(1), tensor_peer(2)
    x_peer, z_peer = {"dp": me ^ 1}, {"dp": me ^ 2}
    greet(core, far, x_peer, z_peer)
    count = units // TILE

    load_w = pltpu.make_async_copy(wup_hbm, w_ref, w_sem)
    load_w.start()

    def tile_cols(t):
        return pl.ds(pl.multiple_of(t * TILE, TILE), TILE)

    def load_ug(t, k):
        return pltpu.make_async_copy(ug_hbm.at[:, tile_cols(t)], ug_ref.at[k], ug_sem.at[k])

    load_ug(0, 0).start()
    load_ug(1, 1).start()
    ready(0)
    for j in range(dp // 2 if turn else 0):
        ht_ref[j * rows : (j + 1) * rows, :] = block_of(h_ref, dp, X_FIRST, j).T
    ready()
    load_w.wait()

    def wire(t, k):
        cols = tile_cols(t)
        d = remote(ds_ref.at[k], d_ref.at[:, cols], d_send.at[t], d_recv.at[t], z_peer)
        u = remote(us_ref.at[k], u_ref.at[:, cols], u_send.at[t], u_recv.at[t], x_peer)
        return d, u

    def terms(t, k):
        cols = tile_cols(t)
        d, u = wire(t, k)
        ds_ref[k] = dot(ogt_ref[:cut, :], act_ref[:, cols])
        d.start()
        us_ref[k] = dot(ht_ref[:cut, :], dpre_ref[:, cols])
        u.start()

    @pl.loop(0, count)
    def _(t):
        k = t % 2
        cols = tile_cols(t)
        load_ug(t, k).wait()
        pre = dot(h_ref[...], w_ref[:, cols])
        c = 0.7978845608028654
        sq = pre * pre
        th = jnp.tanh(c * pre * (1.0 + 0.044715 * sq))
        mid = 0.5 * (1.0 + th)
        act_ref[:, cols] = (pre * mid).astype(BF16)
        slope = mid + 0.5 * pre * (1.0 - th * th) * (c * (1.0 + 0.134145 * sq))
        dpre_ref[:, cols] = (ug_ref[k] * slope).astype(BF16)

        @pl.when(t + 2 < count)
        def _():
            load_ug(t + 2, k).start()

        @pl.when(t < SLOTS)
        def _():
            terms(t, t)

    part_cols = width // 4

    def core_wire(c):
        return remote(cs_ref.at[c], cr_ref.at[c], c_send.at[c], c_recv.at[c], core)

    def far_wire(c):
        cols = pl.ds(c * part_cols, part_cols)
        return remote(part_ref.at[:, cols], far_ref.at[:, cols], y_send.at[c], y_recv.at[c], far)

    def summed(lhs_ref, transposed, out_ref, travels):
        def term(row, c):
            cols = slice(c * part_cols, (c + 1) * part_cols)
            lhs = lhs_ref[row * half : (row + 1) * half, :]
            if transposed:
                return dot_nt(lhs, w_ref[cols, :])
            return dot(lhs, w_ref[:, cols])

        for c in range(4):
            cs_ref[c] = term(1, c)
            core_wire(c).start()
        for c in range(4):
            part = term(0, c)
            core_wire(c).wait()
            out_ref[:, c * part_cols : (c + 1) * part_cols] = part + cr_ref[c]
            if travels:
                far_wire(c).start()

    summed(dpre_ref, True, part_ref, True)
    load_down = pltpu.make_async_copy(wdn_hbm, w_ref, w_sem)
    load_down.start()
    pl.semaphore_signal(free_sem, inc=1, device_id=core, device_id_type=pl.DeviceIdType.MESH)
    for j in range(dp // 2, dp if turn else 0):
        ht_ref[j * rows : (j + 1) * rows, :] = block_of(h_ref, dp, X_FIRST, j).T

    @pl.loop(SLOTS, count)
    def _(t):
        d, u = wire(t - SLOTS, t - SLOTS)
        d.wait_send()
        u.wait_send()
        terms(t, t - SLOTS)

    load_down.wait()
    pl.semaphore_wait(free_sem, 1)
    summed(act_ref, False, part2_ref, False)

    def load_got(src_ref, t, k):
        return pltpu.make_async_copy(src_ref.at[:, tile_cols(t)], ug_ref.at[k], ug_sem.at[k])

    def store_pre(dst_ref, t, k):
        return pltpu.make_async_copy(ug_ref.at[k], dst_ref.at[:, tile_cols(t)], ug_sem.at[k])

    @pl.loop(0, count)
    def _(t):
        d, u = wire(t, 0)

        @pl.when(t > 0)
        def _():
            store_pre(d_pre_ref, t - 1, 0).wait()
            store_pre(u_pre_ref, t - 1, 1).wait()

        d.wait_recv()
        load_got(d_ref, t, 0).start()
        u.wait_recv()
        load_got(u_ref, t, 1).start()
        load_got(d_ref, t, 0).wait()
        ug_ref[0] += dot(ogt_ref[cut:, :], act_ref[:, tile_cols(t)])
        store_pre(d_pre_ref, t, 0).start()
        load_got(u_ref, t, 1).wait()
        ug_ref[1] += dot(ht_ref[cut:, :], dpre_ref[:, tile_cols(t)])
        store_pre(u_pre_ref, t, 1).start()

    store_pre(d_pre_ref, count - 1, 0).wait()
    store_pre(u_pre_ref, count - 1, 1).wait()

    @pl.loop(count - SLOTS, count)
    def _(t):
        d, u = wire(t, t - (count - SLOTS))
        d.wait_send()
        u.wait_send()

    for c in range(4):
        far_wire(c).wait()


def feed(ident, dp, h2, og_t, h_t, w_up, w_down, up_grad):
    tokens, width = h2.shape
    units = w_up.shape[1]
    half = tokens // 2
    cut = width // 2
    count = units // TILE
    full = pl.BlockSpec(memory_space=pltpu.VMEM)
    anywhere = pl.BlockSpec(memory_space=pl.ANY)
    f32 = lambda *shape: jax.ShapeDtypeStruct(shape, F32)
    b16 = jax.ShapeDtypeStruct((tokens, units), BF16)
    dma = pltpu.SemaphoreType.DMA
    turn = h_t is None
    kernel = functools.partial(feed_kernel, dp, turn)
    if turn:

        def kernel(ready, h_ref, ogt_ref, *refs):
            feed_kernel(dp, turn, ready, h_ref, ogt_ref, refs[-1], *refs[:-1])

    operands = (h2, og_t, *([] if turn else [h_t]), w_up, w_down, up_grad)
    kernel, held = preload(kernel, operands, range(len(operands) - 3))
    return pl.pallas_call(
        kernel,
        out_shape=[b16, b16, f32(half, width), f32(half, width), f32(half, width)]
        + [f32(cut, units)] * 4,
        in_specs=[anywhere] * len(operands),
        out_specs=[full] * 4 + [anywhere] * 5,
        scratch_shapes=[
            pltpu.VMEM((width, units), BF16),
            pltpu.VMEM((2, tokens, TILE), F32),
            pltpu.VMEM((SLOTS, cut, TILE), F32),
            pltpu.VMEM((SLOTS, cut, TILE), F32),
            pltpu.VMEM((4, half, width // 4), F32),
            pltpu.VMEM((4, half, width // 4), F32),
            dma, dma((2,)), dma((count,)), dma((count,)), dma((count,)), dma((count,)),
            dma((4,)), dma((4,)), dma((4,)), dma((4,)), pltpu.SemaphoreType.REGULAR,
        ]
        + ([pltpu.VMEM((width, tokens), BF16)] if turn else [])
        + held,
        compiler_params=pltpu.CompilerParams(
            collective_id=ident, has_side_effects=True, vmem_limit_bytes=62 << 20
        ),
        cost_estimate=pl.CostEstimate(
            flops=10 * tokens * width * units, transcendentals=tokens * units,
            bytes_accessed=64 << 20,
        ),
    )(*operands)


def body(
    inputs,
    gain_attn,
    w_query,
    w_key,
    w_value,
    gate_logit,
    w_out,
    gain_mlp,
    w_up,
    w_down,
    seg_parent,
    out_grad,
):
    tokens, width = inputs.shape
    half = tokens // 2
    segs = tokens // SEG
    heads = w_query.shape[1] // DH
    pairs = segs * heads
    units = w_up.shape[1]
    flat = heads * DH
    scale = DH ** (-0.5)
    dp = lax.axis_size("dp")
    tn = lax.axis_size("tensor")
    rows = width // dp
    di = lax.axis_index("dp")
    core = lax.axis_index("tensor") % 2

    one = jnp.where(seg_parent[0] < tokens * dp, 1.0, 2.0)

    def low_after_wire(v):
        return (v * one).astype(BF16)

    def swap_core(v):
        return lax.ppermute(v, "tensor", [(i, i ^ 1) for i in range(tn)])

    def swap_y(v):
        return lax.ppermute(v, "tensor", [(i, i ^ 2) for i in range(tn)])

    def swap_dp(v, mask):
        return lax.ppermute(v, "dp", [(i, i ^ mask) for i in range(dp)])

    def columns(v, order):
        _, seq = halving(dp, order)
        return block_columns(v, [di ^ k for k in seq], rows)

    def blocks_for(v, order):
        return columns(v, order) if rows % DH else v

    cut = width // 2
    quarter = cut // 2

    def pick(v, index, axis):
        size = v.shape[axis] // 2
        return lax.dynamic_slice_in_dim(v, index * size, size, axis)

    def place(own, other, index, axis):
        return jnp.where(
            index == 0,
            jnp.concatenate([own, other], axis),
            jnp.concatenate([other, own], axis),
        )

    def inv_rms(v):
        return lax.rsqrt(jnp.mean(v * v, axis=-1, keepdims=True) + EPS)

    x_own = pick(inputs, core, 0).astype(F32)
    x_oth = pick(inputs, 1 - core, 0).astype(F32)
    inv_own = inv_rms(x_own)
    inv_oth = inv_rms(x_oth)
    h1 = jnp.concatenate(
        [
            (x_own * inv_own * gain_attn).astype(BF16),
            (x_oth * inv_oth * gain_attn).astype(BF16),
        ],
        0,
    )

    sub = segs // 2
    every = jnp.arange(seg_parent.shape[0], dtype=jnp.int32)
    sub_ids = jnp.arange(sub, dtype=jnp.int32)
    seg_local = jnp.concatenate([core * sub + sub_ids, (1 - core) * sub + sub_ids])
    order = spread_order(dp)
    ids = jnp.concatenate([(di ^ j) * segs + seg_local for j in order])
    mine_hot = (ids[:segs, None] == every[None, :]).astype(F32)
    ids_hot = (ids[:, None] == every[None, :]).astype(F32)
    lineage = ancestor_table(seg_parent)

    def weights_of(table):
        mine_rows = jnp.sum(mine_hot[:, :, None] * table[None], axis=1)
        return jnp.sum(mine_rows[:, None, :] * ids_hot[None], axis=-1)

    up_weight = weights_of(lineage)
    down_weight = weights_of(lineage.T)

    gate = jax.nn.sigmoid(gate_logit)
    gate_row = gate[None, :]

    og_own = pick(out_grad, core, 0)
    og = jnp.concatenate([og_own, pick(out_grad, 1 - core, 0)], 0)
    block_rows = pairs * DH + pairs
    act_f32 = jax.ShapeDtypeStruct((tokens, flat), F32)
    act_b16 = jax.ShapeDtypeStruct((tokens, flat), BF16)
    mem_shape = jax.ShapeDtypeStruct((pairs * DH, DH), F32)
    zin_shape = jax.ShapeDtypeStruct((pairs, DH), F32)
    full = pl.BlockSpec(memory_space=pltpu.VMEM)

    anywhere = pl.BlockSpec(memory_space=pl.ANY)

    def attention_call(kernel, ident, outs, out_specs, scratch, args, in_specs, flops):
        which = [i for i, spec in enumerate(in_specs) if spec is full]
        in_specs = [anywhere if spec is full else spec for spec in in_specs]
        wrapped, held = preload(functools.partial(kernel, dp, heads, segs, scale), args, which)
        return pl.pallas_call(
            wrapped,
            out_shape=outs,
            in_specs=in_specs,
            out_specs=out_specs,
            scratch_shapes=scratch
            + [
                pltpu.VMEM((dp, block_rows, DH), F32),
                pltpu.SemaphoreType.DMA((dp,)),
                pltpu.SemaphoreType.DMA((dp,)),
            ]
            + held,
            compiler_params=pltpu.CompilerParams(
                collective_id=ident, has_side_effects=True, vmem_limit_bytes=63 << 20
            ),
            cost_estimate=pl.CostEstimate(
                flops=flops, transcendentals=0, bytes_accessed=64 << 20
            ),
        )(*args)

    head_flops = 2 * segs * heads * SEG * SEG * DH
    dma = pltpu.SemaphoreType.DMA
    qh, kh, vh, a16, a_pair, local, memory, zin, w_out_all = attention_call(
        attention_kernel,
        0,
        [
            act_b16, act_b16, act_b16, act_b16,
            jax.ShapeDtypeStruct((half, 2 * flat), F32),
            act_f32, mem_shape, zin_shape,
            jax.ShapeDtypeStruct((4 * flat, width), BF16),
        ],
        [full] * 9,
        [
            pltpu.VMEM((4, flat, width), F32),
            pltpu.VMEM((half, flat), F32),
            dma((3 * W_CHUNKS,)), dma((3 * W_CHUNKS,)), dma, dma,
        ],
        (up_weight, gate_row, h1, w_query, w_key, w_value, w_out),
        [SMEM, SMEM] + [full] * 5,
        3 * head_flops + 6 * tokens * width * flat,
    )
    up_grad = dot_nt(og, after(w_down, a_pair))

    step = half // AG_CHUNKS
    a_near = [a_pair[c * step : (c + 1) * step] for c in range(AG_CHUNKS)]
    a_far = [swap_y(v) for v in a_near]
    near = [
        x_own[c * step : (c + 1) * step] + dot(v.astype(BF16), w_out_all[: 2 * flat])
        for c, v in enumerate(a_near)
    ]
    og_t = columns(after(og, up_grad), Z_FIRST).T
    resids = [
        n + dot(low_after_wire(after(f, og_t, *near)), w_out_all[2 * flat :])
        for n, f in zip(near, a_far)
    ]
    resid = jnp.concatenate(resids, 0)
    h2 = core_gather(1, resid, gain_mlp)

    h_t = columns(h2, X_FIRST).T if rows % DH else None
    act, dpre, dh2_part, out_part, dh2_far, _, _, d_pre, u_pre = feed(
        2, dp, h2, og_t, h_t, w_up, w_down, up_grad
    )

    dresid, dr, gain_mlp_sum = norm_back(4, dh2_part, dh2_far, resid, og_own, gain_mlp)
    gain_mlp_part = gain_mlp_sum[0]

    da = dot_nt(dr, w_out).astype(BF16)
    anywhere = pl.BlockSpec(memory_space=pl.ANY)
    ride = jax.ShapeDtypeStruct((quarter, units), F32)
    o_shape = jax.ShapeDtypeStruct((cut, flat), F32)
    dq16, dk16, dv16, gate_rows, o_pre, d_rode, u_rode, out_far = attention_call(
        attention_back_kernel,
        5,
        [
            act_b16, act_b16, act_b16, zin_shape, o_shape, ride, ride,
            jax.ShapeDtypeStruct((half, width), F32),
        ],
        [full] * 5 + [anywhere] * 3,
        [pltpu.VMEM((tokens, flat), F32)] * 3
        + [pltpu.VMEM((cut, flat), F32)]
        + [dma((6,)), dma((6,))],
        (
            down_weight, gate_row, qh, kh, vh, da, local, memory, zin,
            blocks_for(dr, Z_FIRST), a16, d_pre, u_pre, out_part,
        ),
        [SMEM, SMEM] + [full] * 9 + [anywhere] * 3,
        9 * head_flops,
    )
    gate_part = jnp.sum(gate_rows.reshape(segs, heads, DH), axis=(0, 2)) * gate * (1.0 - gate)

    eighth = quarter // 2
    d3 = d_pre[quarter : quarter + eighth] + d_rode[:eighth]
    close = near_units(dp, units)
    u3 = u_rode[:eighth] + jnp.where(
        jnp.arange(units)[None, :] < close, u_pre[quarter : quarter + eighth], u_pre[eighth:quarter]
    )
    h1_t = columns(h1, X_FIRST).T if rows % DH else None
    lane = jnp.pad(gate_part, (0, width - heads))
    vec = jnp.zeros((8, width), F32).at[1].set(gain_mlp_part).at[2].set(lane)
    (
        w_query_grad, w_key_grad, w_value_grad, w_out_rows, vec, _, d3, u3, outputs, input_grad
    ) = tail(
        7, dp, h1, h1_t, (dq16, dk16, dv16), (w_query, w_key, w_value), o_pre, gain_attn, vec,
        d3, u3, (resid, out_part, out_far, dresid, x_own),
    )
    w_out_grad = w_out_rows.T

    def finish(pre, rode, got, order):
        masks, _ = halving(dp, order)
        value = pre[quarter + eighth :] + rode[eighth:] + got
        for m in masks[3:]:
            n = value.shape[0] // 2
            value = value[n:] + swap_dp(value[:n], m)
        return value

    w_down_grad = finish(d_pre, d_rode, d3, Z_FIRST).T
    w_up_grad = finish(u_pre, u_rode, u3, X_FIRST)

    gain_attn_grad = lax.dynamic_slice_in_dim(vec[0], di * rows, rows, 0)
    gain_mlp_grad = lax.dynamic_slice_in_dim(vec[1], di * rows, rows, 0)
    gate_grad = vec[2, :heads]

    return (
        outputs,
        input_grad,
        gain_attn_grad,
        w_query_grad,
        w_key_grad,
        w_value_grad,
        gate_grad,
        w_out_grad,
        gain_mlp_grad,
        w_up_grad,
        w_down_grad,
    )


def solution(mesh):
    placed = (
        P("dp", None),
        P(),
        P(None, "tensor"),
        P(None, "tensor"),
        P(None, "tensor"),
        P("tensor"),
        P("tensor", None),
        P(),
        P(None, "tensor"),
        P("tensor", None),
        P(),
        P("dp", None),
    )
    return jax.shard_map(
        body,
        mesh=mesh,
        in_specs=placed,
        out_specs=(
            P("dp", None),
            P("dp", None),
            P("dp"),
            P("dp", "tensor"),
            P("dp", "tensor"),
            P("dp", "tensor"),
            P("tensor"),
            P("tensor", "dp"),
            P("dp"),
            P("dp", "tensor"),
            P("tensor", "dp"),
        ),
        check_vma=False,
    )
```

```python
import functools

import jax
import jax.numpy as jnp
from jax import lax
from jax.experimental import pallas as pl
from jax.experimental.pallas import tpu as pltpu
from jax.sharding import PartitionSpec as P

DH = 128
SEG = 512
DEPTH = 5
EPS = 1e-06

F32 = jnp.float32
BF16 = jnp.bfloat16

AG_CHUNKS = 1
Z_FIRST = (1, 0)
X_FIRST = (0, 1)


def feature_map(values):
    return jnp.where(values > 0, values + 1.0, jnp.exp(jnp.minimum(values, 0.0)))


def feature_slope(values):
    return jnp.where(values > 0, 1.0, jnp.exp(jnp.minimum(values, 0.0)))


def ancestor_table(seg_parent):
    seg_total = seg_parent.shape[0]
    columns = jnp.arange(seg_total, dtype=jnp.int32)
    current = seg_parent
    lineage_table = jnp.zeros((seg_total, seg_total), F32)
    for _ in range(DEPTH):
        onehot = current[:, None] == columns[None, :]
        lineage_table = lineage_table + onehot.astype(F32)
        lifted = jnp.sum(jnp.where(onehot, seg_parent[None, :], 0), axis=1)
        current = jnp.where(current >= 0, lifted, -1)
    return lineage_table


def dot(a, b):
    return jnp.dot(a, b, preferred_element_type=F32)


def dot_t(a, b):
    return lax.dot_general(a, b, (((0,), (0,)), ((), ())), preferred_element_type=F32)


def dot_nt(a, b):
    return lax.dot_general(a, b, (((1,), (1,)), ((), ())), preferred_element_type=F32)


def after(value, *earlier):
    return lax.optimization_barrier((value, earlier))[0]


def nbytes(*arrays):
    return sum(a.size * a.dtype.itemsize for a in arrays)


def copy_kernel(ids_ref, in_ref, out_ref):
    out_ref[...] = in_ref[...]


def block_columns(v, ids, size):
    if size % 128:
        return jnp.concatenate([lax.dynamic_slice_in_dim(v, i * size, size, 1) for i in ids], 1)
    height, width = v.shape
    return pl.pallas_call(
        copy_kernel,
        out_shape=jax.ShapeDtypeStruct(v.shape, v.dtype),
        grid_spec=pltpu.PrefetchScalarGridSpec(
            num_scalar_prefetch=1,
            grid=(width // size,),
            in_specs=[pl.BlockSpec((height, size), lambda k, ids: (0, ids[k]))],
            out_specs=pl.BlockSpec((height, size), lambda k, ids: (0, k)),
        ),
        cost_estimate=pl.CostEstimate(flops=0, transcendentals=0, bytes_accessed=2 * nbytes(v)),
    )(jnp.stack(ids), v)


SMEM = pl.BlockSpec(memory_space=pltpu.SMEM)


def causal_mask():
    row = lax.broadcasted_iota(jnp.int32, (SEG, SEG), 0)
    col = lax.broadcasted_iota(jnp.int32, (SEG, SEG), 1)
    return row >= col


def softmax_rows(q, k, scale):
    scores = dot_nt(q, k) * scale
    scores = jnp.where(causal_mask(), scores, -1e30)
    top = jnp.max(scores, axis=-1, keepdims=True)
    e = jnp.exp(scores - top)
    return e * (1.0 / jnp.sum(e, axis=-1, keepdims=True))


def head_part(heads, p):
    s, h = p // heads, p % heads
    return pl.ds(pl.multiple_of(s * SEG, SEG), SEG), pl.ds(pl.multiple_of(h * DH, DH), DH)


def matrix_part(p):
    return pl.ds(pl.multiple_of(p * DH, DH), DH)


def weighted(w_ref, p, heads, segs, blocks_ref):
    s, h = p // heads, p % heads
    pairs = segs * heads
    big = jnp.zeros((DH, DH), F32)
    small = jnp.zeros((1, DH), F32)
    for d in range(blocks_ref.shape[0]):
        for n in range(segs):
            w = w_ref[s, d * segs + n]
            o = n * heads + h
            big = big + w * blocks_ref[d, matrix_part(o), :]
            small = small + w * blocks_ref[d, pl.ds(pairs * DH + o, 1), :]
    return big, small


def spread_order(dp):
    low = [0]
    for b in reversed(range(1, dp.bit_length() - 1)):
        low = low + [v ^ (1 << b) for v in low]
    return low + [v ^ 1 for v in low]


def greet(*peers):
    barrier = pltpu.get_barrier_semaphore()
    for peer in peers:
        pl.semaphore_signal(barrier, inc=1, device_id=peer, device_id_type=pl.DeviceIdType.MESH)
    pl.semaphore_wait(barrier, len(peers))


def dp_peers(dp):
    me = lax.axis_index("dp")
    return [{"dp": me ^ (1 << b)} for b in range(dp.bit_length() - 1)]


def tensor_peer(mask):
    return {"tensor": lax.axis_index("tensor") ^ mask}


def preload(kernel, ins, which):
    def wrapped(*refs):
        extra = refs[len(refs) - len(which) - 1 :]
        refs = list(refs[: len(refs) - len(which) - 1])
        loads = {}
        for k, i in enumerate(which):
            loads[i] = pltpu.make_async_copy(refs[i], extra[k], extra[-1].at[k])
            loads[i].start()
            refs[i] = extra[k]

        def ready(*places):
            for i in places or tuple(loads):
                loads.pop(i).wait()

        kernel(ready, *refs)

    scratch = [pltpu.VMEM(ins[i].shape, ins[i].dtype) for i in which]
    return wrapped, scratch + [pltpu.SemaphoreType.DMA((len(which),))]


def halving(dp, order):
    masks = [1 << b for b in order]
    masks += [1 << b for b in range(len(order), dp.bit_length() - 1)]
    seq = [0]
    for m in reversed(masks):
        seq = [m ^ v for v in seq] + seq
    return masks, seq


def near_units(dp, units):
    return units // 16 if dp == 8 else units


def block_of(ref, dp, order, k):
    rows = ref.shape[1] // dp
    if rows % DH:
        return ref[:, k * rows : (k + 1) * rows]
    at = (lax.axis_index("dp") ^ halving(dp, order)[1][k]) * rows
    return ref[:, pl.ds(pl.multiple_of(at, rows), rows)]


def remote(src, dst, send_sem, recv_sem, peer):
    return pltpu.make_async_remote_copy(
        src_ref=src,
        dst_ref=dst,
        send_sem=send_sem,
        recv_sem=recv_sem,
        device_id=peer,
        device_id_type=pl.DeviceIdType.MESH,
    )


def spread(dp, blocks_ref, send_sem, recv_sem, compute, then=None):
    me = lax.axis_index("dp")
    slot = {j: k for k, j in enumerate(spread_order(dp))}
    copies = {}

    def send(j, mask):
        to = j ^ mask
        k = slot[to]
        copies[to] = pltpu.make_async_remote_copy(
            src_ref=blocks_ref.at[slot[j]],
            dst_ref=blocks_ref.at[k],
            send_sem=send_sem.at[k],
            recv_sem=recv_sem.at[k],
            device_id={"dp": me ^ mask},
            device_id_type=pl.DeviceIdType.MESH,
        )
        copies[to].start()

    bits = [1 << b for b in range(1, dp.bit_length() - 1)]
    for m in bits:
        send(0, m)
    send(0, 1)
    compute()
    for m in bits:
        copies[m].wait_recv()
        if m == bits[-1]:
            near = [0, m]
            for n in reversed(bits[:-1]):
                for j in near[1:]:
                    send(j, n)
                near = near + [n] + [j ^ n for j in near[1:]]
                if n != bits[0]:
                    for j in near:
                        if j & n and j != n:
                            copies[j].wait_recv()
        send(m, 1)
    if then is not None:
        then()
    last = [j for j in near if j and j not in bits]
    for j in last:
        if j & bits[0] or len(bits) == 1:
            copies[j].wait_recv()
        send(j, 1)
    for j in near:
        copies[j ^ 1].wait_recv()
    for c in copies.values():
        c.wait_send()


W_CHUNKS = 4


def attention_kernel(
    dp, heads, segs, scale, ready, w_ref, g_ref, h_ref, wq_ref, wk_ref, wv_ref, wo_ref,
    q_ref, k_ref, v_ref, a16_ref, pair_ref, local_ref, mem_ref, zin_ref, all_ref,
    wf_ref, asend_ref, w_send, w_recv, a_send, a_recv, blocks_ref, send_sem, recv_sem,
):
    pairs = segs * heads
    flat = heads * DH
    half = segs * SEG // 2
    core, far = tensor_peer(1), tensor_peer(2)
    greet(*dp_peers(dp), core, far)

    size = flat // W_CHUNKS
    w_copies = {}

    def w_send_chunk(j, c, to, peer):
        rows = pl.ds(c * size, size)
        k = (to - 1) * W_CHUNKS + c
        w_copies[to, c] = remote(
            wf_ref.at[j, rows, :], wf_ref.at[to, rows, :], w_send.at[k], w_recv.at[k], peer
        )
        w_copies[to, c].start()

    def w_done(to, c):
        rows = slice(c * size, (c + 1) * size)
        w_copies[to, c].wait_recv()
        all_ref[to * flat + c * size : to * flat + (c + 1) * size, :] = wf_ref[to, rows, :].astype(
            BF16
        )

    ready(6)
    for c in range(W_CHUNKS):
        rows = slice(c * size, (c + 1) * size)
        wf_ref[0, rows, :] = wo_ref[rows, :].astype(F32)
        w_send_chunk(0, c, 2, far)
        w_send_chunk(0, c, 1, core)
    all_ref[:flat, :] = wo_ref[...]

    def project(matrix_ref, out_ref):
        @pl.loop(0, segs * SEG // 256)
        def _(i):
            rows = pl.ds(pl.multiple_of(i * 256, 256), 256)
            out_ref[rows, :] = dot(h_ref[rows, :], matrix_ref[...]).astype(BF16)

    ready()
    project(wk_ref, k_ref)
    project(wv_ref, v_ref)

    @pl.loop(0, pairs)
    def _(p):
        at = head_part(heads, p)
        sk = feature_map(k_ref[at].astype(F32))
        blocks_ref[0, matrix_part(p), :] = dot_t(sk.astype(BF16), v_ref[at])
        blocks_ref[0, pl.ds(pairs * DH + p, 1), :] = jnp.sum(sk, axis=0, keepdims=True)

    def compute():
        project(wq_ref, q_ref)

        @pl.loop(0, pairs)
        def _(p):
            at = head_part(heads, p)
            probs = softmax_rows(q_ref[at], k_ref[at], scale)
            local_ref[at] = dot(probs.astype(BF16), v_ref[at])

    spread(dp, blocks_ref, send_sem, recv_sem, compute)

    @pl.loop(0, pairs)
    def _(p):
        at = head_part(heads, p)
        mem, zin = weighted(w_ref, p, heads, segs, blocks_ref)
        mem_ref[matrix_part(p), :] = mem
        zin_ref[pl.ds(p, 1), :] = zin
        g = g_ref[0, p % heads]
        sq = feature_map(q_ref[at].astype(F32))
        den = jnp.sum(sq * zin, axis=-1, keepdims=True) + 1.0
        retrieved = dot(sq.astype(BF16), mem.astype(BF16)) / den
        a16_ref[at] = (g * retrieved + (1.0 - g) * local_ref[at]).astype(BF16)

    asend_ref[...] = a16_ref[half:, :].astype(F32)
    a_copy = remote(asend_ref, pair_ref.at[:, pl.ds(flat, flat)], a_send, a_recv, core)
    a_copy.start()
    pair_ref[:, :flat] = a16_ref[:half, :].astype(F32)
    for c in range(W_CHUNKS):
        w_done(1, c)
    a_copy.wait_recv()
    for c in range(W_CHUNKS):
        w_copies[2, c].wait_recv()
        w_send_chunk(2, c, 3, core)
        rows = slice(c * size, (c + 1) * size)
        all_ref[2 * flat + c * size : 2 * flat + (c + 1) * size, :] = wf_ref[2, rows, :].astype(BF16)
    for c in range(W_CHUNKS):
        w_done(3, c)
    for copy in w_copies.values():
        copy.wait_send()
    a_copy.wait_send()


def attention_back_kernel(
    dp, heads, segs, scale, ready, w_ref, g_ref, q_ref, k_ref, v_ref, da_ref, local_ref, mem_ref,
    zin_ref, dr_ref, a16_ref, d_pre_ref, u_pre_ref, out_part_ref,
    dq_ref, dk_ref, dv_ref, gate_ref, o_pre_ref, d_rode_ref, u_rode_ref, out_far_ref,
    dqm_ref, dkl_ref, dvl_ref, os_ref, ride_send, ride_recv, blocks_ref, send_sem, recv_sem,
):
    pairs = segs * heads
    me = lax.axis_index("dp")
    far = tensor_peer(2)
    greet(*dp_peers(dp), far)
    legs = [
        (d_pre_ref, d_rode_ref, {"dp": me ^ 1}),
        (out_part_ref, out_far_ref, far),
        (os_ref, o_pre_ref, {"dp": me ^ 2}),
    ]
    quarter, units = d_rode_ref.shape
    eighth = quarter // 2
    legs[0] = (d_pre_ref.at[pl.ds(0, quarter), :], d_rode_ref, {"dp": me ^ 1})
    near = near_units(dp, units)
    cols = pl.ds(0, near)
    legs.append((u_pre_ref.at[pl.ds(0, quarter), cols], u_rode_ref.at[:, cols], {"dp": me ^ 2}))
    if near < units:
        cols = pl.ds(near, units - near)
        for k in range(2):
            legs.append(
                (
                    u_pre_ref.at[pl.ds(2 * k * eighth, eighth), cols],
                    u_rode_ref.at[pl.ds(k * eighth, eighth), cols],
                    {"dp": me ^ 4},
                )
            )
    riders = [
        remote(src, dst, ride_send.at[i], ride_recv.at[i], peer)
        for i, (src, dst, peer) in enumerate(legs)
    ]
    o_rider = riders[2]
    plain = riders[:2] + riders[3:]
    for r in riders[:2] + riders[3:4]:
        r.start()
    ready()

    @pl.loop(0, pairs)
    def _(p):
        at = head_part(heads, p)
        g = g_ref[0, p % heads]
        qf = q_ref[at].astype(F32)
        sq = feature_map(qf)
        sq16 = sq.astype(BF16)
        mem16 = mem_ref[matrix_part(p), :].astype(BF16)
        zin = zin_ref[pl.ds(p, 1), :]
        inv_den = 1.0 / (jnp.sum(sq * zin, axis=-1, keepdims=True) + 1.0)
        retrieved = dot(sq16, mem16) * inv_den
        da = da_ref[at].astype(F32)
        gate_ref[pl.ds(p, 1), :] = jnp.sum(da * (retrieved - local_ref[at]), axis=0, keepdims=True)
        dnum = g * da * inv_den
        dden = -jnp.sum(dnum * retrieved, axis=-1, keepdims=True)
        dnum16 = dnum.astype(BF16)
        blocks_ref[0, matrix_part(p), :] = dot_t(sq16, dnum16)
        blocks_ref[0, pl.ds(pairs * DH + p, 1), :] = jnp.sum(sq * dden, axis=0, keepdims=True)
        dsq = dot_nt(dnum16, mem16) + dden * zin
        dqm_ref[at] = dsq * feature_slope(qf)

    rows = dr_ref.shape[1] // dp
    half_blocks = dp // 2

    def compute():
        for j in range(half_blocks):
            os_ref[j * rows : (j + 1) * rows, :] = dot_t(
                block_of(dr_ref, dp, Z_FIRST, j), a16_ref[...]
            )

        @pl.loop(0, pairs)
        def _(p):
            at = head_part(heads, p)
            g = g_ref[0, p % heads]
            q, k, v, da = q_ref[at], k_ref[at], v_ref[at], da_ref[at]
            probs = softmax_rows(q, k, scale)
            dprobs = (1.0 - g) * dot_nt(da, v)
            inner = jnp.sum(dprobs * probs, axis=-1, keepdims=True)
            ds16 = (probs * (dprobs - inner)).astype(BF16)
            dq_ref[at] = (dot(ds16, k) * scale + dqm_ref[at]).astype(BF16)
            dkl_ref[at] = dot_t(ds16, q) * scale
            dvl_ref[at] = (1.0 - g) * dot_t(probs.astype(BF16), da)

    def then():
        o_rider.start()
        for r in riders[4:]:
            r.start()

    spread(dp, blocks_ref, send_sem, recv_sem, compute, then)

    @pl.loop(0, pairs)
    def _(p):
        at = head_part(heads, p)
        dd, dz = weighted(w_ref, p, heads, segs, blocks_ref)
        dd16 = dd.astype(BF16)
        kf = k_ref[at].astype(F32)
        dsk = dot_nt(v_ref[at], dd16) + dz
        dk_ref[at] = (dkl_ref[at] + dsk * feature_slope(kf)).astype(BF16)
        dv_ref[at] = (dvl_ref[at] + dot(feature_map(kf).astype(BF16), dd16)).astype(BF16)

    o_rider.wait()
    for j in range(half_blocks):
        o_pre_ref[j * rows : (j + 1) * rows, :] += dot_t(
            block_of(dr_ref, dp, Z_FIRST, half_blocks + j), a16_ref[...]
        )
    for r in plain:
        r.wait()


ROWS = 128


def tail_items(flat):
    full = slice(0, flat)
    return [
        (0, full), (1, full), (2, slice(0, flat // 2)), (2, slice(flat // 2, flat)), (3, full)
    ]


def tail_kernel(
    dp, turn, order, o_order, ready,
    h_ref, dq_ref, dk_ref, dv_ref, wq_ref, wk_ref, wv_ref, o_pre_ref, gain_ref, vec_ref,
    d3_ref, u3_ref, resid_hbm, out_part_hbm, out_far_hbm, dresid_hbm, x_hbm,
    gq_ref, gk_ref, gv_ref, go_ref, vec_out_ref, far_ref, d3_got_ref, u3_got_ref, out_hbm, dx_hbm,
    part_ref, cs_ref, cr_ref, in_ref, own_ref, other_ref, turn_ref, vec_got_ref,
    c_send, c_recv, y_send, y_recv, ride_send, ride_recv, e_send, e_recv, v_send, v_recv,
    in_sem, st_sem, turn_sem, free_sem, *bufs,
):
    me = lax.axis_index("dp")
    side = lax.axis_index("tensor") % 2
    core, far = tensor_peer(1), tensor_peer(2)
    greet(*dp_peers(dp), core, far)
    masks, _ = halving(dp, order)
    o_masks, _ = halving(dp, o_order)
    steps = len(masks)
    half, width = far_ref.shape
    rows = width // dp
    chunks = half // ROWS
    ht_ref = bufs[-1] if turn else h_ref
    depth = in_ref.shape[0]
    flat = dq_ref.shape[1]
    lhs = (dq_ref, dk_ref, dv_ref)
    outs = (gq_ref, gk_ref, gv_ref, go_ref)
    items = tail_items(flat)
    copies = {}

    def buffers(i, step):
        k = 2 * (i * steps + step)
        return bufs[k], bufs[k + 1]

    def term(i, step):
        lo = rows * sum(dp >> (n + 1) for n in range(step))
        count = rows * (dp >> (step + 1)) if step < steps else rows
        start = 0
        which, cols = items[i]
        if which < 3:
            value = dot(ht_ref[lo : lo + count, :], lhs[which][:, cols])
        else:
            base = rows * (dp // 2)
            value = o_pre_ref[lo - base : lo - base + count, :]
            start = 1
        for n in range(start, step):
            at = lo - rows * sum(dp >> (m + 1) for m in range(n + 1))
            value = value + buffers(i, n)[1][at : at + count, :]
        return value

    def advance(i, step):
        which, cols = items[i]
        if step > (1 if which == 3 else 0):
            copies[i, step - 1].wait_recv()
        if step == steps:
            outs[which][:, cols] = term(i, step)
            return
        send, recv = buffers(i, step)
        send[...] = term(i, step)
        mask = (o_masks if which == 3 else masks)[step]
        k = i * steps + step
        copies[i, step] = remote(send, recv, e_send.at[k], e_recv.at[k], {"dp": me ^ mask})
        copies[i, step].start()

    third = {"dp": me ^ masks[2]}
    units = u3_ref.shape[1]
    near = near_units(dp, units)
    cols = pl.ds(0, near)
    legs = [(d3_ref, d3_got_ref, third), (u3_ref.at[:, cols], u3_got_ref.at[:, cols], third)]
    if near < units:
        cols = pl.ds(near, units - near)
        legs.append((u3_ref.at[:, cols], u3_got_ref.at[:, cols], {"dp": me ^ 2}))
    riders = [
        remote(src, dst, ride_send.at[i], ride_recv.at[i], peer)
        for i, (src, dst, peer) in enumerate(legs)
    ]
    out_item = len(items) - 1
    ready(7)
    advance(out_item, 1)
    for r in riders:
        r.start()

    def block_load(j):
        at = (me ^ halving(dp, order)[1][j]) * rows
        return pltpu.make_async_copy(
            h_ref.at[:, pl.ds(pl.multiple_of(at, rows), rows)],
            turn_ref.at[j % 2],
            turn_sem.at[j % 2],
        )

    def turn_blocks(lo, hi):
        for j in range(lo, hi if turn else lo):
            block_load(j).wait()
            ht_ref[j * rows : (j + 1) * rows, :] = turn_ref[j % 2].T
            if j + 2 < dp:
                block_load(j + 2).start()

    for j in range(2 if turn else 0):
        block_load(j).start()
    ready()
    turn_blocks(0, dp // 2)
    for i in range(out_item):
        advance(i, 0)

    def part_rows(c):
        return pl.ds(c * ROWS, ROWS)

    def core_wire(c):
        return remote(cs_ref.at[c], cr_ref.at[c], c_send.at[c], c_recv.at[c], core)

    def core_free():
        pl.semaphore_signal(free_sem, inc=1, device_id=core, device_id_type=pl.DeviceIdType.MESH)

    def far_wire(c):
        return remote(part_ref.at[c], far_ref.at[part_rows(c), :], y_send.at[c], y_recv.at[c], far)

    def back(lo):
        return sum(
            dot_nt(v[lo : lo + 2 * ROWS, :], w[...])
            for v, w in zip(lhs, (wq_ref, wk_ref, wv_ref))
        )

    for c in range(0, chunks, 2):
        value = back(half + c * ROWS)
        for k in range(2):
            cs_ref[c + k] = value[k * ROWS : (k + 1) * ROWS, :]
            core_wire(c + k).start()
    for c in range(0, chunks, 2):
        value = back(c * ROWS)
        for k in range(2):
            core_wire(c + k).wait()
            part_ref[c + k] = value[k * ROWS : (k + 1) * ROWS, :] + cr_ref[c + k]
            far_wire(c + k).start()
    core_free()

    def both_cores(sources, compute, dst_hbm):
        def loads(c):
            k = c % depth
            return [
                pltpu.make_async_copy(src.at[part_rows(c), :], in_ref.at[k, i], in_sem.at[k, i])
                for i, src in enumerate(sources)
            ]

        def begin(c):
            if c < chunks:
                for load in loads(c):
                    load.start()

        def store(src_ref, which, c, k):
            at = pl.ds(pl.multiple_of(which * half + c * ROWS, ROWS), ROWS)
            return pltpu.make_async_copy(src_ref, dst_hbm.at[at, :], st_sem.at[k])

        pl.semaphore_wait(free_sem, 1)
        for c in range(depth):
            begin(c)
        for c in range(chunks):
            for load in loads(c):
                load.wait()
            value = compute(c, *(in_ref[c % depth, i] for i in range(3))).astype(BF16)
            if c:
                store(own_ref, side, c - 1, 0).wait()
            own_ref[...] = value
            store(own_ref, side, c, 0).start()
            cs_ref[c] = value.astype(F32)
            core_wire(c).start()
            begin(c + depth)
        for c in range(chunks):
            core_wire(c).wait()
            if c:
                store(other_ref, 1 - side, c - 1, 1).wait()
            other_ref[...] = cr_ref[c].astype(BF16)
            store(other_ref, 1 - side, c, 1).start()
        store(own_ref, side, chunks - 1, 0).wait()
        store(other_ref, 1 - side, chunks - 1, 1).wait()

    def output_rows(c, a, b, d):
        return a + b + d

    def input_rows(c, there, dresid, x):
        grad = part_ref[c] + there
        inv = lax.rsqrt(jnp.mean(x * x, axis=-1, keepdims=True) + EPS)
        gs = grad * gain_ref[...]
        inner = jnp.mean(gs * x, axis=-1, keepdims=True)
        vec_out_ref[0:1, :] += jnp.sum(grad * x * inv, axis=0, keepdims=True)
        return dresid + inv * gs - x * inv * inv * inv * inner

    turn_blocks(dp // 2, dp)
    if steps == 3:
        advance(out_item, 2)
    both_cores((resid_hbm, out_part_hbm, out_far_hbm), output_rows, out_hbm)
    core_free()
    if steps == 3:
        for i, step in ((0, 1), (1, 1), (0, 2), (2, 1), (1, 2)):
            advance(i, step)
        rest = ((3, 1), (2, 2), (3, 2))
    else:
        for step in range(1, steps):
            for i in range(len(items)):
                if step > 1 or i < out_item:
                    advance(i, step)
        rest = ()
    last = [(i, steps) for i in (out_item,) + tuple(range(out_item))]

    for c in range(chunks):
        far_wire(c).wait()
    vec_out_ref[...] = vec_ref[...]
    both_cores((far_ref, dresid_hbm, x_hbm), input_rows, dx_hbm)
    for i, step in rest:
        advance(i, step)

    for k, peer in enumerate([core] + dp_peers(dp)):
        hop = remote(vec_out_ref, vec_got_ref.at[k], v_send.at[k], v_recv.at[k], peer)
        hop.start()
        hop.wait()
        got = vec_got_ref[k]
        if k == 0:
            got = jnp.where(lax.broadcasted_iota(jnp.int32, got.shape, 0) < 2, got, 0.0)
        vec_out_ref[...] += got
    for i, step in last:
        advance(i, step)
    for c in copies.values():
        c.wait_send()
    for r in riders:
        r.wait()


def tail(ident, dp, h1, h1_t, grads, weights, o_pre, gain, vec, d3, u3, streams):
    tokens, width = h1.shape
    turn = h1_t is None
    flat = grads[0].shape[1]
    half = tokens // 2
    rows = width // dp
    steps = dp.bit_length() - 1
    full = pl.BlockSpec(memory_space=pltpu.VMEM)
    anywhere = pl.BlockSpec(memory_space=pl.ANY)
    f32 = lambda *shape: jax.ShapeDtypeStruct(shape, F32)
    dma = pltpu.SemaphoreType.DMA
    bufs = []
    items = tail_items(flat)
    for which, cols in items:
        for step in range(steps):
            count = rows * (dp >> (step + 1)) if which < 3 or step else 8
            bufs += [pltpu.VMEM((count, cols.stop - cols.start), F32)] * 2
    chunks = half // ROWS
    b16 = jax.ShapeDtypeStruct((tokens, width), BF16)
    operands = (
        h1 if turn else h1_t, *grads, *weights, o_pre, gain[None, :], vec, d3, u3, *streams
    )
    kernel, held = preload(
        functools.partial(tail_kernel, dp, turn, X_FIRST, Z_FIRST),
        operands,
        range(1 if turn else 0, 10),
    )
    return pl.pallas_call(
        kernel,
        out_shape=[f32(rows, flat)] * 4
        + [f32(*vec.shape), f32(half, width), f32(*d3.shape), f32(*u3.shape), b16, b16],
        in_specs=[anywhere] * len(operands),
        out_specs=[full] * 5 + [anywhere] * 5,
        scratch_shapes=[
            pltpu.VMEM((chunks, ROWS, width), F32),
            pltpu.VMEM((chunks, ROWS, width), F32),
            pltpu.VMEM((chunks, ROWS, width), F32),
            pltpu.VMEM((2 if turn else 1, 3, ROWS, width), F32),
            pltpu.VMEM((ROWS, width), BF16),
            pltpu.VMEM((ROWS, width), BF16),
            pltpu.VMEM((2, tokens, rows) if turn else (8, DH), BF16),
            pltpu.VMEM((steps + 1,) + vec.shape, F32),
            dma((chunks,)), dma((chunks,)), dma((chunks,)), dma((chunks,)),
            dma((3,)), dma((3,)), dma((len(items) * steps,)), dma((len(items) * steps,)),
            dma((steps + 1,)), dma((steps + 1,)), dma((2, 3)), dma((2,)), dma((2,)),
            pltpu.SemaphoreType.REGULAR,
        ]
        + bufs
        + ([pltpu.VMEM((width, tokens), BF16)] if turn else [])
        + held,
        compiler_params=pltpu.CompilerParams(
            collective_id=ident, has_side_effects=True, vmem_limit_bytes=63 << 20
        ),
        cost_estimate=pl.CostEstimate(
            flops=12 * tokens * width * flat, transcendentals=0, bytes_accessed=96 << 20
        ),
    )(*operands)


def core_gather_kernel(norm, tiles, v_ref, gain_ref, out_ref, send_ref, recv_ref, send_sem, recv_sem):
    peer = tensor_peer(1)
    greet(peer)
    half = v_ref.shape[0]
    size = half // tiles
    copies = []
    for c in range(tiles):
        rows = slice(c * size, (c + 1) * size)
        v = v_ref[rows, :]
        if norm:
            inv = lax.rsqrt(jnp.mean(v * v, axis=-1, keepdims=True) + EPS)
            v = v * inv * gain_ref[...]
            send_ref[rows, :] = v
        out_ref[rows, :] = v.astype(BF16)
        src = send_ref if norm else v_ref
        copies.append(
            remote(
                src.at[rows, :], recv_ref.at[rows, :], send_sem.at[c], recv_sem.at[c], peer
            )
        )
        copies[-1].start()
    for c in range(tiles):
        rows = slice(c * size, (c + 1) * size)
        copies[c].wait_recv()
        out_ref[half + c * size : half + (c + 1) * size, :] = recv_ref[rows, :].astype(BF16)
    for c in copies:
        c.wait_send()


def core_gather(ident, v, gain=None):
    half, n = v.shape
    tiles = 4
    out = jax.ShapeDtypeStruct((2 * half, n), BF16)
    full = pl.BlockSpec(memory_space=pltpu.VMEM)
    norm = gain is not None
    return pl.pallas_call(
        functools.partial(core_gather_kernel, norm, tiles),
        out_shape=out,
        in_specs=[full, full],
        out_specs=full,
        scratch_shapes=[
            pltpu.VMEM((half, n) if norm else (8, DH), F32),
            pltpu.VMEM((half, n), F32),
            pltpu.SemaphoreType.DMA((tiles,)),
            pltpu.SemaphoreType.DMA((tiles,)),
        ],
        compiler_params=pltpu.CompilerParams(
            collective_id=ident, has_side_effects=True, vmem_limit_bytes=48 << 20
        ),
        cost_estimate=pl.CostEstimate(
            flops=0, transcendentals=0, bytes_accessed=nbytes(v, v, v, out)
        ),
    )(v, gain[None, :] if norm else jnp.zeros((8, DH), F32))


def norm_back_kernel(
    part_hbm, far_hbm, resid_hbm, grad_hbm, gain_ref, dresid_hbm, dr_ref, sum_ref,
    in_ref, og_ref, send_ref, recv_ref, c_send, c_recv, in_sem, og_sem, out_sem,
):
    peer = tensor_peer(1)
    greet(peer)
    half, width = dresid_hbm.shape
    chunks = half // ROWS
    sources = (part_hbm, far_hbm, resid_hbm)

    def rows(c):
        return pl.ds(c * ROWS, ROWS)

    def loads(c):
        k = c % 2
        wide = [
            pltpu.make_async_copy(src.at[rows(c), :], in_ref.at[k, i], in_sem.at[k, i])
            for i, src in enumerate(sources)
        ]
        return wide + [
            pltpu.make_async_copy(grad_hbm.at[rows(c), :], og_ref.at[k], og_sem.at[k])
        ]

    def wire(c):
        return remote(send_ref.at[c], recv_ref.at[c], c_send.at[c], c_recv.at[c], peer)

    def store(c):
        return pltpu.make_async_copy(send_ref.at[c], dresid_hbm.at[rows(c), :], out_sem.at[c])

    for c in range(2):
        for load in loads(c):
            load.start()
    sum_ref[...] = jnp.zeros_like(sum_ref)
    for c in range(chunks):
        k = c % 2
        for load in loads(c):
            load.wait()
        grad = in_ref[k, 0] + in_ref[k, 1]
        x = in_ref[k, 2]
        inv = lax.rsqrt(jnp.mean(x * x, axis=-1, keepdims=True) + EPS)
        gs = grad * gain_ref[...]
        inner = jnp.mean(gs * x, axis=-1, keepdims=True)
        sum_ref[0:1, :] += jnp.sum(grad * x * inv, axis=0, keepdims=True)
        value = og_ref[k].astype(F32) + inv * gs - x * inv * inv * inv * inner
        send_ref[c] = value
        wire(c).start()
        store(c).start()
        dr_ref[c * ROWS : (c + 1) * ROWS, :] = value.astype(BF16)
        if c + 2 < chunks:
            for load in loads(c + 2):
                load.start()
    for c in range(chunks):
        wire(c).wait()
        dr_ref[half + c * ROWS : half + (c + 1) * ROWS, :] = recv_ref[c].astype(BF16)
    for c in range(chunks):
        store(c).wait()


def norm_back(ident, part, far, resid, out_grad, gain):
    half, width = resid.shape
    chunks = half // ROWS
    outs = [
        jax.ShapeDtypeStruct((half, width), F32),
        jax.ShapeDtypeStruct((2 * half, width), BF16),
        jax.ShapeDtypeStruct((8, width), F32),
    ]
    full = pl.BlockSpec(memory_space=pltpu.VMEM)
    anywhere = pl.BlockSpec(memory_space=pl.ANY)
    dma = pltpu.SemaphoreType.DMA
    return pl.pallas_call(
        norm_back_kernel,
        out_shape=outs,
        in_specs=[anywhere] * 4 + [full],
        out_specs=[anywhere, full, full],
        scratch_shapes=[
            pltpu.VMEM((2, 3, ROWS, width), F32),
            pltpu.VMEM((2, ROWS, width), BF16),
            pltpu.VMEM((chunks, ROWS, width), F32),
            pltpu.VMEM((chunks, ROWS, width), F32),
            dma((chunks,)), dma((chunks,)), dma((2, 3)), dma((2,)), dma((chunks,)),
        ],
        compiler_params=pltpu.CompilerParams(
            collective_id=ident, has_side_effects=True, vmem_limit_bytes=48 << 20
        ),
        cost_estimate=pl.CostEstimate(
            flops=0, transcendentals=0, bytes_accessed=nbytes(part, far, resid, out_grad, *outs)
        ),
    )(part, far, resid, out_grad, gain[None, :])


TILE = 256
SLOTS = 4


def feed_kernel(
    dp, turn, ready, h_ref, ogt_ref, ht_ref, wup_hbm, wdn_hbm, ug_hbm,
    act_ref, dpre_ref, part_ref, part2_ref, far_ref, d_ref, u_ref, d_pre_ref, u_pre_ref,
    w_ref, ug_ref, ds_ref, us_ref, cs_ref, cr_ref,
    w_sem, ug_sem, d_send, d_recv, u_send, u_recv, c_send, c_recv, y_send, y_recv, free_sem,
):
    tokens, units = act_ref.shape
    half = tokens // 2
    width = h_ref.shape[1]
    cut = width // 2
    rows = width // dp
    me = lax.axis_index("dp")
    core, far = tensor_peer(1), tensor_peer(2)
    x_peer, z_peer = {"dp": me ^ 1}, {"dp": me ^ 2}
    greet(core, far, x_peer, z_peer)
    count = units // TILE

    load_w = pltpu.make_async_copy(wup_hbm, w_ref, w_sem)
    load_w.start()

    def tile_cols(t):
        return pl.ds(pl.multiple_of(t * TILE, TILE), TILE)

    def load_ug(t, k):
        return pltpu.make_async_copy(ug_hbm.at[:, tile_cols(t)], ug_ref.at[k], ug_sem.at[k])

    load_ug(0, 0).start()
    load_ug(1, 1).start()
    ready(0)
    for j in range(dp // 2 if turn else 0):
        ht_ref[j * rows : (j + 1) * rows, :] = block_of(h_ref, dp, X_FIRST, j).T
    ready()
    load_w.wait()

    def wire(t, k):
        cols = tile_cols(t)
        d = remote(ds_ref.at[k], d_ref.at[:, cols], d_send.at[t], d_recv.at[t], z_peer)
        u = remote(us_ref.at[k], u_ref.at[:, cols], u_send.at[t], u_recv.at[t], x_peer)
        return d, u

    def terms(t, k):
        cols = tile_cols(t)
        d, u = wire(t, k)
        ds_ref[k] = dot(ogt_ref[:cut, :], act_ref[:, cols])
        d.start()
        us_ref[k] = dot(ht_ref[:cut, :], dpre_ref[:, cols])
        u.start()

    @pl.loop(0, count)
    def _(t):
        k = t % 2
        cols = tile_cols(t)
        load_ug(t, k).wait()
        pre = dot(h_ref[...], w_ref[:, cols])
        c = 0.7978845608028654
        sq = pre * pre
        th = jnp.tanh(c * pre * (1.0 + 0.044715 * sq))
        mid = 0.5 * (1.0 + th)
        act_ref[:, cols] = (pre * mid).astype(BF16)
        slope = mid + 0.5 * pre * (1.0 - th * th) * (c * (1.0 + 0.134145 * sq))
        dpre_ref[:, cols] = (ug_ref[k] * slope).astype(BF16)

        @pl.when(t + 2 < count)
        def _():
            load_ug(t + 2, k).start()

        @pl.when(t < SLOTS)
        def _():
            terms(t, t)

    part_cols = width // 4

    def core_wire(c):
        return remote(cs_ref.at[c], cr_ref.at[c], c_send.at[c], c_recv.at[c], core)

    def far_wire(c):
        cols = pl.ds(c * part_cols, part_cols)
        return remote(part_ref.at[:, cols], far_ref.at[:, cols], y_send.at[c], y_recv.at[c], far)

    def summed(lhs_ref, transposed, out_ref, travels):
        def term(row, c):
            cols = slice(c * part_cols, (c + 1) * part_cols)
            lhs = lhs_ref[row * half : (row + 1) * half, :]
            if transposed:
                return dot_nt(lhs, w_ref[cols, :])
            return dot(lhs, w_ref[:, cols])

        for c in range(4):
            cs_ref[c] = term(1, c)
            core_wire(c).start()
        for c in range(4):
            part = term(0, c)
            core_wire(c).wait()
            out_ref[:, c * part_cols : (c + 1) * part_cols] = part + cr_ref[c]
            if travels:
                far_wire(c).start()

    summed(dpre_ref, True, part_ref, True)
    load_down = pltpu.make_async_copy(wdn_hbm, w_ref, w_sem)
    load_down.start()
    pl.semaphore_signal(free_sem, inc=1, device_id=core, device_id_type=pl.DeviceIdType.MESH)
    for j in range(dp // 2, dp if turn else 0):
        ht_ref[j * rows : (j + 1) * rows, :] = block_of(h_ref, dp, X_FIRST, j).T

    @pl.loop(SLOTS, count)
    def _(t):
        d, u = wire(t - SLOTS, t - SLOTS)
        d.wait_send()
        u.wait_send()
        terms(t, t - SLOTS)

    load_down.wait()
    pl.semaphore_wait(free_sem, 1)
    summed(act_ref, False, part2_ref, False)

    def load_got(src_ref, t, k):
        return pltpu.make_async_copy(src_ref.at[:, tile_cols(t)], ug_ref.at[k], ug_sem.at[k])

    def store_pre(dst_ref, t, k):
        return pltpu.make_async_copy(ug_ref.at[k], dst_ref.at[:, tile_cols(t)], ug_sem.at[k])

    @pl.loop(0, count)
    def _(t):
        d, u = wire(t, 0)

        @pl.when(t > 0)
        def _():
            store_pre(d_pre_ref, t - 1, 0).wait()
            store_pre(u_pre_ref, t - 1, 1).wait()

        d.wait_recv()
        load_got(d_ref, t, 0).start()
        u.wait_recv()
        load_got(u_ref, t, 1).start()
        load_got(d_ref, t, 0).wait()
        ug_ref[0] += dot(ogt_ref[cut:, :], act_ref[:, tile_cols(t)])
        store_pre(d_pre_ref, t, 0).start()
        load_got(u_ref, t, 1).wait()
        ug_ref[1] += dot(ht_ref[cut:, :], dpre_ref[:, tile_cols(t)])
        store_pre(u_pre_ref, t, 1).start()

    store_pre(d_pre_ref, count - 1, 0).wait()
    store_pre(u_pre_ref, count - 1, 1).wait()

    @pl.loop(count - SLOTS, count)
    def _(t):
        d, u = wire(t, t - (count - SLOTS))
        d.wait_send()
        u.wait_send()

    for c in range(4):
        far_wire(c).wait()


def feed(ident, dp, h2, og_t, h_t, w_up, w_down, up_grad):
    tokens, width = h2.shape
    units = w_up.shape[1]
    half = tokens // 2
    cut = width // 2
    count = units // TILE
    full = pl.BlockSpec(memory_space=pltpu.VMEM)
    anywhere = pl.BlockSpec(memory_space=pl.ANY)
    f32 = lambda *shape: jax.ShapeDtypeStruct(shape, F32)
    b16 = jax.ShapeDtypeStruct((tokens, units), BF16)
    dma = pltpu.SemaphoreType.DMA
    turn = h_t is None
    kernel = functools.partial(feed_kernel, dp, turn)
    if turn:

        def kernel(ready, h_ref, ogt_ref, *refs):
            feed_kernel(dp, turn, ready, h_ref, ogt_ref, refs[-1], *refs[:-1])

    operands = (h2, og_t, *([] if turn else [h_t]), w_up, w_down, up_grad)
    kernel, held = preload(kernel, operands, range(len(operands) - 3))
    return pl.pallas_call(
        kernel,
        out_shape=[b16, b16, f32(half, width), f32(half, width), f32(half, width)]
        + [f32(cut, units)] * 4,
        in_specs=[anywhere] * len(operands),
        out_specs=[full] * 4 + [anywhere] * 5,
        scratch_shapes=[
            pltpu.VMEM((width, units), BF16),
            pltpu.VMEM((2, tokens, TILE), F32),
            pltpu.VMEM((SLOTS, cut, TILE), F32),
            pltpu.VMEM((SLOTS, cut, TILE), F32),
            pltpu.VMEM((4, half, width // 4), F32),
            pltpu.VMEM((4, half, width // 4), F32),
            dma, dma((2,)), dma((count,)), dma((count,)), dma((count,)), dma((count,)),
            dma((4,)), dma((4,)), dma((4,)), dma((4,)), pltpu.SemaphoreType.REGULAR,
        ]
        + ([pltpu.VMEM((width, tokens), BF16)] if turn else [])
        + held,
        compiler_params=pltpu.CompilerParams(
            collective_id=ident, has_side_effects=True, vmem_limit_bytes=62 << 20
        ),
        cost_estimate=pl.CostEstimate(
            flops=10 * tokens * width * units, transcendentals=tokens * units,
            bytes_accessed=64 << 20,
        ),
    )(*operands)


def body(
    inputs,
    gain_attn,
    w_query,
    w_key,
    w_value,
    gate_logit,
    w_out,
    gain_mlp,
    w_up,
    w_down,
    seg_parent,
    out_grad,
):
    tokens, width = inputs.shape
    half = tokens // 2
    segs = tokens // SEG
    heads = w_query.shape[1] // DH
    pairs = segs * heads
    units = w_up.shape[1]
    flat = heads * DH
    scale = DH ** (-0.5)
    dp = lax.axis_size("dp")
    tn = lax.axis_size("tensor")
    rows = width // dp
    di = lax.axis_index("dp")
    core = lax.axis_index("tensor") % 2

    one = jnp.where(seg_parent[0] < tokens * dp, 1.0, 2.0)

    def low_after_wire(v):
        return (v * one).astype(BF16)

    def swap_core(v):
        return lax.ppermute(v, "tensor", [(i, i ^ 1) for i in range(tn)])

    def swap_y(v):
        return lax.ppermute(v, "tensor", [(i, i ^ 2) for i in range(tn)])

    def swap_dp(v, mask):
        return lax.ppermute(v, "dp", [(i, i ^ mask) for i in range(dp)])

    def columns(v, order):
        _, seq = halving(dp, order)
        return block_columns(v, [di ^ k for k in seq], rows)

    def blocks_for(v, order):
        return columns(v, order) if rows % DH else v

    cut = width // 2
    quarter = cut // 2

    def pick(v, index, axis):
        size = v.shape[axis] // 2
        return lax.dynamic_slice_in_dim(v, index * size, size, axis)

    def place(own, other, index, axis):
        return jnp.where(
            index == 0,
            jnp.concatenate([own, other], axis),
            jnp.concatenate([other, own], axis),
        )

    def inv_rms(v):
        return lax.rsqrt(jnp.mean(v * v, axis=-1, keepdims=True) + EPS)

    x_own = pick(inputs, core, 0).astype(F32)
    x_oth = pick(inputs, 1 - core, 0).astype(F32)
    inv_own = inv_rms(x_own)
    inv_oth = inv_rms(x_oth)
    h1 = jnp.concatenate(
        [
            (x_own * inv_own * gain_attn).astype(BF16),
            (x_oth * inv_oth * gain_attn).astype(BF16),
        ],
        0,
    )

    sub = segs // 2
    every = jnp.arange(seg_parent.shape[0], dtype=jnp.int32)
    sub_ids = jnp.arange(sub, dtype=jnp.int32)
    seg_local = jnp.concatenate([core * sub + sub_ids, (1 - core) * sub + sub_ids])
    order = spread_order(dp)
    ids = jnp.concatenate([(di ^ j) * segs + seg_local for j in order])
    mine_hot = (ids[:segs, None] == every[None, :]).astype(F32)
    ids_hot = (ids[:, None] == every[None, :]).astype(F32)
    lineage = ancestor_table(seg_parent)

    def weights_of(table):
        mine_rows = jnp.sum(mine_hot[:, :, None] * table[None], axis=1)
        return jnp.sum(mine_rows[:, None, :] * ids_hot[None], axis=-1)

    up_weight = weights_of(lineage)
    down_weight = weights_of(lineage.T)

    gate = jax.nn.sigmoid(gate_logit)
    gate_row = gate[None, :]

    og_own = pick(out_grad, core, 0)
    og = jnp.concatenate([og_own, pick(out_grad, 1 - core, 0)], 0)
    block_rows = pairs * DH + pairs
    act_f32 = jax.ShapeDtypeStruct((tokens, flat), F32)
    act_b16 = jax.ShapeDtypeStruct((tokens, flat), BF16)
    mem_shape = jax.ShapeDtypeStruct((pairs * DH, DH), F32)
    zin_shape = jax.ShapeDtypeStruct((pairs, DH), F32)
    full = pl.BlockSpec(memory_space=pltpu.VMEM)

    anywhere = pl.BlockSpec(memory_space=pl.ANY)

    def attention_call(kernel, ident, outs, out_specs, scratch, args, in_specs, flops):
        which = [i for i, spec in enumerate(in_specs) if spec is full]
        in_specs = [anywhere if spec is full else spec for spec in in_specs]
        wrapped, held = preload(functools.partial(kernel, dp, heads, segs, scale), args, which)
        return pl.pallas_call(
            wrapped,
            out_shape=outs,
            in_specs=in_specs,
            out_specs=out_specs,
            scratch_shapes=scratch
            + [
                pltpu.VMEM((dp, block_rows, DH), F32),
                pltpu.SemaphoreType.DMA((dp,)),
                pltpu.SemaphoreType.DMA((dp,)),
            ]
            + held,
            compiler_params=pltpu.CompilerParams(
                collective_id=ident, has_side_effects=True, vmem_limit_bytes=63 << 20
            ),
            cost_estimate=pl.CostEstimate(
                flops=flops, transcendentals=0, bytes_accessed=64 << 20
            ),
        )(*args)

    head_flops = 2 * segs * heads * SEG * SEG * DH
    dma = pltpu.SemaphoreType.DMA
    qh, kh, vh, a16, a_pair, local, memory, zin, w_out_all = attention_call(
        attention_kernel,
        0,
        [
            act_b16, act_b16, act_b16, act_b16,
            jax.ShapeDtypeStruct((half, 2 * flat), F32),
            act_f32, mem_shape, zin_shape,
            jax.ShapeDtypeStruct((4 * flat, width), BF16),
        ],
        [full] * 9,
        [
            pltpu.VMEM((4, flat, width), F32),
            pltpu.VMEM((half, flat), F32),
            dma((3 * W_CHUNKS,)), dma((3 * W_CHUNKS,)), dma, dma,
        ],
        (up_weight, gate_row, h1, w_query, w_key, w_value, w_out),
        [SMEM, SMEM] + [full] * 5,
        3 * head_flops + 6 * tokens * width * flat,
    )
    up_grad = dot_nt(og, after(w_down, a_pair))

    step = half // AG_CHUNKS
    a_near = [a_pair[c * step : (c + 1) * step] for c in range(AG_CHUNKS)]
    a_far = [swap_y(v) for v in a_near]
    near = [
        x_own[c * step : (c + 1) * step] + dot(v.astype(BF16), w_out_all[: 2 * flat])
        for c, v in enumerate(a_near)
    ]
    og_t = columns(after(og, up_grad), Z_FIRST).T
    resids = [
        n + dot(low_after_wire(after(f, og_t, *near)), w_out_all[2 * flat :])
        for n, f in zip(near, a_far)
    ]
    resid = jnp.concatenate(resids, 0)
    h2 = core_gather(1, resid, gain_mlp)

    h_t = columns(h2, X_FIRST).T if rows % DH else None
    act, dpre, dh2_part, out_part, dh2_far, _, _, d_pre, u_pre = feed(
        2, dp, h2, og_t, h_t, w_up, w_down, up_grad
    )

    dresid, dr, gain_mlp_sum = norm_back(4, dh2_part, dh2_far, resid, og_own, gain_mlp)
    gain_mlp_part = gain_mlp_sum[0]

    da = dot_nt(dr, w_out).astype(BF16)
    anywhere = pl.BlockSpec(memory_space=pl.ANY)
    ride = jax.ShapeDtypeStruct((quarter, units), F32)
    o_shape = jax.ShapeDtypeStruct((cut, flat), F32)
    dq16, dk16, dv16, gate_rows, o_pre, d_rode, u_rode, out_far = attention_call(
        attention_back_kernel,
        5,
        [
            act_b16, act_b16, act_b16, zin_shape, o_shape, ride, ride,
            jax.ShapeDtypeStruct((half, width), F32),
        ],
        [full] * 5 + [anywhere] * 3,
        [pltpu.VMEM((tokens, flat), F32)] * 3
        + [pltpu.VMEM((cut, flat), F32)]
        + [dma((6,)), dma((6,))],
        (
            down_weight, gate_row, qh, kh, vh, da, local, memory, zin,
            blocks_for(dr, Z_FIRST), a16, d_pre, u_pre, out_part,
        ),
        [SMEM, SMEM] + [full] * 9 + [anywhere] * 3,
        9 * head_flops,
    )
    gate_part = jnp.sum(gate_rows.reshape(segs, heads, DH), axis=(0, 2)) * gate * (1.0 - gate)

    eighth = quarter // 2
    d3 = d_pre[quarter : quarter + eighth] + d_rode[:eighth]
    close = near_units(dp, units)
    u3 = u_rode[:eighth] + jnp.where(
        jnp.arange(units)[None, :] < close, u_pre[quarter : quarter + eighth], u_pre[eighth:quarter]
    )
    h1_t = columns(h1, X_FIRST).T if rows % DH else None
    lane = jnp.pad(gate_part, (0, width - heads))
    vec = jnp.zeros((8, width), F32).at[1].set(gain_mlp_part).at[2].set(lane)
    (
        w_query_grad, w_key_grad, w_value_grad, w_out_rows, vec, _, d3, u3, outputs, input_grad
    ) = tail(
        7, dp, h1, h1_t, (dq16, dk16, dv16), (w_query, w_key, w_value), o_pre, gain_attn, vec,
        d3, u3, (resid, out_part, out_far, dresid, x_own),
    )
    w_out_grad = w_out_rows.T

    def finish(pre, rode, got, order):
        masks, _ = halving(dp, order)
        value = pre[quarter + eighth :] + rode[eighth:] + got
        for m in masks[3:]:
            n = value.shape[0] // 2
            value = value[n:] + swap_dp(value[:n], m)
        return value

    w_down_grad = finish(d_pre, d_rode, d3, Z_FIRST).T
    w_up_grad = finish(u_pre, u_rode, u3, X_FIRST)

    gain_attn_grad = lax.dynamic_slice_in_dim(vec[0], di * rows, rows, 0)
    gain_mlp_grad = lax.dynamic_slice_in_dim(vec[1], di * rows, rows, 0)
    gate_grad = vec[2, :heads]

    return (
        outputs,
        input_grad,
        gain_attn_grad,
        w_query_grad,
        w_key_grad,
        w_value_grad,
        gate_grad,
        w_out_grad,
        gain_mlp_grad,
        w_up_grad,
        w_down_grad,
    )


def solution(mesh):
    placed = (
        P("dp", None),
        P(),
        P(None, "tensor"),
        P(None, "tensor"),
        P(None, "tensor"),
        P("tensor"),
        P("tensor", None),
        P(),
        P(None, "tensor"),
        P("tensor", None),
        P(),
        P("dp", None),
    )
    return jax.shard_map(
        body,
        mesh=mesh,
        in_specs=placed,
        out_specs=(
            P("dp", None),
            P("dp", None),
            P("dp"),
            P("dp", "tensor"),
            P("dp", "tensor"),
            P("dp", "tensor"),
            P("tensor"),
            P("tensor", "dp"),
            P("dp"),
            P("dp", "tensor"),
            P("tensor", "dp"),
        ),
        check_vma=False,
    )
```

```python
import functools

import jax
import jax.numpy as jnp
from jax import lax
from jax.experimental import pallas as pl
from jax.experimental.pallas import tpu as pltpu
from jax.sharding import PartitionSpec as P

DH = 128
SEG = 512
DEPTH = 5
EPS = 1e-06

F32 = jnp.float32
BF16 = jnp.bfloat16

AG_CHUNKS = 1
Z_FIRST = (1, 0)
X_FIRST = (0, 1)


def feature_map(values):
    return jnp.where(values > 0, values + 1.0, jnp.exp(jnp.minimum(values, 0.0)))


def feature_slope(values):
    return jnp.where(values > 0, 1.0, jnp.exp(jnp.minimum(values, 0.0)))


def ancestor_table(seg_parent):
    seg_total = seg_parent.shape[0]
    columns = jnp.arange(seg_total, dtype=jnp.int32)
    current = seg_parent
    lineage_table = jnp.zeros((seg_total, seg_total), F32)
    for _ in range(DEPTH):
        onehot = current[:, None] == columns[None, :]
        lineage_table = lineage_table + onehot.astype(F32)
        lifted = jnp.sum(jnp.where(onehot, seg_parent[None, :], 0), axis=1)
        current = jnp.where(current >= 0, lifted, -1)
    return lineage_table


def dot(a, b):
    return jnp.dot(a, b, preferred_element_type=F32)


def dot_t(a, b):
    return lax.dot_general(a, b, (((0,), (0,)), ((), ())), preferred_element_type=F32)


def dot_nt(a, b):
    return lax.dot_general(a, b, (((1,), (1,)), ((), ())), preferred_element_type=F32)


def after(value, *earlier):
    return lax.optimization_barrier((value, earlier))[0]


def nbytes(*arrays):
    return sum(a.size * a.dtype.itemsize for a in arrays)


def copy_kernel(ids_ref, in_ref, out_ref):
    out_ref[...] = in_ref[...]


def block_columns(v, ids, size):
    if size % 128:
        return jnp.concatenate([lax.dynamic_slice_in_dim(v, i * size, size, 1) for i in ids], 1)
    height, width = v.shape
    return pl.pallas_call(
        copy_kernel,
        out_shape=jax.ShapeDtypeStruct(v.shape, v.dtype),
        grid_spec=pltpu.PrefetchScalarGridSpec(
            num_scalar_prefetch=1,
            grid=(width // size,),
            in_specs=[pl.BlockSpec((height, size), lambda k, ids: (0, ids[k]))],
            out_specs=pl.BlockSpec((height, size), lambda k, ids: (0, k)),
        ),
        cost_estimate=pl.CostEstimate(flops=0, transcendentals=0, bytes_accessed=2 * nbytes(v)),
    )(jnp.stack(ids), v)


SMEM = pl.BlockSpec(memory_space=pltpu.SMEM)


def causal_mask():
    row = lax.broadcasted_iota(jnp.int32, (SEG, SEG), 0)
    col = lax.broadcasted_iota(jnp.int32, (SEG, SEG), 1)
    return row >= col


def softmax_rows(q, k, scale):
    scores = dot_nt(q, k) * scale
    scores = jnp.where(causal_mask(), scores, -1e30)
    top = jnp.max(scores, axis=-1, keepdims=True)
    e = jnp.exp(scores - top)
    return e * (1.0 / jnp.sum(e, axis=-1, keepdims=True))


def head_part(heads, p):
    s, h = p // heads, p % heads
    return pl.ds(pl.multiple_of(s * SEG, SEG), SEG), pl.ds(pl.multiple_of(h * DH, DH), DH)


def matrix_part(p):
    return pl.ds(pl.multiple_of(p * DH, DH), DH)


def weighted(w_ref, p, heads, segs, blocks_ref):
    s, h = p // heads, p % heads
    pairs = segs * heads
    big = jnp.zeros((DH, DH), F32)
    small = jnp.zeros((1, DH), F32)
    for d in range(blocks_ref.shape[0]):
        for n in range(segs):
            w = w_ref[s, d * segs + n]
            o = n * heads + h
            big = big + w * blocks_ref[d, matrix_part(o), :]
            small = small + w * blocks_ref[d, pl.ds(pairs * DH + o, 1), :]
    return big, small


def spread_order(dp):
    low = [0]
    for b in reversed(range(1, dp.bit_length() - 1)):
        low = low + [v ^ (1 << b) for v in low]
    return low + [v ^ 1 for v in low]


def greet(*peers):
    barrier = pltpu.get_barrier_semaphore()
    for peer in peers:
        pl.semaphore_signal(barrier, inc=1, device_id=peer, device_id_type=pl.DeviceIdType.MESH)
    pl.semaphore_wait(barrier, len(peers))


def dp_peers(dp):
    me = lax.axis_index("dp")
    return [{"dp": me ^ (1 << b)} for b in range(dp.bit_length() - 1)]


def tensor_peer(mask):
    return {"tensor": lax.axis_index("tensor") ^ mask}


def preload(kernel, ins, which):
    def wrapped(*refs):
        extra = refs[len(refs) - len(which) - 1 :]
        refs = list(refs[: len(refs) - len(which) - 1])
        loads = {}
        for k, i in enumerate(which):
            loads[i] = pltpu.make_async_copy(refs[i], extra[k], extra[-1].at[k])
            loads[i].start()
            refs[i] = extra[k]

        def ready(*places):
            for i in places or tuple(loads):
                loads.pop(i).wait()

        kernel(ready, *refs)

    scratch = [pltpu.VMEM(ins[i].shape, ins[i].dtype) for i in which]
    return wrapped, scratch + [pltpu.SemaphoreType.DMA((len(which),))]


def halving(dp, order):
    masks = [1 << b for b in order]
    masks += [1 << b for b in range(len(order), dp.bit_length() - 1)]
    seq = [0]
    for m in reversed(masks):
        seq = [m ^ v for v in seq] + seq
    return masks, seq


def near_units(dp, units):
    return units // 4 if dp == 8 else units


def block_of(ref, dp, order, k):
    rows = ref.shape[1] // dp
    if rows % DH:
        return ref[:, k * rows : (k + 1) * rows]
    at = (lax.axis_index("dp") ^ halving(dp, order)[1][k]) * rows
    return ref[:, pl.ds(pl.multiple_of(at, rows), rows)]


def remote(src, dst, send_sem, recv_sem, peer):
    return pltpu.make_async_remote_copy(
        src_ref=src,
        dst_ref=dst,
        send_sem=send_sem,
        recv_sem=recv_sem,
        device_id=peer,
        device_id_type=pl.DeviceIdType.MESH,
    )


def spread(dp, blocks_ref, send_sem, recv_sem, compute, then=None):
    me = lax.axis_index("dp")
    slot = {j: k for k, j in enumerate(spread_order(dp))}
    copies = {}

    def send(j, mask):
        to = j ^ mask
        k = slot[to]
        copies[to] = pltpu.make_async_remote_copy(
            src_ref=blocks_ref.at[slot[j]],
            dst_ref=blocks_ref.at[k],
            send_sem=send_sem.at[k],
            recv_sem=recv_sem.at[k],
            device_id={"dp": me ^ mask},
            device_id_type=pl.DeviceIdType.MESH,
        )
        copies[to].start()

    bits = [1 << b for b in range(1, dp.bit_length() - 1)]
    for m in bits:
        send(0, m)
    send(0, 1)
    compute()
    for m in bits:
        copies[m].wait_recv()
        if m == bits[-1]:
            near = [0, m]
            for n in reversed(bits[:-1]):
                for j in near[1:]:
                    send(j, n)
                near = near + [n] + [j ^ n for j in near[1:]]
                if n != bits[0]:
                    for j in near:
                        if j & n and j != n:
                            copies[j].wait_recv()
        send(m, 1)
    if then is not None:
        then()
    last = [j for j in near if j and j not in bits]
    for j in last:
        if j & bits[0] or len(bits) == 1:
            copies[j].wait_recv()
        send(j, 1)
    for j in near:
        copies[j ^ 1].wait_recv()
    for c in copies.values():
        c.wait_send()


W_CHUNKS = 4


def attention_kernel(
    dp, heads, segs, scale, ready, w_ref, g_ref, h_ref, wq_ref, wk_ref, wv_ref, wo_ref,
    q_ref, k_ref, v_ref, a16_ref, pair_ref, local_ref, mem_ref, zin_ref, all_ref,
    wf_ref, asend_ref, w_send, w_recv, a_send, a_recv, blocks_ref, send_sem, recv_sem,
):
    pairs = segs * heads
    flat = heads * DH
    half = segs * SEG // 2
    core, far = tensor_peer(1), tensor_peer(2)
    greet(*dp_peers(dp), core, far)

    size = flat // W_CHUNKS
    w_copies = {}

    def w_send_chunk(j, c, to, peer):
        rows = pl.ds(c * size, size)
        k = (to - 1) * W_CHUNKS + c
        w_copies[to, c] = remote(
            wf_ref.at[j, rows, :], wf_ref.at[to, rows, :], w_send.at[k], w_recv.at[k], peer
        )
        w_copies[to, c].start()

    def w_done(to, c):
        rows = slice(c * size, (c + 1) * size)
        w_copies[to, c].wait_recv()
        all_ref[to * flat + c * size : to * flat + (c + 1) * size, :] = wf_ref[to, rows, :].astype(
            BF16
        )

    ready(6)
    for c in range(W_CHUNKS):
        rows = slice(c * size, (c + 1) * size)
        wf_ref[0, rows, :] = wo_ref[rows, :].astype(F32)
        w_send_chunk(0, c, 2, far)
        w_send_chunk(0, c, 1, core)
    all_ref[:flat, :] = wo_ref[...]

    def project(matrix_ref, out_ref):
        @pl.loop(0, segs * SEG // 256)
        def _(i):
            rows = pl.ds(pl.multiple_of(i * 256, 256), 256)
            out_ref[rows, :] = dot(h_ref[rows, :], matrix_ref[...]).astype(BF16)

    ready()
    project(wk_ref, k_ref)
    project(wv_ref, v_ref)

    @pl.loop(0, pairs)
    def _(p):
        at = head_part(heads, p)
        sk = feature_map(k_ref[at].astype(F32))
        blocks_ref[0, matrix_part(p), :] = dot_t(sk.astype(BF16), v_ref[at])
        blocks_ref[0, pl.ds(pairs * DH + p, 1), :] = jnp.sum(sk, axis=0, keepdims=True)

    def compute():
        project(wq_ref, q_ref)

        @pl.loop(0, pairs)
        def _(p):
            at = head_part(heads, p)
            probs = softmax_rows(q_ref[at], k_ref[at], scale)
            local_ref[at] = dot(probs.astype(BF16), v_ref[at])

    spread(dp, blocks_ref, send_sem, recv_sem, compute)

    @pl.loop(0, pairs)
    def _(p):
        at = head_part(heads, p)
        mem, zin = weighted(w_ref, p, heads, segs, blocks_ref)
        mem_ref[matrix_part(p), :] = mem
        zin_ref[pl.ds(p, 1), :] = zin
        g = g_ref[0, p % heads]
        sq = feature_map(q_ref[at].astype(F32))
        den = jnp.sum(sq * zin, axis=-1, keepdims=True) + 1.0
        retrieved = dot(sq.astype(BF16), mem.astype(BF16)) / den
        a16_ref[at] = (g * retrieved + (1.0 - g) * local_ref[at]).astype(BF16)

    asend_ref[...] = a16_ref[half:, :].astype(F32)
    a_copy = remote(asend_ref, pair_ref.at[:, pl.ds(flat, flat)], a_send, a_recv, core)
    a_copy.start()
    pair_ref[:, :flat] = a16_ref[:half, :].astype(F32)
    for c in range(W_CHUNKS):
        w_done(1, c)
    a_copy.wait_recv()
    for c in range(W_CHUNKS):
        w_copies[2, c].wait_recv()
        w_send_chunk(2, c, 3, core)
        rows = slice(c * size, (c + 1) * size)
        all_ref[2 * flat + c * size : 2 * flat + (c + 1) * size, :] = wf_ref[2, rows, :].astype(BF16)
    for c in range(W_CHUNKS):
        w_done(3, c)
    for copy in w_copies.values():
        copy.wait_send()
    a_copy.wait_send()


def attention_back_kernel(
    dp, heads, segs, scale, ready, w_ref, g_ref, q_ref, k_ref, v_ref, da_ref, local_ref, mem_ref,
    zin_ref, dr_ref, a16_ref, d_pre_ref, u_pre_ref, out_part_ref,
    dq_ref, dk_ref, dv_ref, gate_ref, o_pre_ref, d_rode_ref, u_rode_ref, out_far_ref,
    dqm_ref, dkl_ref, dvl_ref, os_ref, ride_send, ride_recv, blocks_ref, send_sem, recv_sem,
):
    pairs = segs * heads
    me = lax.axis_index("dp")
    far = tensor_peer(2)
    greet(*dp_peers(dp), far)
    legs = [
        (d_pre_ref, d_rode_ref, {"dp": me ^ 1}),
        (out_part_ref, out_far_ref, far),
        (os_ref, o_pre_ref, {"dp": me ^ 2}),
    ]
    quarter, units = d_rode_ref.shape
    eighth = quarter // 2
    legs[0] = (d_pre_ref.at[pl.ds(0, quarter), :], d_rode_ref, {"dp": me ^ 1})
    near = near_units(dp, units)
    cols = pl.ds(0, near)
    legs.append((u_pre_ref.at[pl.ds(0, quarter), cols], u_rode_ref.at[:, cols], {"dp": me ^ 2}))
    if near < units:
        cols = pl.ds(near, units - near)
        for k in range(2):
            legs.append(
                (
                    u_pre_ref.at[pl.ds(2 * k * eighth, eighth), cols],
                    u_rode_ref.at[pl.ds(k * eighth, eighth), cols],
                    {"dp": me ^ 4},
                )
            )
    riders = [
        remote(src, dst, ride_send.at[i], ride_recv.at[i], peer)
        for i, (src, dst, peer) in enumerate(legs)
    ]
    o_rider = riders[2]
    plain = riders[:2] + riders[3:]
    for r in riders[:2] + riders[3:4]:
        r.start()
    ready()

    @pl.loop(0, pairs)
    def _(p):
        at = head_part(heads, p)
        g = g_ref[0, p % heads]
        qf = q_ref[at].astype(F32)
        sq = feature_map(qf)
        sq16 = sq.astype(BF16)
        mem16 = mem_ref[matrix_part(p), :].astype(BF16)
        zin = zin_ref[pl.ds(p, 1), :]
        inv_den = 1.0 / (jnp.sum(sq * zin, axis=-1, keepdims=True) + 1.0)
        retrieved = dot(sq16, mem16) * inv_den
        da = da_ref[at].astype(F32)
        gate_ref[pl.ds(p, 1), :] = jnp.sum(da * (retrieved - local_ref[at]), axis=0, keepdims=True)
        dnum = g * da * inv_den
        dden = -jnp.sum(dnum * retrieved, axis=-1, keepdims=True)
        dnum16 = dnum.astype(BF16)
        blocks_ref[0, matrix_part(p), :] = dot_t(sq16, dnum16)
        blocks_ref[0, pl.ds(pairs * DH + p, 1), :] = jnp.sum(sq * dden, axis=0, keepdims=True)
        dsq = dot_nt(dnum16, mem16) + dden * zin
        dqm_ref[at] = dsq * feature_slope(qf)

    rows = dr_ref.shape[1] // dp
    half_blocks = dp // 2

    def compute():
        for j in range(half_blocks):
            os_ref[j * rows : (j + 1) * rows, :] = dot_t(
                block_of(dr_ref, dp, Z_FIRST, j), a16_ref[...]
            )

        @pl.loop(0, pairs)
        def _(p):
            at = head_part(heads, p)
            g = g_ref[0, p % heads]
            q, k, v, da = q_ref[at], k_ref[at], v_ref[at], da_ref[at]
            probs = softmax_rows(q, k, scale)
            dprobs = (1.0 - g) * dot_nt(da, v)
            inner = jnp.sum(dprobs * probs, axis=-1, keepdims=True)
            ds16 = (probs * (dprobs - inner)).astype(BF16)
            dq_ref[at] = (dot(ds16, k) * scale + dqm_ref[at]).astype(BF16)
            dkl_ref[at] = dot_t(ds16, q) * scale
            dvl_ref[at] = (1.0 - g) * dot_t(probs.astype(BF16), da)

    def then():
        o_rider.start()
        for r in riders[4:]:
            r.start()

    spread(dp, blocks_ref, send_sem, recv_sem, compute, then)

    @pl.loop(0, pairs)
    def _(p):
        at = head_part(heads, p)
        dd, dz = weighted(w_ref, p, heads, segs, blocks_ref)
        dd16 = dd.astype(BF16)
        kf = k_ref[at].astype(F32)
        dsk = dot_nt(v_ref[at], dd16) + dz
        dk_ref[at] = (dkl_ref[at] + dsk * feature_slope(kf)).astype(BF16)
        dv_ref[at] = (dvl_ref[at] + dot(feature_map(kf).astype(BF16), dd16)).astype(BF16)

    o_rider.wait()
    for j in range(half_blocks):
        o_pre_ref[j * rows : (j + 1) * rows, :] += dot_t(
            block_of(dr_ref, dp, Z_FIRST, half_blocks + j), a16_ref[...]
        )
    for r in plain:
        r.wait()


ROWS = 128


def tail_items(flat):
    full = slice(0, flat)
    return [
        (0, full), (1, full), (2, slice(0, flat // 2)), (2, slice(flat // 2, flat)), (3, full)
    ]


def tail_kernel(
    dp, turn, order, o_order, ready,
    h_ref, dq_ref, dk_ref, dv_ref, wq_ref, wk_ref, wv_ref, o_pre_ref, gain_ref, vec_ref,
    d3_ref, u3_ref, resid_hbm, out_part_hbm, out_far_hbm, dresid_hbm, x_hbm,
    gq_ref, gk_ref, gv_ref, go_ref, vec_out_ref, far_ref, d3_got_ref, u3_got_ref, out_hbm, dx_hbm,
    part_ref, cs_ref, cr_ref, in_ref, own_ref, other_ref, turn_ref, vec_got_ref,
    c_send, c_recv, y_send, y_recv, ride_send, ride_recv, e_send, e_recv, v_send, v_recv,
    in_sem, st_sem, turn_sem, free_sem, *bufs,
):
    me = lax.axis_index("dp")
    side = lax.axis_index("tensor") % 2
    core, far = tensor_peer(1), tensor_peer(2)
    greet(*dp_peers(dp), core, far)
    masks, _ = halving(dp, order)
    o_masks, _ = halving(dp, o_order)
    steps = len(masks)
    half, width = far_ref.shape
    rows = width // dp
    chunks = half // ROWS
    ht_ref = bufs[-1] if turn else h_ref
    depth = in_ref.shape[0]
    flat = dq_ref.shape[1]
    lhs = (dq_ref, dk_ref, dv_ref)
    outs = (gq_ref, gk_ref, gv_ref, go_ref)
    items = tail_items(flat)
    copies = {}

    def buffers(i, step):
        k = 2 * (i * steps + step)
        return bufs[k], bufs[k + 1]

    def term(i, step):
        lo = rows * sum(dp >> (n + 1) for n in range(step))
        count = rows * (dp >> (step + 1)) if step < steps else rows
        start = 0
        which, cols = items[i]
        if which < 3:
            value = dot(ht_ref[lo : lo + count, :], lhs[which][:, cols])
        else:
            base = rows * (dp // 2)
            value = o_pre_ref[lo - base : lo - base + count, :]
            start = 1
        for n in range(start, step):
            at = lo - rows * sum(dp >> (m + 1) for m in range(n + 1))
            value = value + buffers(i, n)[1][at : at + count, :]
        return value

    def advance(i, step):
        which, cols = items[i]
        if step > (1 if which == 3 else 0):
            copies[i, step - 1].wait_recv()
        if step == steps:
            outs[which][:, cols] = term(i, step)
            return
        send, recv = buffers(i, step)
        send[...] = term(i, step)
        mask = (o_masks if which == 3 else masks)[step]
        k = i * steps + step
        copies[i, step] = remote(send, recv, e_send.at[k], e_recv.at[k], {"dp": me ^ mask})
        copies[i, step].start()

    third = {"dp": me ^ masks[2]}
    units = u3_ref.shape[1]
    near = near_units(dp, units)
    cols = pl.ds(0, near)
    legs = [(d3_ref, d3_got_ref, third), (u3_ref.at[:, cols], u3_got_ref.at[:, cols], third)]
    if near < units:
        cols = pl.ds(near, units - near)
        legs.append((u3_ref.at[:, cols], u3_got_ref.at[:, cols], {"dp": me ^ 2}))
    riders = [
        remote(src, dst, ride_send.at[i], ride_recv.at[i], peer)
        for i, (src, dst, peer) in enumerate(legs)
    ]
    out_item = len(items) - 1
    ready(7)
    advance(out_item, 1)
    for r in reversed(riders):
        r.start()

    def block_load(j):
        at = (me ^ halving(dp, order)[1][j]) * rows
        return pltpu.make_async_copy(
            h_ref.at[:, pl.ds(pl.multiple_of(at, rows), rows)],
            turn_ref.at[j % 2],
            turn_sem.at[j % 2],
        )

    def turn_blocks(lo, hi):
        for j in range(lo, hi if turn else lo):
            block_load(j).wait()
            ht_ref[j * rows : (j + 1) * rows, :] = turn_ref[j % 2].T
            if j + 2 < dp:
                block_load(j + 2).start()

    for j in range(2 if turn else 0):
        block_load(j).start()
    ready()
    turn_blocks(0, dp // 2)
    for i in range(out_item):
        advance(i, 0)

    def part_rows(c):
        return pl.ds(c * ROWS, ROWS)

    def core_wire(c):
        return remote(cs_ref.at[c], cr_ref.at[c], c_send.at[c], c_recv.at[c], core)

    def core_free():
        pl.semaphore_signal(free_sem, inc=1, device_id=core, device_id_type=pl.DeviceIdType.MESH)

    def far_wire(c):
        return remote(part_ref.at[c], far_ref.at[part_rows(c), :], y_send.at[c], y_recv.at[c], far)

    def back(lo):
        return sum(
            dot_nt(v[lo : lo + 2 * ROWS, :], w[...])
            for v, w in zip(lhs, (wq_ref, wk_ref, wv_ref))
        )

    for c in range(0, chunks, 2):
        value = back(half + c * ROWS)
        for k in range(2):
            cs_ref[c + k] = value[k * ROWS : (k + 1) * ROWS, :]
            core_wire(c + k).start()
    for c in range(0, chunks, 2):
        value = back(c * ROWS)
        for k in range(2):
            core_wire(c + k).wait()
            part_ref[c + k] = value[k * ROWS : (k + 1) * ROWS, :] + cr_ref[c + k]
            far_wire(c + k).start()
    core_free()

    def both_cores(sources, compute, dst_hbm):
        def loads(c):
            k = c % depth
            return [
                pltpu.make_async_copy(src.at[part_rows(c), :], in_ref.at[k, i], in_sem.at[k, i])
                for i, src in enumerate(sources)
            ]

        def begin(c):
            if c < chunks:
                for load in loads(c):
                    load.start()

        def store(src_ref, which, c, k):
            at = pl.ds(pl.multiple_of(which * half + c * ROWS, ROWS), ROWS)
            return pltpu.make_async_copy(src_ref, dst_hbm.at[at, :], st_sem.at[k])

        pl.semaphore_wait(free_sem, 1)
        for c in range(depth):
            begin(c)
        for c in range(chunks):
            for load in loads(c):
                load.wait()
            value = compute(c, *(in_ref[c % depth, i] for i in range(3))).astype(BF16)
            if c:
                store(own_ref, side, c - 1, 0).wait()
            own_ref[...] = value
            store(own_ref, side, c, 0).start()
            cs_ref[c] = value.astype(F32)
            core_wire(c).start()
            begin(c + depth)
        for c in range(chunks):
            core_wire(c).wait()
            if c:
                store(other_ref, 1 - side, c - 1, 1).wait()
            other_ref[...] = cr_ref[c].astype(BF16)
            store(other_ref, 1 - side, c, 1).start()
        store(own_ref, side, chunks - 1, 0).wait()
        store(other_ref, 1 - side, chunks - 1, 1).wait()

    def output_rows(c, a, b, d):
        return a + b + d

    def input_rows(c, there, dresid, x):
        grad = part_ref[c] + there
        inv = lax.rsqrt(jnp.mean(x * x, axis=-1, keepdims=True) + EPS)
        gs = grad * gain_ref[...]
        inner = jnp.mean(gs * x, axis=-1, keepdims=True)
        vec_out_ref[0:1, :] += jnp.sum(grad * x * inv, axis=0, keepdims=True)
        return dresid + inv * gs - x * inv * inv * inv * inner

    turn_blocks(dp // 2, dp)
    if steps == 3:
        advance(out_item, 2)
    both_cores((resid_hbm, out_part_hbm, out_far_hbm), output_rows, out_hbm)
    core_free()
    if steps == 3:
        for i, step in ((0, 1), (1, 1), (0, 2), (2, 1), (1, 2)):
            advance(i, step)
        rest = ((3, 1), (2, 2), (3, 2))
    else:
        for step in range(1, steps):
            for i in range(len(items)):
                if step > 1 or i < out_item:
                    advance(i, step)
        rest = ()
    last = [(i, steps) for i in (out_item,) + tuple(range(out_item))]

    for c in range(chunks):
        far_wire(c).wait()
    vec_out_ref[...] = vec_ref[...]
    both_cores((far_ref, dresid_hbm, x_hbm), input_rows, dx_hbm)
    for i, step in rest:
        advance(i, step)

    for k, peer in enumerate([core] + dp_peers(dp)):
        hop = remote(vec_out_ref, vec_got_ref.at[k], v_send.at[k], v_recv.at[k], peer)
        hop.start()
        hop.wait()
        got = vec_got_ref[k]
        if k == 0:
            got = jnp.where(lax.broadcasted_iota(jnp.int32, got.shape, 0) < 2, got, 0.0)
        vec_out_ref[...] += got
    for i, step in last:
        advance(i, step)
    for c in copies.values():
        c.wait_send()
    for r in riders:
        r.wait()


def tail(ident, dp, h1, h1_t, grads, weights, o_pre, gain, vec, d3, u3, streams):
    tokens, width = h1.shape
    turn = h1_t is None
    flat = grads[0].shape[1]
    half = tokens // 2
    rows = width // dp
    steps = dp.bit_length() - 1
    full = pl.BlockSpec(memory_space=pltpu.VMEM)
    anywhere = pl.BlockSpec(memory_space=pl.ANY)
    f32 = lambda *shape: jax.ShapeDtypeStruct(shape, F32)
    dma = pltpu.SemaphoreType.DMA
    bufs = []
    items = tail_items(flat)
    for which, cols in items:
        for step in range(steps):
            count = rows * (dp >> (step + 1)) if which < 3 or step else 8
            bufs += [pltpu.VMEM((count, cols.stop - cols.start), F32)] * 2
    chunks = half // ROWS
    b16 = jax.ShapeDtypeStruct((tokens, width), BF16)
    operands = (
        h1 if turn else h1_t, *grads, *weights, o_pre, gain[None, :], vec, d3, u3, *streams
    )
    kernel, held = preload(
        functools.partial(tail_kernel, dp, turn, X_FIRST, Z_FIRST),
        operands,
        range(1 if turn else 0, 10),
    )
    return pl.pallas_call(
        kernel,
        out_shape=[f32(rows, flat)] * 4
        + [f32(*vec.shape), f32(half, width), f32(*d3.shape), f32(*u3.shape), b16, b16],
        in_specs=[anywhere] * len(operands),
        out_specs=[full] * 5 + [anywhere] * 5,
        scratch_shapes=[
            pltpu.VMEM((chunks, ROWS, width), F32),
            pltpu.VMEM((chunks, ROWS, width), F32),
            pltpu.VMEM((chunks, ROWS, width), F32),
            pltpu.VMEM((2 if turn else 1, 3, ROWS, width), F32),
            pltpu.VMEM((ROWS, width), BF16),
            pltpu.VMEM((ROWS, width), BF16),
            pltpu.VMEM((2, tokens, rows) if turn else (8, DH), BF16),
            pltpu.VMEM((steps + 1,) + vec.shape, F32),
            dma((chunks,)), dma((chunks,)), dma((chunks,)), dma((chunks,)),
            dma((3,)), dma((3,)), dma((len(items) * steps,)), dma((len(items) * steps,)),
            dma((steps + 1,)), dma((steps + 1,)), dma((2, 3)), dma((2,)), dma((2,)),
            pltpu.SemaphoreType.REGULAR,
        ]
        + bufs
        + ([pltpu.VMEM((width, tokens), BF16)] if turn else [])
        + held,
        compiler_params=pltpu.CompilerParams(
            collective_id=ident, has_side_effects=True, vmem_limit_bytes=63 << 20
        ),
        cost_estimate=pl.CostEstimate(
            flops=12 * tokens * width * flat, transcendentals=0, bytes_accessed=96 << 20
        ),
    )(*operands)


def core_gather_kernel(norm, tiles, v_ref, gain_ref, out_ref, send_ref, recv_ref, send_sem, recv_sem):
    peer = tensor_peer(1)
    greet(peer)
    half = v_ref.shape[0]
    size = half // tiles
    copies = []
    for c in range(tiles):
        rows = slice(c * size, (c + 1) * size)
        v = v_ref[rows, :]
        if norm:
            inv = lax.rsqrt(jnp.mean(v * v, axis=-1, keepdims=True) + EPS)
            v = v * inv * gain_ref[...]
            send_ref[rows, :] = v
        out_ref[rows, :] = v.astype(BF16)
        src = send_ref if norm else v_ref
        copies.append(
            remote(
                src.at[rows, :], recv_ref.at[rows, :], send_sem.at[c], recv_sem.at[c], peer
            )
        )
        copies[-1].start()
    for c in range(tiles):
        rows = slice(c * size, (c + 1) * size)
        copies[c].wait_recv()
        out_ref[half + c * size : half + (c + 1) * size, :] = recv_ref[rows, :].astype(BF16)
    for c in copies:
        c.wait_send()


def core_gather(ident, v, gain=None):
    half, n = v.shape
    tiles = 4
    out = jax.ShapeDtypeStruct((2 * half, n), BF16)
    full = pl.BlockSpec(memory_space=pltpu.VMEM)
    norm = gain is not None
    return pl.pallas_call(
        functools.partial(core_gather_kernel, norm, tiles),
        out_shape=out,
        in_specs=[full, full],
        out_specs=full,
        scratch_shapes=[
            pltpu.VMEM((half, n) if norm else (8, DH), F32),
            pltpu.VMEM((half, n), F32),
            pltpu.SemaphoreType.DMA((tiles,)),
            pltpu.SemaphoreType.DMA((tiles,)),
        ],
        compiler_params=pltpu.CompilerParams(
            collective_id=ident, has_side_effects=True, vmem_limit_bytes=48 << 20
        ),
        cost_estimate=pl.CostEstimate(
            flops=0, transcendentals=0, bytes_accessed=nbytes(v, v, v, out)
        ),
    )(v, gain[None, :] if norm else jnp.zeros((8, DH), F32))


def norm_back_kernel(
    part_hbm, far_hbm, resid_hbm, grad_hbm, gain_ref, dresid_hbm, dr_ref, sum_ref,
    in_ref, og_ref, send_ref, recv_ref, c_send, c_recv, in_sem, og_sem, out_sem,
):
    peer = tensor_peer(1)
    greet(peer)
    half, width = dresid_hbm.shape
    chunks = half // ROWS
    sources = (part_hbm, far_hbm, resid_hbm)

    def rows(c):
        return pl.ds(c * ROWS, ROWS)

    def loads(c):
        k = c % 2
        wide = [
            pltpu.make_async_copy(src.at[rows(c), :], in_ref.at[k, i], in_sem.at[k, i])
            for i, src in enumerate(sources)
        ]
        return wide + [
            pltpu.make_async_copy(grad_hbm.at[rows(c), :], og_ref.at[k], og_sem.at[k])
        ]

    def wire(c):
        return remote(send_ref.at[c], recv_ref.at[c], c_send.at[c], c_recv.at[c], peer)

    def store(c):
        return pltpu.make_async_copy(send_ref.at[c], dresid_hbm.at[rows(c), :], out_sem.at[c])

    for c in range(2):
        for load in loads(c):
            load.start()
    sum_ref[...] = jnp.zeros_like(sum_ref)
    for c in range(chunks):
        k = c % 2
        for load in loads(c):
            load.wait()
        grad = in_ref[k, 0] + in_ref[k, 1]
        x = in_ref[k, 2]
        inv = lax.rsqrt(jnp.mean(x * x, axis=-1, keepdims=True) + EPS)
        gs = grad * gain_ref[...]
        inner = jnp.mean(gs * x, axis=-1, keepdims=True)
        sum_ref[0:1, :] += jnp.sum(grad * x * inv, axis=0, keepdims=True)
        value = og_ref[k].astype(F32) + inv * gs - x * inv * inv * inv * inner
        send_ref[c] = value
        wire(c).start()
        store(c).start()
        dr_ref[c * ROWS : (c + 1) * ROWS, :] = value.astype(BF16)
        if c + 2 < chunks:
            for load in loads(c + 2):
                load.start()
    for c in range(chunks):
        wire(c).wait()
        dr_ref[half + c * ROWS : half + (c + 1) * ROWS, :] = recv_ref[c].astype(BF16)
    for c in range(chunks):
        store(c).wait()


def norm_back(ident, part, far, resid, out_grad, gain):
    half, width = resid.shape
    chunks = half // ROWS
    outs = [
        jax.ShapeDtypeStruct((half, width), F32),
        jax.ShapeDtypeStruct((2 * half, width), BF16),
        jax.ShapeDtypeStruct((8, width), F32),
    ]
    full = pl.BlockSpec(memory_space=pltpu.VMEM)
    anywhere = pl.BlockSpec(memory_space=pl.ANY)
    dma = pltpu.SemaphoreType.DMA
    return pl.pallas_call(
        norm_back_kernel,
        out_shape=outs,
        in_specs=[anywhere] * 4 + [full],
        out_specs=[anywhere, full, full],
        scratch_shapes=[
            pltpu.VMEM((2, 3, ROWS, width), F32),
            pltpu.VMEM((2, ROWS, width), BF16),
            pltpu.VMEM((chunks, ROWS, width), F32),
            pltpu.VMEM((chunks, ROWS, width), F32),
            dma((chunks,)), dma((chunks,)), dma((2, 3)), dma((2,)), dma((chunks,)),
        ],
        compiler_params=pltpu.CompilerParams(
            collective_id=ident, has_side_effects=True, vmem_limit_bytes=48 << 20
        ),
        cost_estimate=pl.CostEstimate(
            flops=0, transcendentals=0, bytes_accessed=nbytes(part, far, resid, out_grad, *outs)
        ),
    )(part, far, resid, out_grad, gain[None, :])


TILE = 256
SLOTS = 4


def feed_kernel(
    dp, turn, ready, h_ref, ogt_ref, ht_ref, wup_hbm, wdn_hbm, ug_hbm,
    act_ref, dpre_ref, part_ref, part2_ref, far_ref, d_ref, u_ref, d_pre_ref, u_pre_ref,
    w_ref, ug_ref, ds_ref, us_ref, cs_ref, cr_ref,
    w_sem, ug_sem, d_send, d_recv, u_send, u_recv, c_send, c_recv, y_send, y_recv, free_sem,
):
    tokens, units = act_ref.shape
    half = tokens // 2
    width = h_ref.shape[1]
    cut = width // 2
    rows = width // dp
    me = lax.axis_index("dp")
    core, far = tensor_peer(1), tensor_peer(2)
    x_peer, z_peer = {"dp": me ^ 1}, {"dp": me ^ 2}
    greet(core, far, x_peer, z_peer)
    count = units // TILE

    load_w = pltpu.make_async_copy(wup_hbm, w_ref, w_sem)
    load_w.start()

    def tile_cols(t):
        return pl.ds(pl.multiple_of(t * TILE, TILE), TILE)

    def load_ug(t, k):
        return pltpu.make_async_copy(ug_hbm.at[:, tile_cols(t)], ug_ref.at[k], ug_sem.at[k])

    load_ug(0, 0).start()
    load_ug(1, 1).start()
    ready(0)
    for j in range(dp // 2 if turn else 0):
        ht_ref[j * rows : (j + 1) * rows, :] = block_of(h_ref, dp, X_FIRST, j).T
    ready()
    load_w.wait()

    def wire(t, k):
        cols = tile_cols(t)
        d = remote(ds_ref.at[k], d_ref.at[:, cols], d_send.at[t], d_recv.at[t], z_peer)
        u = remote(us_ref.at[k], u_ref.at[:, cols], u_send.at[t], u_recv.at[t], x_peer)
        return d, u

    def terms(t, k):
        cols = tile_cols(t)
        d, u = wire(t, k)
        ds_ref[k] = dot(ogt_ref[:cut, :], act_ref[:, cols])
        d.start()
        us_ref[k] = dot(ht_ref[:cut, :], dpre_ref[:, cols])
        u.start()

    @pl.loop(0, count)
    def _(t):
        k = t % 2
        cols = tile_cols(t)
        load_ug(t, k).wait()
        pre = dot(h_ref[...], w_ref[:, cols])
        c = 0.7978845608028654
        sq = pre * pre
        th = jnp.tanh(c * pre * (1.0 + 0.044715 * sq))
        mid = 0.5 * (1.0 + th)
        act_ref[:, cols] = (pre * mid).astype(BF16)
        slope = mid + 0.5 * pre * (1.0 - th * th) * (c * (1.0 + 0.134145 * sq))
        dpre_ref[:, cols] = (ug_ref[k] * slope).astype(BF16)

        @pl.when(t + 2 < count)
        def _():
            load_ug(t + 2, k).start()

        @pl.when(t < SLOTS)
        def _():
            terms(t, t)

    part_cols = width // 4

    def core_wire(c):
        return remote(cs_ref.at[c], cr_ref.at[c], c_send.at[c], c_recv.at[c], core)

    def far_wire(c):
        cols = pl.ds(c * part_cols, part_cols)
        return remote(part_ref.at[:, cols], far_ref.at[:, cols], y_send.at[c], y_recv.at[c], far)

    def summed(lhs_ref, transposed, out_ref, travels):
        def term(row, c):
            cols = slice(c * part_cols, (c + 1) * part_cols)
            lhs = lhs_ref[row * half : (row + 1) * half, :]
            if transposed:
                return dot_nt(lhs, w_ref[cols, :])
            return dot(lhs, w_ref[:, cols])

        for c in range(4):
            cs_ref[c] = term(1, c)
            core_wire(c).start()
        for c in range(4):
            part = term(0, c)
            core_wire(c).wait()
            out_ref[:, c * part_cols : (c + 1) * part_cols] = part + cr_ref[c]
            if travels:
                far_wire(c).start()

    summed(dpre_ref, True, part_ref, True)
    load_down = pltpu.make_async_copy(wdn_hbm, w_ref, w_sem)
    load_down.start()
    pl.semaphore_signal(free_sem, inc=1, device_id=core, device_id_type=pl.DeviceIdType.MESH)
    for j in range(dp // 2, dp if turn else 0):
        ht_ref[j * rows : (j + 1) * rows, :] = block_of(h_ref, dp, X_FIRST, j).T

    @pl.loop(SLOTS, count)
    def _(t):
        d, u = wire(t - SLOTS, t - SLOTS)
        d.wait_send()
        u.wait_send()
        terms(t, t - SLOTS)

    load_down.wait()
    pl.semaphore_wait(free_sem, 1)
    summed(act_ref, False, part2_ref, False)

    def load_got(src_ref, t, k):
        return pltpu.make_async_copy(src_ref.at[:, tile_cols(t)], ug_ref.at[k], ug_sem.at[k])

    def store_pre(dst_ref, t, k):
        return pltpu.make_async_copy(ug_ref.at[k], dst_ref.at[:, tile_cols(t)], ug_sem.at[k])

    @pl.loop(0, count)
    def _(t):
        d, u = wire(t, 0)

        @pl.when(t > 0)
        def _():
            store_pre(d_pre_ref, t - 1, 0).wait()
            store_pre(u_pre_ref, t - 1, 1).wait()

        d.wait_recv()
        load_got(d_ref, t, 0).start()
        u.wait_recv()
        load_got(u_ref, t, 1).start()
        load_got(d_ref, t, 0).wait()
        ug_ref[0] += dot(ogt_ref[cut:, :], act_ref[:, tile_cols(t)])
        store_pre(d_pre_ref, t, 0).start()
        load_got(u_ref, t, 1).wait()
        ug_ref[1] += dot(ht_ref[cut:, :], dpre_ref[:, tile_cols(t)])
        store_pre(u_pre_ref, t, 1).start()

    store_pre(d_pre_ref, count - 1, 0).wait()
    store_pre(u_pre_ref, count - 1, 1).wait()

    @pl.loop(count - SLOTS, count)
    def _(t):
        d, u = wire(t, t - (count - SLOTS))
        d.wait_send()
        u.wait_send()

    for c in range(4):
        far_wire(c).wait()


def feed(ident, dp, h2, og_t, h_t, w_up, w_down, up_grad):
    tokens, width = h2.shape
    units = w_up.shape[1]
    half = tokens // 2
    cut = width // 2
    count = units // TILE
    full = pl.BlockSpec(memory_space=pltpu.VMEM)
    anywhere = pl.BlockSpec(memory_space=pl.ANY)
    f32 = lambda *shape: jax.ShapeDtypeStruct(shape, F32)
    b16 = jax.ShapeDtypeStruct((tokens, units), BF16)
    dma = pltpu.SemaphoreType.DMA
    turn = h_t is None
    kernel = functools.partial(feed_kernel, dp, turn)
    if turn:

        def kernel(ready, h_ref, ogt_ref, *refs):
            feed_kernel(dp, turn, ready, h_ref, ogt_ref, refs[-1], *refs[:-1])

    operands = (h2, og_t, *([] if turn else [h_t]), w_up, w_down, up_grad)
    kernel, held = preload(kernel, operands, range(len(operands) - 3))
    return pl.pallas_call(
        kernel,
        out_shape=[b16, b16, f32(half, width), f32(half, width), f32(half, width)]
        + [f32(cut, units)] * 4,
        in_specs=[anywhere] * len(operands),
        out_specs=[full] * 4 + [anywhere] * 5,
        scratch_shapes=[
            pltpu.VMEM((width, units), BF16),
            pltpu.VMEM((2, tokens, TILE), F32),
            pltpu.VMEM((SLOTS, cut, TILE), F32),
            pltpu.VMEM((SLOTS, cut, TILE), F32),
            pltpu.VMEM((4, half, width // 4), F32),
            pltpu.VMEM((4, half, width // 4), F32),
            dma, dma((2,)), dma((count,)), dma((count,)), dma((count,)), dma((count,)),
            dma((4,)), dma((4,)), dma((4,)), dma((4,)), pltpu.SemaphoreType.REGULAR,
        ]
        + ([pltpu.VMEM((width, tokens), BF16)] if turn else [])
        + held,
        compiler_params=pltpu.CompilerParams(
            collective_id=ident, has_side_effects=True, vmem_limit_bytes=62 << 20
        ),
        cost_estimate=pl.CostEstimate(
            flops=10 * tokens * width * units, transcendentals=tokens * units,
            bytes_accessed=64 << 20,
        ),
    )(*operands)


def body(
    inputs,
    gain_attn,
    w_query,
    w_key,
    w_value,
    gate_logit,
    w_out,
    gain_mlp,
    w_up,
    w_down,
    seg_parent,
    out_grad,
):
    tokens, width = inputs.shape
    half = tokens // 2
    segs = tokens // SEG
    heads = w_query.shape[1] // DH
    pairs = segs * heads
    units = w_up.shape[1]
    flat = heads * DH
    scale = DH ** (-0.5)
    dp = lax.axis_size("dp")
    tn = lax.axis_size("tensor")
    rows = width // dp
    di = lax.axis_index("dp")
    core = lax.axis_index("tensor") % 2

    one = jnp.where(seg_parent[0] < tokens * dp, 1.0, 2.0)

    def low_after_wire(v):
        return (v * one).astype(BF16)

    def swap_core(v):
        return lax.ppermute(v, "tensor", [(i, i ^ 1) for i in range(tn)])

    def swap_y(v):
        return lax.ppermute(v, "tensor", [(i, i ^ 2) for i in range(tn)])

    def swap_dp(v, mask):
        return lax.ppermute(v, "dp", [(i, i ^ mask) for i in range(dp)])

    def columns(v, order):
        _, seq = halving(dp, order)
        return block_columns(v, [di ^ k for k in seq], rows)

    def blocks_for(v, order):
        return columns(v, order) if rows % DH else v

    cut = width // 2
    quarter = cut // 2

    def pick(v, index, axis):
        size = v.shape[axis] // 2
        return lax.dynamic_slice_in_dim(v, index * size, size, axis)

    def place(own, other, index, axis):
        return jnp.where(
            index == 0,
            jnp.concatenate([own, other], axis),
            jnp.concatenate([other, own], axis),
        )

    def inv_rms(v):
        return lax.rsqrt(jnp.mean(v * v, axis=-1, keepdims=True) + EPS)

    x_own = pick(inputs, core, 0).astype(F32)
    x_oth = pick(inputs, 1 - core, 0).astype(F32)
    inv_own = inv_rms(x_own)
    inv_oth = inv_rms(x_oth)
    h1 = jnp.concatenate(
        [
            (x_own * inv_own * gain_attn).astype(BF16),
            (x_oth * inv_oth * gain_attn).astype(BF16),
        ],
        0,
    )

    sub = segs // 2
    every = jnp.arange(seg_parent.shape[0], dtype=jnp.int32)
    sub_ids = jnp.arange(sub, dtype=jnp.int32)
    seg_local = jnp.concatenate([core * sub + sub_ids, (1 - core) * sub + sub_ids])
    order = spread_order(dp)
    ids = jnp.concatenate([(di ^ j) * segs + seg_local for j in order])
    mine_hot = (ids[:segs, None] == every[None, :]).astype(F32)
    ids_hot = (ids[:, None] == every[None, :]).astype(F32)
    lineage = ancestor_table(seg_parent)

    def weights_of(table):
        mine_rows = jnp.sum(mine_hot[:, :, None] * table[None], axis=1)
        return jnp.sum(mine_rows[:, None, :] * ids_hot[None], axis=-1)

    up_weight = weights_of(lineage)
    down_weight = weights_of(lineage.T)

    gate = jax.nn.sigmoid(gate_logit)
    gate_row = gate[None, :]

    og_own = pick(out_grad, core, 0)
    og = jnp.concatenate([og_own, pick(out_grad, 1 - core, 0)], 0)
    block_rows = pairs * DH + pairs
    act_f32 = jax.ShapeDtypeStruct((tokens, flat), F32)
    act_b16 = jax.ShapeDtypeStruct((tokens, flat), BF16)
    mem_shape = jax.ShapeDtypeStruct((pairs * DH, DH), F32)
    zin_shape = jax.ShapeDtypeStruct((pairs, DH), F32)
    full = pl.BlockSpec(memory_space=pltpu.VMEM)

    anywhere = pl.BlockSpec(memory_space=pl.ANY)

    def attention_call(kernel, ident, outs, out_specs, scratch, args, in_specs, flops):
        which = [i for i, spec in enumerate(in_specs) if spec is full]
        in_specs = [anywhere if spec is full else spec for spec in in_specs]
        wrapped, held = preload(functools.partial(kernel, dp, heads, segs, scale), args, which)
        return pl.pallas_call(
            wrapped,
            out_shape=outs,
            in_specs=in_specs,
            out_specs=out_specs,
            scratch_shapes=scratch
            + [
                pltpu.VMEM((dp, block_rows, DH), F32),
                pltpu.SemaphoreType.DMA((dp,)),
                pltpu.SemaphoreType.DMA((dp,)),
            ]
            + held,
            compiler_params=pltpu.CompilerParams(
                collective_id=ident, has_side_effects=True, vmem_limit_bytes=63 << 20
            ),
            cost_estimate=pl.CostEstimate(
                flops=flops, transcendentals=0, bytes_accessed=64 << 20
            ),
        )(*args)

    head_flops = 2 * segs * heads * SEG * SEG * DH
    dma = pltpu.SemaphoreType.DMA
    qh, kh, vh, a16, a_pair, local, memory, zin, w_out_all = attention_call(
        attention_kernel,
        0,
        [
            act_b16, act_b16, act_b16, act_b16,
            jax.ShapeDtypeStruct((half, 2 * flat), F32),
            act_f32, mem_shape, zin_shape,
            jax.ShapeDtypeStruct((4 * flat, width), BF16),
        ],
        [full] * 9,
        [
            pltpu.VMEM((4, flat, width), F32),
            pltpu.VMEM((half, flat), F32),
            dma((3 * W_CHUNKS,)), dma((3 * W_CHUNKS,)), dma, dma,
        ],
        (up_weight, gate_row, h1, w_query, w_key, w_value, w_out),
        [SMEM, SMEM] + [full] * 5,
        3 * head_flops + 6 * tokens * width * flat,
    )
    up_grad = dot_nt(og, after(w_down, a_pair))

    step = half // AG_CHUNKS
    a_near = [a_pair[c * step : (c + 1) * step] for c in range(AG_CHUNKS)]
    a_far = [swap_y(v) for v in a_near]
    near = [
        x_own[c * step : (c + 1) * step] + dot(v.astype(BF16), w_out_all[: 2 * flat])
        for c, v in enumerate(a_near)
    ]
    og_t = columns(after(og, up_grad), Z_FIRST).T
    resids = [
        n + dot(low_after_wire(after(f, og_t, *near)), w_out_all[2 * flat :])
        for n, f in zip(near, a_far)
    ]
    resid = jnp.concatenate(resids, 0)
    h2 = core_gather(1, resid, gain_mlp)

    h_t = columns(h2, X_FIRST).T if rows % DH else None
    act, dpre, dh2_part, out_part, dh2_far, _, _, d_pre, u_pre = feed(
        2, dp, h2, og_t, h_t, w_up, w_down, up_grad
    )

    dresid, dr, gain_mlp_sum = norm_back(4, dh2_part, dh2_far, resid, og_own, gain_mlp)
    gain_mlp_part = gain_mlp_sum[0]

    da = dot_nt(dr, w_out).astype(BF16)
    anywhere = pl.BlockSpec(memory_space=pl.ANY)
    ride = jax.ShapeDtypeStruct((quarter, units), F32)
    o_shape = jax.ShapeDtypeStruct((cut, flat), F32)
    dq16, dk16, dv16, gate_rows, o_pre, d_rode, u_rode, out_far = attention_call(
        attention_back_kernel,
        5,
        [
            act_b16, act_b16, act_b16, zin_shape, o_shape, ride, ride,
            jax.ShapeDtypeStruct((half, width), F32),
        ],
        [full] * 5 + [anywhere] * 3,
        [pltpu.VMEM((tokens, flat), F32)] * 3
        + [pltpu.VMEM((cut, flat), F32)]
        + [dma((6,)), dma((6,))],
        (
            down_weight, gate_row, qh, kh, vh, da, local, memory, zin,
            blocks_for(dr, Z_FIRST), a16, d_pre, u_pre, out_part,
        ),
        [SMEM, SMEM] + [full] * 9 + [anywhere] * 3,
        9 * head_flops,
    )
    gate_part = jnp.sum(gate_rows.reshape(segs, heads, DH), axis=(0, 2)) * gate * (1.0 - gate)

    eighth = quarter // 2
    d3 = d_pre[quarter : quarter + eighth] + d_rode[:eighth]
    close = near_units(dp, units)
    u3 = u_rode[:eighth] + jnp.where(
        jnp.arange(units)[None, :] < close, u_pre[quarter : quarter + eighth], u_pre[eighth:quarter]
    )
    h1_t = columns(h1, X_FIRST).T if rows % DH else None
    lane = jnp.pad(gate_part, (0, width - heads))
    vec = jnp.zeros((8, width), F32).at[1].set(gain_mlp_part).at[2].set(lane)
    (
        w_query_grad, w_key_grad, w_value_grad, w_out_rows, vec, _, d3, u3, outputs, input_grad
    ) = tail(
        7, dp, h1, h1_t, (dq16, dk16, dv16), (w_query, w_key, w_value), o_pre, gain_attn, vec,
        d3, u3, (resid, out_part, out_far, dresid, x_own),
    )
    w_out_grad = w_out_rows.T

    def finish(pre, rode, got, order):
        masks, _ = halving(dp, order)
        value = pre[quarter + eighth :] + rode[eighth:] + got
        for m in masks[3:]:
            n = value.shape[0] // 2
            value = value[n:] + swap_dp(value[:n], m)
        return value

    w_down_grad = finish(d_pre, d_rode, d3, Z_FIRST).T
    w_up_grad = finish(u_pre, u_rode, u3, X_FIRST)

    gain_attn_grad = lax.dynamic_slice_in_dim(vec[0], di * rows, rows, 0)
    gain_mlp_grad = lax.dynamic_slice_in_dim(vec[1], di * rows, rows, 0)
    gate_grad = vec[2, :heads]

    return (
        outputs,
        input_grad,
        gain_attn_grad,
        w_query_grad,
        w_key_grad,
        w_value_grad,
        gate_grad,
        w_out_grad,
        gain_mlp_grad,
        w_up_grad,
        w_down_grad,
    )


def solution(mesh):
    placed = (
        P("dp", None),
        P(),
        P(None, "tensor"),
        P(None, "tensor"),
        P(None, "tensor"),
        P("tensor"),
        P("tensor", None),
        P(),
        P(None, "tensor"),
        P("tensor", None),
        P(),
        P("dp", None),
    )
    return jax.shard_map(
        body,
        mesh=mesh,
        in_specs=placed,
        out_specs=(
            P("dp", None),
            P("dp", None),
            P("dp"),
            P("dp", "tensor"),
            P("dp", "tensor"),
            P("dp", "tensor"),
            P("tensor"),
            P("tensor", "dp"),
            P("dp"),
            P("dp", "tensor"),
            P("tensor", "dp"),
        ),
        check_vma=False,
    )
```
